32 devices in a mesh: pipe: 2 (over x), dir: 2 (over core), dp: 8 (over z, y).
Axes of the slice: x: 2, y: 2, z: 4, core: 2. Of those that a mesh axis runs over, the one named last changes fastest.
Arguments:
- chars: int32 [128, 16, 50], P('dp'), may hold values from 0 to 261
- lengths: int32 [128], P('dp'), may hold values from 1 to 16, as said below
- char_emb: float32 [262, 16], replicated, may hold values from -6 to 6
- conv_weight: float32 [112, 2048], P(None, ('dir', 'dp')), may hold values from -0.5 to 0.5
- conv_bias: float32 [2048], replicated, may hold values from -6 to 6
- highway_weight: float32 [2, 2048, 4096], P(None, None, ('dir', 'dp')), may hold values from -0.125 to 0.125
- highway_bias: float32 [2, 4096], replicated, may hold values from -6 to 6
- proj_weight: float32 [2048, 512], P(('dir', 'dp')), may hold values from -0.0625 to 0.0625
- proj_bias: float32 [512], replicated, may hold values from -6 to 6
- gate_weight: float32 [2, 2, 1024, 16384], P('pipe', 'dir', 'dp'), may hold values from -0.1875 to 0.1875
- gate_bias: float32 [2, 2, 16384], P('pipe', 'dir'), may hold values from -6 to 6
- cell_proj: float32 [2, 2, 4096, 512], P('pipe', 'dir', 'dp'), may hold values from -0.1875 to 0.1875
- cotangent: bfloat16 [2, 2, 128, 16, 512], P('pipe', 'dir', 'dp'), may hold values from -6 to 6
Outputs:
- activations: bfloat16 [2, 2, 128, 16, 512], P('pipe', 'dir', 'dp')
- char_emb_grad: float32 [262, 16], replicated
- conv_weight_grad: float32 [112, 2048], P(None, ('pipe', 'dir', 'dp'))
- conv_bias_grad: float32 [2048], replicated
- highway_weight_grad: float32 [2, 2048, 4096], P(None, None, ('pipe', 'dir', 'dp'))
- highway_bias_grad: float32 [2, 4096], replicated
- proj_weight_grad: float32 [2048, 512], P(('pipe', 'dir', 'dp'))
- proj_bias_grad: float32 [512], replicated
- gate_weight_grad: float32 [2, 2, 1024, 16384], P('pipe', 'dir', 'dp')
- gate_bias_grad: float32 [2, 2, 16384], P('pipe', 'dir', 'dp')
- cell_proj_grad: float32 [2, 2, 4096, 512], P('pipe', 'dir', 'dp')
The draws below stay inside these ranges and needn't reach their ends.
Inputs may be any that keep to these rules, and one draw needn't show every extreme that they name: `lengths`: in each aligned block of 8 sequences (one micro-batch of one index of dp), one sequence has 16 tokens.
All inputs are finite; a program needn't handle non-finite values.
Results may differ from the reference program's by a relative error of at most 0.023.
The reference program's roundings to bfloat16 on the way count: a program that leaves them out, or rounds other values in their place, can miss the bound.
Values may be sent and summed in bfloat16 or wider, within the bound.
A program may use at most 1.3125 GiB of HBM per device.

```python
import math
import jax
import jax.numpy as jnp
from jax import lax

D = 512
CELLS = 4096
GATES = 16384
FILTERS = 2048
CDIM = 16
CVOCAB = 262
CHARS = 50
KMAX = 7
LEN = 16
ROWS = 8
SEQS = 128


def draw_lengths(key, part):
    bucket_top = jnp.array([max(1, LEN // 8), max(1, LEN // 4), max(1, LEN // 2), LEN], jnp.int32)
    pick_key, size_key, full_key = jax.random.split(key, 3)
    bucket_roll = jax.random.randint(pick_key, (SEQS,), 0, 10)
    bucket = (bucket_roll >= 1).astype(jnp.int32) + (bucket_roll >= 2).astype(jnp.int32) + (bucket_roll >= 5).astype(jnp.int32)
    upper_value = bucket_top[bucket]
    lower_value = jnp.maximum(upper_value // 2, 1)
    lengths_drawn = jax.random.randint(size_key, (SEQS,), lower_value, upper_value + 1)
    full_place = jax.random.randint(full_key, (SEQS // ROWS,), 0, ROWS)
    row_index = jnp.arange(SEQS, dtype=jnp.int32)
    is_full = row_index % ROWS == jnp.repeat(full_place, ROWS)
    return jnp.where(is_full, LEN, lengths_drawn).astype(jnp.int32)


def set_ends(entries, stream_key, low, top_value):
    place = [jax.random.randint(jax.random.fold_in(stream_key, axis), (), 0, length) for axis, length in enumerate(entries.shape)]
    longest = entries.shape.index(max(entries.shape))
    beside = place[:longest] + [(place[longest] + 1) % entries.shape[longest]] + place[longest + 1:]
    return entries.at[tuple(place)].set(low).at[tuple(beside)].set(top_value)


def level_of(own_key, dims, cuts, low, top_value):
    gain, own = 1.0, jax.random.fold_in(own_key, 6)
    for axis_at, blocks in cuts:
        heights = jnp.exp(jax.random.uniform(jax.random.fold_in(own, axis_at), (blocks,), jnp.float32, low / len(cuts), top_value / len(cuts)))
        gain = gain * jnp.repeat(heights, dims[axis_at] // blocks).reshape([-1 if axis == axis_at else 1 for axis in range(len(dims))])
    return gain


def gaussian(key, shape, width, reach, cuts=(), kind=jnp.bfloat16):
    values = width * jax.random.normal(key, shape, jnp.float32)
    if cuts:
        values = values * level_of(key, shape, cuts, -0.22, 0.18)
    return jnp.clip(values, -reach, reach).astype(kind)


def setup_inputs(seed: int = 0) -> dict:
    key_of = jax.random.split(jax.random.key(seed), 14)
    chars = set_ends(jax.random.randint(key_of[0], (SEQS, LEN, CHARS), 0, CVOCAB), jax.random.fold_in(key_of[0], 1), 0, CVOCAB - 1).astype(jnp.int32)
    lengths = draw_lengths(jax.random.fold_in(key_of[13], 71), 0)
    char_emb = gaussian(key_of[2], (CVOCAB, CDIM), 1.0, 6.0, (), jnp.float32)
    conv_weight = gaussian(key_of[3], (KMAX * CDIM, FILTERS), (KMAX * CDIM) ** -0.5, 0.5, ((1, 16),), jnp.float32)
    conv_bias = gaussian(key_of[4], (FILTERS,), 1.0, 6.0, (), jnp.float32)
    highway_weight = gaussian(key_of[5], (2, FILTERS, 2 * FILTERS), FILTERS ** -0.5, 0.125, ((2, 16),), jnp.float32)
    highway_bias = gaussian(key_of[6], (2, 2 * FILTERS), 1.0, 6.0, (), jnp.float32)
    proj_weight = gaussian(key_of[7], (FILTERS, D), (4 * FILTERS) ** -0.5, 0.0625, ((0, 16),), jnp.float32)
    proj_bias = gaussian(key_of[8], (D,), 1.0, 6.0, (), jnp.float32)
    gate_weight = gaussian(key_of[9], (2, 2, 2 * D, GATES), (2 * D) ** -0.5, 0.1875, ((0, 2), (1, 2), (2, 8)), jnp.float32)
    gate_bias = gaussian(key_of[10], (2, 2, GATES), 1.0, 6.0, ((0, 2), (1, 2)), jnp.float32)
    cell_proj = gaussian(key_of[11], (2, 2, CELLS, D), (CELLS // 4) ** -0.5, 0.1875, ((0, 2), (1, 2), (2, 8)), jnp.float32)
    cotangent = gaussian(key_of[12], (2, 2, SEQS, LEN, D), 1.0, 6.0, ((0, 2), (1, 2), (2, 8)))
    return dict(chars=chars, lengths=lengths, char_emb=char_emb, conv_weight=conv_weight, conv_bias=conv_bias, highway_weight=highway_weight, highway_bias=highway_bias, proj_weight=proj_weight, proj_bias=proj_bias, gate_weight=gate_weight, gate_bias=gate_bias, cell_proj=cell_proj, cotangent=cotangent)


full_precision = lax.Precision.HIGHEST
CLIP_LIMIT = 3.0
MASKED_FILL = -1000000000.0

@jax.custom_vjp
def low(v):
    return lax.optimization_barrier(v.astype(jnp.bfloat16)).astype(jnp.float32)

@jax.custom_vjp
def low_back(v):
    return v

def low_keep(v):
    return (low(v), None)

def low_pass(kept, grad):
    return (grad,)

def back_keep(v):
    return (v, None)

def back_low(kept, grad):
    return (low(grad),)
low.defvjp(low_keep, low_pass)
low_back.defvjp(back_keep, back_low)

def soft_clip(value):
    return CLIP_LIMIT * jnp.tanh(value / CLIP_LIMIT)

def filter_widths(filter_count):
    filter_index = jnp.arange(filter_count, dtype=jnp.int32)
    filter_width = jnp.ones((filter_count,), jnp.int32)
    for doubling in range(6):
        filter_width = filter_width + (filter_index >= filter_count // 64 * (1 << doubling)).astype(jnp.int32)
    return filter_width

def conv_masks(filter_count):
    filter_width = filter_widths(filter_count)
    offset_rows = jnp.arange(KMAX * CDIM, dtype=jnp.int32) // CDIM
    weight_mask = (offset_rows[:, None] < filter_width[None, :]).astype(jnp.float32)
    valid_place = jnp.arange(CHARS, dtype=jnp.int32)[:, None] <= CHARS - filter_width[None, :]
    return (weight_mask, valid_place)

def make_windows(embedded):
    padded = jnp.pad(embedded, ((0, 0), (0, KMAX - 1), (0, 0)))
    return jnp.concatenate([padded[:, offset:offset + CHARS, :] for offset in range(KMAX)], axis=2)

def pooled_block(ids_block, table, conv_low, valid_place):
    embedded = low_back(low(jnp.take(table, ids_block, axis=0)))
    windows = make_windows(embedded)
    response = low_back(jnp.einsum('bpk,kf->bpf', windows, conv_low, precision=full_precision))
    response = jnp.where(valid_place[None], response, MASKED_FILL)
    return jax.nn.logsumexp(response, axis=1)

def char_encoder(ids, table, conv_low, conv_bias, highway_low, highway_bias, proj_low, proj_bias):
    token_count = ids.shape[0]
    block_size = math.gcd(token_count, 512)
    valid_place = conv_masks(FILTERS)[1]

    def pool_one(ids_block):
        return pooled_block(ids_block, table, conv_low, valid_place)
    pooled = lax.map(jax.checkpoint(pool_one), ids.reshape(token_count // block_size, block_size, CHARS))
    pooled = pooled.reshape(token_count, FILTERS)
    features = jax.nn.silu(pooled + conv_bias)
    for layer_index in range(2):
        mixed_pre = low_back(jnp.dot(low(features), highway_low[layer_index], precision=full_precision, preferred_element_type=jnp.float32) + highway_bias[layer_index])
        carry_gate = jax.nn.sigmoid(mixed_pre[:, FILTERS:])
        features = carry_gate * features + (1.0 - carry_gate) * jax.nn.silu(mixed_pre[:, :FILTERS])
    return low_back(jnp.dot(low(features), proj_low, precision=full_precision, preferred_element_type=jnp.float32) + proj_bias)

def lstm_layer(inputs, gate_low, gate_bias, cell_low, live_mask, residual):
    model_width = inputs.shape[2]
    cell_count = cell_low.shape[0]
    input_part = jnp.einsum('std,dg->tsg', low(inputs), gate_low[:model_width], precision=full_precision)
    state_weight = gate_low[model_width:]

    def advance(running, step_input):
        cell_state, hidden_state = running
        gate_values = low_back(step_input + jnp.dot(low(hidden_state), state_weight, precision=full_precision, preferred_element_type=jnp.float32) + gate_bias)
        in_gate = jax.nn.sigmoid(gate_values[:, :cell_count])
        forget = jax.nn.sigmoid(gate_values[:, cell_count:2 * cell_count])
        memory = jnp.tanh(gate_values[:, 2 * cell_count:3 * cell_count])
        out_gate = jax.nn.sigmoid(gate_values[:, 3 * cell_count:])
        cell_state = soft_clip(in_gate * memory + forget * cell_state)
        projected = low_back(jnp.dot(low(out_gate * jnp.tanh(cell_state)), cell_low, precision=full_precision, preferred_element_type=jnp.float32))
        hidden_state = soft_clip(projected)
        return ((cell_state, hidden_state), hidden_state)
    row_count = inputs.shape[0]
    start_value = (jnp.zeros((row_count, cell_count), jnp.float32), jnp.zeros((row_count, model_width), jnp.float32))
    _, hidden_all = lax.scan(advance, start_value, input_part)
    hidden_rows = jnp.transpose(hidden_all, (1, 0, 2))
    if residual:
        return live_mask[:, :, None] * (hidden_rows + inputs)
    return live_mask[:, :, None] * hidden_rows

def reference(chars, lengths, char_emb, conv_weight, conv_bias, highway_weight, highway_bias, proj_weight, proj_bias, gate_weight, gate_bias, cell_proj, cotangent):
    seq_count, time_steps, char_count = chars.shape
    position = jnp.arange(time_steps, dtype=jnp.int32)[None, :]
    live = position < lengths[:, None]
    live_mask = live.astype(jnp.float32)
    reversed_place = jnp.where(live, lengths[:, None] - 1 - position, position).astype(jnp.int32)
    orders = [jnp.broadcast_to(position, reversed_place.shape).astype(jnp.int32), reversed_place]
    weight_mask = conv_masks(FILTERS)[0]

    def forward(table, conv_w, conv_b, highway_w, highway_b, proj_w, proj_b, gate_w, gate_b, cell_w):
        conv_low = low(conv_w) * weight_mask
        highway_low = low(highway_w)
        proj_low = low(proj_w)
        gate_low = low(gate_w)
        cell_low = low(cell_w)
        ids = chars.reshape(seq_count * time_steps, char_count)
        encoded_stored = char_encoder(ids, table, conv_low, conv_b, highway_low, highway_b, proj_low, proj_b)
        encoded_stored = encoded_stored.reshape(seq_count, time_steps, -1)
        first_rows = []
        second_rows = []
        for direction in range(2):
            position_order = orders[direction]
            encoded = jnp.take_along_axis(encoded_stored, position_order[:, :, None], axis=1)
            first = lstm_layer(encoded, gate_low[1, direction], gate_b[1, direction], cell_low[1, direction], live_mask, False)
            sent = low_back(low(first))
            second = lstm_layer(sent, gate_low[0, direction], gate_b[0, direction], cell_low[0, direction], live_mask, True)
            first_rows.append(jnp.take_along_axis(first, position_order[:, :, None], axis=1))
            second_rows.append(jnp.take_along_axis(second, position_order[:, :, None], axis=1))
        return jnp.stack([jnp.stack(second_rows), jnp.stack(first_rows)])
    primals = (char_emb, conv_weight, conv_bias, highway_weight, highway_bias, proj_weight, proj_bias, gate_weight, gate_bias, cell_proj)
    acts, pullback = jax.vjp(forward, *primals)
    grads = pullback(cotangent.astype(jnp.float32))
    return (acts.astype(jnp.bfloat16), grads[0], grads[1], grads[2], grads[3], grads[4], grads[5], grads[6], grads[7], grads[8], grads[9])
```

```python
import functools
import math

import jax
import jax.numpy as jnp
from jax import lax
from jax.experimental import pallas as pl
from jax.experimental.pallas import tpu as pltpu
from jax.sharding import PartitionSpec as P

FILTERS = 2048
CDIM = 16
CVOCAB = 262
CHARS = 50
KMAX = 7
CLIP_LIMIT = 3.0
MASKED_FILL = -1000000000.0
MESH = pl.DeviceIdType.MESH
BF = jnp.bfloat16
F32 = jnp.float32
ALL = ("pipe", "dir", "dp")


def silu_slope(value):
    sig = jax.nn.sigmoid(value)
    return sig * (1.0 + value * (1.0 - sig))


def filter_widths(filter_count):
    filter_index = jnp.arange(filter_count, dtype=jnp.int32)
    filter_width = jnp.ones((filter_count,), jnp.int32)
    for doubling in range(6):
        filter_width = filter_width + (filter_index >= filter_count // 64 * (1 << doubling)).astype(
            jnp.int32
        )
    return filter_width


def conv_masks(filter_count):
    filter_width = filter_widths(filter_count)
    offset_rows = jnp.arange(KMAX * CDIM, dtype=jnp.int32) // CDIM
    weight_mask = (offset_rows[:, None] < filter_width[None, :]).astype(jnp.float32)
    valid_place = jnp.arange(CHARS, dtype=jnp.int32)[:, None] <= CHARS - filter_width[None, :]
    return (weight_mask, valid_place)


def make_windows(embedded):
    padded = jnp.pad(embedded, ((0, 0), (0, KMAX - 1), (0, 0)))
    return jnp.concatenate(
        [padded[:, offset : offset + CHARS, :] for offset in range(KMAX)], axis=2
    )


def conv_response(ids_block, table_low, conv_low, valid_place):
    embedded = jnp.take(table_low, ids_block, axis=0)
    windows = make_windows(embedded)
    response = jnp.einsum("bpk,kf->bpf", windows, conv_low, preferred_element_type=jnp.float32)
    return (windows, jnp.where(valid_place[None], response, MASKED_FILL))


def over(count, step):
    if count <= 9:
        for off in range(1, count):
            step(off)
    else:
        lax.fori_loop(1, count, lambda off, _: (step(off), 0)[1], 0)


def lstm_kernel(
    n, chunk,
    x_hbm, wx, wh, bias, p, wxt, wht, pt, cot,
    out_ref, dx_ref, x_all, h_all, da_all, e_all, dq_all,
    xbuf, hbuf, dqbuf, gates, cells, ebuf, hown, gscr, escr, dabuf, ucell,
    stage, inbox, stage2, inbox2, relay, gbuf, rown,
    load_sem, ag_send, ag_recv, dq_send, dq_recv, rs_send, rs_recv, dx_send, dx_recv,
    x_send, x_recv, g_send, g_recv, da_sem, st_sem,
):
    steps, _, rows, width = xbuf.shape
    total = n * rows
    cell = cells.shape[2]
    pipe = lax.axis_index("pipe")
    direction = lax.axis_index("dir")
    me = lax.axis_index("dp")
    first = pipe == 1
    second = pipe == 0
    partner = (1 - pipe, direction, me)

    def peer(off):
        return lax.rem(me + off, n)

    barrier = pltpu.get_barrier_semaphore()
    over(n, lambda off: pl.semaphore_signal(
        barrier, inc=1, device_id=(pipe, direction, peer(off)), device_id_type=MESH))
    pl.semaphore_signal(barrier, inc=1, device_id=partner, device_id_type=MESH)

    @pl.when(first)
    def _():
        load = pltpu.make_async_copy(x_hbm, xbuf, load_sem)
        load.start()
        load.wait()

    hbuf[0] = jnp.zeros((n, rows, width), BF)
    cells[0] = jnp.zeros((total, cell), F32)
    pl.semaphore_wait(barrier, n)

    def ag_copy(buf, slot, off):
        out, into = (ag_send, ag_recv) if buf is hbuf else (dq_send, dq_recv)
        return pltpu.make_async_remote_copy(
            src_ref=buf.at[slot, me], dst_ref=buf.at[slot, me],
            send_sem=out.at[off], recv_sem=into.at[off],
            device_id=(pipe, direction, peer(off)), device_id_type=MESH)

    def rs_copy(off):
        return pltpu.make_async_remote_copy(
            src_ref=stage.at[peer(off)], dst_ref=inbox.at[me],
            send_sem=rs_send.at[off], recv_sem=rs_recv.at[off],
            device_id=(pipe, direction, peer(off)), device_id_type=MESH)

    def dx_copy(slot, off):
        return pltpu.make_async_remote_copy(
            src_ref=stage2.at[slot, peer(off)], dst_ref=inbox2.at[slot, me],
            send_sem=dx_send.at[slot, off], recv_sem=dx_recv.at[slot, off],
            device_id=(pipe, direction, peer(off)), device_id_type=MESH)

    def x_copy(t):
        return pltpu.make_async_remote_copy(
            src_ref=hbuf.at[t + 1], dst_ref=xbuf.at[t],
            send_sem=x_send.at[t], recv_sem=x_recv.at[t],
            device_id=partner, device_id_type=MESH)

    def g_copy(t):
        return pltpu.make_async_remote_copy(
            src_ref=relay.at[t], dst_ref=gbuf.at[t],
            send_sem=g_send.at[t], recv_sem=g_recv.at[t],
            device_id=partner, device_id_type=MESH)

    def ag_wait(buf, slot):
        def both(off):
            ag_copy(buf, slot, off).wait_send()
            ag_copy(buf, slot, off).wait_recv()
        over(n, both)

    def rs_wait():
        def both(off):
            rs_copy(off).wait_send()
            rs_copy(off).wait_recv()
        over(n, both)

    def forward(t, _):
        @pl.when(second)
        def _():
            x_copy(t).wait_recv()

        gscr[...] = jnp.dot(
            xbuf[t].reshape(total, width), wx[...], preferred_element_type=F32) + bias[...]

        @pl.when(t > 0)
        def _():
            ag_wait(hbuf, t)

            @pl.when(first)
            def _():
                x_copy(t - 1).start()

        gscr[...] += jnp.dot(
            hbuf[t].reshape(total, width), wh[...], preferred_element_type=F32)

        def rows_step(k, _):
            at = pl.ds(pl.multiple_of(k * chunk, chunk), chunk)
            g = gscr[at, :]
            i = jax.nn.sigmoid(g[:, :cell])
            f = jax.nn.sigmoid(g[:, cell:2 * cell])
            m = jnp.tanh(g[:, 2 * cell:3 * cell])
            o = jax.nn.sigmoid(g[:, 3 * cell:])
            c = 3.0 * jnp.tanh((i * m + f * cells[t, at, :]) * (1.0 / 3.0))
            cells[t + 1, at, :] = c
            ebuf[t, at, :] = (o * jnp.tanh(c)).astype(BF)
            kind = gates.dtype
            gates[t, at, :cell] = i.astype(kind)
            gates[t, at, cell:2 * cell] = f.astype(kind)
            gates[t, at, 2 * cell:3 * cell] = m.astype(kind)
            gates[t, at, 3 * cell:] = o.astype(kind)
            return 0

        lax.fori_loop(0, total // chunk, rows_step, 0)
        q = jnp.dot(ebuf[t], p[...], preferred_element_type=F32)
        stage[...] = q.astype(BF).reshape(n, rows, width)
        over(n, lambda off: rs_copy(off).start())
        inbox[me] = stage[me]
        rs_wait()
        h = 3.0 * jnp.tanh(jnp.sum(inbox[...].astype(F32), axis=0) * (1.0 / 3.0))
        hown[t] = h
        hbuf[t + 1, me] = h.astype(BF)
        over(n, lambda off: ag_copy(hbuf, t + 1, off).start())
        add = jnp.where(second, 1.0, 0.0)
        out_ref[t] = (h + add * xbuf[t, me].astype(F32)).astype(BF)
        return 0

    lax.fori_loop(0, steps, forward, 0)
    ag_wait(hbuf, steps)

    @pl.when(first)
    def _():
        x_copy(steps - 1).start()
        lax.fori_loop(0, steps, lambda t, _: (x_copy(t).wait_send(), 0)[1], 0)

    rown[...] = jnp.zeros((rows, width), F32)
    ucell[...] = jnp.zeros((total, cell), F32)

    def dx_finish(t):
        slot = lax.rem(t, 2)

        def both(off):
            dx_copy(slot, off).wait_send()
            dx_copy(slot, off).wait_recv()
        over(n, both)
        dx = jnp.sum(inbox2[slot].astype(F32), axis=0)
        dx_ref[t] = dx

        @pl.when(second)
        def _():
            relay[t] = (dx + cot[t].astype(F32)).astype(BF)
            g_copy(t).start()

    def da_copy(t):
        slot = lax.rem(t, 2)
        return pltpu.make_async_copy(dabuf.at[slot], da_all.at[t], da_sem.at[slot])

    def backward(k, _):
        t = steps - 1 - k
        slot = lax.rem(t, 2)
        up = rown[...] + cot[t].astype(F32)
        rown[...] = up

        @pl.when(first)
        def _():
            g_copy(t).wait_recv()
            rown[...] = rown[...] + gbuf[t].astype(F32)

        ratio = hown[t] * (1.0 / 3.0)
        dqbuf[t, me] = (rown[...] * (1.0 - ratio * ratio)).astype(BF)
        over(n, lambda off: ag_copy(dqbuf, t, off).start())

        @pl.when(k > 0)
        def _():
            dx_finish(t + 1)

        @pl.when(k > 1)
        def _():
            da_copy(t + 2).wait()

        ag_wait(dqbuf, t)
        escr[...] = jnp.dot(
            dqbuf[t].reshape(total, width), pt[...], preferred_element_type=F32)

        def rows_step(j, _):
            at = pl.ds(pl.multiple_of(j * chunk, chunk), chunk)
            de = escr[at, :]
            i = gates[t, at, :cell].astype(F32)
            f = gates[t, at, cell:2 * cell].astype(F32)
            m = gates[t, at, 2 * cell:3 * cell].astype(F32)
            o = gates[t, at, 3 * cell:].astype(F32)
            c = cells[t + 1, at, :]
            tc = jnp.tanh(c)
            cr = c * (1.0 / 3.0)
            dc = (de * o * (1.0 - tc * tc) + ucell[at, :]) * (1.0 - cr * cr)
            ucell[at, :] = dc * f
            dabuf[slot, at, :cell] = (dc * m * i * (1.0 - i)).astype(BF)
            dabuf[slot, at, cell:2 * cell] = (dc * cells[t, at, :] * f * (1.0 - f)).astype(BF)
            dabuf[slot, at, 2 * cell:3 * cell] = (dc * i * (1.0 - m * m)).astype(BF)
            dabuf[slot, at, 3 * cell:] = (de * tc * o * (1.0 - o)).astype(BF)
            return 0

        lax.fori_loop(0, total // chunk, rows_step, 0)
        r = jnp.dot(dabuf[slot], wht[...], preferred_element_type=F32)
        stage[...] = r.astype(BF).reshape(n, rows, width)
        over(n, lambda off: rs_copy(off).start())
        inbox[me] = stage[me]
        dx = jnp.dot(dabuf[slot], wxt[...], preferred_element_type=F32)
        stage2[slot] = dx.astype(BF).reshape(n, rows, width)
        over(n, lambda off: dx_copy(slot, off).start())
        inbox2[slot, me] = stage2[slot, me]
        da_copy(t).start()
        rs_wait()
        rown[...] = jnp.sum(inbox[...].astype(F32), axis=0)
        return 0

    lax.fori_loop(0, steps, backward, 0)
    dx_finish(0)

    @pl.when(second)
    def _():
        lax.fori_loop(0, steps, lambda t, _: (g_copy(t).wait_send(), 0)[1], 0)

    da_copy(1).wait()
    da_copy(0).wait()
    for at, (buf, dst) in enumerate(((xbuf, x_all), (hbuf.at[pl.ds(0, steps)], h_all),
                                     (ebuf, e_all), (dqbuf, dq_all))):
        pltpu.make_async_copy(buf, dst, st_sem.at[at]).start()
    for at, (buf, dst) in enumerate(((xbuf, x_all), (hbuf.at[pl.ds(0, steps)], h_all),
                                     (ebuf, e_all), (dqbuf, dq_all))):
        pltpu.make_async_copy(buf, dst, st_sem.at[at]).wait()


def lstm_call(n, x, wx, wh, bias, p, wxt, wht, pt, cot, chunk=16):
    steps, _, rows, width = x.shape
    cell = p.shape[0]
    total = n * rows
    sds = jax.ShapeDtypeStruct
    vm = pl.BlockSpec(memory_space=pltpu.VMEM)
    hb = pl.BlockSpec(memory_space=pl.ANY)
    keep = F32 if n <= 8 else BF
    V = pltpu.VMEM
    dma = pltpu.SemaphoreType.DMA
    return pl.pallas_call(
        functools.partial(lstm_kernel, n, chunk),
        out_shape=(
            sds((steps, rows, width), BF), sds((steps, rows, width), F32),
            sds((steps, n, rows, width), BF), sds((steps, n, rows, width), BF),
            sds((steps, total, 4 * cell), BF), sds((steps, total, cell), BF),
            sds((steps, n, rows, width), BF)),
        in_specs=[hb] + [vm] * 8,
        out_specs=(vm, vm, hb, hb, hb, hb, hb),
        scratch_shapes=[
            V((steps, n, rows, width), BF), V((steps + 1, n, rows, width), BF),
            V((steps, n, rows, width), BF), V((steps, total, 4 * cell), keep),
            V((steps + 1, total, cell), F32), V((steps, total, cell), BF),
            V((steps, rows, width), F32), V((total, 4 * cell), F32),
            V((total, cell), F32), V((2, total, 4 * cell), BF), V((total, cell), F32),
            V((n, rows, width), BF), V((n, rows, width), BF),
            V((2, n, rows, width), BF), V((2, n, rows, width), BF),
            V((steps, rows, width), BF), V((steps, rows, width), BF), V((rows, width), F32),
            dma, dma((n,)), dma((n,)), dma((n,)), dma((n,)), dma((n,)), dma((n,)), dma((2, n)), dma((2, n)),
            dma((steps,)), dma((steps,)), dma((steps,)), dma((steps,)), dma((2,)), dma((4,)),
        ],
        compiler_params=pltpu.CompilerParams(
            collective_id=0, has_side_effects=True, vmem_limit_bytes=60 * 1024 * 1024),
        name="relay_lstm",
    )(x, wx, wh, bias, p, wxt, wht, pt, cot)


def exchange(blocks, axis):
    count = lax.axis_size(axis)
    me = lax.axis_index(axis)
    got = jnp.zeros_like(blocks)
    got = lax.dynamic_update_index_in_dim(
        got, lax.dynamic_index_in_dim(blocks, me, 0, keepdims=False), me, 0
    )
    for off in range(1, count):
        sent = lax.dynamic_index_in_dim(blocks, (me + off) % count, 0, keepdims=False)
        came = lax.ppermute(sent, axis, [(i, (i + off) % count) for i in range(count)])
        got = lax.dynamic_update_index_in_dim(got, came, (me - off) % count, 0)
    return got


def encode_forward(ids, weights):
    table_low, conv_low, conv_bias, highway_low, highway_bias, proj_low, proj_bias = weights
    valid_place = conv_masks(FILTERS)[1]
    pooled = jax.nn.logsumexp(conv_response(ids, table_low, conv_low, valid_place)[1], axis=1)
    features = jax.nn.silu(pooled + conv_bias)
    kept = [features]
    mixed = []
    for layer in range(2):
        pre = (
            jnp.dot(features.astype(BF), highway_low[layer], preferred_element_type=F32)
            + highway_bias[layer]
        )
        mixed.append(pre)
        gate = jax.nn.sigmoid(pre[:, FILTERS:])
        features = gate * features + (1.0 - gate) * jax.nn.silu(pre[:, :FILTERS])
        kept.append(features)
    encoded = jnp.dot(features.astype(BF), proj_low, preferred_element_type=F32) + proj_bias
    return encoded, pooled, kept, mixed


def to_columns(value):
    count = lax.axis_size(ALL)
    tokens, columns = value.shape
    split = jnp.transpose(value.reshape(tokens, count, columns // count), (1, 0, 2))
    return lax.all_to_all(split, ALL, 0, 0).reshape(count * tokens, columns // count)


def conv_backward(ids, table_low, conv_low, grad_before):
    weight_mask, valid_place = conv_masks(FILTERS)
    windows, response = conv_response(ids, table_low, conv_low, valid_place)
    share = jax.nn.softmax(response, axis=1)
    grad_response = (grad_before[:, None, :] * share).astype(BF)
    grad_conv = jnp.einsum("bpk,bpf->kf", windows, grad_response, preferred_element_type=F32)
    grad_windows = jnp.einsum("bpf,kf->bpk", grad_response, conv_low, preferred_element_type=F32)
    grad_embedded = jnp.zeros((ids.shape[0], CHARS + KMAX - 1, CDIM), F32)
    for offset in range(KMAX):
        grad_embedded = grad_embedded + jnp.pad(
            grad_windows[:, :, offset * CDIM : (offset + 1) * CDIM],
            ((0, 0), (offset, KMAX - 1 - offset), (0, 0)),
        )
    grad_embedded = grad_embedded[:, :CHARS].astype(BF)
    one_hot = (ids[:, :, None] == jnp.arange(CVOCAB, dtype=jnp.int32)).astype(BF)
    grad_table = jnp.einsum("bpv,bpc->vc", one_hot, grad_embedded, preferred_element_type=F32)
    return grad_conv * weight_mask, grad_table


def local(
    chars,
    lengths,
    char_emb,
    conv_weight,
    conv_bias,
    highway_weight,
    highway_bias,
    proj_weight,
    proj_bias,
    gate_weight,
    gate_bias,
    cell_proj,
    cotangent,
):
    n = lax.axis_size("dp")
    pipe = lax.axis_index("pipe")
    direction = lax.axis_index("dir")
    me = lax.axis_index("dp")
    everyone = lax.axis_size(ALL)
    seqs, steps, char_count = chars.shape
    parts = everyone // n
    quarter = seqs // parts
    tokens = quarter * steps
    width = cell_proj.shape[3]
    cell = cell_proj.shape[2]

    conv_full = lax.all_gather(conv_weight.astype(BF), ("dir", "dp"), axis=1, tiled=True)
    highway_full = lax.all_gather(highway_weight.astype(BF), ("dir", "dp"), axis=2, tiled=True)
    proj_full = lax.all_gather(proj_weight.astype(BF), ("dir", "dp"), axis=0, tiled=True)
    all_lengths = lax.all_gather(lengths, "dp", axis=0, tiled=True)

    in_rows = gate_weight.shape[2]
    gate_low = gate_weight[0, 0].astype(BF).reshape(in_rows, 4, n, cell)
    gate_low = jnp.transpose(gate_low, (2, 0, 1, 3)).reshape(n, in_rows, 4 * cell)
    gate_own = exchange(gate_low, "dp").reshape(n * in_rows, 4 * cell)
    bias_own = lax.dynamic_index_in_dim(
        gate_bias[0, 0].reshape(4, n, cell), me, 1, keepdims=False
    ).reshape(1, 4 * cell)
    cell_low = cell_proj[0, 0].astype(BF)

    def order_matrix(sizes):
        place = jnp.arange(steps, dtype=jnp.int32)[None, :]
        live = place < sizes[:, None]
        order = jnp.where(live & (direction == 1), sizes[:, None] - 1 - place, place)
        return ((order[:, :, None] == place[:, None, :]) & live[:, :, None]).astype(BF)

    own_order = order_matrix(lengths)
    cot = jnp.einsum("rts,rsd->trd", own_order, cotangent[0, 0], preferred_element_type=BF)

    ids = lax.dynamic_slice_in_dim(
        chars, (pipe * lax.axis_size("dir") + direction) * quarter, quarter, 0
    ).reshape(tokens, char_count)
    weight_mask = conv_masks(FILTERS)[0]
    table_low = char_emb.astype(BF)
    conv_low = conv_full * weight_mask.astype(BF)
    encoded, pooled, kept, mixed = encode_forward(
        ids,
        (table_low, conv_low, conv_bias, highway_full, highway_bias, proj_full, proj_bias),
    )
    encoded_all = lax.all_gather(
        encoded.astype(BF).reshape(quarter, steps, width), ("dp", "pipe", "dir"), axis=0, tiled=True
    )
    inputs = jnp.einsum(
        "rts,rsd->trd", order_matrix(all_lengths), encoded_all, preferred_element_type=BF
    ).reshape(steps, n, seqs, width)
    kept_low = [value.astype(BF) for value in kept]
    kept_all = [lax.all_gather(value, ALL, axis=0, tiled=True) for value in kept_low[:2]]
    last_columns = to_columns(kept_low[2])

    out_own, dx_own, x_all, h_all, da_all, e_all, dq_all = lstm_call(
        n,
        inputs,
        gate_own[:width],
        gate_own[width:],
        bias_own,
        cell_low,
        gate_own[:width].T,
        gate_own[width:].T,
        cell_low.T,
        cot,
    )
    activations = jnp.einsum("rts,srd->rtd", own_order, out_own, preferred_element_type=BF)

    total = steps * n * seqs
    da_flat = da_all.reshape(total, 4 * cell)
    grad_gate = jnp.concatenate(
        [
            jnp.einsum(
                "tk,tg->kg", part.reshape(total, width), da_flat, preferred_element_type=F32
            ).astype(BF)
            for part in (x_all, h_all)
        ]
    ).reshape(n, in_rows, 4 * cell)
    grad_gate = exchange(grad_gate, "dp").reshape(n, in_rows, 4, cell)
    grad_gate = jnp.transpose(grad_gate, (1, 2, 0, 3)).reshape(in_rows, 4 * n * cell).astype(F32)
    grad_bias = jnp.sum(da_flat.astype(F32), axis=0).reshape(4, cell)
    grad_bias = jnp.transpose(lax.all_gather(grad_bias, "dp"), (1, 0, 2)).reshape(n, 4 * cell)
    grad_bias = lax.dynamic_index_in_dim(grad_bias, me, 0, keepdims=False)
    grad_cell = jnp.einsum(
        "tc,td->cd",
        e_all.reshape(total, cell),
        dq_all.reshape(total, width),
        preferred_element_type=F32,
    )

    grad_stored = jnp.einsum(
        "rts,srd->rtd", own_order, dx_own.astype(BF), preferred_element_type=F32
    )
    grad_stored = jnp.where(pipe == 1, grad_stored, 0.0).astype(BF)
    grad_encoded = lax.psum_scatter(
        grad_stored, ("pipe", "dir"), scatter_dimension=0, tiled=True
    ).reshape(tokens, width)
    encoded_grads = lax.all_gather(grad_encoded, ALL, axis=0, tiled=True)

    grad_proj_bias = jnp.sum(grad_encoded.astype(F32), axis=0)
    grad_features = jnp.einsum("td,fd->tf", grad_encoded, proj_full, preferred_element_type=F32)
    grad_highway = [None, None]
    grad_highway_bias = [None, None]
    for layer in (1, 0):
        nonlinear = mixed[layer][:, :FILTERS]
        gate = jax.nn.sigmoid(mixed[layer][:, FILTERS:])
        grad_mixed = jnp.concatenate(
            [
                grad_features * (1.0 - gate) * silu_slope(nonlinear),
                grad_features * (kept[layer] - jax.nn.silu(nonlinear)) * gate * (1.0 - gate),
            ],
            axis=1,
        ).astype(BF)
        grad_highway[layer] = jnp.einsum(
            "tf,tg->fg", kept_all[layer], to_columns(grad_mixed), preferred_element_type=F32
        )
        grad_highway_bias[layer] = jnp.sum(grad_mixed.astype(F32), axis=0)
        grad_features = grad_features * gate + jnp.einsum(
            "tg,fg->tf", grad_mixed, highway_full[layer], preferred_element_type=F32
        )
    grad_proj = jnp.einsum("tf,td->fd", last_columns, encoded_grads, preferred_element_type=F32)
    grad_before = grad_features * silu_slope(pooled + conv_bias)
    grad_conv, grad_table = conv_backward(ids, table_low, conv_low, grad_before)

    small = (
        grad_table,
        jnp.sum(grad_before, axis=0),
        jnp.stack(grad_highway_bias),
        grad_proj_bias,
    )
    flat = jnp.concatenate([value.reshape(-1) for value in small])
    share = -(-flat.shape[0] // (everyone * 128)) * 128
    flat = jnp.pad(flat, (0, share * everyone - flat.shape[0])).reshape(everyone, share)
    columns = FILTERS // everyone
    packed = jnp.concatenate(
        [
            jnp.transpose(
                grad_conv.reshape(KMAX * CDIM, everyone, columns), (1, 0, 2)
            ).reshape(everyone, KMAX * CDIM * columns),
            flat,
        ],
        axis=1,
    ).astype(BF)
    summed = jnp.sum(lax.all_to_all(packed, ALL, 0, 0).astype(F32), axis=0)
    grad_conv = summed[: KMAX * CDIM * columns].reshape(KMAX * CDIM, columns)
    shared = lax.all_to_all(
        jnp.broadcast_to(summed[KMAX * CDIM * columns :], (everyone, share)), ALL, 0, 0
    ).reshape(-1)
    small_sums = []
    start = 0
    for value in small:
        small_sums.append(shared[start : start + value.size].reshape(value.shape))
        start += value.size
    return (
        activations[None, None],
        small_sums[0],
        grad_conv,
        small_sums[1],
        jnp.stack(grad_highway),
        small_sums[2],
        grad_proj,
        small_sums[3],
        grad_gate[None, None],
        grad_bias[None, None],
        grad_cell[None, None],
    )


def solution(mesh):
    return jax.shard_map(
        local,
        mesh=mesh,
        in_specs=(
            P("dp", None, None),
            P("dp"),
            P(),
            P(None, ("dir", "dp")),
            P(),
            P(None, None, ("dir", "dp")),
            P(),
            P(("dir", "dp"), None),
            P(),
            P("pipe", "dir", "dp", None),
            P("pipe", "dir", None),
            P("pipe", "dir", "dp", None),
            P("pipe", "dir", "dp", None, None),
        ),
        out_specs=(
            P("pipe", "dir", "dp", None, None),
            P(),
            P(None, ("pipe", "dir", "dp")),
            P(),
            P(None, None, ("pipe", "dir", "dp")),
            P(),
            P(("pipe", "dir", "dp"), None),
            P(),
            P("pipe", "dir", "dp", None),
            P("pipe", "dir", "dp"),
            P("pipe", "dir", "dp", None),
        ),
        check_vma=False,
    )
```

```python
import functools
import math

import jax
import jax.numpy as jnp
from jax import lax
from jax.experimental import pallas as pl
from jax.experimental.pallas import tpu as pltpu
from jax.sharding import PartitionSpec as P

FILTERS = 2048
CDIM = 16
CVOCAB = 262
CHARS = 50
KMAX = 7
CLIP_LIMIT = 3.0
MASKED_FILL = -1000000000.0
MESH = pl.DeviceIdType.MESH
BF = jnp.bfloat16
F32 = jnp.float32
ALL = ("pipe", "dir", "dp")


def silu_slope(value):
    sig = jax.nn.sigmoid(value)
    return sig * (1.0 + value * (1.0 - sig))


def filter_widths(filter_count):
    filter_index = jnp.arange(filter_count, dtype=jnp.int32)
    filter_width = jnp.ones((filter_count,), jnp.int32)
    for doubling in range(6):
        filter_width = filter_width + (filter_index >= filter_count // 64 * (1 << doubling)).astype(
            jnp.int32
        )
    return filter_width


def conv_masks(filter_count):
    filter_width = filter_widths(filter_count)
    offset_rows = jnp.arange(KMAX * CDIM, dtype=jnp.int32) // CDIM
    weight_mask = (offset_rows[:, None] < filter_width[None, :]).astype(jnp.float32)
    valid_place = jnp.arange(CHARS, dtype=jnp.int32)[:, None] <= CHARS - filter_width[None, :]
    return (weight_mask, valid_place)


def make_windows(embedded):
    padded = jnp.pad(embedded, ((0, 0), (0, KMAX - 1), (0, 0)))
    return jnp.concatenate(
        [padded[:, offset : offset + CHARS, :] for offset in range(KMAX)], axis=2
    )


def conv_response(ids_block, table_low, conv_low, valid_place):
    embedded = jnp.take(table_low, ids_block, axis=0)
    windows = make_windows(embedded)
    response = jnp.einsum("bpk,kf->bpf", windows, conv_low, preferred_element_type=jnp.float32)
    return (windows, jnp.where(valid_place[None], response, MASKED_FILL))


def over(count, step):
    if count <= 9:
        for off in range(1, count):
            step(off)
    else:
        lax.fori_loop(1, count, lambda off, _: (step(off), 0)[1], 0)


def lstm_kernel(
    n, chunk,
    x_hbm, wx, wh, bias, p, wxt, wht, pt, cot,
    out_ref, dx_ref, x_all, h_all, da_all, e_all, dq_all,
    xbuf, hbuf, dqbuf, gates, cells, ebuf, hown, gscr, escr, dabuf, ucell,
    stage, inbox, stage2, inbox2, relay, gbuf, rown,
    load_sem, ag_send, ag_recv, dq_send, dq_recv, rs_send, rs_recv, dx_send, dx_recv,
    x_send, x_recv, g_send, g_recv, da_sem, st_sem,
):
    steps, _, rows, width = xbuf.shape
    total = n * rows
    cell = cells.shape[2]
    pipe = lax.axis_index("pipe")
    direction = lax.axis_index("dir")
    me = lax.axis_index("dp")
    first = pipe == 1
    second = pipe == 0
    partner = (1 - pipe, direction, me)

    def peer(off):
        return lax.rem(me + off, n)

    barrier = pltpu.get_barrier_semaphore()
    over(n, lambda off: pl.semaphore_signal(
        barrier, inc=1, device_id=(pipe, direction, peer(off)), device_id_type=MESH))
    pl.semaphore_signal(barrier, inc=1, device_id=partner, device_id_type=MESH)

    @pl.when(first)
    def _():
        load = pltpu.make_async_copy(x_hbm, xbuf, load_sem)
        load.start()
        load.wait()

    hbuf[0] = jnp.zeros((n, rows, width), BF)
    cells[0] = jnp.zeros((total, cell), F32)
    pl.semaphore_wait(barrier, n)

    def ag_copy(buf, slot, off):
        out, into = (ag_send, ag_recv) if buf is hbuf else (dq_send, dq_recv)
        return pltpu.make_async_remote_copy(
            src_ref=buf.at[slot, me], dst_ref=buf.at[slot, me],
            send_sem=out.at[off], recv_sem=into.at[off],
            device_id=(pipe, direction, peer(off)), device_id_type=MESH)

    def rs_copy(off):
        return pltpu.make_async_remote_copy(
            src_ref=stage.at[peer(off)], dst_ref=inbox.at[me],
            send_sem=rs_send.at[off], recv_sem=rs_recv.at[off],
            device_id=(pipe, direction, peer(off)), device_id_type=MESH)

    def dx_copy(slot, off):
        return pltpu.make_async_remote_copy(
            src_ref=stage2.at[slot, peer(off)], dst_ref=inbox2.at[slot, me],
            send_sem=dx_send.at[slot, off], recv_sem=dx_recv.at[slot, off],
            device_id=(pipe, direction, peer(off)), device_id_type=MESH)

    def x_copy(t):
        return pltpu.make_async_remote_copy(
            src_ref=hbuf.at[t + 1], dst_ref=xbuf.at[t],
            send_sem=x_send.at[t], recv_sem=x_recv.at[t],
            device_id=partner, device_id_type=MESH)

    def g_copy(t):
        return pltpu.make_async_remote_copy(
            src_ref=relay.at[t], dst_ref=gbuf.at[t],
            send_sem=g_send.at[t], recv_sem=g_recv.at[t],
            device_id=partner, device_id_type=MESH)

    def ag_wait(buf, slot):
        def both(off):
            ag_copy(buf, slot, off).wait_send()
            ag_copy(buf, slot, off).wait_recv()
        over(n, both)

    def rs_wait():
        def both(off):
            rs_copy(off).wait_send()
            rs_copy(off).wait_recv()
        over(n, both)

    def forward(t, _):
        @pl.when(second)
        def _():
            x_copy(t).wait_recv()

        gscr[...] = jnp.dot(
            xbuf[t].reshape(total, width), wx[...], preferred_element_type=F32) + bias[...]

        @pl.when(t > 0)
        def _():
            ag_wait(hbuf, t)

            @pl.when(first)
            def _():
                x_copy(t - 1).start()

        gscr[...] += jnp.dot(
            hbuf[t].reshape(total, width), wh[...], preferred_element_type=F32)

        def rows_step(k, _):
            at = pl.ds(pl.multiple_of(k * chunk, chunk), chunk)
            g = gscr[at, :]
            i = jax.nn.sigmoid(g[:, :cell])
            f = jax.nn.sigmoid(g[:, cell:2 * cell])
            m = jnp.tanh(g[:, 2 * cell:3 * cell])
            o = jax.nn.sigmoid(g[:, 3 * cell:])
            c = 3.0 * jnp.tanh((i * m + f * cells[t, at, :]) * (1.0 / 3.0))
            cells[t + 1, at, :] = c
            ebuf[t, at, :] = (o * jnp.tanh(c)).astype(BF)
            kind = gates.dtype
            gates[t, at, :cell] = i.astype(kind)
            gates[t, at, cell:2 * cell] = f.astype(kind)
            gates[t, at, 2 * cell:3 * cell] = m.astype(kind)
            gates[t, at, 3 * cell:] = o.astype(kind)
            return 0

        lax.fori_loop(0, total // chunk, rows_step, 0)
        q = jnp.dot(ebuf[t], p[...], preferred_element_type=F32)
        stage[...] = q.astype(BF).reshape(n, rows, width)
        over(n, lambda off: rs_copy(off).start())
        inbox[me] = stage[me]
        rs_wait()
        h = 3.0 * jnp.tanh(jnp.sum(inbox[...].astype(F32), axis=0) * (1.0 / 3.0))
        hown[t] = h
        hbuf[t + 1, me] = h.astype(BF)
        over(n, lambda off: ag_copy(hbuf, t + 1, off).start())
        add = jnp.where(second, 1.0, 0.0)
        out_ref[t] = (h + add * xbuf[t, me].astype(F32)).astype(BF)
        return 0

    lax.fori_loop(0, steps, forward, 0)
    ag_wait(hbuf, steps)

    @pl.when(first)
    def _():
        x_copy(steps - 1).start()
        lax.fori_loop(0, steps, lambda t, _: (x_copy(t).wait_send(), 0)[1], 0)

    rown[...] = jnp.zeros((rows, width), F32)
    ucell[...] = jnp.zeros((total, cell), F32)

    def dx_finish(t):
        slot = lax.rem(t, 2)

        def both(off):
            dx_copy(slot, off).wait_send()
            dx_copy(slot, off).wait_recv()
        over(n, both)
        dx = jnp.sum(inbox2[slot].astype(F32), axis=0)
        dx_ref[t] = dx

        @pl.when(second)
        def _():
            relay[t] = (dx + cot[t].astype(F32)).astype(BF)
            g_copy(t).start()

    def da_copy(t):
        slot = lax.rem(t, 2)
        return pltpu.make_async_copy(dabuf.at[slot], da_all.at[t], da_sem.at[slot])

    def backward(k, _):
        t = steps - 1 - k
        slot = lax.rem(t, 2)
        up = rown[...] + cot[t].astype(F32)
        rown[...] = up

        @pl.when(first)
        def _():
            g_copy(t).wait_recv()
            rown[...] = rown[...] + gbuf[t].astype(F32)

        ratio = hown[t] * (1.0 / 3.0)
        dqbuf[t, me] = (rown[...] * (1.0 - ratio * ratio)).astype(BF)
        over(n, lambda off: ag_copy(dqbuf, t, off).start())

        @pl.when(k > 0)
        def _():
            dx_finish(t + 1)

        @pl.when(k > 1)
        def _():
            da_copy(t + 2).wait()

        ag_wait(dqbuf, t)
        escr[...] = jnp.dot(
            dqbuf[t].reshape(total, width), pt[...], preferred_element_type=F32)

        def rows_step(j, _):
            at = pl.ds(pl.multiple_of(j * chunk, chunk), chunk)
            de = escr[at, :]
            i = gates[t, at, :cell].astype(F32)
            f = gates[t, at, cell:2 * cell].astype(F32)
            m = gates[t, at, 2 * cell:3 * cell].astype(F32)
            o = gates[t, at, 3 * cell:].astype(F32)
            c = cells[t + 1, at, :]
            tc = jnp.tanh(c)
            cr = c * (1.0 / 3.0)
            dc = (de * o * (1.0 - tc * tc) + ucell[at, :]) * (1.0 - cr * cr)
            ucell[at, :] = dc * f
            dabuf[slot, at, :cell] = (dc * m * i * (1.0 - i)).astype(BF)
            dabuf[slot, at, cell:2 * cell] = (dc * cells[t, at, :] * f * (1.0 - f)).astype(BF)
            dabuf[slot, at, 2 * cell:3 * cell] = (dc * i * (1.0 - m * m)).astype(BF)
            dabuf[slot, at, 3 * cell:] = (de * tc * o * (1.0 - o)).astype(BF)
            return 0

        lax.fori_loop(0, total // chunk, rows_step, 0)
        r = jnp.dot(dabuf[slot], wht[...], preferred_element_type=F32)
        stage[...] = r.astype(BF).reshape(n, rows, width)
        over(n, lambda off: rs_copy(off).start())
        inbox[me] = stage[me]
        dx = jnp.dot(dabuf[slot], wxt[...], preferred_element_type=F32)
        stage2[slot] = dx.astype(BF).reshape(n, rows, width)
        over(n, lambda off: dx_copy(slot, off).start())
        inbox2[slot, me] = stage2[slot, me]
        da_copy(t).start()
        rs_wait()
        rown[...] = jnp.sum(inbox[...].astype(F32), axis=0)
        return 0

    lax.fori_loop(0, steps, backward, 0)
    dx_finish(0)

    @pl.when(second)
    def _():
        lax.fori_loop(0, steps, lambda t, _: (g_copy(t).wait_send(), 0)[1], 0)

    da_copy(1).wait()
    da_copy(0).wait()
    for at, (buf, dst) in enumerate(((xbuf, x_all), (hbuf.at[pl.ds(0, steps)], h_all),
                                     (ebuf, e_all), (dqbuf, dq_all))):
        pltpu.make_async_copy(buf, dst, st_sem.at[at]).start()
    for at, (buf, dst) in enumerate(((xbuf, x_all), (hbuf.at[pl.ds(0, steps)], h_all),
                                     (ebuf, e_all), (dqbuf, dq_all))):
        pltpu.make_async_copy(buf, dst, st_sem.at[at]).wait()


def lstm_call(n, x, wx, wh, bias, p, wxt, wht, pt, cot, chunk=16):
    steps, _, rows, width = x.shape
    cell = p.shape[0]
    total = n * rows
    sds = jax.ShapeDtypeStruct
    vm = pl.BlockSpec(memory_space=pltpu.VMEM)
    hb = pl.BlockSpec(memory_space=pl.ANY)
    keep = F32 if n <= 8 else BF
    V = pltpu.VMEM
    dma = pltpu.SemaphoreType.DMA
    return pl.pallas_call(
        functools.partial(lstm_kernel, n, chunk),
        out_shape=(
            sds((steps, rows, width), BF), sds((steps, rows, width), F32),
            sds((steps, n, rows, width), BF), sds((steps, n, rows, width), BF),
            sds((steps, total, 4 * cell), BF), sds((steps, total, cell), BF),
            sds((steps, n, rows, width), BF)),
        in_specs=[hb] + [vm] * 8,
        out_specs=(vm, vm, hb, hb, hb, hb, hb),
        scratch_shapes=[
            V((steps, n, rows, width), BF), V((steps + 1, n, rows, width), BF),
            V((steps, n, rows, width), BF), V((steps, total, 4 * cell), keep),
            V((steps + 1, total, cell), F32), V((steps, total, cell), BF),
            V((steps, rows, width), F32), V((total, 4 * cell), F32),
            V((total, cell), F32), V((2, total, 4 * cell), BF), V((total, cell), F32),
            V((n, rows, width), BF), V((n, rows, width), BF),
            V((2, n, rows, width), BF), V((2, n, rows, width), BF),
            V((steps, rows, width), BF), V((steps, rows, width), BF), V((rows, width), F32),
            dma, dma((n,)), dma((n,)), dma((n,)), dma((n,)), dma((n,)), dma((n,)), dma((2, n)), dma((2, n)),
            dma((steps,)), dma((steps,)), dma((steps,)), dma((steps,)), dma((2,)), dma((4,)),
        ],
        compiler_params=pltpu.CompilerParams(
            collective_id=0, has_side_effects=True, vmem_limit_bytes=60 * 1024 * 1024),
        name="relay_lstm",
    )(x, wx, wh, bias, p, wxt, wht, pt, cot)


def encode_forward(ids, weights):
    table_low, conv_low, conv_bias, highway_low, highway_bias, proj_low, proj_bias = weights
    valid_place = conv_masks(FILTERS)[1]
    pooled = jax.nn.logsumexp(conv_response(ids, table_low, conv_low, valid_place)[1], axis=1)
    features = jax.nn.silu(pooled + conv_bias)
    kept = [features]
    mixed = []
    for layer in range(2):
        pre = (
            jnp.dot(features.astype(BF), highway_low[layer], preferred_element_type=F32)
            + highway_bias[layer]
        )
        mixed.append(pre)
        gate = jax.nn.sigmoid(pre[:, FILTERS:])
        features = gate * features + (1.0 - gate) * jax.nn.silu(pre[:, :FILTERS])
        kept.append(features)
    encoded = jnp.dot(features.astype(BF), proj_low, preferred_element_type=F32) + proj_bias
    return encoded, pooled, kept, mixed


def to_columns(value):
    count = lax.axis_size(ALL)
    tokens, columns = value.shape
    split = jnp.transpose(value.reshape(tokens, count, columns // count), (1, 0, 2))
    return lax.all_to_all(split, ALL, 0, 0).reshape(count * tokens, columns // count)


def conv_backward(ids, table_low, conv_low, grad_before):
    weight_mask, valid_place = conv_masks(FILTERS)
    windows, response = conv_response(ids, table_low, conv_low, valid_place)
    share = jax.nn.softmax(response, axis=1)
    grad_response = (grad_before[:, None, :] * share).astype(BF)
    grad_conv = jnp.einsum("bpk,bpf->kf", windows, grad_response, preferred_element_type=F32)
    grad_windows = jnp.einsum("bpf,kf->bpk", grad_response, conv_low, preferred_element_type=F32)
    grad_embedded = jnp.zeros((ids.shape[0], CHARS + KMAX - 1, CDIM), F32)
    for offset in range(KMAX):
        grad_embedded = grad_embedded + jnp.pad(
            grad_windows[:, :, offset * CDIM : (offset + 1) * CDIM],
            ((0, 0), (offset, KMAX - 1 - offset), (0, 0)),
        )
    grad_embedded = grad_embedded[:, :CHARS].astype(BF)
    one_hot = (ids[:, :, None] == jnp.arange(CVOCAB, dtype=jnp.int32)).astype(BF)
    grad_table = jnp.einsum("bpv,bpc->vc", one_hot, grad_embedded, preferred_element_type=F32)
    return grad_conv * weight_mask, grad_table


def local(
    chars,
    lengths,
    char_emb,
    conv_weight,
    conv_bias,
    highway_weight,
    highway_bias,
    proj_weight,
    proj_bias,
    gate_weight,
    gate_bias,
    cell_proj,
    cotangent,
):
    n = lax.axis_size("dp")
    pipe = lax.axis_index("pipe")
    direction = lax.axis_index("dir")
    me = lax.axis_index("dp")
    everyone = lax.axis_size(ALL)
    seqs, steps, char_count = chars.shape
    parts = everyone // n
    quarter = seqs // parts
    tokens = quarter * steps
    width = cell_proj.shape[3]
    cell = cell_proj.shape[2]

    conv_full = lax.all_gather(conv_weight.astype(BF), ("dir", "dp"), axis=1, tiled=True)
    highway_full = lax.all_gather(highway_weight.astype(BF), ("dir", "dp"), axis=2, tiled=True)
    proj_full = lax.all_gather(proj_weight.astype(BF), ("dir", "dp"), axis=0, tiled=True)
    all_lengths = lax.all_to_all(
        jnp.broadcast_to(lengths, (n, seqs)), "dp", 0, 0
    ).reshape(n * seqs)

    in_rows = gate_weight.shape[2]
    gate_low = gate_weight[0, 0].astype(BF).reshape(in_rows, 4, n, cell)
    gate_low = jnp.transpose(gate_low, (2, 0, 1, 3)).reshape(n, in_rows, 4 * cell)
    gate_own = lax.all_to_all(gate_low, "dp", 0, 0).reshape(n * in_rows, 4 * cell)
    bias_own = lax.dynamic_index_in_dim(
        gate_bias[0, 0].reshape(4, n, cell), me, 1, keepdims=False
    ).reshape(1, 4 * cell)
    cell_low = cell_proj[0, 0].astype(BF)

    def order_matrix(sizes):
        place = jnp.arange(steps, dtype=jnp.int32)[None, :]
        live = place < sizes[:, None]
        order = jnp.where(live & (direction == 1), sizes[:, None] - 1 - place, place)
        return ((order[:, :, None] == place[:, None, :]) & live[:, :, None]).astype(BF)

    own_order = order_matrix(lengths)
    cot = jnp.einsum("rts,rsd->trd", own_order, cotangent[0, 0], preferred_element_type=BF)

    ids = lax.dynamic_slice_in_dim(
        chars, (pipe * lax.axis_size("dir") + direction) * quarter, quarter, 0
    ).reshape(tokens, char_count)
    weight_mask = conv_masks(FILTERS)[0]
    table_low = char_emb.astype(BF)
    conv_low = conv_full * weight_mask.astype(BF)
    encoded, pooled, kept, mixed = encode_forward(
        ids,
        (table_low, conv_low, conv_bias, highway_full, highway_bias, proj_full, proj_bias),
    )
    encoded_all = lax.all_gather(
        encoded.astype(BF).reshape(quarter, steps, width), ("dp", "pipe", "dir"), axis=0, tiled=True
    )
    inputs = jnp.einsum(
        "rts,rsd->trd", order_matrix(all_lengths), encoded_all, preferred_element_type=BF
    ).reshape(steps, n, seqs, width)
    kept_low = [value.astype(BF) for value in kept]
    kept_all = [lax.all_gather(value, ALL, axis=0, tiled=True) for value in kept_low[:2]]
    last_columns = to_columns(kept_low[2])

    out_own, dx_own, x_all, h_all, da_all, e_all, dq_all = lstm_call(
        n,
        inputs,
        gate_own[:width],
        gate_own[width:],
        bias_own,
        cell_low,
        gate_own[:width].T,
        gate_own[width:].T,
        cell_low.T,
        cot,
    )
    activations = jnp.einsum("rts,srd->rtd", own_order, out_own, preferred_element_type=BF)

    total = steps * n * seqs
    da_flat = da_all.reshape(total, 4 * cell)
    grad_gate = jnp.concatenate(
        [
            jnp.einsum(
                "tk,tg->kg", part.reshape(total, width), da_flat, preferred_element_type=F32
            ).astype(BF)
            for part in (x_all, h_all)
        ]
    ).reshape(n, in_rows, 4 * cell)
    grad_gate = lax.all_to_all(grad_gate, "dp", 0, 0).reshape(n, in_rows, 4, cell)
    grad_gate = jnp.transpose(grad_gate, (1, 2, 0, 3)).reshape(in_rows, 4 * n * cell).astype(F32)
    grad_bias = jnp.sum(da_flat.astype(F32), axis=0).reshape(4, cell)
    grad_bias = jnp.transpose(lax.all_gather(grad_bias, "dp"), (1, 0, 2)).reshape(n, 4 * cell)
    grad_bias = lax.dynamic_index_in_dim(grad_bias, me, 0, keepdims=False)
    grad_cell = jnp.einsum(
        "tc,td->cd",
        e_all.reshape(total, cell),
        dq_all.reshape(total, width),
        preferred_element_type=F32,
    )

    grad_stored = jnp.einsum(
        "rts,srd->rtd", own_order, dx_own.astype(BF), preferred_element_type=F32
    )
    grad_stored = jnp.where(pipe == 1, grad_stored, 0.0).astype(BF)
    grad_encoded = lax.psum_scatter(
        grad_stored, ("pipe", "dir"), scatter_dimension=0, tiled=True
    ).reshape(tokens, width)
    encoded_grads = lax.all_gather(grad_encoded, ALL, axis=0, tiled=True)

    grad_proj_bias = jnp.sum(grad_encoded.astype(F32), axis=0)
    grad_features = jnp.einsum("td,fd->tf", grad_encoded, proj_full, preferred_element_type=F32)
    grad_highway = [None, None]
    grad_highway_bias = [None, None]
    for layer in (1, 0):
        nonlinear = mixed[layer][:, :FILTERS]
        gate = jax.nn.sigmoid(mixed[layer][:, FILTERS:])
        grad_mixed = jnp.concatenate(
            [
                grad_features * (1.0 - gate) * silu_slope(nonlinear),
                grad_features * (kept[layer] - jax.nn.silu(nonlinear)) * gate * (1.0 - gate),
            ],
            axis=1,
        ).astype(BF)
        grad_highway[layer] = jnp.einsum(
            "tf,tg->fg", kept_all[layer], to_columns(grad_mixed), preferred_element_type=F32
        )
        grad_highway_bias[layer] = jnp.sum(grad_mixed.astype(F32), axis=0)
        grad_features = grad_features * gate + jnp.einsum(
            "tg,fg->tf", grad_mixed, highway_full[layer], preferred_element_type=F32
        )
    grad_proj = jnp.einsum("tf,td->fd", last_columns, encoded_grads, preferred_element_type=F32)
    grad_before = grad_features * silu_slope(pooled + conv_bias)
    grad_conv, grad_table = conv_backward(ids, table_low, conv_low, grad_before)

    small = (
        grad_table,
        jnp.sum(grad_before, axis=0),
        jnp.stack(grad_highway_bias),
        grad_proj_bias,
    )
    flat = jnp.concatenate([value.reshape(-1) for value in small])
    share = -(-flat.shape[0] // (everyone * 128)) * 128
    flat = jnp.pad(flat, (0, share * everyone - flat.shape[0])).reshape(everyone, share)
    columns = FILTERS // everyone
    packed = jnp.concatenate(
        [
            jnp.transpose(
                grad_conv.reshape(KMAX * CDIM, everyone, columns), (1, 0, 2)
            ).reshape(everyone, KMAX * CDIM * columns),
            flat,
        ],
        axis=1,
    ).astype(BF)
    summed = jnp.sum(lax.all_to_all(packed, ALL, 0, 0).astype(F32), axis=0)
    grad_conv = summed[: KMAX * CDIM * columns].reshape(KMAX * CDIM, columns)
    shared = lax.all_to_all(
        jnp.broadcast_to(summed[KMAX * CDIM * columns :], (everyone, share)), ALL, 0, 0
    ).reshape(-1)
    small_sums = []
    start = 0
    for value in small:
        small_sums.append(shared[start : start + value.size].reshape(value.shape))
        start += value.size
    return (
        activations[None, None],
        small_sums[0],
        grad_conv,
        small_sums[1],
        jnp.stack(grad_highway),
        small_sums[2],
        grad_proj,
        small_sums[3],
        grad_gate[None, None],
        grad_bias[None, None],
        grad_cell[None, None],
    )


def solution(mesh):
    return jax.shard_map(
        local,
        mesh=mesh,
        in_specs=(
            P("dp", None, None),
            P("dp"),
            P(),
            P(None, ("dir", "dp")),
            P(),
            P(None, None, ("dir", "dp")),
            P(),
            P(("dir", "dp"), None),
            P(),
            P("pipe", "dir", "dp", None),
            P("pipe", "dir", None),
            P("pipe", "dir", "dp", None),
            P("pipe", "dir", "dp", None, None),
        ),
        out_specs=(
            P("pipe", "dir", "dp", None, None),
            P(),
            P(None, ("pipe", "dir", "dp")),
            P(),
            P(None, None, ("pipe", "dir", "dp")),
            P(),
            P(("pipe", "dir", "dp"), None),
            P(),
            P("pipe", "dir", "dp", None),
            P("pipe", "dir", "dp"),
            P("pipe", "dir", "dp", None),
        ),
        check_vma=False,
    )
```

```python
import functools
import math

import jax
import jax.numpy as jnp
from jax import lax
from jax.experimental import pallas as pl
from jax.experimental.pallas import tpu as pltpu
from jax.sharding import PartitionSpec as P

FILTERS = 2048
CDIM = 16
CVOCAB = 262
CHARS = 50
KMAX = 7
CLIP_LIMIT = 3.0
MASKED_FILL = -1000000000.0
MESH = pl.DeviceIdType.MESH
BF = jnp.bfloat16
F32 = jnp.float32
ALL = ("pipe", "dir", "dp")


def silu_slope(value):
    sig = jax.nn.sigmoid(value)
    return sig * (1.0 + value * (1.0 - sig))


def filter_widths(filter_count):
    filter_index = jnp.arange(filter_count, dtype=jnp.int32)
    filter_width = jnp.ones((filter_count,), jnp.int32)
    for doubling in range(6):
        filter_width = filter_width + (filter_index >= filter_count // 64 * (1 << doubling)).astype(
            jnp.int32
        )
    return filter_width


def conv_masks(filter_count):
    filter_width = filter_widths(filter_count)
    offset_rows = jnp.arange(KMAX * CDIM, dtype=jnp.int32) // CDIM
    weight_mask = (offset_rows[:, None] < filter_width[None, :]).astype(jnp.float32)
    valid_place = jnp.arange(CHARS, dtype=jnp.int32)[:, None] <= CHARS - filter_width[None, :]
    return (weight_mask, valid_place)


def make_windows(embedded):
    padded = jnp.pad(embedded, ((0, 0), (0, KMAX - 1), (0, 0)))
    return jnp.concatenate(
        [padded[:, offset : offset + CHARS, :] for offset in range(KMAX)], axis=2
    )


def conv_response(ids_block, table_low, conv_low, valid_place):
    embedded = jnp.take(table_low, ids_block, axis=0)
    windows = make_windows(embedded)
    response = jnp.einsum("bpk,kf->bpf", windows, conv_low, preferred_element_type=jnp.float32)
    return (windows, jnp.where(valid_place[None], response, MASKED_FILL))


def over(count, step):
    if count <= 9:
        for off in range(1, count):
            step(off)
    else:
        lax.fori_loop(1, count, lambda off, _: (step(off), 0)[1], 0)


def lstm_kernel(
    n, chunk,
    x_hbm, wx, wh, bias, p, wxt, wht, pt, cot,
    out_ref, dx_ref, dw_hbm, db_ref, dp_ref,
    xbuf, hbuf, dqbuf, gates, cells, ebuf, hown, gscr, escr, dabuf, ucell, dwacc,
    stage, inbox, stage2, inbox2, relay, gbuf, rown,
    load_sem, ag_send, ag_recv, dq_send, dq_recv, rs_send, rs_recv, dx_send, dx_recv,
    x_send, x_recv, g_send, g_recv, st_sem,
):
    steps, _, rows, width = xbuf.shape
    total = n * rows
    cell = cells.shape[2]
    pipe = lax.axis_index("pipe")
    direction = lax.axis_index("dir")
    me = lax.axis_index("dp")
    first = pipe == 1
    second = pipe == 0
    partner = (1 - pipe, direction, me)

    def peer(off):
        return lax.rem(me + off, n)

    barrier = pltpu.get_barrier_semaphore()
    over(n, lambda off: pl.semaphore_signal(
        barrier, inc=1, device_id=(pipe, direction, peer(off)), device_id_type=MESH))
    pl.semaphore_signal(barrier, inc=1, device_id=partner, device_id_type=MESH)

    @pl.when(first)
    def _():
        load = pltpu.make_async_copy(x_hbm, xbuf, load_sem)
        load.start()
        load.wait()

    hbuf[0] = jnp.zeros((n, rows, width), BF)
    cells[0] = jnp.zeros((total, cell), F32)
    pl.semaphore_wait(barrier, n)

    def ag_copy(buf, slot, off):
        out, into = (ag_send, ag_recv) if buf is hbuf else (dq_send, dq_recv)
        return pltpu.make_async_remote_copy(
            src_ref=buf.at[slot, me], dst_ref=buf.at[slot, me],
            send_sem=out.at[off], recv_sem=into.at[off],
            device_id=(pipe, direction, peer(off)), device_id_type=MESH)

    def rs_copy(off):
        return pltpu.make_async_remote_copy(
            src_ref=stage.at[peer(off)], dst_ref=inbox.at[me],
            send_sem=rs_send.at[off], recv_sem=rs_recv.at[off],
            device_id=(pipe, direction, peer(off)), device_id_type=MESH)

    def dx_copy(slot, off):
        return pltpu.make_async_remote_copy(
            src_ref=stage2.at[slot, peer(off)], dst_ref=inbox2.at[slot, me],
            send_sem=dx_send.at[slot, off], recv_sem=dx_recv.at[slot, off],
            device_id=(pipe, direction, peer(off)), device_id_type=MESH)

    def x_copy(t):
        return pltpu.make_async_remote_copy(
            src_ref=hbuf.at[t + 1], dst_ref=xbuf.at[t],
            send_sem=x_send.at[t], recv_sem=x_recv.at[t],
            device_id=partner, device_id_type=MESH)

    def g_copy(t):
        return pltpu.make_async_remote_copy(
            src_ref=relay.at[t], dst_ref=gbuf.at[t],
            send_sem=g_send.at[t], recv_sem=g_recv.at[t],
            device_id=partner, device_id_type=MESH)

    def ag_wait(buf, slot):
        def both(off):
            ag_copy(buf, slot, off).wait_send()
            ag_copy(buf, slot, off).wait_recv()
        over(n, both)

    def rs_wait():
        def both(off):
            rs_copy(off).wait_send()
            rs_copy(off).wait_recv()
        over(n, both)

    def forward(t, _):
        @pl.when(second)
        def _():
            x_copy(t).wait_recv()

        gscr[...] = jnp.dot(
            xbuf[t].reshape(total, width), wx[...], preferred_element_type=F32) + bias[...]

        @pl.when(t > 0)
        def _():
            ag_wait(hbuf, t)

            @pl.when(first)
            def _():
                x_copy(t - 1).start()

        gscr[...] += jnp.dot(
            hbuf[t].reshape(total, width), wh[...], preferred_element_type=F32)

        def rows_step(k, _):
            at = pl.ds(pl.multiple_of(k * chunk, chunk), chunk)
            g = gscr[at, :]
            i = jax.nn.sigmoid(g[:, :cell])
            f = jax.nn.sigmoid(g[:, cell:2 * cell])
            m = jnp.tanh(g[:, 2 * cell:3 * cell])
            o = jax.nn.sigmoid(g[:, 3 * cell:])
            c = 3.0 * jnp.tanh((i * m + f * cells[t, at, :]) * (1.0 / 3.0))
            cells[t + 1, at, :] = c
            ebuf[t, at, :] = (o * jnp.tanh(c)).astype(BF)
            kind = gates.dtype
            gates[t, at, :cell] = i.astype(kind)
            gates[t, at, cell:2 * cell] = f.astype(kind)
            gates[t, at, 2 * cell:3 * cell] = m.astype(kind)
            gates[t, at, 3 * cell:] = o.astype(kind)
            return 0

        lax.fori_loop(0, total // chunk, rows_step, 0)
        q = jnp.dot(ebuf[t], p[...], preferred_element_type=F32)
        stage[...] = q.astype(BF).reshape(n, rows, width)
        over(n, lambda off: rs_copy(off).start())
        inbox[me] = stage[me]
        rs_wait()
        h = 3.0 * jnp.tanh(jnp.sum(inbox[...].astype(F32), axis=0) * (1.0 / 3.0))
        hown[t] = h
        hbuf[t + 1, me] = h.astype(BF)
        over(n, lambda off: ag_copy(hbuf, t + 1, off).start())
        add = jnp.where(second, 1.0, 0.0)
        out_ref[t] = (h + add * xbuf[t, me].astype(F32)).astype(BF)
        return 0

    lax.fori_loop(0, steps, forward, 0)
    ag_wait(hbuf, steps)

    @pl.when(first)
    def _():
        x_copy(steps - 1).start()
        lax.fori_loop(0, steps, lambda t, _: (x_copy(t).wait_send(), 0)[1], 0)

    rown[...] = jnp.zeros((rows, width), F32)
    ucell[...] = jnp.zeros((total, cell), F32)
    dwacc[...] = jnp.zeros(dwacc.shape, F32)
    db_ref[...] = jnp.zeros(db_ref.shape, F32)
    dp_ref[...] = jnp.zeros(dp_ref.shape, F32)

    def dx_finish(t):
        slot = lax.rem(t, 2)

        def both(off):
            dx_copy(slot, off).wait_send()
            dx_copy(slot, off).wait_recv()
        over(n, both)
        dx = jnp.sum(inbox2[slot].astype(F32), axis=0)
        dx_ref[t] = dx

        @pl.when(second)
        def _():
            relay[t] = (dx + cot[t].astype(F32)).astype(BF)
            g_copy(t).start()

    def backward(k, _):
        t = steps - 1 - k
        slot = lax.rem(t, 2)
        up = rown[...] + cot[t].astype(F32)
        rown[...] = up

        @pl.when(first)
        def _():
            g_copy(t).wait_recv()
            rown[...] = rown[...] + gbuf[t].astype(F32)

        ratio = hown[t] * (1.0 / 3.0)
        dqbuf[t, me] = (rown[...] * (1.0 - ratio * ratio)).astype(BF)
        over(n, lambda off: ag_copy(dqbuf, t, off).start())

        @pl.when(k > 0)
        def _():
            dx_finish(t + 1)

        ag_wait(dqbuf, t)
        escr[...] = jnp.dot(
            dqbuf[t].reshape(total, width), pt[...], preferred_element_type=F32)

        def rows_step(j, _):
            at = pl.ds(pl.multiple_of(j * chunk, chunk), chunk)
            de = escr[at, :]
            i = gates[t, at, :cell].astype(F32)
            f = gates[t, at, cell:2 * cell].astype(F32)
            m = gates[t, at, 2 * cell:3 * cell].astype(F32)
            o = gates[t, at, 3 * cell:].astype(F32)
            c = cells[t + 1, at, :]
            tc = jnp.tanh(c)
            cr = c * (1.0 / 3.0)
            dc = (de * o * (1.0 - tc * tc) + ucell[at, :]) * (1.0 - cr * cr)
            ucell[at, :] = dc * f
            for block, value in enumerate((
                dc * m * i * (1.0 - i),
                dc * cells[t, at, :] * f * (1.0 - f),
                dc * i * (1.0 - m * m),
                de * tc * o * (1.0 - o),
            )):
                value = value.astype(BF)
                where = pl.ds(block * cell, cell)
                dabuf[0, at, where] = value
                db_ref[:, where] += jnp.sum(value.astype(F32), axis=0, keepdims=True)
            return 0

        lax.fori_loop(0, total // chunk, rows_step, 0)
        r = jnp.dot(dabuf[0], wht[...], preferred_element_type=F32)
        stage[...] = r.astype(BF).reshape(n, rows, width)
        over(n, lambda off: rs_copy(off).start())
        inbox[me] = stage[me]
        dx = jnp.dot(dabuf[0], wxt[...], preferred_element_type=F32)
        stage2[slot] = dx.astype(BF).reshape(n, rows, width)
        over(n, lambda off: dx_copy(slot, off).start())
        inbox2[slot, me] = stage2[slot, me]
        for half, buf in enumerate((xbuf, hbuf)):
            dwacc[pl.ds(half * width, width), :] += lax.dot_general(
                buf[t].reshape(total, width), dabuf[0], (((0,), (0,)), ((), ())),
                preferred_element_type=F32)
        dp_ref[...] += lax.dot_general(
            ebuf[t], dqbuf[t].reshape(total, width), (((0,), (0,)), ((), ())),
            preferred_element_type=F32)
        rs_wait()
        rown[...] = jnp.sum(inbox[...].astype(F32), axis=0)
        return 0

    lax.fori_loop(0, steps, backward, 0)
    dx_finish(0)

    @pl.when(second)
    def _():
        lax.fori_loop(0, steps, lambda t, _: (g_copy(t).wait_send(), 0)[1], 0)

    pieces = 2 * width // total

    def dw_copy(piece):
        return pltpu.make_async_copy(
            dabuf.at[piece % 2], dw_hbm.at[pl.ds(piece * total, total)], st_sem.at[piece % 2])

    for piece in range(pieces):
        if piece > 1:
            dw_copy(piece - 2).wait()
        dabuf[piece % 2] = dwacc[pl.ds(piece * total, total), :].astype(BF)
        dw_copy(piece).start()
    for piece in range(max(0, pieces - 2), pieces):
        dw_copy(piece).wait()


def lstm_call(n, x, wx, wh, bias, p, wxt, wht, pt, cot, chunk=16):
    steps, _, rows, width = x.shape
    cell = p.shape[0]
    total = n * rows
    sds = jax.ShapeDtypeStruct
    vm = pl.BlockSpec(memory_space=pltpu.VMEM)
    hb = pl.BlockSpec(memory_space=pl.ANY)
    keep = F32 if n <= 8 else BF
    V = pltpu.VMEM
    dma = pltpu.SemaphoreType.DMA
    return pl.pallas_call(
        functools.partial(lstm_kernel, n, chunk),
        out_shape=(
            sds((steps, rows, width), BF), sds((steps, rows, width), F32),
            sds((2 * width, 4 * cell), BF), sds((1, 4 * cell), F32), sds((cell, width), F32)),
        in_specs=[hb] + [vm] * 8,
        out_specs=(vm, vm, hb, vm, vm),
        scratch_shapes=[
            V((steps, n, rows, width), BF), V((steps + 1, n, rows, width), BF),
            V((steps, n, rows, width), BF), V((steps, total, 4 * cell), keep),
            V((steps + 1, total, cell), F32), V((steps, total, cell), BF),
            V((steps, rows, width), F32), V((total, 4 * cell), F32),
            V((total, cell), F32), V((2, total, 4 * cell), BF), V((total, cell), F32),
            V((2 * width, 4 * cell), F32),
            V((n, rows, width), BF), V((n, rows, width), BF),
            V((2, n, rows, width), BF), V((2, n, rows, width), BF),
            V((steps, rows, width), BF), V((steps, rows, width), BF), V((rows, width), F32),
            dma, dma((n,)), dma((n,)), dma((n,)), dma((n,)), dma((n,)), dma((n,)), dma((2, n)), dma((2, n)),
            dma((steps,)), dma((steps,)), dma((steps,)), dma((steps,)), dma((2,)),
        ],
        compiler_params=pltpu.CompilerParams(
            collective_id=0, has_side_effects=True, vmem_limit_bytes=60 * 1024 * 1024),
        cost_estimate=pl.CostEstimate(
            flops=300_000_000_000, bytes_accessed=64 * 1024 * 1024, transcendentals=0),
        name="relay_lstm",
    )(x, wx, wh, bias, p, wxt, wht, pt, cot)


def split_cells(weight, n):
    rows, gates = weight.shape
    cell = gates // (4 * n)

    def body(src, dst):
        for k in range(n):
            dst[k] = src[:, k * cell : (k + 1) * cell].astype(BF)

    return pl.pallas_call(
        body,
        grid=(4,),
        out_shape=jax.ShapeDtypeStruct((n, rows, 4 * cell), BF),
        in_specs=[pl.BlockSpec((rows, n * cell), lambda b: (0, b))],
        out_specs=pl.BlockSpec((n, rows, cell), lambda b: (0, 0, b)),
        cost_estimate=pl.CostEstimate(
            flops=0, bytes_accessed=6 * rows * gates, transcendentals=0
        ),
        name="split_cells",
    )(weight)


def join_cells(blocks):
    n, rows, gates = blocks.shape
    cell = gates // 4

    def body(src, dst):
        for k in range(n):
            dst[:, k * cell : (k + 1) * cell] = src[k].astype(F32)

    return pl.pallas_call(
        body,
        grid=(4,),
        out_shape=jax.ShapeDtypeStruct((rows, n * gates), F32),
        in_specs=[pl.BlockSpec((n, rows, cell), lambda b: (0, 0, b))],
        out_specs=pl.BlockSpec((rows, n * cell), lambda b: (0, b)),
        cost_estimate=pl.CostEstimate(
            flops=0, bytes_accessed=6 * n * rows * gates, transcendentals=0
        ),
        name="join_cells",
    )(blocks)


def encode_forward(ids, weights):
    table_low, conv_low, conv_bias, highway_low, highway_bias, proj_low, proj_bias = weights
    valid_place = conv_masks(FILTERS)[1]
    pooled = jax.nn.logsumexp(conv_response(ids, table_low, conv_low, valid_place)[1], axis=1)
    features = jax.nn.silu(pooled + conv_bias)
    kept = [features]
    mixed = []
    for layer in range(2):
        pre = (
            jnp.dot(features.astype(BF), highway_low[layer], preferred_element_type=F32)
            + highway_bias[layer]
        )
        mixed.append(pre)
        gate = jax.nn.sigmoid(pre[:, FILTERS:])
        features = gate * features + (1.0 - gate) * jax.nn.silu(pre[:, :FILTERS])
        kept.append(features)
    encoded = jnp.dot(features.astype(BF), proj_low, preferred_element_type=F32) + proj_bias
    return encoded, pooled, kept, mixed


def to_columns(value):
    count = lax.axis_size(ALL)
    tokens, columns = value.shape
    split = jnp.transpose(value.reshape(tokens, count, columns // count), (1, 0, 2))
    return lax.all_to_all(split, ALL, 0, 0).reshape(count * tokens, columns // count)


def conv_backward(ids, table_low, conv_low, grad_before):
    weight_mask, valid_place = conv_masks(FILTERS)
    windows, response = conv_response(ids, table_low, conv_low, valid_place)
    share = jax.nn.softmax(response, axis=1)
    grad_response = (grad_before[:, None, :] * share).astype(BF)
    grad_conv = jnp.einsum("bpk,bpf->kf", windows, grad_response, preferred_element_type=F32)
    grad_windows = jnp.einsum("bpf,kf->bpk", grad_response, conv_low, preferred_element_type=F32)
    grad_embedded = jnp.zeros((ids.shape[0], CHARS + KMAX - 1, CDIM), F32)
    for offset in range(KMAX):
        grad_embedded = grad_embedded + jnp.pad(
            grad_windows[:, :, offset * CDIM : (offset + 1) * CDIM],
            ((0, 0), (offset, KMAX - 1 - offset), (0, 0)),
        )
    grad_embedded = grad_embedded[:, :CHARS].astype(BF)
    one_hot = (ids[:, :, None] == jnp.arange(CVOCAB, dtype=jnp.int32)).astype(BF)
    grad_table = jnp.einsum("bpv,bpc->vc", one_hot, grad_embedded, preferred_element_type=F32)
    return grad_conv * weight_mask, grad_table


def local(
    chars,
    lengths,
    char_emb,
    conv_weight,
    conv_bias,
    highway_weight,
    highway_bias,
    proj_weight,
    proj_bias,
    gate_weight,
    gate_bias,
    cell_proj,
    cotangent,
):
    n = lax.axis_size("dp")
    pipe = lax.axis_index("pipe")
    direction = lax.axis_index("dir")
    me = lax.axis_index("dp")
    everyone = lax.axis_size(ALL)
    seqs, steps, char_count = chars.shape
    parts = everyone // n
    quarter = seqs // parts
    tokens = quarter * steps
    width = cell_proj.shape[3]
    cell = cell_proj.shape[2]

    holders = lax.axis_size(("dir", "dp"))
    mine = conv_weight.shape[1]
    conv_full = lax.all_to_all(
        jnp.broadcast_to(conv_weight.astype(BF), (holders, KMAX * CDIM, mine)), ("dir", "dp"), 0, 0
    )
    conv_full = jnp.transpose(conv_full, (1, 0, 2)).reshape(KMAX * CDIM, FILTERS)
    proj_rows = proj_weight.shape[0]
    block = highway_weight.shape[2]
    pieces = width // block
    proj_blocks = jnp.transpose(proj_weight.reshape(proj_rows, pieces, block), (1, 0, 2))
    proj_blocks = proj_blocks.reshape(2, pieces * proj_rows // 2, block)
    gathered = lax.all_gather(
        jnp.concatenate([highway_weight, proj_blocks], axis=1).astype(BF),
        ("dir", "dp"),
        axis=2,
        tiled=True,
    )
    all_lengths = lax.all_to_all(
        jnp.broadcast_to(lengths, (n, seqs)), "dp", 0, 0
    ).reshape(n * seqs)

    in_rows = gate_weight.shape[2]
    gate_low, gathered = lax.optimization_barrier(
        (split_cells(gate_weight[0, 0], n), gathered)
    )
    gate_own = lax.all_to_all(gate_low, "dp", 0, 0).reshape(n * in_rows, 4 * cell)
    highway_full = gathered[:, :FILTERS]
    proj_full = gathered[:, FILTERS:].reshape(pieces, proj_rows, holders, block)
    proj_full = jnp.transpose(proj_full, (2, 1, 0, 3)).reshape(FILTERS, width)
    bias_own = lax.dynamic_index_in_dim(
        gate_bias[0, 0].reshape(4, n, cell), me, 1, keepdims=False
    ).reshape(1, 4 * cell)
    cell_low = cell_proj[0, 0].astype(BF)

    def order_matrix(sizes):
        place = jnp.arange(steps, dtype=jnp.int32)[None, :]
        live = place < sizes[:, None]
        order = jnp.where(live & (direction == 1), sizes[:, None] - 1 - place, place)
        return ((order[:, :, None] == place[:, None, :]) & live[:, :, None]).astype(BF)

    own_order = order_matrix(lengths)
    cot = jnp.einsum("rts,rsd->trd", own_order, cotangent[0, 0], preferred_element_type=BF)

    ids = lax.dynamic_slice_in_dim(
        chars, (pipe * lax.axis_size("dir") + direction) * quarter, quarter, 0
    ).reshape(tokens, char_count)
    weight_mask = conv_masks(FILTERS)[0]
    table_low = char_emb.astype(BF)
    conv_low = conv_full * weight_mask.astype(BF)
    encoded, pooled, kept, mixed = encode_forward(
        ids,
        (table_low, conv_low, conv_bias, highway_full, highway_bias, proj_full, proj_bias),
    )
    encoded_all = lax.all_gather(
        encoded.astype(BF).reshape(quarter, steps, width), ("dp", "pipe", "dir"), axis=0, tiled=True
    )
    kept_low = [value.astype(BF) for value in kept]
    kept_low, encoded_all, gate_own = lax.optimization_barrier((kept_low, encoded_all, gate_own))
    kept_all = [lax.all_gather(value, ALL, axis=0, tiled=True) for value in kept_low[:2]]
    last_columns = to_columns(kept_low[2])
    inputs = jnp.einsum(
        "rts,rsd->trd", order_matrix(all_lengths), encoded_all, preferred_element_type=BF
    ).reshape(steps, n, seqs, width)

    out_own, dx_own, grad_gate, grad_bias, grad_cell = lstm_call(
        n,
        inputs,
        gate_own[:width],
        gate_own[width:],
        bias_own,
        cell_low,
        gate_own[:width].T,
        gate_own[width:].T,
        cell_low.T,
        cot,
    )
    dx_own, kept_all, last_columns = lax.optimization_barrier((dx_own, kept_all, last_columns))
    activations = jnp.einsum("rts,srd->rtd", own_order, out_own, preferred_element_type=BF)

    grad_gate = grad_gate.reshape(n, 2, in_rows // 2, 4 * cell)
    gate_halves = [lax.all_to_all(grad_gate[:, half], "dp", 0, 0) for half in range(2)]
    grad_bias = lax.all_to_all(
        jnp.broadcast_to(grad_bias, (n, 4 * cell)), "dp", 0, 0
    ).reshape(n, 4, cell)
    grad_bias = jnp.transpose(grad_bias, (1, 0, 2)).reshape(n, 4 * cell)
    grad_bias = lax.dynamic_index_in_dim(grad_bias, me, 0, keepdims=False)

    grad_stored = jnp.einsum(
        "rts,srd->rtd", own_order, dx_own.astype(BF), preferred_element_type=F32
    )
    grad_stored = jnp.where(pipe == 1, grad_stored, 0.0).astype(BF)
    grad_encoded = lax.psum_scatter(
        grad_stored, ("pipe", "dir"), scatter_dimension=0, tiled=True
    ).reshape(tokens, width)
    encoded_grads = lax.all_gather(grad_encoded, ALL, axis=0, tiled=True)

    grad_proj_bias = jnp.sum(grad_encoded.astype(F32), axis=0)
    grad_features = jnp.einsum("td,fd->tf", grad_encoded, proj_full, preferred_element_type=F32)
    columns = [None, None]
    grad_highway_bias = [None, None]
    for layer in (1, 0):
        nonlinear = mixed[layer][:, :FILTERS]
        gate = jax.nn.sigmoid(mixed[layer][:, FILTERS:])
        grad_mixed = jnp.concatenate(
            [
                grad_features * (1.0 - gate) * silu_slope(nonlinear),
                grad_features * (kept[layer] - jax.nn.silu(nonlinear)) * gate * (1.0 - gate),
            ],
            axis=1,
        ).astype(BF)
        columns[layer] = to_columns(grad_mixed)
        grad_highway_bias[layer] = jnp.sum(grad_mixed.astype(F32), axis=0)
        grad_features = grad_features * gate + jnp.einsum(
            "tg,fg->tf", grad_mixed, highway_full[layer], preferred_element_type=F32
        )
        if layer == 1:
            grad_features, gate_halves[0] = lax.optimization_barrier(
                (grad_features, gate_halves[0])
            )
    grad_features, columns[1] = lax.optimization_barrier((grad_features, columns[1]))
    grad_proj = jnp.einsum("tf,td->fd", last_columns, encoded_grads, preferred_element_type=F32)
    grad_before = grad_features * silu_slope(pooled + conv_bias)
    grad_conv, grad_table = conv_backward(ids, table_low, conv_low, grad_before)
    grad_conv, gate_halves[1], columns[0] = lax.optimization_barrier(
        (grad_conv, gate_halves[1], columns[0])
    )
    grad_highway = [
        jnp.einsum("tf,tg->fg", kept_all[layer], columns[layer], preferred_element_type=F32)
        for layer in range(2)
    ]
    grad_gate = join_cells(jnp.concatenate(gate_halves, axis=1))

    small = (
        grad_table,
        jnp.sum(grad_before, axis=0),
        jnp.stack(grad_highway_bias),
        grad_proj_bias,
    )
    flat = jnp.concatenate([value.reshape(-1) for value in small])
    share = -(-flat.shape[0] // (everyone * 128)) * 128
    flat = jnp.pad(flat, (0, share * everyone - flat.shape[0])).reshape(everyone, share)
    columns = FILTERS // everyone
    packed = jnp.concatenate(
        [
            jnp.transpose(
                grad_conv.reshape(KMAX * CDIM, everyone, columns), (1, 0, 2)
            ).reshape(everyone, KMAX * CDIM * columns),
            flat,
        ],
        axis=1,
    ).astype(BF)
    summed = jnp.sum(lax.all_to_all(packed, ALL, 0, 0).astype(F32), axis=0)
    grad_conv = summed[: KMAX * CDIM * columns].reshape(KMAX * CDIM, columns)
    shared = lax.all_to_all(
        jnp.broadcast_to(summed[KMAX * CDIM * columns :], (everyone, share)), ALL, 0, 0
    ).reshape(-1)
    small_sums = []
    start = 0
    for value in small:
        small_sums.append(shared[start : start + value.size].reshape(value.shape))
        start += value.size
    return (
        activations[None, None],
        small_sums[0],
        grad_conv,
        small_sums[1],
        jnp.stack(grad_highway),
        small_sums[2],
        grad_proj,
        small_sums[3],
        grad_gate[None, None],
        grad_bias[None, None],
        grad_cell[None, None],
    )


def solution(mesh):
    return jax.shard_map(
        local,
        mesh=mesh,
        in_specs=(
            P("dp", None, None),
            P("dp"),
            P(),
            P(None, ("dir", "dp")),
            P(),
            P(None, None, ("dir", "dp")),
            P(),
            P(("dir", "dp"), None),
            P(),
            P("pipe", "dir", "dp", None),
            P("pipe", "dir", None),
            P("pipe", "dir", "dp", None),
            P("pipe", "dir", "dp", None, None),
        ),
        out_specs=(
            P("pipe", "dir", "dp", None, None),
            P(),
            P(None, ("pipe", "dir", "dp")),
            P(),
            P(None, None, ("pipe", "dir", "dp")),
            P(),
            P(("pipe", "dir", "dp"), None),
            P(),
            P("pipe", "dir", "dp", None),
            P("pipe", "dir", "dp"),
            P("pipe", "dir", "dp", None),
        ),
        check_vma=False,
    )
```

```python
import functools
import math

import jax
import jax.numpy as jnp
from jax import lax
from jax.experimental import pallas as pl
from jax.experimental.pallas import tpu as pltpu
from jax.sharding import PartitionSpec as P

FILTERS = 2048
CDIM = 16
CVOCAB = 262
CHARS = 50
KMAX = 7
CLIP_LIMIT = 3.0
MASKED_FILL = -1000000000.0
MESH = pl.DeviceIdType.MESH
BF = jnp.bfloat16
F32 = jnp.float32
ALL = ("pipe", "dir", "dp")


def silu_slope(value):
    sig = jax.nn.sigmoid(value)
    return sig * (1.0 + value * (1.0 - sig))


def filter_widths(filter_count):
    filter_index = jnp.arange(filter_count, dtype=jnp.int32)
    filter_width = jnp.ones((filter_count,), jnp.int32)
    for doubling in range(6):
        filter_width = filter_width + (filter_index >= filter_count // 64 * (1 << doubling)).astype(
            jnp.int32
        )
    return filter_width


def conv_masks(filter_count):
    filter_width = filter_widths(filter_count)
    offset_rows = jnp.arange(KMAX * CDIM, dtype=jnp.int32) // CDIM
    weight_mask = (offset_rows[:, None] < filter_width[None, :]).astype(jnp.float32)
    valid_place = jnp.arange(CHARS, dtype=jnp.int32)[:, None] <= CHARS - filter_width[None, :]
    return (weight_mask, valid_place)


def make_windows(embedded):
    padded = jnp.pad(embedded, ((0, 0), (0, KMAX - 1), (0, 0)))
    return jnp.concatenate(
        [padded[:, offset : offset + CHARS, :] for offset in range(KMAX)], axis=2
    )


def conv_response(ids_block, table_low, conv_low, valid_place):
    embedded = jnp.take(table_low, ids_block, axis=0)
    windows = make_windows(embedded)
    response = jnp.einsum("bpk,kf->bpf", windows, conv_low, preferred_element_type=jnp.float32)
    return (windows, jnp.where(valid_place[None], response, MASKED_FILL))


def over(count, step):
    if count <= 9:
        for off in range(count - 1, 0, -1):
            step(off)
    else:
        lax.fori_loop(1, count, lambda off, _: (step(off), 0)[1], 0)


def lstm_kernel(
    n, chunk,
    x_own, wx, wh, bias, p, wxt, wht, pt, cot,
    out_ref, dx_ref, dw_hbm, db_ref, dp_ref,
    xbuf, hbuf, dqbuf, gates, cells, ebuf, hown, gscr, escr, dabuf, ucell, dwacc,
    stage, inbox, stage2, inbox2, relay, gbuf, rown,
    in_send, in_recv, ag_send, ag_recv, dq_send, dq_recv, rs_send, rs_recv, dx_send, dx_recv,
    x_send, x_recv, g_send, g_recv, st_sem,
):
    steps, _, rows, width = xbuf.shape
    total = n * rows
    cell = cells.shape[2]
    pipe = lax.axis_index("pipe")
    direction = lax.axis_index("dir")
    me = lax.axis_index("dp")
    first = pipe == 1
    second = pipe == 0
    partner = (1 - pipe, direction, me)

    def peer(off):
        if n & (n - 1):
            return lax.rem(me + off, n)
        return me ^ off

    barrier = pltpu.get_barrier_semaphore()
    over(n, lambda off: pl.semaphore_signal(
        barrier, inc=1, device_id=(pipe, direction, peer(off)), device_id_type=MESH))
    pl.semaphore_signal(barrier, inc=1, device_id=partner, device_id_type=MESH)

    @pl.when(first)
    def _():
        for t in range(steps):
            xbuf[t, me] = x_own[t]

    hbuf[0] = jnp.zeros((n, rows, width), BF)
    cells[0] = jnp.zeros((total, cell), F32)
    pl.semaphore_wait(barrier, n)

    def ag_copy(buf, slot, off):
        out, into = (ag_send, ag_recv) if buf is hbuf else (dq_send, dq_recv)
        return pltpu.make_async_remote_copy(
            src_ref=buf.at[slot, me], dst_ref=buf.at[slot, me],
            send_sem=out.at[off], recv_sem=into.at[off],
            device_id=(pipe, direction, peer(off)), device_id_type=MESH)

    def rs_copy(off):
        return pltpu.make_async_remote_copy(
            src_ref=stage.at[peer(off)], dst_ref=inbox.at[me],
            send_sem=rs_send.at[off], recv_sem=rs_recv.at[off],
            device_id=(pipe, direction, peer(off)), device_id_type=MESH)

    def dx_copy(slot, off):
        return pltpu.make_async_remote_copy(
            src_ref=stage2.at[slot, peer(off)], dst_ref=inbox2.at[slot, me],
            send_sem=dx_send.at[slot, off], recv_sem=dx_recv.at[slot, off],
            device_id=(pipe, direction, peer(off)), device_id_type=MESH)

    def x_copy(t):
        return pltpu.make_async_remote_copy(
            src_ref=hbuf.at[t + 1], dst_ref=xbuf.at[t],
            send_sem=x_send.at[t], recv_sem=x_recv.at[t],
            device_id=partner, device_id_type=MESH)

    def g_copy(t):
        return pltpu.make_async_remote_copy(
            src_ref=relay.at[t], dst_ref=gbuf.at[t],
            send_sem=g_send.at[t], recv_sem=g_recv.at[t],
            device_id=partner, device_id_type=MESH)

    def in_start(t):
        over(n, lambda off: pltpu.make_async_remote_copy(
            src_ref=xbuf.at[t, me], dst_ref=xbuf.at[t, me],
            send_sem=in_send.at[t], recv_sem=in_recv.at[t],
            device_id=(pipe, direction, peer(off)), device_id_type=MESH).start())

    def in_wait(sem, t):
        blocks = xbuf.at[t, pl.ds(0, n - 1)]
        pltpu.make_async_copy(blocks, blocks, sem.at[t]).wait()

    @pl.when(first)
    def _():
        in_start(0)
        in_start(1)

    def ag_wait(buf, slot):
        def both(off):
            ag_copy(buf, slot, off).wait_send()
            ag_copy(buf, slot, off).wait_recv()
        over(n, both)

    def rs_wait():
        def both(off):
            rs_copy(off).wait_send()
            rs_copy(off).wait_recv()
        over(n, both)

    def forward(t, _):
        @pl.when(second)
        def _():
            x_copy(t).wait_recv()

        @pl.when(first)
        def _():
            in_wait(in_recv, t)

        gscr[...] = jnp.dot(
            xbuf[t].reshape(total, width), wx[...], preferred_element_type=F32) + bias[...]

        @pl.when(t > 0)
        def _():
            ag_wait(hbuf, t)

            @pl.when(first)
            def _():
                x_copy(t - 1).start()

        gscr[...] += jnp.dot(
            hbuf[t].reshape(total, width), wh[...], preferred_element_type=F32)

        def rows_step(k, _):
            at = pl.ds(pl.multiple_of(k * chunk, chunk), chunk)
            g = gscr[at, :]
            i = jax.nn.sigmoid(g[:, :cell])
            f = jax.nn.sigmoid(g[:, cell:2 * cell])
            m = jnp.tanh(g[:, 2 * cell:3 * cell])
            o = jax.nn.sigmoid(g[:, 3 * cell:])
            c = 3.0 * jnp.tanh((i * m + f * cells[t, at, :]) * (1.0 / 3.0))
            cells[t + 1, at, :] = c
            ebuf[t, at, :] = (o * jnp.tanh(c)).astype(BF)
            kind = gates.dtype
            gates[t, at, :cell] = i.astype(kind)
            gates[t, at, cell:2 * cell] = f.astype(kind)
            gates[t, at, 2 * cell:3 * cell] = m.astype(kind)
            gates[t, at, 3 * cell:] = o.astype(kind)
            return 0

        lax.fori_loop(0, total // chunk, rows_step, 0)
        q = jnp.dot(ebuf[t], p[...], preferred_element_type=F32)
        stage[...] = q.astype(BF).reshape(n, rows, width)
        over(n, lambda off: rs_copy(off).start())
        inbox[me] = stage[me]

        @pl.when(first & (t + 2 < steps))
        def _():
            in_start(t + 2)

        rs_wait()
        h = 3.0 * jnp.tanh(jnp.sum(inbox[...].astype(F32), axis=0) * (1.0 / 3.0))
        hown[t] = h
        hbuf[t + 1, me] = h.astype(BF)
        over(n, lambda off: ag_copy(hbuf, t + 1, off).start())
        add = jnp.where(second, 1.0, 0.0)
        out_ref[t] = (h + add * xbuf[t, me].astype(F32)).astype(BF)
        return 0

    lax.fori_loop(0, steps, forward, 0)
    ag_wait(hbuf, steps)

    @pl.when(first)
    def _():
        x_copy(steps - 1).start()
        lax.fori_loop(0, steps, lambda t, _: (x_copy(t).wait_send(), 0)[1], 0)
        lax.fori_loop(0, steps, lambda t, _: (in_wait(in_send, t), 0)[1], 0)

    rown[...] = jnp.zeros((rows, width), F32)
    ucell[...] = jnp.zeros((total, cell), F32)
    dwacc[...] = jnp.zeros(dwacc.shape, F32)
    db_ref[...] = jnp.zeros(db_ref.shape, F32)
    dp_ref[...] = jnp.zeros(dp_ref.shape, F32)

    def dx_finish(t):
        slot = lax.rem(t, 2)

        def both(off):
            dx_copy(slot, off).wait_send()
            dx_copy(slot, off).wait_recv()
        over(n, both)
        dx = jnp.sum(inbox2[slot].astype(F32), axis=0)
        dx_ref[t] = dx

        @pl.when(second)
        def _():
            relay[t] = (dx + cot[t].astype(F32)).astype(BF)
            g_copy(t).start()

    def backward(k, _):
        t = steps - 1 - k
        slot = lax.rem(t, 2)
        up = rown[...] + cot[t].astype(F32)
        rown[...] = up

        @pl.when(first)
        def _():
            g_copy(t).wait_recv()
            rown[...] = rown[...] + gbuf[t].astype(F32)

        ratio = hown[t] * (1.0 / 3.0)
        dqbuf[t, me] = (rown[...] * (1.0 - ratio * ratio)).astype(BF)
        over(n, lambda off: ag_copy(dqbuf, t, off).start())

        @pl.when(k > 0)
        def _():
            dx_finish(t + 1)

        ag_wait(dqbuf, t)
        escr[...] = jnp.dot(
            dqbuf[t].reshape(total, width), pt[...], preferred_element_type=F32)

        def rows_step(j, _):
            at = pl.ds(pl.multiple_of(j * chunk, chunk), chunk)
            de = escr[at, :]
            i = gates[t, at, :cell].astype(F32)
            f = gates[t, at, cell:2 * cell].astype(F32)
            m = gates[t, at, 2 * cell:3 * cell].astype(F32)
            o = gates[t, at, 3 * cell:].astype(F32)
            c = cells[t + 1, at, :]
            tc = jnp.tanh(c)
            cr = c * (1.0 / 3.0)
            dc = (de * o * (1.0 - tc * tc) + ucell[at, :]) * (1.0 - cr * cr)
            ucell[at, :] = dc * f
            for block, value in enumerate((
                dc * m * i * (1.0 - i),
                dc * cells[t, at, :] * f * (1.0 - f),
                dc * i * (1.0 - m * m),
                de * tc * o * (1.0 - o),
            )):
                value = value.astype(BF)
                where = pl.ds(block * cell, cell)
                dabuf[0, at, where] = value
                db_ref[:, where] += jnp.sum(value.astype(F32), axis=0, keepdims=True)
            return 0

        lax.fori_loop(0, total // chunk, rows_step, 0)
        r = jnp.dot(dabuf[0], wht[...], preferred_element_type=F32)
        stage[...] = r.astype(BF).reshape(n, rows, width)
        over(n, lambda off: rs_copy(off).start())
        inbox[me] = stage[me]
        dx = jnp.dot(dabuf[0], wxt[...], preferred_element_type=F32)
        stage2[slot] = dx.astype(BF).reshape(n, rows, width)
        over(n, lambda off: dx_copy(slot, off).start())
        inbox2[slot, me] = stage2[slot, me]
        for half, buf in enumerate((xbuf, hbuf)):
            dwacc[pl.ds(half * width, width), :] += lax.dot_general(
                buf[t].reshape(total, width), dabuf[0], (((0,), (0,)), ((), ())),
                preferred_element_type=F32)
        dp_ref[...] += lax.dot_general(
            ebuf[t], dqbuf[t].reshape(total, width), (((0,), (0,)), ((), ())),
            preferred_element_type=F32)
        rs_wait()
        rown[...] = jnp.sum(inbox[...].astype(F32), axis=0)
        return 0

    lax.fori_loop(0, steps, backward, 0)
    dx_finish(0)

    @pl.when(second)
    def _():
        lax.fori_loop(0, steps, lambda t, _: (g_copy(t).wait_send(), 0)[1], 0)

    pieces = 2 * width // total

    def dw_copy(piece):
        return pltpu.make_async_copy(
            dabuf.at[piece % 2], dw_hbm.at[pl.ds(piece * total, total)], st_sem.at[piece % 2])

    for piece in range(pieces):
        if piece > 1:
            dw_copy(piece - 2).wait()
        dabuf[piece % 2] = dwacc[pl.ds(piece * total, total), :].astype(BF)
        dw_copy(piece).start()
    for piece in range(max(0, pieces - 2), pieces):
        dw_copy(piece).wait()


def lstm_call(n, x, wx, wh, bias, p, wxt, wht, pt, cot, chunk=16):
    steps, rows, width = x.shape
    cell = p.shape[0]
    total = n * rows
    sds = jax.ShapeDtypeStruct
    vm = pl.BlockSpec(memory_space=pltpu.VMEM)
    hb = pl.BlockSpec(memory_space=pl.ANY)
    keep = F32 if n <= 8 else BF
    V = pltpu.VMEM
    dma = pltpu.SemaphoreType.DMA
    return pl.pallas_call(
        functools.partial(lstm_kernel, n, chunk),
        out_shape=(
            sds((steps, rows, width), BF), sds((steps, rows, width), F32),
            sds((2 * width, 4 * cell), BF), sds((1, 4 * cell), F32), sds((cell, width), F32)),
        in_specs=[vm] * 9,
        out_specs=(vm, vm, hb, vm, vm),
        scratch_shapes=[
            V((steps, n, rows, width), BF), V((steps + 1, n, rows, width), BF),
            V((steps, n, rows, width), BF), V((steps, total, 4 * cell), keep),
            V((steps + 1, total, cell), F32), V((steps, total, cell), BF),
            V((steps, rows, width), F32), V((total, 4 * cell), F32),
            V((total, cell), F32), V((2, total, 4 * cell), BF), V((total, cell), F32),
            V((2 * width, 4 * cell), F32),
            V((n, rows, width), BF), V((n, rows, width), BF),
            V((2, n, rows, width), BF), V((2, n, rows, width), BF),
            V((steps, rows, width), BF), V((steps, rows, width), BF), V((rows, width), F32),
            dma((steps,)), dma((steps,)), dma((n,)), dma((n,)), dma((n,)), dma((n,)), dma((n,)), dma((n,)), dma((2, n)), dma((2, n)),
            dma((steps,)), dma((steps,)), dma((steps,)), dma((steps,)), dma((2,)),
        ],
        compiler_params=pltpu.CompilerParams(
            collective_id=0, has_side_effects=True, vmem_limit_bytes=60 * 1024 * 1024),
        cost_estimate=pl.CostEstimate(
            flops=300_000_000_000, bytes_accessed=64 * 1024 * 1024, transcendentals=0),
        name="relay_lstm",
    )(x, wx, wh, bias, p, wxt, wht, pt, cot)


def split_cells(weight, n):
    rows, gates = weight.shape
    cell = gates // (4 * n)

    def body(src, dst):
        for k in range(n):
            dst[k] = src[:, k * cell : (k + 1) * cell].astype(BF)

    return pl.pallas_call(
        body,
        grid=(4,),
        out_shape=jax.ShapeDtypeStruct((n, rows, 4 * cell), BF),
        in_specs=[pl.BlockSpec((rows, n * cell), lambda b: (0, b))],
        out_specs=pl.BlockSpec((n, rows, cell), lambda b: (0, 0, b)),
        cost_estimate=pl.CostEstimate(
            flops=0, bytes_accessed=6 * rows * gates, transcendentals=0
        ),
        name="split_cells",
    )(weight)


def join_cells(blocks):
    n, rows, gates = blocks.shape
    cell = gates // 4

    def body(src, dst):
        for k in range(n):
            dst[:, k * cell : (k + 1) * cell] = src[k].astype(F32)

    return pl.pallas_call(
        body,
        grid=(4,),
        out_shape=jax.ShapeDtypeStruct((rows, n * gates), F32),
        in_specs=[pl.BlockSpec((n, rows, cell), lambda b: (0, 0, b))],
        out_specs=pl.BlockSpec((rows, n * cell), lambda b: (0, b)),
        cost_estimate=pl.CostEstimate(
            flops=0, bytes_accessed=6 * n * rows * gates, transcendentals=0
        ),
        name="join_cells",
    )(blocks)


def conv_forward(ids, table_low, conv_low):
    valid_place = conv_masks(FILTERS)[1]
    return jax.nn.logsumexp(conv_response(ids, table_low, conv_low, valid_place)[1], axis=1)


def encode_forward(features, weights):
    highway_low, highway_bias, proj_low, proj_bias = weights
    kept = [features]
    mixed = []
    for layer in range(2):
        pre = (
            jnp.dot(features.astype(BF), highway_low[layer], preferred_element_type=F32)
            + highway_bias[layer]
        )
        mixed.append(pre)
        gate = jax.nn.sigmoid(pre[:, FILTERS:])
        features = gate * features + (1.0 - gate) * jax.nn.silu(pre[:, :FILTERS])
        kept.append(features)
    encoded = jnp.dot(features.astype(BF), proj_low, preferred_element_type=F32) + proj_bias
    return encoded, kept, mixed


def to_columns(value):
    count = lax.axis_size(ALL)
    tokens, columns = value.shape
    split = jnp.transpose(value.reshape(tokens, count, columns // count), (1, 0, 2))
    return lax.all_to_all(split, ALL, 0, 0).reshape(count * tokens, columns // count)


def conv_backward(ids, table_low, conv_low, grad_before):
    weight_mask, valid_place = conv_masks(FILTERS)
    windows, response = conv_response(ids, table_low, conv_low, valid_place)
    share = jax.nn.softmax(response, axis=1)
    grad_response = (grad_before[:, None, :] * share).astype(BF)
    grad_conv = jnp.einsum("bpk,bpf->kf", windows, grad_response, preferred_element_type=F32)
    grad_windows = jnp.einsum("bpf,kf->bpk", grad_response, conv_low, preferred_element_type=F32)
    grad_embedded = jnp.zeros((ids.shape[0], CHARS + KMAX - 1, CDIM), F32)
    for offset in range(KMAX):
        grad_embedded = grad_embedded + jnp.pad(
            grad_windows[:, :, offset * CDIM : (offset + 1) * CDIM],
            ((0, 0), (offset, KMAX - 1 - offset), (0, 0)),
        )
    grad_embedded = grad_embedded[:, :CHARS].astype(BF)
    one_hot = (ids[:, :, None] == jnp.arange(CVOCAB, dtype=jnp.int32)).astype(BF)
    grad_table = jnp.einsum("bpv,bpc->vc", one_hot, grad_embedded, preferred_element_type=F32)
    return grad_conv * weight_mask, grad_table


def local(
    chars,
    lengths,
    char_emb,
    conv_weight,
    conv_bias,
    highway_weight,
    highway_bias,
    proj_weight,
    proj_bias,
    gate_weight,
    gate_bias,
    cell_proj,
    cotangent,
):
    n = lax.axis_size("dp")
    pipe = lax.axis_index("pipe")
    direction = lax.axis_index("dir")
    me = lax.axis_index("dp")
    everyone = lax.axis_size(ALL)
    seqs, steps, char_count = chars.shape
    parts = everyone // n
    quarter = seqs // parts
    tokens = quarter * steps
    width = cell_proj.shape[3]
    cell = cell_proj.shape[2]

    holders = lax.axis_size(("dir", "dp"))
    mine = conv_weight.shape[1]
    conv_full = lax.all_to_all(
        jnp.broadcast_to(conv_weight.astype(BF), (holders, KMAX * CDIM, mine)), ("dir", "dp"), 0, 0
    )
    conv_full = jnp.transpose(conv_full, (1, 0, 2)).reshape(KMAX * CDIM, FILTERS)
    proj_rows = proj_weight.shape[0]
    block = highway_weight.shape[2]
    pieces = width // block
    proj_blocks = jnp.transpose(proj_weight.reshape(proj_rows, pieces, block), (1, 0, 2))
    proj_blocks = proj_blocks.reshape(2, pieces * proj_rows // 2, block)
    gathered = lax.all_gather(
        jnp.concatenate([highway_weight, proj_blocks], axis=1).astype(BF),
        ("dir", "dp"),
        axis=2,
        tiled=True,
    )
    in_rows = gate_weight.shape[2]
    ids = lax.dynamic_slice_in_dim(
        chars, (pipe * lax.axis_size("dir") + direction) * quarter, quarter, 0
    ).reshape(tokens, char_count)
    weight_mask = conv_masks(FILTERS)[0]
    table_low = char_emb.astype(BF)
    conv_low = conv_full * weight_mask.astype(BF)
    pooled = conv_forward(ids, table_low, conv_low)
    features = jax.nn.silu(pooled + conv_bias)
    gate_low, gathered, features = lax.optimization_barrier(
        (split_cells(gate_weight[0, 0], n), gathered, features)
    )
    gate_own = lax.all_to_all(gate_low, "dp", 0, 0).reshape(n * in_rows, 4 * cell)
    highway_full = gathered[:, :FILTERS]
    proj_full = gathered[:, FILTERS:].reshape(pieces, proj_rows, holders, block)
    proj_full = jnp.transpose(proj_full, (2, 1, 0, 3)).reshape(FILTERS, width)
    bias_own = lax.dynamic_index_in_dim(
        gate_bias[0, 0].reshape(4, n, cell), me, 1, keepdims=False
    ).reshape(1, 4 * cell)
    cell_low = cell_proj[0, 0].astype(BF)

    def order_matrix(sizes):
        place = jnp.arange(steps, dtype=jnp.int32)[None, :]
        live = place < sizes[:, None]
        order = jnp.where(live & (direction == 1), sizes[:, None] - 1 - place, place)
        return ((order[:, :, None] == place[:, None, :]) & live[:, :, None]).astype(BF)

    own_order = order_matrix(lengths)
    cot = jnp.einsum("rts,rsd->trd", own_order, cotangent[0, 0], preferred_element_type=BF)

    encoded, kept, mixed = encode_forward(
        features, (highway_full, highway_bias, proj_full, proj_bias)
    )
    encoded_own = lax.all_gather(
        encoded.astype(BF).reshape(quarter, steps, width), ("pipe", "dir"), axis=0, tiled=True
    )
    kept_low = [value.astype(BF) for value in kept]
    kept_low, encoded_own, gate_own = lax.optimization_barrier((kept_low, encoded_own, gate_own))
    kept_all = [lax.all_gather(value, ALL, axis=0, tiled=True) for value in kept_low[:2]]
    inputs = jnp.einsum("rts,rsd->trd", own_order, encoded_own, preferred_element_type=BF)

    out_own, dx_own, grad_gate, grad_bias, grad_cell = lstm_call(
        n,
        inputs,
        gate_own[:width],
        gate_own[width:],
        bias_own,
        cell_low,
        gate_own[:width].T,
        gate_own[width:].T,
        cell_low.T,
        cot,
    )
    dx_own, kept_all = lax.optimization_barrier((dx_own, kept_all))
    activations = jnp.einsum("rts,srd->rtd", own_order, out_own, preferred_element_type=BF)

    grad_gate = grad_gate.reshape(n, 2, in_rows // 2, 4 * cell)
    gate_halves = [lax.all_to_all(grad_gate[:, half], "dp", 0, 0) for half in range(2)]
    grad_stored = jnp.einsum(
        "rts,srd->rtd", own_order, dx_own.astype(BF), preferred_element_type=F32
    )
    grad_stored = jnp.where(pipe == 1, grad_stored, 0.0).astype(BF)
    grad_encoded = lax.all_to_all(
        grad_stored.reshape(parts, tokens, width), ("pipe", "dir"), 0, 0
    )
    grad_encoded = jnp.sum(grad_encoded.astype(F32), axis=0).astype(BF)
    encoded_grads = lax.all_gather(grad_encoded, ALL, axis=0, tiled=True)

    grad_proj_bias = jnp.sum(grad_encoded.astype(F32), axis=0)
    grad_features = jnp.einsum("td,fd->tf", grad_encoded, proj_full, preferred_element_type=F32)
    columns = [None, None]
    grad_highway_bias = [None, None]
    for layer in (1, 0):
        nonlinear = mixed[layer][:, :FILTERS]
        gate = jax.nn.sigmoid(mixed[layer][:, FILTERS:])
        grad_mixed = jnp.concatenate(
            [
                grad_features * (1.0 - gate) * silu_slope(nonlinear),
                grad_features * (kept[layer] - jax.nn.silu(nonlinear)) * gate * (1.0 - gate),
            ],
            axis=1,
        ).astype(BF)
        columns[layer] = to_columns(grad_mixed)
        grad_highway_bias[layer] = jnp.sum(grad_mixed.astype(F32), axis=0)
        grad_features = grad_features * gate + jnp.einsum(
            "tg,fg->tf", grad_mixed, highway_full[layer], preferred_element_type=F32
        )
        if layer == 1:
            grad_features, gate_halves[0] = lax.optimization_barrier(
                (grad_features, gate_halves[0])
            )
    grad_features, columns[1], grad_bias = lax.optimization_barrier(
        (grad_features, columns[1], grad_bias)
    )
    grad_bias = lax.all_to_all(
        jnp.broadcast_to(grad_bias, (n, 4 * cell)), "dp", 0, 0
    ).reshape(n, 4, cell)
    grad_bias = jnp.transpose(grad_bias, (1, 0, 2)).reshape(n, 4 * cell)
    grad_bias = lax.dynamic_index_in_dim(grad_bias, me, 0, keepdims=False)

    last_columns = to_columns(kept_low[2])
    grad_proj = jnp.einsum("tf,td->fd", last_columns, encoded_grads, preferred_element_type=F32)
    grad_before = grad_features * silu_slope(pooled + conv_bias)
    grad_conv, grad_table = conv_backward(ids, table_low, conv_low, grad_before)
    grad_conv, gate_halves[1], columns[0] = lax.optimization_barrier(
        (grad_conv, gate_halves[1], columns[0])
    )
    grad_highway = [
        jnp.einsum("tf,tg->fg", kept_all[layer], columns[layer], preferred_element_type=F32)
        for layer in range(2)
    ]
    grad_gate = join_cells(jnp.concatenate(gate_halves, axis=1))

    small = (
        grad_table,
        jnp.sum(grad_before, axis=0),
        jnp.stack(grad_highway_bias),
        grad_proj_bias,
    )
    flat = jnp.concatenate([value.reshape(-1) for value in small])
    share = -(-flat.shape[0] // (everyone * 128)) * 128
    flat = jnp.pad(flat, (0, share * everyone - flat.shape[0])).reshape(everyone, share)
    columns = FILTERS // everyone
    packed = jnp.concatenate(
        [
            jnp.transpose(
                grad_conv.reshape(KMAX * CDIM, everyone, columns), (1, 0, 2)
            ).reshape(everyone, KMAX * CDIM * columns),
            flat,
        ],
        axis=1,
    ).astype(BF)
    summed = jnp.sum(lax.all_to_all(packed, ALL, 0, 0).astype(F32), axis=0)
    grad_conv = summed[: KMAX * CDIM * columns].reshape(KMAX * CDIM, columns)
    shared = lax.all_to_all(
        jnp.broadcast_to(summed[KMAX * CDIM * columns :], (everyone, share)), ALL, 0, 0
    ).reshape(-1)
    small_sums = []
    start = 0
    for value in small:
        small_sums.append(shared[start : start + value.size].reshape(value.shape))
        start += value.size
    return (
        activations[None, None],
        small_sums[0],
        grad_conv,
        small_sums[1],
        jnp.stack(grad_highway),
        small_sums[2],
        grad_proj,
        small_sums[3],
        grad_gate[None, None],
        grad_bias[None, None],
        grad_cell[None, None],
    )


def solution(mesh):
    return jax.shard_map(
        local,
        mesh=mesh,
        in_specs=(
            P("dp", None, None),
            P("dp"),
            P(),
            P(None, ("dir", "dp")),
            P(),
            P(None, None, ("dir", "dp")),
            P(),
            P(("dir", "dp"), None),
            P(),
            P("pipe", "dir", "dp", None),
            P("pipe", "dir", None),
            P("pipe", "dir", "dp", None),
            P("pipe", "dir", "dp", None, None),
        ),
        out_specs=(
            P("pipe", "dir", "dp", None, None),
            P(),
            P(None, ("pipe", "dir", "dp")),
            P(),
            P(None, None, ("pipe", "dir", "dp")),
            P(),
            P(("pipe", "dir", "dp"), None),
            P(),
            P("pipe", "dir", "dp", None),
            P("pipe", "dir", "dp"),
            P("pipe", "dir", "dp", None),
        ),
        check_vma=False,
    )
```

```python
import functools
import math

import jax
import jax.numpy as jnp
from jax import lax
from jax.experimental import pallas as pl
from jax.experimental.pallas import tpu as pltpu
from jax.sharding import PartitionSpec as P

FILTERS = 2048
CDIM = 16
CVOCAB = 262
CHARS = 50
KMAX = 7
CLIP_LIMIT = 3.0
MASKED_FILL = -1000000000.0
MESH = pl.DeviceIdType.MESH
BF = jnp.bfloat16
F32 = jnp.float32
ALL = ("pipe", "dir", "dp")


def silu_slope(value):
    sig = jax.nn.sigmoid(value)
    return sig * (1.0 + value * (1.0 - sig))


def conv_masks(filter_index):
    filter_width = jnp.ones(filter_index.shape, jnp.int32)
    for doubling in range(6):
        filter_width = filter_width + (filter_index >= FILTERS // 64 * (1 << doubling)).astype(
            jnp.int32
        )
    offset_rows = jnp.arange(KMAX * CDIM, dtype=jnp.int32) // CDIM
    weight_mask = (offset_rows[:, None] < filter_width[None, :]).astype(jnp.float32)
    valid_place = jnp.arange(CHARS, dtype=jnp.int32)[:, None] <= CHARS - filter_width[None, :]
    return (weight_mask, valid_place)


def make_windows(embedded):
    padded = jnp.pad(embedded, ((0, 0), (0, KMAX - 1), (0, 0)))
    return jnp.concatenate(
        [padded[:, offset : offset + CHARS, :] for offset in range(KMAX)], axis=2
    )


def conv_response(ids_block, table_low, conv_low, valid_place):
    embedded = jnp.take(table_low, ids_block, axis=0)
    windows = make_windows(embedded)
    response = jnp.einsum("bpk,kf->bpf", windows, conv_low, preferred_element_type=jnp.float32)
    return (windows, jnp.where(valid_place[None], response, MASKED_FILL))


def over(count, step):
    if count <= 9:
        for off in range(count - 1, 0, -1):
            step(off)
    else:
        lax.fori_loop(1, count, lambda off, _: (step(off), 0)[1], 0)


def lstm_kernel(
    n, chunk,
    x_own, wx, wh, bias, p, wxt, wht, pt, cot,
    out_ref, dx_ref, dw_hbm, db_ref, dp_ref,
    xbuf, hbuf, dqbuf, gates, cells, ebuf, hown, gscr, escr, dabuf, ucell, dwacc,
    stage, inbox, stage2, inbox2, relay, gbuf, rown,
    in_send, in_recv, ag_send, ag_recv, dq_send, dq_recv, rs_send, rs_recv, dx_send, dx_recv,
    x_send, x_recv, g_send, g_recv, st_sem,
):
    steps, _, rows, width = xbuf.shape
    total = n * rows
    cell = cells.shape[2]
    pipe = lax.axis_index("pipe")
    direction = lax.axis_index("dir")
    me = lax.axis_index("dp")
    first = pipe == 1
    second = pipe == 0
    partner = (1 - pipe, direction, me)

    def peer(off):
        if n & (n - 1):
            return lax.rem(me + off, n)
        return me ^ off

    barrier = pltpu.get_barrier_semaphore()
    over(n, lambda off: pl.semaphore_signal(
        barrier, inc=1, device_id=(pipe, direction, peer(off)), device_id_type=MESH))
    pl.semaphore_signal(barrier, inc=1, device_id=partner, device_id_type=MESH)

    @pl.when(first)
    def _():
        for t in range(steps):
            xbuf[t, me] = x_own[t]

    hbuf[0] = jnp.zeros((n, rows, width), BF)
    cells[0] = jnp.zeros((total, cell), F32)
    pl.semaphore_wait(barrier, n)

    def ag_copy(buf, slot, off):
        out, into = (ag_send, ag_recv) if buf is hbuf else (dq_send, dq_recv)
        return pltpu.make_async_remote_copy(
            src_ref=buf.at[slot, me], dst_ref=buf.at[slot, me],
            send_sem=out.at[off], recv_sem=into.at[off],
            device_id=(pipe, direction, peer(off)), device_id_type=MESH)

    def rs_copy(off):
        return pltpu.make_async_remote_copy(
            src_ref=stage.at[peer(off)], dst_ref=inbox.at[me],
            send_sem=rs_send.at[off], recv_sem=rs_recv.at[off],
            device_id=(pipe, direction, peer(off)), device_id_type=MESH)

    def dx_copy(slot, off):
        return pltpu.make_async_remote_copy(
            src_ref=stage2.at[slot, peer(off)], dst_ref=inbox2.at[slot, me],
            send_sem=dx_send.at[slot, off], recv_sem=dx_recv.at[slot, off],
            device_id=(pipe, direction, peer(off)), device_id_type=MESH)

    def x_copy(t):
        return pltpu.make_async_remote_copy(
            src_ref=hbuf.at[t + 1], dst_ref=xbuf.at[t],
            send_sem=x_send.at[t], recv_sem=x_recv.at[t],
            device_id=partner, device_id_type=MESH)

    def g_copy(t):
        return pltpu.make_async_remote_copy(
            src_ref=relay.at[t], dst_ref=gbuf.at[t],
            send_sem=g_send.at[t], recv_sem=g_recv.at[t],
            device_id=partner, device_id_type=MESH)

    def in_start(t):
        over(n, lambda off: pltpu.make_async_remote_copy(
            src_ref=xbuf.at[t, me], dst_ref=xbuf.at[t, me],
            send_sem=in_send.at[t], recv_sem=in_recv.at[t],
            device_id=(pipe, direction, peer(off)), device_id_type=MESH).start())

    def in_wait(sem, t):
        blocks = xbuf.at[t, pl.ds(0, n - 1)]
        pltpu.make_async_copy(blocks, blocks, sem.at[t]).wait()

    @pl.when(first)
    def _():
        in_start(0)
        in_start(1)

    def ag_wait(buf, slot):
        def both(off):
            ag_copy(buf, slot, off).wait_send()
            ag_copy(buf, slot, off).wait_recv()
        over(n, both)

    def rs_wait():
        def both(off):
            rs_copy(off).wait_send()
            rs_copy(off).wait_recv()
        over(n, both)

    def forward(t, _):
        @pl.when(second)
        def _():
            x_copy(t).wait_recv()

        @pl.when(first)
        def _():
            in_wait(in_recv, t)

        gscr[...] = jnp.dot(
            xbuf[t].reshape(total, width), wx[...], preferred_element_type=F32) + bias[...]

        @pl.when(t > 0)
        def _():
            ag_wait(hbuf, t)

            @pl.when(first)
            def _():
                x_copy(t - 1).start()

        gscr[...] += jnp.dot(
            hbuf[t].reshape(total, width), wh[...], preferred_element_type=F32)

        def rows_step(k, _):
            at = pl.ds(pl.multiple_of(k * chunk, chunk), chunk)
            g = gscr[at, :]
            i = jax.nn.sigmoid(g[:, :cell])
            f = jax.nn.sigmoid(g[:, cell:2 * cell])
            m = jnp.tanh(g[:, 2 * cell:3 * cell])
            o = jax.nn.sigmoid(g[:, 3 * cell:])
            c = 3.0 * jnp.tanh((i * m + f * cells[t, at, :]) * (1.0 / 3.0))
            cells[t + 1, at, :] = c
            ebuf[t, at, :] = (o * jnp.tanh(c)).astype(BF)
            kind = gates.dtype
            gates[t, at, :cell] = i.astype(kind)
            gates[t, at, cell:2 * cell] = f.astype(kind)
            gates[t, at, 2 * cell:3 * cell] = m.astype(kind)
            gates[t, at, 3 * cell:] = o.astype(kind)
            return 0

        lax.fori_loop(0, total // chunk, rows_step, 0)
        q = jnp.dot(ebuf[t], p[...], preferred_element_type=F32)
        stage[...] = q.astype(BF).reshape(n, rows, width)
        over(n, lambda off: rs_copy(off).start())
        inbox[me] = stage[me]

        @pl.when(first & (t + 2 < steps))
        def _():
            in_start(t + 2)

        rs_wait()
        h = 3.0 * jnp.tanh(jnp.sum(inbox[...].astype(F32), axis=0) * (1.0 / 3.0))
        hown[t] = h
        hbuf[t + 1, me] = h.astype(BF)
        over(n, lambda off: ag_copy(hbuf, t + 1, off).start())
        add = jnp.where(second, 1.0, 0.0)
        out_ref[t] = (h + add * xbuf[t, me].astype(F32)).astype(BF)
        return 0

    lax.fori_loop(0, steps, forward, 0)
    ag_wait(hbuf, steps)

    @pl.when(first)
    def _():
        x_copy(steps - 1).start()
        lax.fori_loop(0, steps, lambda t, _: (x_copy(t).wait_send(), 0)[1], 0)
        lax.fori_loop(0, steps, lambda t, _: (in_wait(in_send, t), 0)[1], 0)

    rown[...] = jnp.zeros((rows, width), F32)
    ucell[...] = jnp.zeros((total, cell), F32)
    dwacc[...] = jnp.zeros(dwacc.shape, F32)
    db_ref[...] = jnp.zeros(db_ref.shape, F32)
    dp_ref[...] = jnp.zeros(dp_ref.shape, F32)

    def dx_finish(t):
        slot = lax.rem(t, 2)

        def both(off):
            dx_copy(slot, off).wait_send()
            dx_copy(slot, off).wait_recv()
        over(n, both)
        dx = jnp.sum(inbox2[slot].astype(F32), axis=0)
        dx_ref[t] = dx

        @pl.when(second)
        def _():
            relay[t] = (dx + cot[t].astype(F32)).astype(BF)
            g_copy(t).start()

    def backward(k, _):
        t = steps - 1 - k
        slot = lax.rem(t, 2)
        up = rown[...] + cot[t].astype(F32)
        rown[...] = up

        @pl.when(first)
        def _():
            g_copy(t).wait_recv()
            rown[...] = rown[...] + gbuf[t].astype(F32)

        ratio = hown[t] * (1.0 / 3.0)
        dqbuf[t, me] = (rown[...] * (1.0 - ratio * ratio)).astype(BF)
        over(n, lambda off: ag_copy(dqbuf, t, off).start())

        @pl.when(k > 0)
        def _():
            dx_finish(t + 1)

        ag_wait(dqbuf, t)
        escr[...] = jnp.dot(
            dqbuf[t].reshape(total, width), pt[...], preferred_element_type=F32)

        def rows_step(j, _):
            at = pl.ds(pl.multiple_of(j * chunk, chunk), chunk)
            de = escr[at, :]
            i = gates[t, at, :cell].astype(F32)
            f = gates[t, at, cell:2 * cell].astype(F32)
            m = gates[t, at, 2 * cell:3 * cell].astype(F32)
            o = gates[t, at, 3 * cell:].astype(F32)
            c = cells[t + 1, at, :]
            tc = jnp.tanh(c)
            cr = c * (1.0 / 3.0)
            dc = (de * o * (1.0 - tc * tc) + ucell[at, :]) * (1.0 - cr * cr)
            ucell[at, :] = dc * f
            for block, value in enumerate((
                dc * m * i * (1.0 - i),
                dc * cells[t, at, :] * f * (1.0 - f),
                dc * i * (1.0 - m * m),
                de * tc * o * (1.0 - o),
            )):
                value = value.astype(BF)
                where = pl.ds(block * cell, cell)
                dabuf[0, at, where] = value
                db_ref[:, where] += jnp.sum(value.astype(F32), axis=0, keepdims=True)
            return 0

        lax.fori_loop(0, total // chunk, rows_step, 0)
        r = jnp.dot(dabuf[0], wht[...], preferred_element_type=F32)
        stage[...] = r.astype(BF).reshape(n, rows, width)
        over(n, lambda off: rs_copy(off).start())
        inbox[me] = stage[me]
        dx = jnp.dot(dabuf[0], wxt[...], preferred_element_type=F32)
        stage2[slot] = dx.astype(BF).reshape(n, rows, width)
        over(n, lambda off: dx_copy(slot, off).start())
        inbox2[slot, me] = stage2[slot, me]
        for half, buf in enumerate((xbuf, hbuf)):
            dwacc[pl.ds(half * width, width), :] += lax.dot_general(
                buf[t].reshape(total, width), dabuf[0], (((0,), (0,)), ((), ())),
                preferred_element_type=F32)
        dp_ref[...] += lax.dot_general(
            ebuf[t], dqbuf[t].reshape(total, width), (((0,), (0,)), ((), ())),
            preferred_element_type=F32)
        rs_wait()
        rown[...] = jnp.sum(inbox[...].astype(F32), axis=0)
        return 0

    lax.fori_loop(0, steps, backward, 0)
    dx_finish(0)

    @pl.when(second)
    def _():
        lax.fori_loop(0, steps, lambda t, _: (g_copy(t).wait_send(), 0)[1], 0)

    pieces = 2 * width // total

    def dw_copy(piece):
        return pltpu.make_async_copy(
            dabuf.at[piece % 2], dw_hbm.at[pl.ds(piece * total, total)], st_sem.at[piece % 2])

    for piece in range(pieces):
        if piece > 1:
            dw_copy(piece - 2).wait()
        dabuf[piece % 2] = dwacc[pl.ds(piece * total, total), :].astype(BF)
        dw_copy(piece).start()
    for piece in range(max(0, pieces - 2), pieces):
        dw_copy(piece).wait()


def lstm_call(n, x, wx, wh, bias, p, wxt, wht, pt, cot, chunk=16):
    steps, rows, width = x.shape
    cell = p.shape[0]
    total = n * rows
    sds = jax.ShapeDtypeStruct
    vm = pl.BlockSpec(memory_space=pltpu.VMEM)
    hb = pl.BlockSpec(memory_space=pl.ANY)
    keep = F32 if n <= 8 else BF
    V = pltpu.VMEM
    dma = pltpu.SemaphoreType.DMA
    return pl.pallas_call(
        functools.partial(lstm_kernel, n, chunk),
        out_shape=(
            sds((steps, rows, width), BF), sds((steps, rows, width), F32),
            sds((2 * width, 4 * cell), BF), sds((1, 4 * cell), F32), sds((cell, width), F32)),
        in_specs=[vm] * 9,
        out_specs=(vm, vm, hb, vm, vm),
        scratch_shapes=[
            V((steps, n, rows, width), BF), V((steps + 1, n, rows, width), BF),
            V((steps, n, rows, width), BF), V((steps, total, 4 * cell), keep),
            V((steps + 1, total, cell), F32), V((steps, total, cell), BF),
            V((steps, rows, width), F32), V((total, 4 * cell), F32),
            V((total, cell), F32), V((2, total, 4 * cell), BF), V((total, cell), F32),
            V((2 * width, 4 * cell), F32),
            V((n, rows, width), BF), V((n, rows, width), BF),
            V((2, n, rows, width), BF), V((2, n, rows, width), BF),
            V((steps, rows, width), BF), V((steps, rows, width), BF), V((rows, width), F32),
            dma((steps,)), dma((steps,)), dma((n,)), dma((n,)), dma((n,)), dma((n,)), dma((n,)), dma((n,)), dma((2, n)), dma((2, n)),
            dma((steps,)), dma((steps,)), dma((steps,)), dma((steps,)), dma((2,)),
        ],
        compiler_params=pltpu.CompilerParams(
            collective_id=0, has_side_effects=True, vmem_limit_bytes=60 * 1024 * 1024),
        cost_estimate=pl.CostEstimate(
            flops=300_000_000_000, bytes_accessed=64 * 1024 * 1024, transcendentals=0),
        name="relay_lstm",
    )(x, wx, wh, bias, p, wxt, wht, pt, cot)


def split_cells(weight, n):
    rows, gates = weight.shape
    cell = gates // (4 * n)

    def body(src, dst):
        for k in range(n):
            dst[k] = src[:, k * cell : (k + 1) * cell].astype(BF)

    return pl.pallas_call(
        body,
        grid=(4,),
        out_shape=jax.ShapeDtypeStruct((n, rows, 4 * cell), BF),
        in_specs=[pl.BlockSpec((rows, n * cell), lambda b: (0, b))],
        out_specs=pl.BlockSpec((n, rows, cell), lambda b: (0, 0, b)),
        cost_estimate=pl.CostEstimate(
            flops=0, bytes_accessed=6 * rows * gates, transcendentals=0
        ),
        name="split_cells",
    )(weight)


def join_cells(blocks):
    n, rows, gates = blocks.shape
    cell = gates // 4

    def body(src, dst):
        for k in range(n):
            dst[:, k * cell : (k + 1) * cell] = src[k].astype(F32)

    return pl.pallas_call(
        body,
        grid=(4,),
        out_shape=jax.ShapeDtypeStruct((rows, n * gates), F32),
        in_specs=[pl.BlockSpec((n, rows, cell), lambda b: (0, 0, b))],
        out_specs=pl.BlockSpec((rows, n * cell), lambda b: (0, b)),
        cost_estimate=pl.CostEstimate(
            flops=0, bytes_accessed=6 * n * rows * gates, transcendentals=0
        ),
        name="join_cells",
    )(blocks)


def conv_forward(ids, table_low, conv_low, valid_place):
    return jax.nn.logsumexp(conv_response(ids, table_low, conv_low, valid_place)[1], axis=1)


def own_half(value, blocks):
    sub = value.shape[-1] // (2 * blocks)
    split = value.reshape(*value.shape[:-1], blocks, 2, sub)
    mine = lax.dynamic_index_in_dim(split, lax.axis_index("pipe"), split.ndim - 2, keepdims=False)
    return mine.reshape(*value.shape[:-1], blocks * sub)


def both_halves(value, blocks):
    tokens, half = value.shape
    pair = lax.all_gather(value, "pipe").reshape(2, tokens, blocks, half // blocks)
    return jnp.transpose(pair, (1, 2, 0, 3)).reshape(tokens, 2 * half)


def to_columns(value):
    count = lax.axis_size(ALL)
    tokens, columns = value.shape
    split = jnp.transpose(value.reshape(tokens, count, columns // count), (1, 0, 2))
    return lax.all_to_all(split, ALL, 0, 0).reshape(count * tokens, columns // count)


def conv_backward(ids, table_low, conv_low, masks, grad_before):
    weight_mask, valid_place = masks
    windows, response = conv_response(ids, table_low, conv_low, valid_place)
    share = jax.nn.softmax(response, axis=1)
    grad_response = (grad_before[:, None, :] * share).astype(BF)
    grad_conv = jnp.einsum("bpk,bpf->kf", windows, grad_response, preferred_element_type=F32)
    grad_windows = jnp.einsum("bpf,kf->bpk", grad_response, conv_low, preferred_element_type=F32)
    grad_embedded = jnp.zeros((ids.shape[0], CHARS + KMAX - 1, CDIM), F32)
    for offset in range(KMAX):
        grad_embedded = grad_embedded + jnp.pad(
            grad_windows[:, :, offset * CDIM : (offset + 1) * CDIM],
            ((0, 0), (offset, KMAX - 1 - offset), (0, 0)),
        )
    grad_embedded = grad_embedded[:, :CHARS].astype(BF)
    one_hot = (ids[:, :, None] == jnp.arange(CVOCAB, dtype=jnp.int32)).astype(BF)
    grad_table = jnp.einsum("bpv,bpc->vc", one_hot, grad_embedded, preferred_element_type=F32)
    return grad_conv * weight_mask, grad_table


def local(
    chars,
    lengths,
    char_emb,
    conv_weight,
    conv_bias,
    highway_weight,
    highway_bias,
    proj_weight,
    proj_bias,
    gate_weight,
    gate_bias,
    cell_proj,
    cotangent,
):
    n = lax.axis_size("dp")
    pipe = lax.axis_index("pipe")
    direction = lax.axis_index("dir")
    me = lax.axis_index("dp")
    everyone = lax.axis_size(ALL)
    holders = lax.axis_size(("dir", "dp"))
    seqs, steps, char_count = chars.shape
    group = seqs // lax.axis_size("dir")
    quarter = group // 2
    group_tokens = group * steps
    tokens = quarter * steps
    width = cell_proj.shape[3]
    cell = cell_proj.shape[2]
    blocks = holders // 2
    sub = FILTERS // holders
    half = FILTERS // 2
    filter_index = (
        (2 * jnp.arange(blocks, dtype=jnp.int32) + pipe)[:, None] * sub
        + jnp.arange(sub, dtype=jnp.int32)[None, :]
    ).reshape(half)
    masks = conv_masks(filter_index)

    proj_rows = proj_weight.shape[0]
    pieces = width // sub
    proj_blocks = jnp.transpose(proj_weight.reshape(proj_rows, pieces, sub), (1, 0, 2))
    proj_blocks = proj_blocks.reshape(2, pieces * proj_rows // 2, sub)
    mine = lax.dynamic_slice_in_dim(highway_weight, pipe * sub, sub, 2)
    gathered = lax.all_gather(
        jnp.concatenate([mine, proj_blocks], axis=1).astype(BF), ("dir", "dp"), axis=2, tiled=True
    )
    conv_full = lax.all_to_all(
        jnp.broadcast_to(conv_weight.astype(BF), (holders, KMAX * CDIM, sub)), ("dir", "dp"), 0, 0
    ).reshape(blocks, 2, KMAX * CDIM, sub)
    conv_low = lax.dynamic_index_in_dim(conv_full, pipe, 1, keepdims=False)
    conv_low = jnp.transpose(conv_low, (1, 0, 2)).reshape(KMAX * CDIM, half)
    conv_low = conv_low * masks[0].astype(BF)
    conv_bias_own = own_half(conv_bias, blocks)
    highway_bias_own = own_half(highway_bias.reshape(2, 2, FILTERS), blocks).reshape(2, FILTERS)

    def order_matrix(sizes):
        place = jnp.arange(steps, dtype=jnp.int32)[None, :]
        live = place < sizes[:, None]
        order = jnp.where(live & (direction == 1), sizes[:, None] - 1 - place, place)
        return ((order[:, :, None] == place[:, None, :]) & live[:, :, None]).astype(BF)

    own_order = order_matrix(lengths)
    cot = jnp.einsum("rts,rsd->trd", own_order, cotangent[0, 0], preferred_element_type=BF)

    ids = lax.dynamic_slice_in_dim(chars, direction * group, group, 0).reshape(
        group_tokens, char_count
    )
    table_low = char_emb.astype(BF)
    pooled = conv_forward(ids, table_low, conv_low, masks[1])
    features = jax.nn.silu(pooled + conv_bias_own)
    features_low = both_halves(features.astype(BF), blocks)
    in_rows = gate_weight.shape[2]
    gate_low, gathered, features_low = lax.optimization_barrier(
        (split_cells(gate_weight[0, 0], n), gathered, features_low)
    )
    gate_own = lax.all_to_all(gate_low, "dp", 0, 0).reshape(n * in_rows, 4 * cell)
    bias_own = lax.dynamic_index_in_dim(
        gate_bias[0, 0].reshape(4, n, cell), me, 1, keepdims=False
    ).reshape(1, 4 * cell)
    cell_low = cell_proj[0, 0].astype(BF)
    highway_half = gathered[:, :FILTERS]
    proj_full = gathered[:, FILTERS:].reshape(pieces, proj_rows, holders, sub)
    proj_full = jnp.transpose(proj_full, (2, 1, 0, 3)).reshape(FILTERS, width)

    kept = [features]
    kept_low = [features_low]
    mixed = []
    for layer in range(2):
        pre = (
            jnp.dot(kept_low[layer], highway_half[layer], preferred_element_type=F32)
            + highway_bias_own[layer]
        )
        mixed.append(pre)
        gate = jax.nn.sigmoid(pre[:, half:])
        features = gate * features + (1.0 - gate) * jax.nn.silu(pre[:, :half])
        kept.append(features)
        kept_low.append(both_halves(features.astype(BF), blocks))
    own_last = lax.dynamic_slice_in_dim(kept_low[2], pipe * tokens, tokens, 0)
    encoded = jnp.dot(own_last, proj_full, preferred_element_type=F32) + proj_bias
    encoded_own = lax.all_gather(
        encoded.astype(BF).reshape(quarter, steps, width), ("dir", "pipe"), axis=0, tiled=True
    )
    kept_low, encoded_own, gate_own = lax.optimization_barrier((kept_low, encoded_own, gate_own))
    kept_all = [
        lax.all_gather(value, ("dir", "dp"), axis=0, tiled=True) for value in kept_low[:2]
    ]
    inputs = jnp.einsum("rts,rsd->trd", own_order, encoded_own, preferred_element_type=BF)

    out_own, dx_own, grad_gate, grad_bias, grad_cell = lstm_call(
        n,
        inputs,
        gate_own[:width],
        gate_own[width:],
        bias_own,
        cell_low,
        gate_own[:width].T,
        gate_own[width:].T,
        cell_low.T,
        cot,
    )
    dx_own, kept_all = lax.optimization_barrier((dx_own, kept_all))
    activations = jnp.einsum("rts,srd->rtd", own_order, out_own, preferred_element_type=BF)

    grad_stored = jnp.einsum(
        "rts,srd->rtd", own_order, dx_own.astype(BF), preferred_element_type=F32
    )
    grad_stored = jnp.where(pipe == 1, grad_stored, 0.0).astype(BF)
    grad_stored = grad_stored.reshape(1, -1, group_tokens, width)
    grad_encoded = lax.all_to_all(
        jnp.concatenate([grad_stored, grad_stored]).reshape(-1, group_tokens, width),
        ("pipe", "dir"),
        0,
        0,
    )
    grad_encoded = jnp.sum(grad_encoded.astype(F32), axis=0).astype(BF)
    grad_encoded, grad_gate = lax.optimization_barrier((grad_encoded, grad_gate))
    grad_gate = lax.all_to_all(grad_gate.reshape(n, in_rows, 4 * cell), "dp", 0, 0)
    own_grads = lax.dynamic_slice_in_dim(grad_encoded, pipe * tokens, tokens, 0)
    encoded_grads = lax.all_gather(own_grads, ALL, axis=0, tiled=True)

    grad_proj_bias = jnp.sum(own_grads.astype(F32), axis=0)
    proj_half = lax.dynamic_index_in_dim(
        proj_full.reshape(blocks, 2, sub, width), pipe, 1, keepdims=False
    ).reshape(half, width)
    grad_features = jnp.einsum("td,fd->tf", grad_encoded, proj_half, preferred_element_type=F32)
    columns = [None, None]
    grad_highway_bias = [None, None]
    for layer in (1, 0):
        nonlinear = mixed[layer][:, :half]
        gate = jax.nn.sigmoid(mixed[layer][:, half:])
        grad_mixed = jnp.concatenate(
            [
                grad_features * (1.0 - gate) * silu_slope(nonlinear),
                grad_features * (kept[layer] - jax.nn.silu(nonlinear)) * gate * (1.0 - gate),
            ],
            axis=1,
        ).astype(BF)
        columns[layer] = grad_mixed
        grad_highway_bias[layer] = jnp.sum(grad_mixed.astype(F32), axis=0)
        partial = jnp.einsum(
            "tg,fg->tf", grad_mixed, highway_half[layer], preferred_element_type=F32
        ).reshape(group_tokens, blocks, 2, sub)
        sent = lax.dynamic_index_in_dim(partial, 1 - pipe, 2, keepdims=False).astype(BF)
        came = lax.ppermute(sent, "pipe", [(0, 1), (1, 0)])
        mine = lax.dynamic_index_in_dim(partial, pipe, 2, keepdims=False)
        grad_features = grad_features * gate + (mine + came.astype(F32)).reshape(
            group_tokens, half
        )
    grad_before = grad_features * silu_slope(pooled + conv_bias_own)
    grad_conv, grad_table = conv_backward(ids, table_low, conv_low, masks, grad_before)

    def spread(value):
        split = value.reshape(*value.shape[:-1], -1, 1, sub)
        shown = jnp.arange(2, dtype=jnp.int32)[:, None] == pipe
        return jnp.where(shown, split, jnp.zeros_like(split)).reshape(*value.shape[:-1], -1)

    grad_conv, grad_gate = lax.optimization_barrier((grad_conv, grad_gate))
    grad_gate = join_cells(grad_gate)
    small = (
        grad_table,
        spread(jnp.sum(grad_before, axis=0)),
        spread(jnp.stack(grad_highway_bias)),
        grad_proj_bias,
    )
    flat = jnp.concatenate([value.reshape(-1) for value in small])
    share = -(-flat.shape[0] // (everyone * 128)) * 128
    flat = jnp.pad(flat, (0, share * everyone - flat.shape[0])).reshape(everyone, share)
    cols = FILTERS // everyone
    packed = jnp.concatenate(
        [
            jnp.transpose(
                spread(grad_conv).reshape(KMAX * CDIM, everyone, cols), (1, 0, 2)
            ).reshape(everyone, KMAX * CDIM * cols),
            flat,
        ],
        axis=1,
    ).astype(BF)
    summed = jnp.sum(lax.all_to_all(packed, ALL, 0, 0).astype(F32), axis=0)
    grad_conv = summed[: KMAX * CDIM * cols].reshape(KMAX * CDIM, cols)
    both = jnp.stack(columns, axis=1).reshape(group_tokens, 2, 2, blocks, sub)
    both = jnp.transpose(both, (2, 3, 0, 1, 4))[:, :, None]
    shown = (jnp.arange(2, dtype=jnp.int32) == pipe)[None, None, :, None, None, None]
    both = jnp.where(shown, both, jnp.zeros_like(both))
    both, summed = lax.optimization_barrier((both, summed))
    both = lax.all_to_all(both.reshape(everyone, group_tokens, 2 * sub), ALL, 0, 0)
    parity = lax.rem(lax.axis_index(("dir", "dp")), 2)
    both = lax.dynamic_index_in_dim(
        both.reshape(2, holders * group_tokens, 2, sub), parity, 0, keepdims=False
    )
    grad_highway = [
        jnp.einsum("tf,tg->fg", kept_all[layer], both[:, layer], preferred_element_type=F32)
        for layer in range(2)
    ]
    grad_bias = lax.all_to_all(
        jnp.broadcast_to(grad_bias, (n, 4 * cell)), "dp", 0, 0
    ).reshape(n, 4, cell)
    grad_bias = jnp.transpose(grad_bias, (1, 0, 2)).reshape(n, 4 * cell)
    grad_bias = lax.dynamic_index_in_dim(grad_bias, me, 0, keepdims=False)
    grad_proj = jnp.einsum(
        "tf,td->fd", to_columns(own_last), encoded_grads, preferred_element_type=F32
    )
    shared = lax.all_to_all(
        jnp.broadcast_to(summed[KMAX * CDIM * cols :], (everyone, share)), ALL, 0, 0
    ).reshape(-1)
    small_sums = []
    start = 0
    for value in small:
        small_sums.append(shared[start : start + value.size].reshape(value.shape))
        start += value.size
    return (
        activations[None, None],
        small_sums[0],
        grad_conv,
        small_sums[1],
        jnp.stack(grad_highway),
        small_sums[2],
        grad_proj,
        small_sums[3],
        grad_gate[None, None],
        grad_bias[None, None],
        grad_cell[None, None],
    )


def solution(mesh):
    return jax.shard_map(
        local,
        mesh=mesh,
        in_specs=(
            P("dp", None, None),
            P("dp"),
            P(),
            P(None, ("dir", "dp")),
            P(),
            P(None, None, ("dir", "dp")),
            P(),
            P(("dir", "dp"), None),
            P(),
            P("pipe", "dir", "dp", None),
            P("pipe", "dir", None),
            P("pipe", "dir", "dp", None),
            P("pipe", "dir", "dp", None, None),
        ),
        out_specs=(
            P("pipe", "dir", "dp", None, None),
            P(),
            P(None, ("pipe", "dir", "dp")),
            P(),
            P(None, None, ("pipe", "dir", "dp")),
            P(),
            P(("pipe", "dir", "dp"), None),
            P(),
            P("pipe", "dir", "dp", None),
            P("pipe", "dir", "dp"),
            P("pipe", "dir", "dp", None),
        ),
        check_vma=False,
    )
```

```python
import functools
import math

import jax
import jax.numpy as jnp
from jax import lax
from jax.experimental import pallas as pl
from jax.experimental.pallas import tpu as pltpu
from jax.sharding import PartitionSpec as P

FILTERS = 2048
CDIM = 16
CVOCAB = 262
CHARS = 50
KMAX = 7
CLIP_LIMIT = 3.0
MASKED_FILL = -1000000000.0
MESH = pl.DeviceIdType.MESH
BF = jnp.bfloat16
F32 = jnp.float32
ALL = ("pipe", "dir", "dp")


def silu_slope(value):
    sig = jax.nn.sigmoid(value)
    return sig * (1.0 + value * (1.0 - sig))


def conv_masks(filter_index):
    filter_width = jnp.ones(filter_index.shape, jnp.int32)
    for doubling in range(6):
        filter_width = filter_width + (filter_index >= FILTERS // 64 * (1 << doubling)).astype(
            jnp.int32
        )
    offset_rows = jnp.arange(KMAX * CDIM, dtype=jnp.int32) // CDIM
    weight_mask = (offset_rows[:, None] < filter_width[None, :]).astype(jnp.float32)
    valid_place = jnp.arange(CHARS, dtype=jnp.int32)[:, None] <= CHARS - filter_width[None, :]
    return (weight_mask, valid_place)


def make_windows(embedded):
    padded = jnp.pad(embedded, ((0, 0), (0, KMAX - 1), (0, 0)))
    return jnp.concatenate(
        [padded[:, offset : offset + CHARS, :] for offset in range(KMAX)], axis=2
    )


def conv_response(ids_block, table_low, conv_low, valid_place):
    embedded = jnp.take(table_low, ids_block, axis=0)
    windows = make_windows(embedded)
    response = jnp.einsum("bpk,kf->bpf", windows, conv_low, preferred_element_type=jnp.float32)
    return (windows, jnp.where(valid_place[None], response, MASKED_FILL))


def over(count, step):
    if count <= 9:
        for off in range(count - 1, 0, -1):
            step(off)
    else:
        lax.fori_loop(1, count, lambda off, _: (step(off), 0)[1], 0)


def lstm_kernel(n, chunk, x_own, bias, p, pt, cot, *refs):
    w_in = refs[:n]
    out_ref, dx_ref, db_ref, dp_ref = refs[n:n + 4]
    dw_out = refs[n + 4:2 * n + 4]
    (xbuf, hbuf, dqbuf, gates, cells, ebuf, hown, gscr, escr, dabuf, ucell, dwacc, w, wt,
     stage, inbox, stage2, inbox2, relay, gbuf, rown,
     in_send, in_recv, ag_send, ag_recv, dq_send, dq_recv, rs_send, rs_recv,
     dx_send, dx_recv, x_send, x_recv, g_send, g_recv, st_sem, w_sem) = refs[2 * n + 4:]
    steps, _, rows, width = xbuf.shape
    total = n * rows
    cell = cells.shape[2]
    pipe = lax.axis_index("pipe")
    direction = lax.axis_index("dir")
    me = lax.axis_index("dp")
    first = pipe == 1
    second = pipe == 0
    partner = (1 - pipe, direction, me)

    def peer(off):
        if n & (n - 1):
            return lax.rem(me + off, n)
        return me ^ off

    barrier = pltpu.get_barrier_semaphore()
    over(n, lambda off: pl.semaphore_signal(
        barrier, inc=1, device_id=(pipe, direction, peer(off)), device_id_type=MESH))
    pl.semaphore_signal(barrier, inc=1, device_id=partner, device_id_type=MESH)

    each = 2 * width // n
    loads = []
    for off in range(n):
        at = pl.multiple_of(lax.rem(me + (n - off), n) * each, each)
        loads.append(pltpu.make_async_copy(w_in[off], w.at[pl.ds(at, each)], w_sem.at[off]))
        loads[-1].start()

    @pl.when(first)
    def _():
        for t in range(steps):
            xbuf[t, me] = x_own[t]

    hbuf[0] = jnp.zeros((n, rows, width), BF)
    cells[0] = jnp.zeros((total, cell), F32)
    pl.semaphore_wait(barrier, n)

    def ag_copy(buf, slot, off):
        out, into = (ag_send, ag_recv) if buf is hbuf else (dq_send, dq_recv)
        return pltpu.make_async_remote_copy(
            src_ref=buf.at[slot, me], dst_ref=buf.at[slot, me],
            send_sem=out.at[off], recv_sem=into.at[off],
            device_id=(pipe, direction, peer(off)), device_id_type=MESH)

    def rs_copy(off):
        return pltpu.make_async_remote_copy(
            src_ref=stage.at[peer(off)], dst_ref=inbox.at[me],
            send_sem=rs_send.at[off], recv_sem=rs_recv.at[off],
            device_id=(pipe, direction, peer(off)), device_id_type=MESH)

    def dx_copy(slot, off):
        return pltpu.make_async_remote_copy(
            src_ref=stage2.at[slot, peer(off)], dst_ref=inbox2.at[slot, me],
            send_sem=dx_send.at[slot, off], recv_sem=dx_recv.at[slot, off],
            device_id=(pipe, direction, peer(off)), device_id_type=MESH)

    def x_copy(t):
        return pltpu.make_async_remote_copy(
            src_ref=hbuf.at[t + 1], dst_ref=xbuf.at[t],
            send_sem=x_send.at[t], recv_sem=x_recv.at[t],
            device_id=partner, device_id_type=MESH)

    def g_copy(t):
        return pltpu.make_async_remote_copy(
            src_ref=relay.at[t], dst_ref=gbuf.at[t],
            send_sem=g_send.at[t], recv_sem=g_recv.at[t],
            device_id=partner, device_id_type=MESH)

    def in_start(t):
        over(n, lambda off: pltpu.make_async_remote_copy(
            src_ref=xbuf.at[t, me], dst_ref=xbuf.at[t, me],
            send_sem=in_send.at[t], recv_sem=in_recv.at[t],
            device_id=(pipe, direction, peer(off)), device_id_type=MESH).start())

    def in_wait(sem, t):
        blocks = xbuf.at[t, pl.ds(0, n - 1)]
        pltpu.make_async_copy(blocks, blocks, sem.at[t]).wait()

    @pl.when(first)
    def _():
        in_start(0)
        in_start(1)

    for load in loads:
        load.wait()
    for at in range(0, 2 * width, 128):
        wt[:, at:at + 128] = w[at:at + 128, :].T

    def ag_wait(buf, slot):
        def both(off):
            ag_copy(buf, slot, off).wait_send()
            ag_copy(buf, slot, off).wait_recv()
        over(n, both)

    def rs_wait():
        def both(off):
            rs_copy(off).wait_send()
            rs_copy(off).wait_recv()
        over(n, both)

    def forward(t, _):
        @pl.when(second)
        def _():
            x_copy(t).wait_recv()

        @pl.when(first)
        def _():
            in_wait(in_recv, t)

        gscr[...] = jnp.dot(
            xbuf[t].reshape(total, width), w[:width, :], preferred_element_type=F32) + bias[...]

        @pl.when(t > 0)
        def _():
            ag_wait(hbuf, t)

            @pl.when(first)
            def _():
                x_copy(t - 1).start()

        gscr[...] += jnp.dot(
            hbuf[t].reshape(total, width), w[width:, :], preferred_element_type=F32)

        def rows_step(k, _):
            at = pl.ds(pl.multiple_of(k * chunk, chunk), chunk)
            g = gscr[at, :]
            i = jax.nn.sigmoid(g[:, :cell])
            f = jax.nn.sigmoid(g[:, cell:2 * cell])
            m = jnp.tanh(g[:, 2 * cell:3 * cell])
            o = jax.nn.sigmoid(g[:, 3 * cell:])
            c = 3.0 * jnp.tanh((i * m + f * cells[t, at, :]) * (1.0 / 3.0))
            cells[t + 1, at, :] = c
            ebuf[t, at, :] = (o * jnp.tanh(c)).astype(BF)
            kind = gates.dtype
            gates[t, at, :cell] = i.astype(kind)
            gates[t, at, cell:2 * cell] = f.astype(kind)
            gates[t, at, 2 * cell:3 * cell] = m.astype(kind)
            gates[t, at, 3 * cell:] = o.astype(kind)
            return 0

        lax.fori_loop(0, total // chunk, rows_step, 0)
        q = jnp.dot(ebuf[t], p[...], preferred_element_type=F32)
        stage[...] = q.astype(BF).reshape(n, rows, width)
        over(n, lambda off: rs_copy(off).start())
        inbox[me] = stage[me]

        @pl.when(first & (t + 2 < steps))
        def _():
            in_start(t + 2)

        rs_wait()
        h = 3.0 * jnp.tanh(jnp.sum(inbox[...].astype(F32), axis=0) * (1.0 / 3.0))
        hown[t] = h
        hbuf[t + 1, me] = h.astype(BF)
        over(n, lambda off: ag_copy(hbuf, t + 1, off).start())
        add = jnp.where(second, 1.0, 0.0)
        out_ref[t] = (h + add * xbuf[t, me].astype(F32)).astype(BF)
        return 0

    lax.fori_loop(0, steps, forward, 0)
    ag_wait(hbuf, steps)

    @pl.when(first)
    def _():
        x_copy(steps - 1).start()
        lax.fori_loop(0, steps, lambda t, _: (x_copy(t).wait_send(), 0)[1], 0)
        lax.fori_loop(0, steps, lambda t, _: (in_wait(in_send, t), 0)[1], 0)

    rown[...] = jnp.zeros((rows, width), F32)
    ucell[...] = jnp.zeros((total, cell), F32)
    dwacc[...] = jnp.zeros(dwacc.shape, F32)
    db_ref[...] = jnp.zeros(db_ref.shape, F32)
    dp_ref[...] = jnp.zeros(dp_ref.shape, F32)

    def dx_finish(t):
        slot = lax.rem(t, 2)

        def both(off):
            dx_copy(slot, off).wait_send()
            dx_copy(slot, off).wait_recv()
        over(n, both)
        dx = jnp.sum(inbox2[slot].astype(F32), axis=0)
        dx_ref[t] = dx

        @pl.when(second)
        def _():
            relay[t] = (dx + cot[t].astype(F32)).astype(BF)
            g_copy(t).start()

    def backward(k, _):
        t = steps - 1 - k
        slot = lax.rem(t, 2)
        up = rown[...] + cot[t].astype(F32)
        rown[...] = up

        @pl.when(first)
        def _():
            g_copy(t).wait_recv()
            rown[...] = rown[...] + gbuf[t].astype(F32)

        ratio = hown[t] * (1.0 / 3.0)
        dqbuf[t, me] = (rown[...] * (1.0 - ratio * ratio)).astype(BF)
        over(n, lambda off: ag_copy(dqbuf, t, off).start())

        @pl.when(k > 0)
        def _():
            dx_finish(t + 1)

        ag_wait(dqbuf, t)
        escr[...] = jnp.dot(
            dqbuf[t].reshape(total, width), pt[...], preferred_element_type=F32)

        def rows_step(j, _):
            at = pl.ds(pl.multiple_of(j * chunk, chunk), chunk)
            de = escr[at, :]
            i = gates[t, at, :cell].astype(F32)
            f = gates[t, at, cell:2 * cell].astype(F32)
            m = gates[t, at, 2 * cell:3 * cell].astype(F32)
            o = gates[t, at, 3 * cell:].astype(F32)
            c = cells[t + 1, at, :]
            tc = jnp.tanh(c)
            cr = c * (1.0 / 3.0)
            dc = (de * o * (1.0 - tc * tc) + ucell[at, :]) * (1.0 - cr * cr)
            ucell[at, :] = dc * f
            for block, value in enumerate((
                dc * m * i * (1.0 - i),
                dc * cells[t, at, :] * f * (1.0 - f),
                dc * i * (1.0 - m * m),
                de * tc * o * (1.0 - o),
            )):
                value = value.astype(BF)
                where = pl.ds(block * cell, cell)
                dabuf[0, at, where] = value
                db_ref[:, where] += jnp.sum(value.astype(F32), axis=0, keepdims=True)
            return 0

        lax.fori_loop(0, total // chunk, rows_step, 0)
        r = jnp.dot(dabuf[0], wt[:, width:], preferred_element_type=F32)
        stage[...] = r.astype(BF).reshape(n, rows, width)
        over(n, lambda off: rs_copy(off).start())
        inbox[me] = stage[me]
        dx = jnp.dot(dabuf[0], wt[:, :width], preferred_element_type=F32)
        stage2[slot] = dx.astype(BF).reshape(n, rows, width)
        over(n, lambda off: dx_copy(slot, off).start())
        inbox2[slot, me] = stage2[slot, me]
        for half, buf in enumerate((xbuf, hbuf)):
            dwacc[pl.ds(half * width, width), :] += lax.dot_general(
                buf[t].reshape(total, width), dabuf[0], (((0,), (0,)), ((), ())),
                preferred_element_type=F32)
        dp_ref[...] += lax.dot_general(
            ebuf[t], dqbuf[t].reshape(total, width), (((0,), (0,)), ((), ())),
            preferred_element_type=F32)
        rs_wait()
        rown[...] = jnp.sum(inbox[...].astype(F32), axis=0)
        return 0

    lax.fori_loop(0, steps, backward, 0)
    dx_finish(0)

    @pl.when(second)
    def _():
        lax.fori_loop(0, steps, lambda t, _: (g_copy(t).wait_send(), 0)[1], 0)

    def dw_copy(off):
        return pltpu.make_async_copy(
            dabuf.at[off % 2, pl.ds(0, each)], dw_out[off], st_sem.at[off % 2])

    for off in range(n):
        if off > 1:
            dw_copy(off - 2).wait()
        at = pl.multiple_of(lax.rem(me + off, n) * each, each)
        dabuf[off % 2, :each, :] = dwacc[pl.ds(at, each), :].astype(BF)
        dw_copy(off).start()
    for off in range(n - 2, n):
        dw_copy(off).wait()


def lstm_call(n, x, weights, bias, p, pt, cot, chunk=16):
    steps, rows, width = x.shape
    cell = p.shape[0]
    total = n * rows
    sds = jax.ShapeDtypeStruct
    vm = pl.BlockSpec(memory_space=pltpu.VMEM)
    hb = pl.BlockSpec(memory_space=pl.ANY)
    keep = F32 if n <= 8 else BF
    V = pltpu.VMEM
    dma = pltpu.SemaphoreType.DMA
    return pl.pallas_call(
        functools.partial(lstm_kernel, n, chunk),
        out_shape=(
            sds((steps, rows, width), BF), sds((steps, rows, width), F32),
            sds((1, 4 * cell), F32), sds((cell, width), F32),
            *[sds((2 * width // n, 4 * cell), BF)] * n),
        in_specs=[vm] * 5 + [hb] * n,
        out_specs=[vm] * 4 + [hb] * n,
        scratch_shapes=[
            V((steps, n, rows, width), BF), V((steps + 1, n, rows, width), BF),
            V((steps, n, rows, width), BF), V((steps, total, 4 * cell), keep),
            V((steps + 1, total, cell), F32), V((steps, total, cell), BF),
            V((steps, rows, width), F32), V((total, 4 * cell), F32),
            V((total, cell), F32), V((2, total, 4 * cell), BF), V((total, cell), F32),
            V((2 * width, 4 * cell), F32), V((2 * width, 4 * cell), BF),
            V((4 * cell, 2 * width), BF),
            V((n, rows, width), BF), V((n, rows, width), BF),
            V((2, n, rows, width), BF), V((2, n, rows, width), BF),
            V((steps, rows, width), BF), V((steps, rows, width), BF), V((rows, width), F32),
            dma((steps,)), dma((steps,)), dma((n,)), dma((n,)), dma((n,)), dma((n,)), dma((n,)), dma((n,)), dma((2, n)), dma((2, n)),
            dma((steps,)), dma((steps,)), dma((steps,)), dma((steps,)), dma((2,)), dma((n,)),
        ],
        compiler_params=pltpu.CompilerParams(
            collective_id=0, has_side_effects=True, vmem_limit_bytes=60 * 1024 * 1024),
        cost_estimate=pl.CostEstimate(
            flops=300_000_000_000, bytes_accessed=64 * 1024 * 1024, transcendentals=0),
        name="relay_lstm",
    )(x, bias, p, pt, cot, *weights)


def turned(off, n, sign):
    return lax.rem(lax.axis_index("dp") + (off if sign > 0 else n - off), n)


def split_cells(weight, n):
    rows, gates = weight.shape
    cell = gates // (4 * n)

    def body(src, *dst):
        for off in range(n):
            at = pl.multiple_of(turned(off, n, 1) * cell, cell)
            dst[off][...] = src[:, pl.ds(at, cell)].astype(BF)

    return pl.pallas_call(
        body,
        grid=(4,),
        out_shape=[jax.ShapeDtypeStruct((rows, 4 * cell), BF)] * n,
        in_specs=[pl.BlockSpec((rows, n * cell), lambda b: (0, b))],
        out_specs=[pl.BlockSpec((rows, cell), lambda b: (0, b))] * n,
        cost_estimate=pl.CostEstimate(
            flops=0, bytes_accessed=6 * rows * gates, transcendentals=0
        ),
        name="split_cells",
    )(weight)


def join_cells(blocks):
    n = len(blocks)
    rows, gates = blocks[0].shape
    cell = gates // 4

    def body(*refs):
        dst = refs[n]
        for off in range(n):
            at = pl.multiple_of(turned(off, n, -1) * cell, cell)
            dst[:, pl.ds(at, cell)] = refs[off][...].astype(F32)

    return pl.pallas_call(
        body,
        grid=(4,),
        out_shape=jax.ShapeDtypeStruct((rows, n * gates), F32),
        in_specs=[pl.BlockSpec((rows, cell), lambda b: (0, b))] * n,
        out_specs=pl.BlockSpec((rows, n * cell), lambda b: (0, b)),
        cost_estimate=pl.CostEstimate(
            flops=0, bytes_accessed=6 * n * rows * gates, transcendentals=0
        ),
        name="join_cells",
    )(*blocks)


def exchange(blocks):
    n = len(blocks)
    return [blocks[0]] + [
        lax.ppermute(blocks[off], "dp", [(i, (i + off) % n) for i in range(n)])
        for off in range(1, n)
    ]


def conv_forward(ids, table_low, conv_low, valid_place):
    return jax.nn.logsumexp(conv_response(ids, table_low, conv_low, valid_place)[1], axis=1)


def own_half(value, blocks):
    sub = value.shape[-1] // (2 * blocks)
    split = value.reshape(*value.shape[:-1], blocks, 2, sub)
    mine = lax.dynamic_index_in_dim(split, lax.axis_index("pipe"), split.ndim - 2, keepdims=False)
    return mine.reshape(*value.shape[:-1], blocks * sub)


def both_halves(value, blocks):
    tokens, half = value.shape
    pair = lax.all_gather(value, "pipe").reshape(2, tokens, blocks, half // blocks)
    return jnp.transpose(pair, (1, 2, 0, 3)).reshape(tokens, 2 * half)


def conv_backward(ids, table_low, conv_low, masks, grad_before):
    weight_mask, valid_place = masks
    windows, response = conv_response(ids, table_low, conv_low, valid_place)
    share = jax.nn.softmax(response, axis=1)
    grad_response = (grad_before[:, None, :] * share).astype(BF)
    grad_conv = jnp.einsum("bpk,bpf->kf", windows, grad_response, preferred_element_type=F32)
    grad_windows = jnp.einsum("bpf,kf->bpk", grad_response, conv_low, preferred_element_type=F32)
    grad_embedded = jnp.zeros((ids.shape[0], CHARS + KMAX - 1, CDIM), F32)
    for offset in range(KMAX):
        grad_embedded = grad_embedded + jnp.pad(
            grad_windows[:, :, offset * CDIM : (offset + 1) * CDIM],
            ((0, 0), (offset, KMAX - 1 - offset), (0, 0)),
        )
    grad_embedded = grad_embedded[:, :CHARS].astype(BF)
    one_hot = (ids[:, :, None] == jnp.arange(CVOCAB, dtype=jnp.int32)).astype(BF)
    grad_table = jnp.einsum("bpv,bpc->vc", one_hot, grad_embedded, preferred_element_type=F32)
    return grad_conv * weight_mask, grad_table


def local(
    chars,
    lengths,
    char_emb,
    conv_weight,
    conv_bias,
    highway_weight,
    highway_bias,
    proj_weight,
    proj_bias,
    gate_weight,
    gate_bias,
    cell_proj,
    cotangent,
):
    n = lax.axis_size("dp")
    pipe = lax.axis_index("pipe")
    direction = lax.axis_index("dir")
    me = lax.axis_index("dp")
    everyone = lax.axis_size(ALL)
    holders = lax.axis_size(("dir", "dp"))
    seqs, steps, char_count = chars.shape
    group = seqs // lax.axis_size("dir")
    quarter = group // 2
    group_tokens = group * steps
    tokens = quarter * steps
    width = cell_proj.shape[3]
    cell = cell_proj.shape[2]
    blocks = holders // 2
    sub = FILTERS // holders
    half = FILTERS // 2
    filter_index = (
        (2 * jnp.arange(blocks, dtype=jnp.int32) + pipe)[:, None] * sub
        + jnp.arange(sub, dtype=jnp.int32)[None, :]
    ).reshape(half)
    masks = conv_masks(filter_index)

    proj_rows = proj_weight.shape[0]
    pieces = width // sub
    proj_blocks = jnp.transpose(proj_weight.reshape(proj_rows, pieces, sub), (1, 0, 2))
    proj_blocks = proj_blocks.reshape(2, pieces * proj_rows // 2, sub)
    mine = lax.dynamic_slice_in_dim(highway_weight, pipe * sub, sub, 2)
    gathered = lax.all_gather(
        jnp.concatenate([mine, proj_blocks], axis=1).astype(BF), ("dir", "dp"), axis=2, tiled=True
    )
    conv_full = lax.all_to_all(
        jnp.broadcast_to(conv_weight.astype(BF), (holders, KMAX * CDIM, sub)), ("dir", "dp"), 0, 0
    ).reshape(blocks, 2, KMAX * CDIM, sub)
    conv_low = lax.dynamic_index_in_dim(conv_full, pipe, 1, keepdims=False)
    conv_low = jnp.transpose(conv_low, (1, 0, 2)).reshape(KMAX * CDIM, half)
    conv_low = conv_low * masks[0].astype(BF)
    conv_bias_own = own_half(conv_bias, blocks)
    highway_bias_own = own_half(highway_bias.reshape(2, 2, FILTERS), blocks).reshape(2, FILTERS)

    def order_matrix(sizes):
        place = jnp.arange(steps, dtype=jnp.int32)[None, :]
        live = place < sizes[:, None]
        order = jnp.where(live & (direction == 1), sizes[:, None] - 1 - place, place)
        return ((order[:, :, None] == place[:, None, :]) & live[:, :, None]).astype(BF)

    own_order = order_matrix(lengths)
    cot = jnp.einsum("rts,rsd->trd", own_order, cotangent[0, 0], preferred_element_type=BF)

    ids = lax.dynamic_slice_in_dim(chars, direction * group, group, 0).reshape(
        group_tokens, char_count
    )
    table_low = char_emb.astype(BF)
    pooled = conv_forward(ids, table_low, conv_low, masks[1])
    features = jax.nn.silu(pooled + conv_bias_own)
    features_low = both_halves(features.astype(BF), blocks)
    gate_low, gathered, features_low = lax.optimization_barrier(
        (split_cells(gate_weight[0, 0], n), gathered, features_low)
    )
    gate_own = exchange(gate_low)
    bias_own = lax.dynamic_index_in_dim(
        gate_bias[0, 0].reshape(4, n, cell), me, 1, keepdims=False
    ).reshape(1, 4 * cell)
    cell_low = cell_proj[0, 0].astype(BF)
    highway_half = gathered[:, :FILTERS]
    proj_full = gathered[:, FILTERS:].reshape(pieces, proj_rows, holders, sub)
    proj_full = jnp.transpose(proj_full, (2, 1, 0, 3)).reshape(FILTERS, width)

    kept = [features]
    kept_low = [features_low]
    mixed = []
    for layer in range(2):
        pre = (
            jnp.dot(kept_low[layer], highway_half[layer], preferred_element_type=F32)
            + highway_bias_own[layer]
        )
        mixed.append(pre)
        gate = jax.nn.sigmoid(pre[:, half:])
        features = gate * features + (1.0 - gate) * jax.nn.silu(pre[:, :half])
        kept.append(features)
        kept_low.append(both_halves(features.astype(BF), blocks))
    own_last = lax.dynamic_slice_in_dim(kept_low[2], pipe * tokens, tokens, 0)
    encoded = jnp.dot(own_last, proj_full, preferred_element_type=F32) + proj_bias
    encoded_own = lax.all_gather(
        encoded.astype(BF).reshape(quarter, steps, width), ("dir", "pipe"), axis=0, tiled=True
    )
    kept_low, encoded_own, gate_own = lax.optimization_barrier((kept_low, encoded_own, gate_own))
    kept_all = [
        lax.all_gather(
            lax.dynamic_slice_in_dim(value, pipe * tokens, tokens, 0),
            ("dir", "dp"),
            axis=0,
            tiled=True,
        )
        for value in kept_low[:2]
    ]
    inputs = jnp.einsum("rts,rsd->trd", own_order, encoded_own, preferred_element_type=BF)

    out_own, dx_own, grad_bias, grad_cell, *grad_gate = lstm_call(
        n, inputs, gate_own, bias_own, cell_low, cell_low.T, cot
    )
    grad_gate = exchange(grad_gate)
    dx_own, kept_all = lax.optimization_barrier((dx_own, kept_all))
    activations = jnp.einsum("rts,srd->rtd", own_order, out_own, preferred_element_type=BF)

    grad_stored = jnp.einsum(
        "rts,srd->rtd", own_order, dx_own.astype(BF), preferred_element_type=F32
    )
    grad_stored = jnp.where(pipe == 1, grad_stored, 0.0).astype(BF)
    grad_stored = grad_stored.reshape(1, -1, group_tokens, width)
    grad_encoded = lax.all_to_all(
        jnp.concatenate([grad_stored, grad_stored]).reshape(-1, group_tokens, width),
        ("pipe", "dir"),
        0,
        0,
    )
    grad_encoded = jnp.sum(grad_encoded.astype(F32), axis=0).astype(BF)
    own_grads = lax.dynamic_slice_in_dim(grad_encoded, pipe * tokens, tokens, 0)
    encoded_grads = lax.all_gather(own_grads, ("dir", "dp"), axis=0, tiled=True)

    grad_proj_bias = jnp.sum(own_grads.astype(F32), axis=0)
    proj_half = lax.dynamic_index_in_dim(
        proj_full.reshape(blocks, 2, sub, width), pipe, 1, keepdims=False
    ).reshape(half, width)
    grad_features = jnp.einsum("td,fd->tf", grad_encoded, proj_half, preferred_element_type=F32)
    columns = [None, None]
    grad_highway_bias = [None, None]
    for layer in (1, 0):
        nonlinear = mixed[layer][:, :half]
        gate = jax.nn.sigmoid(mixed[layer][:, half:])
        grad_mixed = jnp.concatenate(
            [
                grad_features * (1.0 - gate) * silu_slope(nonlinear),
                grad_features * (kept[layer] - jax.nn.silu(nonlinear)) * gate * (1.0 - gate),
            ],
            axis=1,
        ).astype(BF)
        columns[layer] = grad_mixed
        grad_highway_bias[layer] = jnp.sum(grad_mixed.astype(F32), axis=0)
        partial = jnp.einsum(
            "tg,fg->tf", grad_mixed, highway_half[layer], preferred_element_type=F32
        )
        partial = lax.optimization_barrier(partial).reshape(group_tokens, blocks, 2, sub)
        sent = lax.dynamic_index_in_dim(partial, 1 - pipe, 2, keepdims=False).astype(BF)
        came = lax.ppermute(sent, "pipe", [(0, 1), (1, 0)])
        mine = lax.dynamic_index_in_dim(partial, pipe, 2, keepdims=False)
        grad_features = grad_features * gate + (mine + came.astype(F32)).reshape(
            group_tokens, half
        )
    grad_before = grad_features * silu_slope(pooled + conv_bias_own)
    grad_before, grad_gate[1:4] = lax.optimization_barrier((grad_before, grad_gate[1:4]))
    grad_conv, grad_table = conv_backward(ids, table_low, conv_low, masks, grad_before)

    def spread(value):
        split = value.reshape(*value.shape[:-1], -1, 1, sub)
        shown = jnp.arange(2, dtype=jnp.int32)[:, None] == pipe
        return jnp.where(shown, split, jnp.zeros_like(split)).reshape(*value.shape[:-1], -1)

    cols = FILTERS // everyone
    pair = jnp.stack(columns, axis=1).reshape(2, tokens, 2, 2, blocks, 1, sub)
    sent = lax.dynamic_index_in_dim(pair, 1 - pipe, 0, keepdims=False)
    came = lax.ppermute(sent, "pipe", [(0, 1), (1, 0)])
    mine = lax.dynamic_index_in_dim(pair, pipe, 0, keepdims=False)
    shown = (jnp.arange(2, dtype=jnp.int32) == pipe)[:, None]
    pair = jnp.where(shown, mine, came)
    pair = jnp.transpose(pair, (3, 4, 0, 1, 2, 5)).reshape(holders, tokens, 4 * sub)
    last = jnp.transpose(own_last.reshape(tokens, 2, holders, cols), (2, 0, 1, 3))
    pair = jnp.concatenate([pair, last.reshape(holders, tokens, 2 * cols)], axis=2)
    pair = lax.all_to_all(pair, ("dir", "dp"), 0, 0).reshape(holders * tokens, -1)
    grad_conv, pair, grad_gate = lax.optimization_barrier((grad_conv, pair, grad_gate))
    grad_gate = join_cells(grad_gate)
    small = (
        grad_table,
        spread(jnp.sum(grad_before, axis=0)),
        spread(jnp.stack(grad_highway_bias)),
        grad_proj_bias,
    )
    flat = jnp.concatenate([value.reshape(-1) for value in small])
    share = -(-flat.shape[0] // (everyone * 128)) * 128
    flat = jnp.pad(flat, (0, share * everyone - flat.shape[0])).reshape(everyone, share)
    mine = jnp.arange(n, dtype=jnp.int32)[None, :, None] == me
    bias_parts = jnp.where(mine, grad_bias.reshape(4, 1, cell), 0.0).reshape(1, n, 4 * cell)
    mine = jnp.arange(everyone // n, dtype=jnp.int32) == lax.axis_index(("pipe", "dir"))
    bias_parts = jnp.where(mine[:, None, None], bias_parts, 0.0).reshape(everyone, 4 * cell)
    packed = jnp.concatenate(
        [
            jnp.transpose(
                spread(grad_conv).reshape(KMAX * CDIM, everyone, cols), (1, 0, 2)
            ).reshape(everyone, KMAX * CDIM * cols),
            flat,
            bias_parts,
        ],
        axis=1,
    ).astype(BF)
    summed = jnp.sum(lax.all_to_all(packed, ALL, 0, 0).astype(F32), axis=0)
    grad_conv = summed[: KMAX * CDIM * cols].reshape(KMAX * CDIM, cols)
    grad_bias = summed[KMAX * CDIM * cols + share :]
    last = pair[:, 4 * sub :].reshape(holders * tokens, 2, cols)
    pair = pair[:, : 4 * sub].reshape(holders * tokens, 2, 2, sub)

    def partial_sums(owner):
        return [
            jnp.einsum(
                "tf,tg->fg",
                kept_all[layer],
                lax.dynamic_index_in_dim(pair[:, layer], owner, 1, keepdims=False),
                preferred_element_type=F32,
            )
            for layer in range(2)
        ] + [
            jnp.einsum(
                "tf,td->fd",
                lax.dynamic_index_in_dim(last, owner, 1, keepdims=False),
                encoded_grads,
                preferred_element_type=F32,
            )
        ]

    sent = jnp.concatenate(
        [value.astype(BF).reshape(-1, sub) for value in partial_sums(1 - pipe)]
    )
    came = lax.ppermute(sent, "pipe", [(0, 1), (1, 0)]).astype(F32)
    mine = partial_sums(pipe)
    grad_highway = jnp.stack(mine[:2]) + came[: 2 * FILTERS].reshape(2, FILTERS, sub)
    grad_proj = mine[2] + came[2 * FILTERS :].reshape(cols, width)
    shared = lax.all_to_all(
        jnp.broadcast_to(summed[KMAX * CDIM * cols :][:share], (everyone, share)), ALL, 0, 0
    ).reshape(-1)
    small_sums = []
    start = 0
    for value in small:
        small_sums.append(shared[start : start + value.size].reshape(value.shape))
        start += value.size
    return (
        activations[None, None],
        small_sums[0],
        grad_conv,
        small_sums[1],
        grad_highway,
        small_sums[2],
        grad_proj,
        small_sums[3],
        grad_gate[None, None],
        grad_bias[None, None],
        grad_cell[None, None],
    )


def solution(mesh):
    return jax.shard_map(
        local,
        mesh=mesh,
        in_specs=(
            P("dp", None, None),
            P("dp"),
            P(),
            P(None, ("dir", "dp")),
            P(),
            P(None, None, ("dir", "dp")),
            P(),
            P(("dir", "dp"), None),
            P(),
            P("pipe", "dir", "dp", None),
            P("pipe", "dir", None),
            P("pipe", "dir", "dp", None),
            P("pipe", "dir", "dp", None, None),
        ),
        out_specs=(
            P("pipe", "dir", "dp", None, None),
            P(),
            P(None, ("pipe", "dir", "dp")),
            P(),
            P(None, None, ("pipe", "dir", "dp")),
            P(),
            P(("pipe", "dir", "dp"), None),
            P(),
            P("pipe", "dir", "dp", None),
            P("pipe", "dir", "dp"),
            P("pipe", "dir", "dp", None),
        ),
        check_vma=False,
    )
```

```python
import functools
import math

import jax
import jax.numpy as jnp
from jax import lax
from jax.experimental import pallas as pl
from jax.experimental.pallas import tpu as pltpu
from jax.sharding import PartitionSpec as P

FILTERS = 2048
CDIM = 16
CVOCAB = 262
CHARS = 50
KMAX = 7
CLIP_LIMIT = 3.0
MASKED_FILL = -1000000000.0
MESH = pl.DeviceIdType.MESH
BF = jnp.bfloat16
F32 = jnp.float32
ALL = ("pipe", "dir", "dp")


def silu_slope(value):
    sig = jax.nn.sigmoid(value)
    return sig * (1.0 + value * (1.0 - sig))


def conv_masks(filter_index):
    filter_width = jnp.ones(filter_index.shape, jnp.int32)
    for doubling in range(6):
        filter_width = filter_width + (filter_index >= FILTERS // 64 * (1 << doubling)).astype(
            jnp.int32
        )
    offset_rows = jnp.arange(KMAX * CDIM, dtype=jnp.int32) // CDIM
    weight_mask = (offset_rows[:, None] < filter_width[None, :]).astype(jnp.float32)
    valid_place = jnp.arange(CHARS, dtype=jnp.int32)[:, None] <= CHARS - filter_width[None, :]
    return (weight_mask, valid_place)


def make_windows(embedded):
    padded = jnp.pad(embedded, ((0, 0), (0, KMAX - 1), (0, 0)))
    return jnp.concatenate(
        [padded[:, offset : offset + CHARS, :] for offset in range(KMAX)], axis=2
    )


def conv_response(ids_block, table_low, conv_low, valid_place):
    embedded = jnp.take(table_low, ids_block, axis=0)
    windows = make_windows(embedded)
    response = jnp.einsum("bpk,kf->bpf", windows, conv_low, preferred_element_type=jnp.float32)
    return (windows, jnp.where(valid_place[None], response, MASKED_FILL))


def over(count, step):
    if count <= 9:
        for off in range(count - 1, 0, -1):
            step(off)
    else:
        lax.fori_loop(1, count, lambda off, _: (step(off), 0)[1], 0)


def lstm_kernel(n, chunk, x_own, bias, p, pt, cot, *refs):
    w_in = refs[:n]
    out_ref, dx_ref, db_ref, dp_ref = refs[n:n + 4]
    dw_out = refs[n + 4:2 * n + 4]
    (xbuf, hbuf, dqbuf, gates, cells, ebuf, hown, gscr, escr, dabuf, ucell, dwacc, w, wt,
     stage, inbox, stage2, inbox2, relay, gbuf, rown,
     in_send, in_recv, ag_send, ag_recv, dq_send, dq_recv, rs_send, rs_recv,
     dx_send, dx_recv, x_send, x_recv, g_send, g_recv, st_sem, w_sem) = refs[2 * n + 4:]
    steps, _, rows, width = xbuf.shape
    total = n * rows
    cell = cells.shape[2]
    pipe = lax.axis_index("pipe")
    direction = lax.axis_index("dir")
    place = lax.axis_index("dp")
    wing = n // 2
    first = place >= wing
    second = place < wing
    me = pipe * wing + lax.rem(place, wing)
    base = place - lax.rem(place, wing)
    partner = (pipe, direction, lax.rem(place + wing, n))

    def peer(off):
        if n & (n - 1):
            return lax.rem(me + off, n)
        return me ^ off

    def at_peer(off):
        rank = peer(off)
        return (lax.div(rank, wing), direction, base + lax.rem(rank, wing))

    barrier = pltpu.get_barrier_semaphore()
    over(n, lambda off: pl.semaphore_signal(
        barrier, inc=1, device_id=at_peer(off), device_id_type=MESH))
    pl.semaphore_signal(barrier, inc=1, device_id=partner, device_id_type=MESH)

    each = 2 * width // n
    loads = []
    for off in range(n):
        at = pl.multiple_of(lax.rem(me + (n - off), n) * each, each)
        loads.append(pltpu.make_async_copy(w_in[off], w.at[pl.ds(at, each)], w_sem.at[off]))
        loads[-1].start()

    @pl.when(first)
    def _():
        for t in range(steps):
            xbuf[t, me] = x_own[t]

    hbuf[0] = jnp.zeros((n, rows, width), BF)
    cells[0] = jnp.zeros((total, cell), F32)
    pl.semaphore_wait(barrier, n)

    def ag_copy(buf, slot, off):
        out, into = (ag_send, ag_recv) if buf is hbuf else (dq_send, dq_recv)
        return pltpu.make_async_remote_copy(
            src_ref=buf.at[slot, me], dst_ref=buf.at[slot, me],
            send_sem=out.at[off], recv_sem=into.at[off],
            device_id=at_peer(off), device_id_type=MESH)

    def rs_copy(off):
        return pltpu.make_async_remote_copy(
            src_ref=stage.at[peer(off)], dst_ref=inbox.at[me],
            send_sem=rs_send.at[off], recv_sem=rs_recv.at[off],
            device_id=at_peer(off), device_id_type=MESH)

    def dx_copy(slot, off):
        return pltpu.make_async_remote_copy(
            src_ref=stage2.at[slot, peer(off)], dst_ref=inbox2.at[slot, me],
            send_sem=dx_send.at[slot, off], recv_sem=dx_recv.at[slot, off],
            device_id=at_peer(off), device_id_type=MESH)

    def x_copy(t):
        return pltpu.make_async_remote_copy(
            src_ref=hbuf.at[t + 1, me], dst_ref=xbuf.at[t, me],
            send_sem=x_send.at[t], recv_sem=x_recv.at[t],
            device_id=partner, device_id_type=MESH)

    def g_copy(t):
        return pltpu.make_async_remote_copy(
            src_ref=relay.at[t], dst_ref=gbuf.at[t],
            send_sem=g_send.at[t], recv_sem=g_recv.at[t],
            device_id=partner, device_id_type=MESH)

    def in_start(t):
        over(n, lambda off: pltpu.make_async_remote_copy(
            src_ref=xbuf.at[t, me], dst_ref=xbuf.at[t, me],
            send_sem=in_send.at[t], recv_sem=in_recv.at[t],
            device_id=at_peer(off), device_id_type=MESH).start())

    def in_wait(sem, t):
        blocks = xbuf.at[t, pl.ds(0, n - 1)]
        pltpu.make_async_copy(blocks, blocks, sem.at[t]).wait()

    @pl.when(first)
    def _():
        in_start(0)
        in_start(1)

    @pl.when(second)
    def _():
        x_copy(0).wait_recv()
        in_start(0)

    for load in loads:
        load.wait()
    for at in range(0, 2 * width, 128):
        wt[:, at:at + 128] = w[at:at + 128, :].T

    def ag_wait(buf, slot):
        def both(off):
            ag_copy(buf, slot, off).wait_send()
            ag_copy(buf, slot, off).wait_recv()
        over(n, both)

    def rs_wait():
        def both(off):
            rs_copy(off).wait_send()
            rs_copy(off).wait_recv()
        over(n, both)

    def forward(t, _):
        in_wait(in_recv, t)
        gscr[...] = jnp.dot(
            xbuf[t].reshape(total, width), w[:width, :], preferred_element_type=F32) + bias[...]

        @pl.when(t > 0)
        def _():
            ag_wait(hbuf, t)

        gscr[...] += jnp.dot(
            hbuf[t].reshape(total, width), w[width:, :], preferred_element_type=F32)

        def rows_step(k, _):
            at = pl.ds(pl.multiple_of(k * chunk, chunk), chunk)
            g = gscr[at, :]
            i = jax.nn.sigmoid(g[:, :cell])
            f = jax.nn.sigmoid(g[:, cell:2 * cell])
            m = jnp.tanh(g[:, 2 * cell:3 * cell])
            o = jax.nn.sigmoid(g[:, 3 * cell:])
            c = 3.0 * jnp.tanh((i * m + f * cells[t, at, :]) * (1.0 / 3.0))
            cells[t + 1, at, :] = c
            ebuf[t, at, :] = (o * jnp.tanh(c)).astype(BF)
            kind = gates.dtype
            gates[t, at, :cell] = i.astype(kind)
            gates[t, at, cell:2 * cell] = f.astype(kind)
            gates[t, at, 2 * cell:3 * cell] = m.astype(kind)
            gates[t, at, 3 * cell:] = o.astype(kind)
            return 0

        lax.fori_loop(0, total // chunk, rows_step, 0)
        q = jnp.dot(ebuf[t], p[...], preferred_element_type=F32)
        stage[...] = q.astype(BF).reshape(n, rows, width)
        over(n, lambda off: rs_copy(off).start())
        inbox[me] = stage[me]

        @pl.when(first & (t + 2 < steps))
        def _():
            in_start(t + 2)

        @pl.when(second & (t + 1 < steps))
        def _():
            x_copy(t + 1).wait_recv()
            in_start(t + 1)

        rs_wait()
        h = 3.0 * jnp.tanh(jnp.sum(inbox[...].astype(F32), axis=0) * (1.0 / 3.0))
        hown[t] = h
        hbuf[t + 1, me] = h.astype(BF)
        over(n, lambda off: ag_copy(hbuf, t + 1, off).start())

        @pl.when(first)
        def _():
            x_copy(t).start()

        add = jnp.where(second, 1.0, 0.0)
        out_ref[t] = (h + add * xbuf[t, me].astype(F32)).astype(BF)
        return 0

    lax.fori_loop(0, steps, forward, 0)
    ag_wait(hbuf, steps)

    lax.fori_loop(0, steps, lambda t, _: (in_wait(in_send, t), 0)[1], 0)

    @pl.when(first)
    def _():
        lax.fori_loop(0, steps, lambda t, _: (x_copy(t).wait_send(), 0)[1], 0)

    rown[...] = jnp.zeros((rows, width), F32)
    ucell[...] = jnp.zeros((total, cell), F32)
    dwacc[...] = jnp.zeros(dwacc.shape, F32)
    db_ref[...] = jnp.zeros(db_ref.shape, F32)
    dp_ref[...] = jnp.zeros(dp_ref.shape, F32)

    def dx_finish(t):
        slot = lax.rem(t, 2)

        def both(off):
            dx_copy(slot, off).wait_send()
            dx_copy(slot, off).wait_recv()
        over(n, both)
        dx = jnp.sum(inbox2[slot].astype(F32), axis=0)
        dx_ref[t] = dx

        @pl.when(second)
        def _():
            relay[t] = (dx + cot[t].astype(F32)).astype(BF)
            g_copy(t).start()

    def backward(k, _):
        t = steps - 1 - k
        slot = lax.rem(t, 2)
        up = rown[...] + cot[t].astype(F32)
        rown[...] = up

        @pl.when(first)
        def _():
            g_copy(t).wait_recv()
            rown[...] = rown[...] + gbuf[t].astype(F32)

        ratio = hown[t] * (1.0 / 3.0)
        dqbuf[t, me] = (rown[...] * (1.0 - ratio * ratio)).astype(BF)
        over(n, lambda off: ag_copy(dqbuf, t, off).start())

        @pl.when(k > 0)
        def _():
            dx_finish(t + 1)

        ag_wait(dqbuf, t)
        escr[...] = jnp.dot(
            dqbuf[t].reshape(total, width), pt[...], preferred_element_type=F32)

        def rows_step(j, _):
            at = pl.ds(pl.multiple_of(j * chunk, chunk), chunk)
            de = escr[at, :]
            i = gates[t, at, :cell].astype(F32)
            f = gates[t, at, cell:2 * cell].astype(F32)
            m = gates[t, at, 2 * cell:3 * cell].astype(F32)
            o = gates[t, at, 3 * cell:].astype(F32)
            c = cells[t + 1, at, :]
            tc = jnp.tanh(c)
            cr = c * (1.0 / 3.0)
            dc = (de * o * (1.0 - tc * tc) + ucell[at, :]) * (1.0 - cr * cr)
            ucell[at, :] = dc * f
            for block, value in enumerate((
                dc * m * i * (1.0 - i),
                dc * cells[t, at, :] * f * (1.0 - f),
                dc * i * (1.0 - m * m),
                de * tc * o * (1.0 - o),
            )):
                value = value.astype(BF)
                where = pl.ds(block * cell, cell)
                dabuf[0, at, where] = value
                db_ref[:, where] += jnp.sum(value.astype(F32), axis=0, keepdims=True)
            return 0

        lax.fori_loop(0, total // chunk, rows_step, 0)
        r = jnp.dot(dabuf[0], wt[:, width:], preferred_element_type=F32)
        stage[...] = r.astype(BF).reshape(n, rows, width)
        over(n, lambda off: rs_copy(off).start())
        inbox[me] = stage[me]
        dx = jnp.dot(dabuf[0], wt[:, :width], preferred_element_type=F32)
        stage2[slot] = dx.astype(BF).reshape(n, rows, width)
        over(n, lambda off: dx_copy(slot, off).start())
        inbox2[slot, me] = stage2[slot, me]
        for half, buf in enumerate((xbuf, hbuf)):
            dwacc[pl.ds(half * width, width), :] += lax.dot_general(
                buf[t].reshape(total, width), dabuf[0], (((0,), (0,)), ((), ())),
                preferred_element_type=F32)
        dp_ref[...] += lax.dot_general(
            ebuf[t], dqbuf[t].reshape(total, width), (((0,), (0,)), ((), ())),
            preferred_element_type=F32)
        rs_wait()
        rown[...] = jnp.sum(inbox[...].astype(F32), axis=0)
        return 0

    lax.fori_loop(0, steps, backward, 0)
    dx_finish(0)

    @pl.when(second)
    def _():
        lax.fori_loop(0, steps, lambda t, _: (g_copy(t).wait_send(), 0)[1], 0)

    def dw_copy(off):
        return pltpu.make_async_copy(
            dabuf.at[off % 2, pl.ds(0, each)], dw_out[off], st_sem.at[off % 2])

    for off in range(n):
        if off > 1:
            dw_copy(off - 2).wait()
        at = pl.multiple_of(lax.rem(me + off, n) * each, each)
        dabuf[off % 2, :each, :] = dwacc[pl.ds(at, each), :].astype(BF)
        dw_copy(off).start()
    for off in range(n - 2, n):
        dw_copy(off).wait()


def lstm_call(n, x, weights, bias, p, pt, cot, chunk=16):
    steps, rows, width = x.shape
    cell = p.shape[0]
    total = n * rows
    sds = jax.ShapeDtypeStruct
    vm = pl.BlockSpec(memory_space=pltpu.VMEM)
    hb = pl.BlockSpec(memory_space=pl.ANY)
    keep = F32 if n <= 8 else BF
    V = pltpu.VMEM
    dma = pltpu.SemaphoreType.DMA
    return pl.pallas_call(
        functools.partial(lstm_kernel, n, chunk),
        out_shape=(
            sds((steps, rows, width), BF), sds((steps, rows, width), F32),
            sds((1, 4 * cell), F32), sds((cell, width), F32),
            *[sds((2 * width // n, 4 * cell), BF)] * n),
        in_specs=[vm] * 5 + [hb] * n,
        out_specs=[vm] * 4 + [hb] * n,
        scratch_shapes=[
            V((steps, n, rows, width), BF), V((steps + 1, n, rows, width), BF),
            V((steps, n, rows, width), BF), V((steps, total, 4 * cell), keep),
            V((steps + 1, total, cell), F32), V((steps, total, cell), BF),
            V((steps, rows, width), F32), V((total, 4 * cell), F32),
            V((total, cell), F32), V((2, total, 4 * cell), BF), V((total, cell), F32),
            V((2 * width, 4 * cell), F32), V((2 * width, 4 * cell), BF),
            V((4 * cell, 2 * width), BF),
            V((n, rows, width), BF), V((n, rows, width), BF),
            V((2, n, rows, width), BF), V((2, n, rows, width), BF),
            V((steps, rows, width), BF), V((steps, rows, width), BF), V((rows, width), F32),
            dma((steps,)), dma((steps,)), dma((n,)), dma((n,)), dma((n,)), dma((n,)), dma((n,)), dma((n,)), dma((2, n)), dma((2, n)),
            dma((steps,)), dma((steps,)), dma((steps,)), dma((steps,)), dma((2,)), dma((n,)),
        ],
        compiler_params=pltpu.CompilerParams(
            collective_id=0, has_side_effects=True, vmem_limit_bytes=60 * 1024 * 1024),
        cost_estimate=pl.CostEstimate(
            flops=300_000_000_000, bytes_accessed=64 * 1024 * 1024, transcendentals=0),
        name="relay_lstm",
    )(x, bias, p, pt, cot, *weights)


def turned(off, n, sign):
    return lax.rem(lax.axis_index("dp") + (off if sign > 0 else n - off), n)


def split_cells(weight, n):
    rows, gates = weight.shape
    cell = gates // (4 * n)

    def body(src, *dst):
        for off in range(n):
            at = pl.multiple_of(turned(off, n, 1) * cell, cell)
            dst[off][...] = src[:, pl.ds(at, cell)].astype(BF)

    return pl.pallas_call(
        body,
        grid=(4,),
        out_shape=[jax.ShapeDtypeStruct((rows, 4 * cell), BF)] * n,
        in_specs=[pl.BlockSpec((rows, n * cell), lambda b: (0, b))],
        out_specs=[pl.BlockSpec((rows, cell), lambda b: (0, b))] * n,
        cost_estimate=pl.CostEstimate(
            flops=0, bytes_accessed=6 * rows * gates, transcendentals=0
        ),
        name="split_cells",
    )(weight)


def join_cells(blocks):
    n = len(blocks)
    rows, gates = blocks[0].shape
    cell = gates // 4

    def body(*refs):
        dst = refs[n]
        for off in range(n):
            at = pl.multiple_of(turned(off, n, -1) * cell, cell)
            dst[:, pl.ds(at, cell)] = refs[off][...].astype(F32)

    return pl.pallas_call(
        body,
        grid=(4,),
        out_shape=jax.ShapeDtypeStruct((rows, n * gates), F32),
        in_specs=[pl.BlockSpec((rows, cell), lambda b: (0, b))] * n,
        out_specs=pl.BlockSpec((rows, n * cell), lambda b: (0, b)),
        cost_estimate=pl.CostEstimate(
            flops=0, bytes_accessed=6 * n * rows * gates, transcendentals=0
        ),
        name="join_cells",
    )(*blocks)


def rank_pairs(n, off, layers=(0, 1)):
    wing = n // 2
    pairs = []
    for layer in layers:
        for j in range(n):
            rank = (j + off) % n
            pairs.append((layer * n + j, rank // wing * n + layer * wing + rank % wing))
    return pairs


def to_ranks(value, off):
    return lax.ppermute(value, ("pipe", "dp"), rank_pairs(lax.axis_size("dp"), off))


def from_ranks(value, off, layers=(0, 1)):
    pairs = rank_pairs(lax.axis_size("dp"), -off, layers)
    return lax.ppermute(value, ("pipe", "dp"), [(there, here) for here, there in pairs])


def conv_forward(ids, table_low, conv_low, valid_place):
    return jax.nn.logsumexp(conv_response(ids, table_low, conv_low, valid_place)[1], axis=1)


def own_half(value, blocks):
    sub = value.shape[-1] // (2 * blocks)
    split = value.reshape(*value.shape[:-1], blocks, 2, sub)
    mine = lax.dynamic_index_in_dim(split, lax.axis_index("pipe"), split.ndim - 2, keepdims=False)
    return mine.reshape(*value.shape[:-1], blocks * sub)


def both_halves(value, blocks):
    tokens, half = value.shape
    pair = lax.all_gather(value, "pipe").reshape(2, tokens, blocks, half // blocks)
    return jnp.transpose(pair, (1, 2, 0, 3)).reshape(tokens, 2 * half)


def conv_backward(ids, table_low, conv_low, masks, grad_before):
    weight_mask, valid_place = masks
    windows, response = conv_response(ids, table_low, conv_low, valid_place)
    share = jax.nn.softmax(response, axis=1)
    grad_response = (grad_before[:, None, :] * share).astype(BF)
    grad_conv = jnp.einsum("bpk,bpf->kf", windows, grad_response, preferred_element_type=F32)
    grad_windows = jnp.einsum("bpf,kf->bpk", grad_response, conv_low, preferred_element_type=F32)
    grad_embedded = jnp.zeros((ids.shape[0], CHARS + KMAX - 1, CDIM), F32)
    for offset in range(KMAX):
        grad_embedded = grad_embedded + jnp.pad(
            grad_windows[:, :, offset * CDIM : (offset + 1) * CDIM],
            ((0, 0), (offset, KMAX - 1 - offset), (0, 0)),
        )
    grad_embedded = grad_embedded[:, :CHARS].astype(BF)
    one_hot = (ids[:, :, None] == jnp.arange(CVOCAB, dtype=jnp.int32)).astype(BF)
    grad_table = jnp.einsum("bpv,bpc->vc", one_hot, grad_embedded, preferred_element_type=F32)
    return grad_conv * weight_mask, grad_table


def local(
    chars,
    lengths,
    char_emb,
    conv_weight,
    conv_bias,
    highway_weight,
    highway_bias,
    proj_weight,
    proj_bias,
    gate_weight,
    gate_bias,
    cell_proj,
    cotangent,
):
    n = lax.axis_size("dp")
    pipe = lax.axis_index("pipe")
    direction = lax.axis_index("dir")
    me = lax.axis_index("dp")
    everyone = lax.axis_size(ALL)
    holders = lax.axis_size(("dir", "dp"))
    seqs, steps, char_count = chars.shape
    group = seqs // lax.axis_size("dir")
    quarter = group // 2
    group_tokens = group * steps
    tokens = quarter * steps
    width = cell_proj.shape[3]
    cell = cell_proj.shape[2]
    blocks = holders // 2
    sub = FILTERS // holders
    half = FILTERS // 2
    filter_index = (
        (2 * jnp.arange(blocks, dtype=jnp.int32) + pipe)[:, None] * sub
        + jnp.arange(sub, dtype=jnp.int32)[None, :]
    ).reshape(half)
    masks = conv_masks(filter_index)

    proj_rows = proj_weight.shape[0]
    pieces = width // sub
    proj_blocks = jnp.transpose(proj_weight.reshape(proj_rows, pieces, sub), (1, 0, 2))
    proj_blocks = proj_blocks.reshape(2, pieces * proj_rows // 2, sub)
    mine = lax.dynamic_slice_in_dim(highway_weight, pipe * sub, sub, 2)
    gathered = lax.all_gather(
        jnp.concatenate([mine, proj_blocks], axis=1).astype(BF), ("dir", "dp"), axis=2, tiled=True
    )
    conv_full = lax.all_to_all(
        jnp.broadcast_to(conv_weight.astype(BF), (holders, KMAX * CDIM, sub)), ("dir", "dp"), 0, 0
    ).reshape(blocks, 2, KMAX * CDIM, sub)
    conv_low = lax.dynamic_index_in_dim(conv_full, pipe, 1, keepdims=False)
    conv_low = jnp.transpose(conv_low, (1, 0, 2)).reshape(KMAX * CDIM, half)
    conv_low = conv_low * masks[0].astype(BF)
    conv_bias_own = own_half(conv_bias, blocks)
    highway_bias_own = own_half(highway_bias.reshape(2, 2, FILTERS), blocks).reshape(2, FILTERS)

    def order_matrix(sizes):
        place = jnp.arange(steps, dtype=jnp.int32)[None, :]
        live = place < sizes[:, None]
        order = jnp.where(live & (direction == 1), sizes[:, None] - 1 - place, place)
        return ((order[:, :, None] == place[:, None, :]) & live[:, :, None]).astype(BF)

    own_order = order_matrix(lengths)
    cot = jnp.einsum("rts,rsd->trd", own_order, cotangent[0, 0], preferred_element_type=BF)

    ids = lax.dynamic_slice_in_dim(chars, direction * group, group, 0).reshape(
        group_tokens, char_count
    )
    table_low = char_emb.astype(BF)
    pooled = conv_forward(ids, table_low, conv_low, masks[1])
    features = jax.nn.silu(pooled + conv_bias_own)
    features_low = both_halves(features.astype(BF), blocks)
    bias_own = lax.dynamic_index_in_dim(
        gate_bias[0, 0].reshape(4, n, cell), me, 1, keepdims=False
    ).reshape(1, 4 * cell)
    bias_own = to_ranks(bias_own, 0)
    moved = to_ranks(
        jnp.concatenate([cell_proj[0, 0].astype(BF), cot.reshape(steps * seqs, width)]), 0
    )
    gate_low, gathered, features_low, bias_own, moved = lax.optimization_barrier(
        (split_cells(gate_weight[0, 0], n), gathered, features_low, bias_own, moved)
    )
    cell_low = moved[:cell]
    cot = moved[cell:].reshape(steps, seqs, width)
    gate_own = [to_ranks(block, off) for off, block in enumerate(gate_low)]
    highway_half = gathered[:, :FILTERS]
    proj_full = gathered[:, FILTERS:].reshape(pieces, proj_rows, holders, sub)
    proj_full = jnp.transpose(proj_full, (2, 1, 0, 3)).reshape(FILTERS, width)

    kept = [features]
    kept_low = [features_low]
    mixed = []
    for layer in range(2):
        pre = (
            jnp.dot(kept_low[layer], highway_half[layer], preferred_element_type=F32)
            + highway_bias_own[layer]
        )
        mixed.append(pre)
        gate = jax.nn.sigmoid(pre[:, half:])
        features = gate * features + (1.0 - gate) * jax.nn.silu(pre[:, :half])
        kept.append(features)
        kept_low.append(both_halves(features.astype(BF), blocks))
    own_last = lax.dynamic_slice_in_dim(kept_low[2], pipe * tokens, tokens, 0)
    encoded = jnp.dot(own_last, proj_full, preferred_element_type=F32) + proj_bias
    encoded_own = lax.all_gather(
        encoded.astype(BF).reshape(quarter, steps, width), ("dir", "pipe"), axis=0, tiled=True
    )
    kept_low, encoded_own, gate_own = lax.optimization_barrier((kept_low, encoded_own, gate_own))
    kept_all = [
        lax.all_gather(
            lax.dynamic_slice_in_dim(value, pipe * tokens, tokens, 0),
            ("dir", "dp"),
            axis=0,
            tiled=True,
        )
        for value in kept_low[:2]
    ]
    inputs = jnp.einsum("rts,rsd->trd", own_order, encoded_own, preferred_element_type=BF)
    wing = n // 2
    inputs = lax.ppermute(
        inputs,
        ("pipe", "dp"),
        [(k, wing + k) for k in range(wing)] + [(n + k, n + k) for k in range(wing, n)],
    )

    out_own, dx_own, grad_bias, grad_cell, *grad_gate = lstm_call(
        n, inputs, gate_own, bias_own, cell_low, cell_low.T, cot
    )
    dx_own = from_ranks(dx_own.astype(BF), 0, (1,))
    grad_gate = [from_ranks(block, off) for off, block in enumerate(grad_gate)]
    dx_own, kept_all = lax.optimization_barrier((dx_own, kept_all))

    grad_stored = jnp.einsum(
        "rts,srd->rtd", own_order, dx_own, preferred_element_type=F32
    )
    grad_stored = jnp.where(pipe == 1, grad_stored, 0.0).astype(BF)
    grad_stored = grad_stored.reshape(1, -1, group_tokens, width)
    grad_encoded = lax.all_to_all(
        jnp.concatenate([grad_stored, grad_stored]).reshape(-1, group_tokens, width),
        ("pipe", "dir"),
        0,
        0,
    )
    grad_encoded = jnp.sum(grad_encoded.astype(F32), axis=0).astype(BF)
    own_grads = lax.dynamic_slice_in_dim(grad_encoded, pipe * tokens, tokens, 0)
    encoded_grads = lax.all_gather(own_grads, ("dir", "dp"), axis=0, tiled=True)

    grad_proj_bias = jnp.sum(own_grads.astype(F32), axis=0)
    proj_half = lax.dynamic_index_in_dim(
        proj_full.reshape(blocks, 2, sub, width), pipe, 1, keepdims=False
    ).reshape(half, width)
    grad_features = jnp.einsum("td,fd->tf", grad_encoded, proj_half, preferred_element_type=F32)
    columns = [None, None]
    grad_highway_bias = [None, None]
    for layer in (1, 0):
        nonlinear = mixed[layer][:, :half]
        gate = jax.nn.sigmoid(mixed[layer][:, half:])
        grad_mixed = jnp.concatenate(
            [
                grad_features * (1.0 - gate) * silu_slope(nonlinear),
                grad_features * (kept[layer] - jax.nn.silu(nonlinear)) * gate * (1.0 - gate),
            ],
            axis=1,
        ).astype(BF)
        columns[layer] = grad_mixed
        grad_highway_bias[layer] = jnp.sum(grad_mixed.astype(F32), axis=0)
        partial = jnp.einsum(
            "tg,fg->tf", grad_mixed, highway_half[layer], preferred_element_type=F32
        )
        partial = lax.optimization_barrier(partial).reshape(group_tokens, blocks, 2, sub)
        sent = lax.dynamic_index_in_dim(partial, 1 - pipe, 2, keepdims=False).astype(BF)
        came = lax.ppermute(sent, "pipe", [(0, 1), (1, 0)])
        mine = lax.dynamic_index_in_dim(partial, pipe, 2, keepdims=False)
        grad_features = grad_features * gate + (mine + came.astype(F32)).reshape(
            group_tokens, half
        )
    grad_before = grad_features * silu_slope(pooled + conv_bias_own)
    grad_before, grad_gate[1:5] = lax.optimization_barrier((grad_before, grad_gate[1:5]))
    grad_conv, grad_table = conv_backward(ids, table_low, conv_low, masks, grad_before)

    def spread(value):
        split = value.reshape(*value.shape[:-1], -1, 1, sub)
        shown = jnp.arange(2, dtype=jnp.int32)[:, None] == pipe
        return jnp.where(shown, split, jnp.zeros_like(split)).reshape(*value.shape[:-1], -1)

    cols = FILTERS // everyone
    pair = jnp.stack(columns, axis=1).reshape(2, tokens, 2, 2, blocks, 1, sub)
    sent = lax.dynamic_index_in_dim(pair, 1 - pipe, 0, keepdims=False)
    came = lax.ppermute(sent, "pipe", [(0, 1), (1, 0)])
    mine = lax.dynamic_index_in_dim(pair, pipe, 0, keepdims=False)
    shown = (jnp.arange(2, dtype=jnp.int32) == pipe)[:, None]
    pair = jnp.where(shown, mine, came)
    pair = jnp.transpose(pair, (3, 4, 0, 1, 2, 5)).reshape(holders, tokens, 4 * sub)
    last = jnp.transpose(own_last.reshape(tokens, 2, holders, cols), (2, 0, 1, 3))
    pair = jnp.concatenate([pair, last.reshape(holders, tokens, 2 * cols)], axis=2)
    pair = lax.all_to_all(pair, ("dir", "dp"), 0, 0).reshape(holders * tokens, -1)
    grad_conv, pair, grad_gate = lax.optimization_barrier((grad_conv, pair, grad_gate))
    grad_gate = join_cells(grad_gate)
    small = (
        grad_table,
        spread(jnp.sum(grad_before, axis=0)),
        spread(jnp.stack(grad_highway_bias)),
        grad_proj_bias,
    )
    flat = jnp.concatenate([value.reshape(-1) for value in small])
    share = -(-flat.shape[0] // (everyone * 128)) * 128
    flat = jnp.pad(flat, (0, share * everyone - flat.shape[0])).reshape(everyone, share)
    rank = pipe * wing + lax.rem(me, wing)
    mine = jnp.arange(n, dtype=jnp.int32)[None, :, None] == rank
    bias_parts = jnp.where(mine, grad_bias.reshape(4, 1, cell), 0.0).reshape(1, n, 4 * cell)
    layer = lax.div(me, wing) * lax.axis_size("dir") + direction
    mine = jnp.arange(everyone // n, dtype=jnp.int32) == layer
    bias_parts = jnp.where(mine[:, None, None], bias_parts, 0.0).reshape(everyone, 4 * cell)
    packed = jnp.concatenate(
        [
            jnp.transpose(
                spread(grad_conv).reshape(KMAX * CDIM, everyone, cols), (1, 0, 2)
            ).reshape(everyone, KMAX * CDIM * cols),
            flat,
            bias_parts,
        ],
        axis=1,
    ).astype(BF)
    summed = jnp.sum(lax.all_to_all(packed, ALL, 0, 0).astype(F32), axis=0)
    out_own = from_ranks(out_own, 0)
    grad_cell = from_ranks(grad_cell.astype(BF), 0)
    summed, out_own, grad_cell = lax.optimization_barrier((summed, out_own, grad_cell))
    activations = jnp.einsum("rts,srd->rtd", own_order, out_own, preferred_element_type=BF)
    grad_cell = grad_cell.astype(F32)
    grad_conv = summed[: KMAX * CDIM * cols].reshape(KMAX * CDIM, cols)
    grad_bias = summed[KMAX * CDIM * cols + share :]
    last = pair[:, 4 * sub :].reshape(holders * tokens, 2, cols)
    pair = pair[:, : 4 * sub].reshape(holders * tokens, 2, 2, sub)

    def partial_sums(owner):
        return [
            jnp.einsum(
                "tf,tg->fg",
                kept_all[layer],
                lax.dynamic_index_in_dim(pair[:, layer], owner, 1, keepdims=False),
                preferred_element_type=F32,
            )
            for layer in range(2)
        ] + [
            jnp.einsum(
                "tf,td->fd",
                lax.dynamic_index_in_dim(last, owner, 1, keepdims=False),
                encoded_grads,
                preferred_element_type=F32,
            )
        ]

    sent = jnp.concatenate(
        [value.astype(BF).reshape(-1, sub) for value in partial_sums(1 - pipe)]
    )
    came = lax.ppermute(sent, "pipe", [(0, 1), (1, 0)]).astype(F32)
    mine = partial_sums(pipe)
    grad_highway = jnp.stack(mine[:2]) + came[: 2 * FILTERS].reshape(2, FILTERS, sub)
    grad_proj = mine[2] + came[2 * FILTERS :].reshape(cols, width)
    shared = lax.all_to_all(
        jnp.broadcast_to(summed[KMAX * CDIM * cols :][:share], (everyone, share)), ALL, 0, 0
    ).reshape(-1)
    small_sums = []
    start = 0
    for value in small:
        small_sums.append(shared[start : start + value.size].reshape(value.shape))
        start += value.size
    return (
        activations[None, None],
        small_sums[0],
        grad_conv,
        small_sums[1],
        grad_highway,
        small_sums[2],
        grad_proj,
        small_sums[3],
        grad_gate[None, None],
        grad_bias[None, None],
        grad_cell[None, None],
    )


def solution(mesh):
    return jax.shard_map(
        local,
        mesh=mesh,
        in_specs=(
            P("dp", None, None),
            P("dp"),
            P(),
            P(None, ("dir", "dp")),
            P(),
            P(None, None, ("dir", "dp")),
            P(),
            P(("dir", "dp"), None),
            P(),
            P("pipe", "dir", "dp", None),
            P("pipe", "dir", None),
            P("pipe", "dir", "dp", None),
            P("pipe", "dir", "dp", None, None),
        ),
        out_specs=(
            P("pipe", "dir", "dp", None, None),
            P(),
            P(None, ("pipe", "dir", "dp")),
            P(),
            P(None, None, ("pipe", "dir", "dp")),
            P(),
            P(("pipe", "dir", "dp"), None),
            P(),
            P("pipe", "dir", "dp", None),
            P("pipe", "dir", "dp"),
            P("pipe", "dir", "dp", None),
        ),
        check_vma=False,
    )
```

```python
import functools
import math

import jax
import jax.numpy as jnp
from jax import lax
from jax.experimental import pallas as pl
from jax.experimental.pallas import tpu as pltpu
from jax.sharding import PartitionSpec as P

FILTERS = 2048
CDIM = 16
CVOCAB = 262
CHARS = 50
KMAX = 7
CLIP_LIMIT = 3.0
MASKED_FILL = -1000000000.0
MESH = pl.DeviceIdType.MESH
BF = jnp.bfloat16
F32 = jnp.float32
ALL = ("pipe", "dir", "dp")


def silu_slope(value):
    sig = jax.nn.sigmoid(value)
    return sig * (1.0 + value * (1.0 - sig))


def conv_masks(filter_index):
    filter_width = jnp.ones(filter_index.shape, jnp.int32)
    for doubling in range(6):
        filter_width = filter_width + (filter_index >= FILTERS // 64 * (1 << doubling)).astype(
            jnp.int32
        )
    offset_rows = jnp.arange(KMAX * CDIM, dtype=jnp.int32) // CDIM
    weight_mask = (offset_rows[:, None] < filter_width[None, :]).astype(jnp.float32)
    valid_place = jnp.arange(CHARS, dtype=jnp.int32)[:, None] <= CHARS - filter_width[None, :]
    return (weight_mask, valid_place)


def make_windows(embedded):
    padded = jnp.pad(embedded, ((0, 0), (0, KMAX - 1), (0, 0)))
    return jnp.concatenate(
        [padded[:, offset : offset + CHARS, :] for offset in range(KMAX)], axis=2
    )


def conv_response(ids_block, table_low, conv_low, valid_place):
    embedded = jnp.take(table_low, ids_block, axis=0)
    windows = make_windows(embedded)
    response = jnp.einsum("bpk,kf->bpf", windows, conv_low, preferred_element_type=jnp.float32)
    return (windows, jnp.where(valid_place[None], response, MASKED_FILL))


def over(count, step):
    if count <= 9:
        for off in range(count - 1, 0, -1):
            step(off)
    else:
        lax.fori_loop(1, count, lambda off, _: (step(off), 0)[1], 0)


def lstm_kernel(n, chunk, x_own, bias, p, pt, cot, w_in, *refs):
    out_ref, dx_ref, db_ref, dp_ref = refs[:4]
    dw_out = refs[4:n + 4]
    (xbuf, hbuf, dqbuf, gates, cells, ebuf, hown, gscr, escr, dabuf, ucell, dwacc, w, wt,
     stage, inbox, stage2, inbox2, relay, gbuf, rown,
     in_send, in_recv, ag_send, ag_recv, dq_send, dq_recv, rs_send, rs_recv,
     dx_send, dx_recv, x_send, x_recv, g_send, g_recv, st_sem, w_sem) = refs[n + 4:]
    steps, _, rows, width = xbuf.shape
    total = n * rows
    cell = cells.shape[2]
    pipe = lax.axis_index("pipe")
    direction = lax.axis_index("dir")
    place = lax.axis_index("dp")
    wing = n // 2
    first = place >= wing
    second = place < wing
    me = pipe * wing + lax.rem(place, wing)
    base = place - lax.rem(place, wing)
    partner = (pipe, direction, lax.rem(place + wing, n))

    def peer(off):
        if n & (n - 1):
            return lax.rem(me + off, n)
        return me ^ off

    def at_peer(off):
        rank = peer(off)
        return (lax.div(rank, wing), direction, base + lax.rem(rank, wing))

    barrier = pltpu.get_barrier_semaphore()
    over(n, lambda off: pl.semaphore_signal(
        barrier, inc=1, device_id=at_peer(off), device_id_type=MESH))
    pl.semaphore_signal(barrier, inc=1, device_id=partner, device_id_type=MESH)

    each = 2 * width // n
    load = pltpu.make_async_copy(w_in, w, w_sem)
    load.start()

    @pl.when(first)
    def _():
        for t in range(steps):
            xbuf[t, me] = x_own[t]

    hbuf[0] = jnp.zeros((n, rows, width), BF)
    cells[0] = jnp.zeros((total, cell), F32)
    pl.semaphore_wait(barrier, n)

    def ag_copy(buf, slot, off):
        out, into = (ag_send, ag_recv) if buf is hbuf else (dq_send, dq_recv)
        return pltpu.make_async_remote_copy(
            src_ref=buf.at[slot, me], dst_ref=buf.at[slot, me],
            send_sem=out.at[off], recv_sem=into.at[off],
            device_id=at_peer(off), device_id_type=MESH)

    def rs_copy(off):
        return pltpu.make_async_remote_copy(
            src_ref=stage.at[peer(off)], dst_ref=inbox.at[me],
            send_sem=rs_send.at[off], recv_sem=rs_recv.at[off],
            device_id=at_peer(off), device_id_type=MESH)

    def dx_copy(slot, off):
        return pltpu.make_async_remote_copy(
            src_ref=stage2.at[slot, peer(off)], dst_ref=inbox2.at[slot, me],
            send_sem=dx_send.at[slot, off], recv_sem=dx_recv.at[slot, off],
            device_id=at_peer(off), device_id_type=MESH)

    def x_copy(t):
        return pltpu.make_async_remote_copy(
            src_ref=hbuf.at[t + 1, me], dst_ref=xbuf.at[t, me],
            send_sem=x_send.at[t], recv_sem=x_recv.at[t],
            device_id=partner, device_id_type=MESH)

    def g_copy(t):
        return pltpu.make_async_remote_copy(
            src_ref=relay.at[t], dst_ref=gbuf.at[t],
            send_sem=g_send.at[t], recv_sem=g_recv.at[t],
            device_id=partner, device_id_type=MESH)

    def in_start(t):
        over(n, lambda off: pltpu.make_async_remote_copy(
            src_ref=xbuf.at[t, me], dst_ref=xbuf.at[t, me],
            send_sem=in_send.at[t], recv_sem=in_recv.at[t],
            device_id=at_peer(off), device_id_type=MESH).start())

    def in_wait(sem, t):
        blocks = xbuf.at[t, pl.ds(0, n - 1)]
        pltpu.make_async_copy(blocks, blocks, sem.at[t]).wait()

    @pl.when(first)
    def _():
        in_start(0)
        in_start(1)

    @pl.when(second)
    def _():
        x_copy(0).wait_recv()
        in_start(0)

    load.wait()
    for at in range(0, 2 * width, 128):
        wt[:, at:at + 128] = w[at:at + 128, :].T

    def ag_wait(buf, slot):
        def both(off):
            ag_copy(buf, slot, off).wait_send()
            ag_copy(buf, slot, off).wait_recv()
        over(n, both)

    def rs_wait():
        def both(off):
            rs_copy(off).wait_send()
            rs_copy(off).wait_recv()
        over(n, both)

    def forward(t, _):
        in_wait(in_recv, t)
        gscr[...] = jnp.dot(
            xbuf[t].reshape(total, width), w[:width, :], preferred_element_type=F32) + bias[...]

        @pl.when(t > 0)
        def _():
            ag_wait(hbuf, t)

        gscr[...] += jnp.dot(
            hbuf[t].reshape(total, width), w[width:, :], preferred_element_type=F32)

        def rows_step(k, _):
            at = pl.ds(pl.multiple_of(k * chunk, chunk), chunk)
            g = gscr[at, :]
            i = jax.nn.sigmoid(g[:, :cell])
            f = jax.nn.sigmoid(g[:, cell:2 * cell])
            m = jnp.tanh(g[:, 2 * cell:3 * cell])
            o = jax.nn.sigmoid(g[:, 3 * cell:])
            c = 3.0 * jnp.tanh((i * m + f * cells[t, at, :]) * (1.0 / 3.0))
            cells[t + 1, at, :] = c
            ebuf[t, at, :] = (o * jnp.tanh(c)).astype(BF)
            kind = gates.dtype
            gates[t, at, :cell] = i.astype(kind)
            gates[t, at, cell:2 * cell] = f.astype(kind)
            gates[t, at, 2 * cell:3 * cell] = m.astype(kind)
            gates[t, at, 3 * cell:] = o.astype(kind)
            return 0

        lax.fori_loop(0, total // chunk, rows_step, 0)
        q = jnp.dot(ebuf[t], p[...], preferred_element_type=F32)
        stage[...] = q.astype(BF).reshape(n, rows, width)
        over(n, lambda off: rs_copy(off).start())
        inbox[me] = stage[me]

        @pl.when(first & (t + 2 < steps))
        def _():
            in_start(t + 2)

        @pl.when(second & (t + 1 < steps))
        def _():
            x_copy(t + 1).wait_recv()
            in_start(t + 1)

        rs_wait()
        h = 3.0 * jnp.tanh(jnp.sum(inbox[...].astype(F32), axis=0) * (1.0 / 3.0))
        hown[t] = h
        hbuf[t + 1, me] = h.astype(BF)
        over(n, lambda off: ag_copy(hbuf, t + 1, off).start())

        @pl.when(first)
        def _():
            x_copy(t).start()

        add = jnp.where(second, 1.0, 0.0)
        out_ref[t] = (h + add * xbuf[t, me].astype(F32)).astype(BF)
        return 0

    lax.fori_loop(0, steps, forward, 0)
    ag_wait(hbuf, steps)

    lax.fori_loop(0, steps, lambda t, _: (in_wait(in_send, t), 0)[1], 0)

    @pl.when(first)
    def _():
        lax.fori_loop(0, steps, lambda t, _: (x_copy(t).wait_send(), 0)[1], 0)

    rown[...] = jnp.zeros((rows, width), F32)
    ucell[...] = jnp.zeros((total, cell), F32)
    dwacc[...] = jnp.zeros(dwacc.shape, F32)
    db_ref[...] = jnp.zeros(db_ref.shape, F32)
    dp_ref[...] = jnp.zeros(dp_ref.shape, F32)

    def dx_finish(t):
        slot = lax.rem(t, 2)

        def both(off):
            dx_copy(slot, off).wait_send()
            dx_copy(slot, off).wait_recv()
        over(n, both)
        dx = jnp.sum(inbox2[slot].astype(F32), axis=0)
        dx_ref[t] = dx

        @pl.when(second)
        def _():
            relay[t] = (dx + cot[t].astype(F32)).astype(BF)
            g_copy(t).start()

    def backward(k, _):
        t = steps - 1 - k
        slot = lax.rem(t, 2)
        up = rown[...] + cot[t].astype(F32)
        rown[...] = up

        @pl.when(first)
        def _():
            g_copy(t).wait_recv()
            rown[...] = rown[...] + gbuf[t].astype(F32)

        ratio = hown[t] * (1.0 / 3.0)
        dqbuf[t, me] = (rown[...] * (1.0 - ratio * ratio)).astype(BF)
        over(n, lambda off: ag_copy(dqbuf, t, off).start())

        @pl.when(k > 0)
        def _():
            dx_finish(t + 1)

        ag_wait(dqbuf, t)
        escr[...] = jnp.dot(
            dqbuf[t].reshape(total, width), pt[...], preferred_element_type=F32)

        def rows_step(j, _):
            at = pl.ds(pl.multiple_of(j * chunk, chunk), chunk)
            de = escr[at, :]
            i = gates[t, at, :cell].astype(F32)
            f = gates[t, at, cell:2 * cell].astype(F32)
            m = gates[t, at, 2 * cell:3 * cell].astype(F32)
            o = gates[t, at, 3 * cell:].astype(F32)
            c = cells[t + 1, at, :]
            tc = jnp.tanh(c)
            cr = c * (1.0 / 3.0)
            dc = (de * o * (1.0 - tc * tc) + ucell[at, :]) * (1.0 - cr * cr)
            ucell[at, :] = dc * f
            for block, value in enumerate((
                dc * m * i * (1.0 - i),
                dc * cells[t, at, :] * f * (1.0 - f),
                dc * i * (1.0 - m * m),
                de * tc * o * (1.0 - o),
            )):
                value = value.astype(BF)
                where = pl.ds(block * cell, cell)
                dabuf[0, at, where] = value
                db_ref[:, where] += jnp.sum(value.astype(F32), axis=0, keepdims=True)
            return 0

        lax.fori_loop(0, total // chunk, rows_step, 0)
        r = jnp.dot(dabuf[0], wt[:, width:], preferred_element_type=F32)
        stage[...] = r.astype(BF).reshape(n, rows, width)
        over(n, lambda off: rs_copy(off).start())
        inbox[me] = stage[me]
        dx = jnp.dot(dabuf[0], wt[:, :width], preferred_element_type=F32)
        stage2[slot] = dx.astype(BF).reshape(n, rows, width)
        over(n, lambda off: dx_copy(slot, off).start())
        inbox2[slot, me] = stage2[slot, me]
        for half, buf in enumerate((xbuf, hbuf)):
            dwacc[pl.ds(half * width, width), :] += lax.dot_general(
                buf[t].reshape(total, width), dabuf[0], (((0,), (0,)), ((), ())),
                preferred_element_type=F32)
        dp_ref[...] += lax.dot_general(
            ebuf[t], dqbuf[t].reshape(total, width), (((0,), (0,)), ((), ())),
            preferred_element_type=F32)
        rs_wait()
        rown[...] = jnp.sum(inbox[...].astype(F32), axis=0)
        return 0

    lax.fori_loop(0, steps, backward, 0)
    dx_finish(0)

    @pl.when(second)
    def _():
        lax.fori_loop(0, steps, lambda t, _: (g_copy(t).wait_send(), 0)[1], 0)

    def dw_copy(off):
        return pltpu.make_async_copy(
            dabuf.at[off % 2, pl.ds(0, each)], dw_out[off], st_sem.at[off % 2])

    for off in range(n):
        if off > 1:
            dw_copy(off - 2).wait()
        at = pl.multiple_of(lax.rem(place + off, n) * each, each)
        dabuf[off % 2, :each, :] = dwacc[pl.ds(at, each), :].astype(BF)
        dw_copy(off).start()
    for off in range(n - 2, n):
        dw_copy(off).wait()


def lstm_call(n, x, weights, bias, p, pt, cot, chunk=16):
    steps, rows, width = x.shape
    cell = p.shape[0]
    total = n * rows
    sds = jax.ShapeDtypeStruct
    vm = pl.BlockSpec(memory_space=pltpu.VMEM)
    hb = pl.BlockSpec(memory_space=pl.ANY)
    keep = F32 if n <= 8 else BF
    V = pltpu.VMEM
    dma = pltpu.SemaphoreType.DMA
    return pl.pallas_call(
        functools.partial(lstm_kernel, n, chunk),
        out_shape=(
            sds((steps, rows, width), BF), sds((steps, rows, width), F32),
            sds((1, 4 * cell), F32), sds((cell, width), F32),
            *[sds((2 * width // n, 4 * cell), BF)] * n),
        in_specs=[vm] * 5 + [hb],
        out_specs=[vm] * 4 + [hb] * n,
        scratch_shapes=[
            V((steps, n, rows, width), BF), V((steps + 1, n, rows, width), BF),
            V((steps, n, rows, width), BF), V((steps, total, 4 * cell), keep),
            V((steps + 1, total, cell), F32), V((steps, total, cell), BF),
            V((steps, rows, width), F32), V((total, 4 * cell), F32),
            V((total, cell), F32), V((2, total, 4 * cell), BF), V((total, cell), F32),
            V((2 * width, 4 * cell), F32), V((2 * width, 4 * cell), BF),
            V((4 * cell, 2 * width), BF),
            V((n, rows, width), BF), V((n, rows, width), BF),
            V((2, n, rows, width), BF), V((2, n, rows, width), BF),
            V((steps, rows, width), BF), V((steps, rows, width), BF), V((rows, width), F32),
            dma((steps,)), dma((steps,)), dma((n,)), dma((n,)), dma((n,)), dma((n,)), dma((n,)), dma((n,)), dma((2, n)), dma((2, n)),
            dma((steps,)), dma((steps,)), dma((steps,)), dma((steps,)), dma((2,)), dma,
        ],
        compiler_params=pltpu.CompilerParams(
            collective_id=0, has_side_effects=True, vmem_limit_bytes=60 * 1024 * 1024),
        cost_estimate=pl.CostEstimate(
            flops=300_000_000_000, bytes_accessed=64 * 1024 * 1024, transcendentals=0),
        name="relay_lstm",
    )(x, bias, p, pt, cot, weights)


def split_cells(weight, n):
    rows, gates = weight.shape
    cell = gates // (4 * n)
    wing = n // 2

    def body(src, keep, give):
        pipe = lax.axis_index("pipe")
        for k in range(wing):
            for dst, side in ((keep, pipe), (give, 1 - pipe)):
                at = pl.multiple_of((side * wing + k) * cell, cell)
                dst[k] = src[:, pl.ds(at, cell)].astype(BF)

    return pl.pallas_call(
        body,
        grid=(4,),
        out_shape=[jax.ShapeDtypeStruct((wing, rows, 4 * cell), BF)] * 2,
        in_specs=[pl.BlockSpec((rows, n * cell), lambda b: (0, b))],
        out_specs=[pl.BlockSpec((wing, rows, cell), lambda b: (0, 0, b))] * 2,
        cost_estimate=pl.CostEstimate(
            flops=0, bytes_accessed=6 * rows * gates, transcendentals=0
        ),
        name="split_cells",
    )(weight)


def sort_blocks(blocks):
    n = len(blocks)
    wing = n // 2

    def body(*refs):
        src, (keep, give, sems) = refs[:n], refs[n:]
        pipe = lax.axis_index("pipe")
        for off in range(n):
            place = lax.rem(lax.axis_index("dp") + (n - off), n)
            stays = lax.div(place, wing) == pipe

            @pl.when(stays)
            def _():
                pltpu.make_async_copy(
                    src[off], keep.at[lax.rem(place, wing)], sems.at[off]
                ).start()

            @pl.when(jnp.logical_not(stays))
            def _():
                pltpu.make_async_copy(
                    src[off], give.at[lax.rem(place, wing)], sems.at[off]
                ).start()

        for off in range(n):
            pltpu.make_async_copy(src[off], keep.at[0], sems.at[off]).wait()

    return pl.pallas_call(
        body,
        out_shape=[jax.ShapeDtypeStruct((wing, *blocks[0].shape), BF)] * 2,
        in_specs=[pl.BlockSpec(memory_space=pl.ANY)] * n,
        out_specs=[pl.BlockSpec(memory_space=pl.ANY)] * 2,
        scratch_shapes=[pltpu.SemaphoreType.DMA((n,))],
        cost_estimate=pl.CostEstimate(
            flops=0, bytes_accessed=4 * n * blocks[0].size, transcendentals=0
        ),
        name="sort_blocks",
    )(*blocks)


def join_cells(keep, came):
    wing, rows, gates = keep.shape
    cell = gates // 4
    n = 2 * wing

    def body(keep, came, dst):
        pipe = lax.axis_index("pipe")
        for k in range(wing):
            for src, side in ((keep, pipe), (came, 1 - pipe)):
                at = pl.multiple_of((side * wing + k) * cell, cell)
                dst[:, pl.ds(at, cell)] = src[k].astype(F32)

    return pl.pallas_call(
        body,
        grid=(4,),
        out_shape=jax.ShapeDtypeStruct((rows, n * gates), F32),
        in_specs=[pl.BlockSpec((wing, rows, cell), lambda b: (0, 0, b))] * 2,
        out_specs=pl.BlockSpec((rows, n * cell), lambda b: (0, b)),
        cost_estimate=pl.CostEstimate(
            flops=0, bytes_accessed=6 * n * rows * gates, transcendentals=0
        ),
        name="join_cells",
    )(keep, came)


def swap_pipes(value):
    return lax.ppermute(value, "pipe", [(0, 1), (1, 0)])


def exchange(blocks):
    n = len(blocks)
    return [blocks[0]] + [
        lax.ppermute(blocks[off], "dp", [(i, (i + off) % n) for i in range(n)])
        for off in range(1, n)
    ]


def rank_pairs(n, off, layers=(0, 1)):
    wing = n // 2
    pairs = []
    for layer in layers:
        for j in range(n):
            rank = (j + off) % n
            pairs.append((layer * n + j, rank // wing * n + layer * wing + rank % wing))
    return pairs


def to_ranks(value, off):
    return lax.ppermute(value, ("pipe", "dp"), rank_pairs(lax.axis_size("dp"), off))


def from_ranks(value, off, layers=(0, 1)):
    pairs = rank_pairs(lax.axis_size("dp"), -off, layers)
    return lax.ppermute(value, ("pipe", "dp"), [(there, here) for here, there in pairs])


def conv_forward(ids, table_low, conv_low, valid_place):
    return jax.nn.logsumexp(conv_response(ids, table_low, conv_low, valid_place)[1], axis=1)


def own_half(value, blocks):
    sub = value.shape[-1] // (2 * blocks)
    split = value.reshape(*value.shape[:-1], blocks, 2, sub)
    mine = lax.dynamic_index_in_dim(split, lax.axis_index("pipe"), split.ndim - 2, keepdims=False)
    return mine.reshape(*value.shape[:-1], blocks * sub)


def both_halves(value, blocks):
    tokens, half = value.shape
    pair = lax.all_gather(value, "pipe").reshape(2, tokens, blocks, half // blocks)
    return jnp.transpose(pair, (1, 2, 0, 3)).reshape(tokens, 2 * half)


def conv_backward(ids, table_low, conv_low, masks, grad_before):
    weight_mask, valid_place = masks
    windows, response = conv_response(ids, table_low, conv_low, valid_place)
    share = jax.nn.softmax(response, axis=1)
    grad_response = (grad_before[:, None, :] * share).astype(BF)
    grad_conv = jnp.einsum("bpk,bpf->kf", windows, grad_response, preferred_element_type=F32)
    grad_windows = jnp.einsum("bpf,kf->bpk", grad_response, conv_low, preferred_element_type=F32)
    grad_embedded = jnp.zeros((ids.shape[0], CHARS + KMAX - 1, CDIM), F32)
    for offset in range(KMAX):
        grad_embedded = grad_embedded + jnp.pad(
            grad_windows[:, :, offset * CDIM : (offset + 1) * CDIM],
            ((0, 0), (offset, KMAX - 1 - offset), (0, 0)),
        )
    grad_embedded = grad_embedded[:, :CHARS].astype(BF)
    one_hot = (ids[:, :, None] == jnp.arange(CVOCAB, dtype=jnp.int32)).astype(BF)
    grad_table = jnp.einsum("bpv,bpc->vc", one_hot, grad_embedded, preferred_element_type=F32)
    return grad_conv * weight_mask, grad_table


def local(
    chars,
    lengths,
    char_emb,
    conv_weight,
    conv_bias,
    highway_weight,
    highway_bias,
    proj_weight,
    proj_bias,
    gate_weight,
    gate_bias,
    cell_proj,
    cotangent,
):
    n = lax.axis_size("dp")
    pipe = lax.axis_index("pipe")
    direction = lax.axis_index("dir")
    me = lax.axis_index("dp")
    everyone = lax.axis_size(ALL)
    holders = lax.axis_size(("dir", "dp"))
    seqs, steps, char_count = chars.shape
    group = seqs // lax.axis_size("dir")
    quarter = group // 2
    group_tokens = group * steps
    tokens = quarter * steps
    width = cell_proj.shape[3]
    cell = cell_proj.shape[2]
    blocks = holders // 2
    sub = FILTERS // holders
    half = FILTERS // 2
    filter_index = (
        (2 * jnp.arange(blocks, dtype=jnp.int32) + pipe)[:, None] * sub
        + jnp.arange(sub, dtype=jnp.int32)[None, :]
    ).reshape(half)
    masks = conv_masks(filter_index)

    proj_rows = proj_weight.shape[0]
    pieces = width // sub
    proj_blocks = jnp.transpose(proj_weight.reshape(proj_rows, pieces, sub), (1, 0, 2))
    proj_blocks = proj_blocks.reshape(2, pieces * proj_rows // 2, sub)
    mine = lax.dynamic_slice_in_dim(highway_weight, pipe * sub, sub, 2)
    gathered = lax.all_gather(
        jnp.concatenate([mine, proj_blocks], axis=1).astype(BF), ("dir", "dp"), axis=2, tiled=True
    )
    conv_full = lax.all_to_all(
        jnp.broadcast_to(conv_weight.astype(BF), (holders, KMAX * CDIM, sub)), ("dir", "dp"), 0, 0
    ).reshape(blocks, 2, KMAX * CDIM, sub)
    conv_low = lax.dynamic_index_in_dim(conv_full, pipe, 1, keepdims=False)
    conv_low = jnp.transpose(conv_low, (1, 0, 2)).reshape(KMAX * CDIM, half)
    conv_low = conv_low * masks[0].astype(BF)
    conv_bias_own = own_half(conv_bias, blocks)
    highway_bias_own = own_half(highway_bias.reshape(2, 2, FILTERS), blocks).reshape(2, FILTERS)

    def order_matrix(sizes):
        place = jnp.arange(steps, dtype=jnp.int32)[None, :]
        live = place < sizes[:, None]
        order = jnp.where(live & (direction == 1), sizes[:, None] - 1 - place, place)
        return ((order[:, :, None] == place[:, None, :]) & live[:, :, None]).astype(BF)

    own_order = order_matrix(lengths)
    cot = jnp.einsum("rts,rsd->trd", own_order, cotangent[0, 0], preferred_element_type=BF)

    ids = lax.dynamic_slice_in_dim(chars, direction * group, group, 0).reshape(
        group_tokens, char_count
    )
    table_low = char_emb.astype(BF)
    pooled = conv_forward(ids, table_low, conv_low, masks[1])
    features = jax.nn.silu(pooled + conv_bias_own)
    features_low = both_halves(features.astype(BF), blocks)
    bias_own = lax.dynamic_index_in_dim(
        gate_bias[0, 0].reshape(4, n, cell), me, 1, keepdims=False
    ).reshape(1, 4 * cell)
    bias_own = to_ranks(bias_own, 0)
    moved = to_ranks(
        jnp.concatenate([cell_proj[0, 0].astype(BF), cot.reshape(steps * seqs, width)]), 0
    )
    gate_kept, gate_given = split_cells(gate_weight[0, 0], n)
    gate_came = swap_pipes(gate_given)
    gate_low = jnp.concatenate(
        [
            jnp.where(pipe == 0, gate_kept, gate_came),
            jnp.where(pipe == 0, gate_came, gate_kept),
        ]
    )
    gate_low, gathered, features_low, bias_own, moved = lax.optimization_barrier(
        (gate_low, gathered, features_low, bias_own, moved)
    )
    cell_low = moved[:cell]
    cot = moved[cell:].reshape(steps, seqs, width)
    gate_own = lax.all_to_all(gate_low, "dp", 0, 0).reshape(2 * width, 4 * cell)
    highway_half = gathered[:, :FILTERS]
    proj_full = gathered[:, FILTERS:].reshape(pieces, proj_rows, holders, sub)
    proj_full = jnp.transpose(proj_full, (2, 1, 0, 3)).reshape(FILTERS, width)

    kept = [features]
    kept_low = [features_low]
    mixed = []
    for layer in range(2):
        pre = (
            jnp.dot(kept_low[layer], highway_half[layer], preferred_element_type=F32)
            + highway_bias_own[layer]
        )
        mixed.append(pre)
        gate = jax.nn.sigmoid(pre[:, half:])
        features = gate * features + (1.0 - gate) * jax.nn.silu(pre[:, :half])
        kept.append(features)
        kept_low.append(both_halves(features.astype(BF), blocks))
    own_last = lax.dynamic_slice_in_dim(kept_low[2], pipe * tokens, tokens, 0)
    encoded = jnp.dot(own_last, proj_full, preferred_element_type=F32) + proj_bias
    encoded_own = lax.all_gather(
        encoded.astype(BF).reshape(quarter, steps, width), ("dir", "pipe"), axis=0, tiled=True
    )
    kept_low, encoded_own, gate_own = lax.optimization_barrier((kept_low, encoded_own, gate_own))
    kept_all = [
        lax.all_gather(
            lax.dynamic_slice_in_dim(value, pipe * tokens, tokens, 0),
            ("dir", "dp"),
            axis=0,
            tiled=True,
        )
        for value in kept_low[:2]
    ]
    inputs = jnp.einsum("rts,rsd->trd", own_order, encoded_own, preferred_element_type=BF)
    wing = n // 2
    inputs = lax.ppermute(
        inputs,
        ("pipe", "dp"),
        [(k, wing + k) for k in range(wing)] + [(n + k, n + k) for k in range(wing, n)],
    )

    out_own, dx_own, grad_bias, grad_cell, *grad_gate = lstm_call(
        n, inputs, gate_own, bias_own, cell_low, cell_low.T, cot
    )
    dx_own = from_ranks(dx_own.astype(BF), 0, (1,))
    grad_gate = exchange(grad_gate)
    dx_own, kept_all = lax.optimization_barrier((dx_own, kept_all))

    grad_stored = jnp.einsum(
        "rts,srd->rtd", own_order, dx_own, preferred_element_type=F32
    )
    grad_stored = jnp.where(pipe == 1, grad_stored, 0.0).astype(BF)
    grad_stored = grad_stored.reshape(1, -1, group_tokens, width)
    grad_encoded = lax.all_to_all(
        jnp.concatenate([grad_stored, grad_stored]).reshape(-1, group_tokens, width),
        ("pipe", "dir"),
        0,
        0,
    )
    grad_encoded = jnp.sum(grad_encoded.astype(F32), axis=0).astype(BF)
    own_grads = lax.dynamic_slice_in_dim(grad_encoded, pipe * tokens, tokens, 0)
    encoded_grads = lax.all_gather(own_grads, ("dir", "dp"), axis=0, tiled=True)

    grad_proj_bias = jnp.sum(own_grads.astype(F32), axis=0)
    proj_half = lax.dynamic_index_in_dim(
        proj_full.reshape(blocks, 2, sub, width), pipe, 1, keepdims=False
    ).reshape(half, width)
    grad_features = jnp.einsum("td,fd->tf", grad_encoded, proj_half, preferred_element_type=F32)
    columns = [None, None]
    grad_highway_bias = [None, None]
    for layer in (1, 0):
        nonlinear = mixed[layer][:, :half]
        gate = jax.nn.sigmoid(mixed[layer][:, half:])
        grad_mixed = jnp.concatenate(
            [
                grad_features * (1.0 - gate) * silu_slope(nonlinear),
                grad_features * (kept[layer] - jax.nn.silu(nonlinear)) * gate * (1.0 - gate),
            ],
            axis=1,
        ).astype(BF)
        columns[layer] = grad_mixed
        grad_highway_bias[layer] = jnp.sum(grad_mixed.astype(F32), axis=0)
        partial = jnp.einsum(
            "tg,fg->tf", grad_mixed, highway_half[layer], preferred_element_type=F32
        )
        partial = lax.optimization_barrier(partial).reshape(group_tokens, blocks, 2, sub)
        sent = lax.dynamic_index_in_dim(partial, 1 - pipe, 2, keepdims=False).astype(BF)
        came = lax.ppermute(sent, "pipe", [(0, 1), (1, 0)])
        mine = lax.dynamic_index_in_dim(partial, pipe, 2, keepdims=False)
        grad_features = grad_features * gate + (mine + came.astype(F32)).reshape(
            group_tokens, half
        )
    grad_before = grad_features * silu_slope(pooled + conv_bias_own)
    grad_before, grad_gate[1:5] = lax.optimization_barrier((grad_before, grad_gate[1:5]))
    grad_conv, grad_table = conv_backward(ids, table_low, conv_low, masks, grad_before)

    def spread(value):
        split = value.reshape(*value.shape[:-1], -1, 1, sub)
        shown = jnp.arange(2, dtype=jnp.int32)[:, None] == pipe
        return jnp.where(shown, split, jnp.zeros_like(split)).reshape(*value.shape[:-1], -1)

    cols = FILTERS // everyone
    pair = jnp.stack(columns, axis=1).reshape(2, tokens, 2, 2, blocks, 1, sub)
    sent = lax.dynamic_index_in_dim(pair, 1 - pipe, 0, keepdims=False)
    came = lax.ppermute(sent, "pipe", [(0, 1), (1, 0)])
    mine = lax.dynamic_index_in_dim(pair, pipe, 0, keepdims=False)
    shown = (jnp.arange(2, dtype=jnp.int32) == pipe)[:, None]
    pair = jnp.where(shown, mine, came)
    pair = jnp.transpose(pair, (3, 4, 0, 1, 2, 5)).reshape(holders, tokens, 4 * sub)
    last = jnp.transpose(own_last.reshape(tokens, 2, holders, cols), (2, 0, 1, 3))
    pair = jnp.concatenate([pair, last.reshape(holders, tokens, 2 * cols)], axis=2)
    pair = lax.all_to_all(pair, ("dir", "dp"), 0, 0).reshape(holders * tokens, -1)
    grad_conv, pair, grad_gate = lax.optimization_barrier((grad_conv, pair, grad_gate))
    gate_kept, gate_given = sort_blocks(grad_gate)
    gate_came = swap_pipes(gate_given)
    grad_gate = join_cells(gate_kept, gate_came)
    small = (
        grad_table,
        spread(jnp.sum(grad_before, axis=0)),
        spread(jnp.stack(grad_highway_bias)),
        grad_proj_bias,
    )
    flat = jnp.concatenate([value.reshape(-1) for value in small])
    share = -(-flat.shape[0] // (everyone * 128)) * 128
    flat = jnp.pad(flat, (0, share * everyone - flat.shape[0])).reshape(everyone, share)
    rank = pipe * wing + lax.rem(me, wing)
    mine = jnp.arange(n, dtype=jnp.int32)[None, :, None] == rank
    bias_parts = jnp.where(mine, grad_bias.reshape(4, 1, cell), 0.0).reshape(1, n, 4 * cell)
    layer = lax.div(me, wing) * lax.axis_size("dir") + direction
    mine = jnp.arange(everyone // n, dtype=jnp.int32) == layer
    bias_parts = jnp.where(mine[:, None, None], bias_parts, 0.0).reshape(everyone, 4 * cell)
    packed = jnp.concatenate(
        [
            jnp.transpose(
                spread(grad_conv).reshape(KMAX * CDIM, everyone, cols), (1, 0, 2)
            ).reshape(everyone, KMAX * CDIM * cols),
            flat,
            bias_parts,
        ],
        axis=1,
    ).astype(BF)
    summed = jnp.sum(lax.all_to_all(packed, ALL, 0, 0).astype(F32), axis=0)
    out_own = from_ranks(out_own, 0)
    grad_cell = from_ranks(grad_cell.astype(BF), 0)
    summed, out_own, grad_cell = lax.optimization_barrier((summed, out_own, grad_cell))
    activations = jnp.einsum("rts,srd->rtd", own_order, out_own, preferred_element_type=BF)
    grad_cell = grad_cell.astype(F32)
    grad_conv = summed[: KMAX * CDIM * cols].reshape(KMAX * CDIM, cols)
    grad_bias = summed[KMAX * CDIM * cols + share :]
    last = pair[:, 4 * sub :].reshape(holders * tokens, 2, cols)
    pair = pair[:, : 4 * sub].reshape(holders * tokens, 2, 2, sub)

    def partial_sums(owner):
        return [
            jnp.einsum(
                "tf,tg->fg",
                kept_all[layer],
                lax.dynamic_index_in_dim(pair[:, layer], owner, 1, keepdims=False),
                preferred_element_type=F32,
            )
            for layer in range(2)
        ] + [
            jnp.einsum(
                "tf,td->fd",
                lax.dynamic_index_in_dim(last, owner, 1, keepdims=False),
                encoded_grads,
                preferred_element_type=F32,
            )
        ]

    sent = jnp.concatenate(
        [value.astype(BF).reshape(-1, sub) for value in partial_sums(1 - pipe)]
    )
    came = lax.ppermute(sent, "pipe", [(0, 1), (1, 0)]).astype(F32)
    mine = partial_sums(pipe)
    grad_highway = jnp.stack(mine[:2]) + came[: 2 * FILTERS].reshape(2, FILTERS, sub)
    grad_proj = mine[2] + came[2 * FILTERS :].reshape(cols, width)
    shared = lax.all_to_all(
        jnp.broadcast_to(summed[KMAX * CDIM * cols :][:share], (everyone, share)), ALL, 0, 0
    ).reshape(-1)
    small_sums = []
    start = 0
    for value in small:
        small_sums.append(shared[start : start + value.size].reshape(value.shape))
        start += value.size
    return (
        activations[None, None],
        small_sums[0],
        grad_conv,
        small_sums[1],
        grad_highway,
        small_sums[2],
        grad_proj,
        small_sums[3],
        grad_gate[None, None],
        grad_bias[None, None],
        grad_cell[None, None],
    )


def solution(mesh):
    return jax.shard_map(
        local,
        mesh=mesh,
        in_specs=(
            P("dp", None, None),
            P("dp"),
            P(),
            P(None, ("dir", "dp")),
            P(),
            P(None, None, ("dir", "dp")),
            P(),
            P(("dir", "dp"), None),
            P(),
            P("pipe", "dir", "dp", None),
            P("pipe", "dir", None),
            P("pipe", "dir", "dp", None),
            P("pipe", "dir", "dp", None, None),
        ),
        out_specs=(
            P("pipe", "dir", "dp", None, None),
            P(),
            P(None, ("pipe", "dir", "dp")),
            P(),
            P(None, None, ("pipe", "dir", "dp")),
            P(),
            P(("pipe", "dir", "dp"), None),
            P(),
            P("pipe", "dir", "dp", None),
            P("pipe", "dir", "dp"),
            P("pipe", "dir", "dp", None),
        ),
        check_vma=False,
    )
```

```python
import functools
import math

import jax
import jax.numpy as jnp
from jax import lax
from jax.experimental import pallas as pl
from jax.experimental.pallas import tpu as pltpu
from jax.sharding import PartitionSpec as P

FILTERS = 2048
CDIM = 16
CVOCAB = 262
CHARS = 50
KMAX = 7
CLIP_LIMIT = 3.0
MASKED_FILL = -1000000000.0
MESH = pl.DeviceIdType.MESH
BF = jnp.bfloat16
F32 = jnp.float32
ALL = ("pipe", "dir", "dp")


def silu_slope(value):
    sig = jax.nn.sigmoid(value)
    return sig * (1.0 + value * (1.0 - sig))


def conv_masks(filter_index):
    filter_width = jnp.ones(filter_index.shape, jnp.int32)
    for doubling in range(6):
        filter_width = filter_width + (filter_index >= FILTERS // 64 * (1 << doubling)).astype(
            jnp.int32
        )
    offset_rows = jnp.arange(KMAX * CDIM, dtype=jnp.int32) // CDIM
    weight_mask = (offset_rows[:, None] < filter_width[None, :]).astype(jnp.float32)
    valid_place = jnp.arange(CHARS, dtype=jnp.int32)[:, None] <= CHARS - filter_width[None, :]
    return (weight_mask, valid_place)


def make_windows(embedded):
    padded = jnp.pad(embedded, ((0, 0), (0, KMAX - 1), (0, 0)))
    return jnp.concatenate(
        [padded[:, offset : offset + CHARS, :] for offset in range(KMAX)], axis=2
    )


def conv_response(ids_block, table_low, conv_low, valid_place):
    embedded = jnp.take(table_low, ids_block, axis=0)
    windows = make_windows(embedded)
    response = jnp.einsum("bpk,kf->bpf", windows, conv_low, preferred_element_type=jnp.float32)
    return (windows, jnp.where(valid_place[None], response, MASKED_FILL))


def over(count, step):
    if count <= 9:
        for off in range(count - 1, 0, -1):
            step(off)
    else:
        lax.fori_loop(1, count, lambda off, _: (step(off), 0)[1], 0)


def lstm_kernel(n, chunk, x_own, bias, p, pt, cot, w_in, *refs):
    out_ref, dx_ref, db_ref, dp_ref = refs[:4]
    dw_out = refs[4:n + 4]
    (xbuf, hbuf, dqbuf, gates, cells, ebuf, hown, gscr, escr, dabuf, ucell, dwacc, w, wt,
     stage, inbox, stage2, inbox2, relay, gbuf, rown,
     in_send, in_recv, ag_send, ag_recv, dq_send, dq_recv, rs_send, rs_recv,
     dx_send, dx_recv, x_send, x_recv, g_send, g_recv, st_sem, w_sem) = refs[n + 4:]
    steps, _, rows, width = xbuf.shape
    total = n * rows
    cell = cells.shape[2]
    pipe = lax.axis_index("pipe")
    direction = lax.axis_index("dir")
    place = lax.axis_index("dp")
    wing = n // 2
    first = place >= wing
    second = place < wing
    me = pipe * wing + lax.rem(place, wing)
    base = place - lax.rem(place, wing)
    partner = (pipe, direction, lax.rem(place + wing, n))

    def peer(off):
        if n & (n - 1):
            return lax.rem(me + off, n)
        return me ^ off

    def at_peer(off):
        rank = peer(off)
        return (lax.div(rank, wing), direction, base + lax.rem(rank, wing))

    barrier = pltpu.get_barrier_semaphore()
    over(n, lambda off: pl.semaphore_signal(
        barrier, inc=1, device_id=at_peer(off), device_id_type=MESH))
    pl.semaphore_signal(barrier, inc=1, device_id=partner, device_id_type=MESH)

    each = 2 * width // n
    load = pltpu.make_async_copy(w_in, w, w_sem)
    load.start()

    @pl.when(first)
    def _():
        for t in range(steps):
            xbuf[t, me] = x_own[t]

    hbuf[0] = jnp.zeros((n, rows, width), BF)
    cells[0] = jnp.zeros((total, cell), F32)
    pl.semaphore_wait(barrier, n)

    def ag_copy(buf, slot, off):
        out, into = (ag_send, ag_recv) if buf is hbuf else (dq_send, dq_recv)
        return pltpu.make_async_remote_copy(
            src_ref=buf.at[slot, me], dst_ref=buf.at[slot, me],
            send_sem=out.at[off], recv_sem=into.at[off],
            device_id=at_peer(off), device_id_type=MESH)

    def rs_copy(off):
        return pltpu.make_async_remote_copy(
            src_ref=stage.at[peer(off)], dst_ref=inbox.at[me],
            send_sem=rs_send.at[off], recv_sem=rs_recv.at[off],
            device_id=at_peer(off), device_id_type=MESH)

    def dx_copy(slot, off):
        return pltpu.make_async_remote_copy(
            src_ref=stage2.at[slot, peer(off)], dst_ref=inbox2.at[slot, me],
            send_sem=dx_send.at[slot, off], recv_sem=dx_recv.at[slot, off],
            device_id=at_peer(off), device_id_type=MESH)

    def x_copy(t):
        return pltpu.make_async_remote_copy(
            src_ref=hbuf.at[t + 1, me], dst_ref=xbuf.at[t, me],
            send_sem=x_send.at[t], recv_sem=x_recv.at[t],
            device_id=partner, device_id_type=MESH)

    def g_copy(t):
        return pltpu.make_async_remote_copy(
            src_ref=relay.at[t], dst_ref=gbuf.at[t],
            send_sem=g_send.at[t], recv_sem=g_recv.at[t],
            device_id=partner, device_id_type=MESH)

    def in_start(t):
        over(n, lambda off: pltpu.make_async_remote_copy(
            src_ref=xbuf.at[t, me], dst_ref=xbuf.at[t, me],
            send_sem=in_send.at[t], recv_sem=in_recv.at[t],
            device_id=at_peer(off), device_id_type=MESH).start())

    def in_wait(sem, t):
        blocks = xbuf.at[t, pl.ds(0, n - 1)]
        pltpu.make_async_copy(blocks, blocks, sem.at[t]).wait()

    @pl.when(first)
    def _():
        in_start(0)
        in_start(1)

    @pl.when(second)
    def _():
        x_copy(0).wait_recv()
        in_start(0)

    load.wait()
    for at in range(0, 2 * width, 128):
        wt[:, at:at + 128] = w[at:at + 128, :].T

    def ag_wait(buf, slot):
        def both(off):
            ag_copy(buf, slot, off).wait_send()
            ag_copy(buf, slot, off).wait_recv()
        over(n, both)

    def rs_wait():
        def both(off):
            rs_copy(off).wait_send()
            rs_copy(off).wait_recv()
        over(n, both)

    def forward(t, _):
        in_wait(in_recv, t)
        gscr[...] = jnp.dot(
            xbuf[t].reshape(total, width), w[:width, :], preferred_element_type=F32) + bias[...]

        @pl.when(t > 0)
        def _():
            ag_wait(hbuf, t)

        gscr[...] += jnp.dot(
            hbuf[t].reshape(total, width), w[width:, :], preferred_element_type=F32)

        def rows_step(k, _):
            at = pl.ds(pl.multiple_of(k * chunk, chunk), chunk)
            g = gscr[at, :]
            i = jax.nn.sigmoid(g[:, :cell])
            f = jax.nn.sigmoid(g[:, cell:2 * cell])
            m = jnp.tanh(g[:, 2 * cell:3 * cell])
            o = jax.nn.sigmoid(g[:, 3 * cell:])
            c = 3.0 * jnp.tanh((i * m + f * cells[t, at, :]) * (1.0 / 3.0))
            cells[t + 1, at, :] = c
            ebuf[t, at, :] = (o * jnp.tanh(c)).astype(BF)
            kind = gates.dtype
            gates[t, at, :cell] = i.astype(kind)
            gates[t, at, cell:2 * cell] = f.astype(kind)
            gates[t, at, 2 * cell:3 * cell] = m.astype(kind)
            gates[t, at, 3 * cell:] = o.astype(kind)
            return 0

        lax.fori_loop(0, total // chunk, rows_step, 0)
        q = jnp.dot(ebuf[t], p[...], preferred_element_type=F32)
        stage[...] = q.astype(BF).reshape(n, rows, width)
        over(n, lambda off: rs_copy(off).start())
        inbox[me] = stage[me]

        @pl.when(first & (t + 2 < steps))
        def _():
            in_start(t + 2)

        @pl.when(second & (t + 1 < steps))
        def _():
            x_copy(t + 1).wait_recv()
            in_start(t + 1)

        rs_wait()
        h = 3.0 * jnp.tanh(jnp.sum(inbox[...].astype(F32), axis=0) * (1.0 / 3.0))
        hown[t] = h
        hbuf[t + 1, me] = h.astype(BF)
        over(n, lambda off: ag_copy(hbuf, t + 1, off).start())

        @pl.when(first)
        def _():
            x_copy(t).start()

        add = jnp.where(second, 1.0, 0.0)
        out_ref[t] = (h + add * xbuf[t, me].astype(F32)).astype(BF)
        return 0

    lax.fori_loop(0, steps, forward, 0)
    ag_wait(hbuf, steps)

    lax.fori_loop(0, steps, lambda t, _: (in_wait(in_send, t), 0)[1], 0)

    @pl.when(first)
    def _():
        lax.fori_loop(0, steps, lambda t, _: (x_copy(t).wait_send(), 0)[1], 0)

    rown[...] = jnp.zeros((rows, width), F32)
    ucell[...] = jnp.zeros((total, cell), F32)
    dwacc[...] = jnp.zeros(dwacc.shape, F32)
    db_ref[...] = jnp.zeros(db_ref.shape, F32)
    dp_ref[...] = jnp.zeros(dp_ref.shape, F32)

    def dx_finish(t):
        slot = lax.rem(t, 2)

        def both(off):
            dx_copy(slot, off).wait_send()
            dx_copy(slot, off).wait_recv()
        over(n, both)
        dx = jnp.sum(inbox2[slot].astype(F32), axis=0)
        dx_ref[t] = dx

        @pl.when(second)
        def _():
            relay[t] = (dx + cot[t].astype(F32)).astype(BF)
            g_copy(t).start()

    def backward(k, _):
        t = steps - 1 - k
        slot = lax.rem(t, 2)
        up = rown[...] + cot[t].astype(F32)
        rown[...] = up

        @pl.when(first)
        def _():
            g_copy(t).wait_recv()
            rown[...] = rown[...] + gbuf[t].astype(F32)

        ratio = hown[t] * (1.0 / 3.0)
        dqbuf[t, me] = (rown[...] * (1.0 - ratio * ratio)).astype(BF)
        over(n, lambda off: ag_copy(dqbuf, t, off).start())

        @pl.when(k > 0)
        def _():
            dx_finish(t + 1)

        ag_wait(dqbuf, t)
        escr[...] = jnp.dot(
            dqbuf[t].reshape(total, width), pt[...], preferred_element_type=F32)

        def rows_step(j, _):
            at = pl.ds(pl.multiple_of(j * chunk, chunk), chunk)
            de = escr[at, :]
            i = gates[t, at, :cell].astype(F32)
            f = gates[t, at, cell:2 * cell].astype(F32)
            m = gates[t, at, 2 * cell:3 * cell].astype(F32)
            o = gates[t, at, 3 * cell:].astype(F32)
            c = cells[t + 1, at, :]
            tc = jnp.tanh(c)
            cr = c * (1.0 / 3.0)
            dc = (de * o * (1.0 - tc * tc) + ucell[at, :]) * (1.0 - cr * cr)
            ucell[at, :] = dc * f
            for block, value in enumerate((
                dc * m * i * (1.0 - i),
                dc * cells[t, at, :] * f * (1.0 - f),
                dc * i * (1.0 - m * m),
                de * tc * o * (1.0 - o),
            )):
                value = value.astype(BF)
                where = pl.ds(block * cell, cell)
                dabuf[0, at, where] = value
                db_ref[:, where] += jnp.sum(value.astype(F32), axis=0, keepdims=True)
            return 0

        lax.fori_loop(0, total // chunk, rows_step, 0)
        r = jnp.dot(dabuf[0], wt[:, width:], preferred_element_type=F32)
        stage[...] = r.astype(BF).reshape(n, rows, width)
        over(n, lambda off: rs_copy(off).start())
        inbox[me] = stage[me]
        dx = jnp.dot(dabuf[0], wt[:, :width], preferred_element_type=F32)
        stage2[slot] = dx.astype(BF).reshape(n, rows, width)
        over(n, lambda off: dx_copy(slot, off).start())
        inbox2[slot, me] = stage2[slot, me]
        for half, buf in enumerate((xbuf, hbuf)):
            dwacc[pl.ds(half * width, width), :] += lax.dot_general(
                buf[t].reshape(total, width), dabuf[0], (((0,), (0,)), ((), ())),
                preferred_element_type=F32)
        dp_ref[...] += lax.dot_general(
            ebuf[t], dqbuf[t].reshape(total, width), (((0,), (0,)), ((), ())),
            preferred_element_type=F32)
        rs_wait()
        rown[...] = jnp.sum(inbox[...].astype(F32), axis=0)
        return 0

    lax.fori_loop(0, steps, backward, 0)
    dx_finish(0)

    @pl.when(second)
    def _():
        lax.fori_loop(0, steps, lambda t, _: (g_copy(t).wait_send(), 0)[1], 0)

    def dw_copy(off):
        return pltpu.make_async_copy(
            dabuf.at[off % 2, pl.ds(0, each)], dw_out[off], st_sem.at[off % 2])

    for off in range(n):
        if off > 1:
            dw_copy(off - 2).wait()
        at = pl.multiple_of(lax.rem(place + off, n) * each, each)
        dabuf[off % 2, :each, :] = dwacc[pl.ds(at, each), :].astype(BF)
        dw_copy(off).start()
    for off in range(n - 2, n):
        dw_copy(off).wait()


def lstm_call(n, x, weights, bias, p, pt, cot, chunk=16):
    steps, rows, width = x.shape
    cell = p.shape[0]
    total = n * rows
    sds = jax.ShapeDtypeStruct
    vm = pl.BlockSpec(memory_space=pltpu.VMEM)
    hb = pl.BlockSpec(memory_space=pl.ANY)
    keep = F32 if n <= 8 else BF
    V = pltpu.VMEM
    dma = pltpu.SemaphoreType.DMA
    return pl.pallas_call(
        functools.partial(lstm_kernel, n, chunk),
        out_shape=(
            sds((steps, rows, width), BF), sds((steps, rows, width), F32),
            sds((1, 4 * cell), F32), sds((cell, width), F32),
            *[sds((2 * width // n, 4 * cell), BF)] * n),
        in_specs=[vm] * 5 + [hb],
        out_specs=[vm] * 4 + [hb] * n,
        scratch_shapes=[
            V((steps, n, rows, width), BF), V((steps + 1, n, rows, width), BF),
            V((steps, n, rows, width), BF), V((steps, total, 4 * cell), keep),
            V((steps + 1, total, cell), F32), V((steps, total, cell), BF),
            V((steps, rows, width), F32), V((total, 4 * cell), F32),
            V((total, cell), F32), V((2, total, 4 * cell), BF), V((total, cell), F32),
            V((2 * width, 4 * cell), F32), V((2 * width, 4 * cell), BF),
            V((4 * cell, 2 * width), BF),
            V((n, rows, width), BF), V((n, rows, width), BF),
            V((2, n, rows, width), BF), V((2, n, rows, width), BF),
            V((steps, rows, width), BF), V((steps, rows, width), BF), V((rows, width), F32),
            dma((steps,)), dma((steps,)), dma((n,)), dma((n,)), dma((n,)), dma((n,)), dma((n,)), dma((n,)), dma((2, n)), dma((2, n)),
            dma((steps,)), dma((steps,)), dma((steps,)), dma((steps,)), dma((2,)), dma,
        ],
        compiler_params=pltpu.CompilerParams(
            collective_id=0, has_side_effects=True, vmem_limit_bytes=60 * 1024 * 1024),
        cost_estimate=pl.CostEstimate(
            flops=300_000_000_000, bytes_accessed=64 * 1024 * 1024, transcendentals=0),
        name="relay_lstm",
    )(x, bias, p, pt, cot, weights)


def split_cells(weight, n):
    rows, gates = weight.shape
    cell = gates // (4 * n)
    wing = n // 2

    def body(src, keep, give):
        pipe = lax.axis_index("pipe")
        for k in range(wing):
            for dst, side in ((keep, pipe), (give, 1 - pipe)):
                at = pl.multiple_of((side * wing + k) * cell, cell)
                dst[k] = src[:, pl.ds(at, cell)].astype(BF)

    return pl.pallas_call(
        body,
        grid=(4,),
        out_shape=[jax.ShapeDtypeStruct((wing, rows, 4 * cell), BF)] * 2,
        in_specs=[pl.BlockSpec((rows, n * cell), lambda b: (0, b))],
        out_specs=[pl.BlockSpec((wing, rows, cell), lambda b: (0, 0, b))] * 2,
        cost_estimate=pl.CostEstimate(
            flops=0, bytes_accessed=6 * rows * gates, transcendentals=0
        ),
        name="split_cells",
    )(weight)


def sort_blocks(blocks):
    n = len(blocks)
    wing = n // 2

    rows, gates = blocks[0].shape
    cell = gates // 4

    def body(*refs):
        src, (keep, give) = refs[:n], refs[n:]
        pipe = lax.axis_index("pipe")
        for off in range(n):
            place = lax.rem(lax.axis_index("dp") + (n - off), n)
            stays = lax.div(place, wing) == pipe

            @pl.when(stays)
            def _():
                keep[lax.rem(place, wing)] = src[off][...]

            @pl.when(jnp.logical_not(stays))
            def _():
                give[lax.rem(place, wing)] = src[off][...]

    return pl.pallas_call(
        body,
        grid=(4,),
        out_shape=[jax.ShapeDtypeStruct((wing, rows, gates), BF)] * 2,
        in_specs=[pl.BlockSpec((rows, cell), lambda b: (0, b))] * n,
        out_specs=[pl.BlockSpec((wing, rows, cell), lambda b: (0, 0, b))] * 2,
        cost_estimate=pl.CostEstimate(
            flops=0, bytes_accessed=4 * n * blocks[0].size, transcendentals=0
        ),
        name="sort_blocks",
    )(*blocks)


def join_cells(keep, came):
    wing, rows, gates = keep.shape
    cell = gates // 4
    n = 2 * wing

    def body(keep, came, dst):
        pipe = lax.axis_index("pipe")
        for k in range(wing):
            for src, side in ((keep, pipe), (came, 1 - pipe)):
                at = pl.multiple_of((side * wing + k) * cell, cell)
                dst[:, pl.ds(at, cell)] = src[k].astype(F32)

    return pl.pallas_call(
        body,
        grid=(4,),
        out_shape=jax.ShapeDtypeStruct((rows, n * gates), F32),
        in_specs=[pl.BlockSpec((wing, rows, cell), lambda b: (0, 0, b))] * 2,
        out_specs=pl.BlockSpec((rows, n * cell), lambda b: (0, b)),
        cost_estimate=pl.CostEstimate(
            flops=0, bytes_accessed=6 * n * rows * gates, transcendentals=0
        ),
        name="join_cells",
    )(keep, came)


def swap_pipes(value):
    return lax.ppermute(value, "pipe", [(0, 1), (1, 0)])


def exchange(blocks):
    n = len(blocks)
    return [blocks[0]] + [
        lax.ppermute(blocks[off], "dp", [(i, (i + off) % n) for i in range(n)])
        for off in range(1, n)
    ]


def rank_pairs(n, off, layers=(0, 1)):
    wing = n // 2
    pairs = []
    for layer in layers:
        for j in range(n):
            rank = (j + off) % n
            pairs.append((layer * n + j, rank // wing * n + layer * wing + rank % wing))
    return pairs


def to_ranks(value, off):
    return lax.ppermute(value, ("pipe", "dp"), rank_pairs(lax.axis_size("dp"), off))


def from_ranks(value, off, layers=(0, 1)):
    pairs = rank_pairs(lax.axis_size("dp"), -off, layers)
    return lax.ppermute(value, ("pipe", "dp"), [(there, here) for here, there in pairs])


def conv_forward(ids, table_low, conv_low, valid_place):
    return jax.nn.logsumexp(conv_response(ids, table_low, conv_low, valid_place)[1], axis=1)


def own_half(value, blocks):
    sub = value.shape[-1] // (2 * blocks)
    split = value.reshape(*value.shape[:-1], blocks, 2, sub)
    mine = lax.dynamic_index_in_dim(split, lax.axis_index("pipe"), split.ndim - 2, keepdims=False)
    return mine.reshape(*value.shape[:-1], blocks * sub)


def both_halves(value, blocks):
    tokens, half = value.shape
    pair = lax.all_gather(value, "pipe").reshape(2, tokens, blocks, half // blocks)
    return jnp.transpose(pair, (1, 2, 0, 3)).reshape(tokens, 2 * half)


def conv_backward(ids, table_low, conv_low, masks, grad_before):
    weight_mask, valid_place = masks
    windows, response = conv_response(ids, table_low, conv_low, valid_place)
    share = jax.nn.softmax(response, axis=1)
    grad_response = (grad_before[:, None, :] * share).astype(BF)
    grad_conv = jnp.einsum("bpk,bpf->kf", windows, grad_response, preferred_element_type=F32)
    grad_windows = jnp.einsum("bpf,kf->bpk", grad_response, conv_low, preferred_element_type=F32)
    grad_embedded = jnp.zeros((ids.shape[0], CHARS + KMAX - 1, CDIM), F32)
    for offset in range(KMAX):
        grad_embedded = grad_embedded + jnp.pad(
            grad_windows[:, :, offset * CDIM : (offset + 1) * CDIM],
            ((0, 0), (offset, KMAX - 1 - offset), (0, 0)),
        )
    grad_embedded = grad_embedded[:, :CHARS].astype(BF)
    one_hot = (ids[:, :, None] == jnp.arange(CVOCAB, dtype=jnp.int32)).astype(BF)
    grad_table = jnp.einsum("bpv,bpc->vc", one_hot, grad_embedded, preferred_element_type=F32)
    return grad_conv * weight_mask, grad_table


def local(
    chars,
    lengths,
    char_emb,
    conv_weight,
    conv_bias,
    highway_weight,
    highway_bias,
    proj_weight,
    proj_bias,
    gate_weight,
    gate_bias,
    cell_proj,
    cotangent,
):
    n = lax.axis_size("dp")
    pipe = lax.axis_index("pipe")
    direction = lax.axis_index("dir")
    me = lax.axis_index("dp")
    everyone = lax.axis_size(ALL)
    holders = lax.axis_size(("dir", "dp"))
    seqs, steps, char_count = chars.shape
    group = seqs // lax.axis_size("dir")
    quarter = group // 2
    group_tokens = group * steps
    tokens = quarter * steps
    width = cell_proj.shape[3]
    cell = cell_proj.shape[2]
    blocks = holders // 2
    sub = FILTERS // holders
    half = FILTERS // 2
    filter_index = (
        (2 * jnp.arange(blocks, dtype=jnp.int32) + pipe)[:, None] * sub
        + jnp.arange(sub, dtype=jnp.int32)[None, :]
    ).reshape(half)
    masks = conv_masks(filter_index)

    proj_rows = proj_weight.shape[0]
    pieces = width // sub
    proj_blocks = jnp.transpose(proj_weight.reshape(proj_rows, pieces, sub), (1, 0, 2))
    proj_blocks = proj_blocks.reshape(2, pieces * proj_rows // 2, sub)
    mine = lax.dynamic_slice_in_dim(highway_weight, pipe * sub, sub, 2)
    gathered = lax.all_gather(
        jnp.concatenate([mine, proj_blocks], axis=1).astype(BF), ("dir", "dp"), axis=2, tiled=True
    )
    conv_full = lax.all_to_all(
        jnp.broadcast_to(conv_weight.astype(BF), (holders, KMAX * CDIM, sub)), ("dir", "dp"), 0, 0
    ).reshape(blocks, 2, KMAX * CDIM, sub)
    conv_low = lax.dynamic_index_in_dim(conv_full, pipe, 1, keepdims=False)
    conv_low = jnp.transpose(conv_low, (1, 0, 2)).reshape(KMAX * CDIM, half)
    conv_low = conv_low * masks[0].astype(BF)
    conv_bias_own = own_half(conv_bias, blocks)
    highway_bias_own = own_half(highway_bias.reshape(2, 2, FILTERS), blocks).reshape(2, FILTERS)

    def order_matrix(sizes):
        place = jnp.arange(steps, dtype=jnp.int32)[None, :]
        live = place < sizes[:, None]
        order = jnp.where(live & (direction == 1), sizes[:, None] - 1 - place, place)
        return ((order[:, :, None] == place[:, None, :]) & live[:, :, None]).astype(BF)

    own_order = order_matrix(lengths)
    cot = jnp.einsum("rts,rsd->trd", own_order, cotangent[0, 0], preferred_element_type=BF)

    ids = lax.dynamic_slice_in_dim(chars, direction * group, group, 0).reshape(
        group_tokens, char_count
    )
    table_low = char_emb.astype(BF)
    pooled = conv_forward(ids, table_low, conv_low, masks[1])
    features = jax.nn.silu(pooled + conv_bias_own)
    features_low = both_halves(features.astype(BF), blocks)
    bias_own = lax.dynamic_index_in_dim(
        gate_bias[0, 0].reshape(4, n, cell), me, 1, keepdims=False
    ).reshape(1, 4 * cell)
    moved = jnp.concatenate([cell_proj[0, 0].astype(BF), cot.reshape(steps * seqs, width)])
    gate_kept, gate_given = split_cells(gate_weight[0, 0], n)
    gate_came = swap_pipes(gate_given)
    gate_low = jnp.concatenate(
        [
            jnp.where(pipe == 0, gate_kept, gate_came),
            jnp.where(pipe == 0, gate_came, gate_kept),
        ]
    )
    gate_low, gathered, features_low, bias_own, moved = lax.optimization_barrier(
        (gate_low, gathered, features_low, bias_own, moved)
    )
    bias_own = to_ranks(bias_own, 0)
    moved = to_ranks(moved, 0)
    gate_own = lax.all_to_all(gate_low, "dp", 0, 0).reshape(2 * width, 4 * cell)
    highway_half = gathered[:, :FILTERS]
    proj_full = gathered[:, FILTERS:].reshape(pieces, proj_rows, holders, sub)
    proj_full = jnp.transpose(proj_full, (2, 1, 0, 3)).reshape(FILTERS, width)

    kept = [features]
    kept_low = [features_low]
    mixed = []
    for layer in range(2):
        pre = (
            jnp.dot(kept_low[layer], highway_half[layer], preferred_element_type=F32)
            + highway_bias_own[layer]
        )
        mixed.append(pre)
        gate = jax.nn.sigmoid(pre[:, half:])
        features = gate * features + (1.0 - gate) * jax.nn.silu(pre[:, :half])
        kept.append(features)
        kept_low.append(both_halves(features.astype(BF), blocks))
    own_last = lax.dynamic_slice_in_dim(kept_low[2], pipe * tokens, tokens, 0)
    encoded = jnp.dot(own_last, proj_full, preferred_element_type=F32) + proj_bias
    encoded_own = lax.all_gather(
        encoded.astype(BF).reshape(quarter, steps, width), ("dir", "pipe"), axis=0, tiled=True
    )
    inputs = jnp.einsum("rts,rsd->trd", own_order, encoded_own, preferred_element_type=BF)
    wing = n // 2
    inputs = lax.ppermute(
        inputs,
        ("pipe", "dp"),
        [(k, wing + k) for k in range(wing)] + [(n + k, n + k) for k in range(wing, n)],
    )
    kept_low, gate_own, inputs, moved, bias_own = lax.optimization_barrier(
        (kept_low, gate_own, inputs, moved, bias_own)
    )
    cell_low = moved[:cell]
    cot = moved[cell:].reshape(steps, seqs, width)
    kept_all = [
        lax.all_gather(
            lax.dynamic_slice_in_dim(value, pipe * tokens, tokens, 0),
            ("dir", "dp"),
            axis=0,
            tiled=True,
        )
        for value in kept_low[:2]
    ]

    out_own, dx_own, grad_bias, grad_cell, *grad_gate = lstm_call(
        n, inputs, gate_own, bias_own, cell_low, cell_low.T, cot
    )
    dx_own = from_ranks(dx_own.astype(BF), 0, (1,))
    grad_gate = exchange(grad_gate)
    dx_own, kept_all = lax.optimization_barrier((dx_own, kept_all))

    grad_stored = jnp.einsum(
        "rts,srd->rtd", own_order, dx_own, preferred_element_type=F32
    )
    grad_stored = jnp.where(pipe == 1, grad_stored, 0.0).astype(BF)
    grad_stored = grad_stored.reshape(1, -1, group_tokens, width)
    grad_encoded = lax.all_to_all(
        jnp.concatenate([grad_stored, grad_stored]).reshape(-1, group_tokens, width),
        ("pipe", "dir"),
        0,
        0,
    )
    grad_encoded = jnp.sum(grad_encoded.astype(F32), axis=0).astype(BF)
    own_grads = lax.dynamic_slice_in_dim(grad_encoded, pipe * tokens, tokens, 0)
    encoded_grads = lax.all_gather(own_grads, ("dir", "dp"), axis=0, tiled=True)

    grad_proj_bias = jnp.sum(own_grads.astype(F32), axis=0)
    proj_half = lax.dynamic_index_in_dim(
        proj_full.reshape(blocks, 2, sub, width), pipe, 1, keepdims=False
    ).reshape(half, width)
    grad_features = jnp.einsum("td,fd->tf", grad_encoded, proj_half, preferred_element_type=F32)
    columns = [None, None]
    grad_highway_bias = [None, None]
    for layer in (1, 0):
        nonlinear = mixed[layer][:, :half]
        gate = jax.nn.sigmoid(mixed[layer][:, half:])
        grad_mixed = jnp.concatenate(
            [
                grad_features * (1.0 - gate) * silu_slope(nonlinear),
                grad_features * (kept[layer] - jax.nn.silu(nonlinear)) * gate * (1.0 - gate),
            ],
            axis=1,
        ).astype(BF)
        columns[layer] = grad_mixed
        grad_highway_bias[layer] = jnp.sum(grad_mixed.astype(F32), axis=0)
        partial = jnp.einsum(
            "tg,fg->tf", grad_mixed, highway_half[layer], preferred_element_type=F32
        )
        partial = lax.optimization_barrier(partial).reshape(group_tokens, blocks, 2, sub)
        sent = lax.dynamic_index_in_dim(partial, 1 - pipe, 2, keepdims=False).astype(BF)
        came = lax.ppermute(sent, "pipe", [(0, 1), (1, 0)])
        mine = lax.dynamic_index_in_dim(partial, pipe, 2, keepdims=False)
        grad_features = grad_features * gate + (mine + came.astype(F32)).reshape(
            group_tokens, half
        )
    grad_before = grad_features * silu_slope(pooled + conv_bias_own)
    grad_before, grad_gate[1:5] = lax.optimization_barrier((grad_before, grad_gate[1:5]))
    grad_conv, grad_table = conv_backward(ids, table_low, conv_low, masks, grad_before)

    def spread(value):
        split = value.reshape(*value.shape[:-1], -1, 1, sub)
        shown = jnp.arange(2, dtype=jnp.int32)[:, None] == pipe
        return jnp.where(shown, split, jnp.zeros_like(split)).reshape(*value.shape[:-1], -1)

    cols = FILTERS // everyone
    pair = jnp.stack(columns, axis=1).reshape(2, tokens, 2, 2, blocks, 1, sub)
    sent = lax.dynamic_index_in_dim(pair, 1 - pipe, 0, keepdims=False)
    came = lax.ppermute(sent, "pipe", [(0, 1), (1, 0)])
    mine = lax.dynamic_index_in_dim(pair, pipe, 0, keepdims=False)
    shown = (jnp.arange(2, dtype=jnp.int32) == pipe)[:, None]
    pair = jnp.where(shown, mine, came)
    pair = jnp.transpose(pair, (3, 4, 0, 1, 2, 5)).reshape(holders, tokens, 4 * sub)
    last = jnp.transpose(own_last.reshape(tokens, 2, holders, cols), (2, 0, 1, 3))
    pair = jnp.concatenate([pair, last.reshape(holders, tokens, 2 * cols)], axis=2)
    pair = lax.all_to_all(pair, ("dir", "dp"), 0, 0).reshape(holders * tokens, -1)
    grad_conv, pair, grad_gate, out_own, grad_cell = lax.optimization_barrier(
        (grad_conv, pair, grad_gate, out_own, grad_cell)
    )
    gate_kept, gate_given = sort_blocks(grad_gate)
    gate_came = swap_pipes(gate_given)
    grad_gate = join_cells(gate_kept, gate_came)
    small = (
        grad_table,
        spread(jnp.sum(grad_before, axis=0)),
        spread(jnp.stack(grad_highway_bias)),
        grad_proj_bias,
    )
    flat = jnp.concatenate([value.reshape(-1) for value in small])
    share = -(-flat.shape[0] // (everyone * 128)) * 128
    flat = jnp.pad(flat, (0, share * everyone - flat.shape[0])).reshape(everyone, share)
    rank = pipe * wing + lax.rem(me, wing)
    mine = jnp.arange(n, dtype=jnp.int32)[None, :, None] == rank
    bias_parts = jnp.where(mine, grad_bias.reshape(4, 1, cell), 0.0).reshape(1, n, 4 * cell)
    layer = lax.div(me, wing) * lax.axis_size("dir") + direction
    mine = jnp.arange(everyone // n, dtype=jnp.int32) == layer
    bias_parts = jnp.where(mine[:, None, None], bias_parts, 0.0).reshape(everyone, 4 * cell)
    packed = jnp.concatenate(
        [
            jnp.transpose(
                spread(grad_conv).reshape(KMAX * CDIM, everyone, cols), (1, 0, 2)
            ).reshape(everyone, KMAX * CDIM * cols),
            flat,
            bias_parts,
        ],
        axis=1,
    ).astype(BF)
    summed = jnp.sum(lax.all_to_all(packed, ALL, 0, 0).astype(F32), axis=0)
    out_own = from_ranks(out_own, 0)
    grad_cell = from_ranks(grad_cell.astype(BF), 0)
    summed, out_own, grad_cell = lax.optimization_barrier((summed, out_own, grad_cell))
    activations = jnp.einsum("rts,srd->rtd", own_order, out_own, preferred_element_type=BF)
    grad_cell = grad_cell.astype(F32)
    grad_conv = summed[: KMAX * CDIM * cols].reshape(KMAX * CDIM, cols)
    grad_bias = summed[KMAX * CDIM * cols + share :]
    last = pair[:, 4 * sub :].reshape(holders * tokens, 2, cols)
    pair = pair[:, : 4 * sub].reshape(holders * tokens, 2, 2, sub)

    def partial_sums(owner):
        return [
            jnp.einsum(
                "tf,tg->fg",
                kept_all[layer],
                lax.dynamic_index_in_dim(pair[:, layer], owner, 1, keepdims=False),
                preferred_element_type=F32,
            )
            for layer in range(2)
        ] + [
            jnp.einsum(
                "tf,td->fd",
                lax.dynamic_index_in_dim(last, owner, 1, keepdims=False),
                encoded_grads,
                preferred_element_type=F32,
            )
        ]

    sent = jnp.concatenate(
        [value.astype(BF).reshape(-1, sub) for value in partial_sums(1 - pipe)]
    )
    came = lax.ppermute(sent, "pipe", [(0, 1), (1, 0)]).astype(F32)
    mine = partial_sums(pipe)
    grad_highway = jnp.stack(mine[:2]) + came[: 2 * FILTERS].reshape(2, FILTERS, sub)
    grad_proj = mine[2] + came[2 * FILTERS :].reshape(cols, width)
    shared = lax.all_to_all(
        jnp.broadcast_to(summed[KMAX * CDIM * cols :][:share], (everyone, share)), ALL, 0, 0
    ).reshape(-1)
    small_sums = []
    start = 0
    for value in small:
        small_sums.append(shared[start : start + value.size].reshape(value.shape))
        start += value.size
    return (
        activations[None, None],
        small_sums[0],
        grad_conv,
        small_sums[1],
        grad_highway,
        small_sums[2],
        grad_proj,
        small_sums[3],
        grad_gate[None, None],
        grad_bias[None, None],
        grad_cell[None, None],
    )


def solution(mesh):
    return jax.shard_map(
        local,
        mesh=mesh,
        in_specs=(
            P("dp", None, None),
            P("dp"),
            P(),
            P(None, ("dir", "dp")),
            P(),
            P(None, None, ("dir", "dp")),
            P(),
            P(("dir", "dp"), None),
            P(),
            P("pipe", "dir", "dp", None),
            P("pipe", "dir", None),
            P("pipe", "dir", "dp", None),
            P("pipe", "dir", "dp", None, None),
        ),
        out_specs=(
            P("pipe", "dir", "dp", None, None),
            P(),
            P(None, ("pipe", "dir", "dp")),
            P(),
            P(None, None, ("pipe", "dir", "dp")),
            P(),
            P(("pipe", "dir", "dp"), None),
            P(),
            P("pipe", "dir", "dp", None),
            P("pipe", "dir", "dp"),
            P("pipe", "dir", "dp", None),
        ),
        check_vma=False,
    )
```

```python
import functools
import math

import jax
import jax.numpy as jnp
from jax import lax
from jax.experimental import pallas as pl
from jax.experimental.pallas import tpu as pltpu
from jax.sharding import PartitionSpec as P

FILTERS = 2048
CDIM = 16
CVOCAB = 262
CHARS = 50
KMAX = 7
CLIP_LIMIT = 3.0
MASKED_FILL = -1000000000.0
MESH = pl.DeviceIdType.MESH
BF = jnp.bfloat16
F32 = jnp.float32
ALL = ("pipe", "dir", "dp")


def silu_slope(value):
    sig = jax.nn.sigmoid(value)
    return sig * (1.0 + value * (1.0 - sig))


def conv_masks(filter_index):
    filter_width = jnp.ones(filter_index.shape, jnp.int32)
    for doubling in range(6):
        filter_width = filter_width + (filter_index >= FILTERS // 64 * (1 << doubling)).astype(
            jnp.int32
        )
    offset_rows = jnp.arange(KMAX * CDIM, dtype=jnp.int32) // CDIM
    weight_mask = (offset_rows[:, None] < filter_width[None, :]).astype(jnp.float32)
    valid_place = jnp.arange(CHARS, dtype=jnp.int32)[:, None] <= CHARS - filter_width[None, :]
    return (weight_mask, valid_place)


def make_windows(embedded):
    padded = jnp.pad(embedded, ((0, 0), (0, KMAX - 1), (0, 0)))
    return jnp.concatenate(
        [padded[:, offset : offset + CHARS, :] for offset in range(KMAX)], axis=2
    )


def conv_response(ids_block, table_low, conv_low, valid_place):
    embedded = jnp.take(table_low, ids_block, axis=0)
    windows = make_windows(embedded)
    response = jnp.einsum("bpk,kf->bpf", windows, conv_low, preferred_element_type=jnp.float32)
    return (windows, jnp.where(valid_place[None], response, MASKED_FILL))


def over(count, step):
    if count <= 9:
        for off in range(count - 1, 0, -1):
            step(off)
    else:
        lax.fori_loop(1, count, lambda off, _: (step(off), 0)[1], 0)


def lstm_kernel(n, chunk, x_own, bias, p, pt, cot, w_in, *refs):
    out_ref, dx_ref, db_ref, dp_ref = refs[:4]
    dw_out = refs[4:n + 4]
    (xbuf, hbuf, dqbuf, gates, cells, ebuf, hown, gscr, escr, dabuf, ucell, dwacc, w, wt,
     stage, inbox, stage2, inbox2, relay, gbuf, rown,
     in_send, in_recv, ag_send, ag_recv, dq_send, dq_recv, rs_send, rs_recv,
     dx_send, dx_recv, x_send, x_recv, g_send, g_recv, st_sem, w_sem) = refs[n + 4:]
    steps, _, rows, width = xbuf.shape
    total = n * rows
    cell = cells.shape[2]
    pipe = lax.axis_index("pipe")
    direction = lax.axis_index("dir")
    place = lax.axis_index("dp")
    wing = n // 2
    first = place >= wing
    second = place < wing
    me = pipe * wing + lax.rem(place, wing)
    base = place - lax.rem(place, wing)
    partner = (pipe, direction, lax.rem(place + wing, n))

    def peer(off):
        if n & (n - 1):
            return lax.rem(me + off, n)
        return me ^ off

    def at_peer(off):
        rank = peer(off)
        return (lax.div(rank, wing), direction, base + lax.rem(rank, wing))

    barrier = pltpu.get_barrier_semaphore()
    over(n, lambda off: pl.semaphore_signal(
        barrier, inc=1, device_id=at_peer(off), device_id_type=MESH))
    pl.semaphore_signal(barrier, inc=1, device_id=partner, device_id_type=MESH)

    each = 2 * width // n
    load = pltpu.make_async_copy(w_in, w, w_sem)
    load.start()

    @pl.when(first)
    def _():
        for t in range(steps):
            xbuf[t, me] = x_own[t]

    hbuf[0] = jnp.zeros((n, rows, width), BF)
    cells[0] = jnp.zeros((total, cell), F32)
    pl.semaphore_wait(barrier, n)

    def ag_copy(buf, slot, off):
        out, into = (ag_send, ag_recv) if buf is hbuf else (dq_send, dq_recv)
        return pltpu.make_async_remote_copy(
            src_ref=buf.at[slot, me], dst_ref=buf.at[slot, me],
            send_sem=out.at[off], recv_sem=into.at[off],
            device_id=at_peer(off), device_id_type=MESH)

    def rs_copy(off):
        return pltpu.make_async_remote_copy(
            src_ref=stage.at[peer(off)], dst_ref=inbox.at[me],
            send_sem=rs_send.at[off], recv_sem=rs_recv.at[off],
            device_id=at_peer(off), device_id_type=MESH)

    def dx_copy(slot, off):
        return pltpu.make_async_remote_copy(
            src_ref=stage2.at[slot, peer(off)], dst_ref=inbox2.at[slot, me],
            send_sem=dx_send.at[slot, off], recv_sem=dx_recv.at[slot, off],
            device_id=at_peer(off), device_id_type=MESH)

    def x_copy(t):
        return pltpu.make_async_remote_copy(
            src_ref=hbuf.at[t + 1, me], dst_ref=xbuf.at[t, me],
            send_sem=x_send.at[t], recv_sem=x_recv.at[t],
            device_id=partner, device_id_type=MESH)

    def g_copy(t):
        return pltpu.make_async_remote_copy(
            src_ref=relay.at[t], dst_ref=gbuf.at[t],
            send_sem=g_send.at[t], recv_sem=g_recv.at[t],
            device_id=partner, device_id_type=MESH)

    def in_start(t):
        over(n, lambda off: pltpu.make_async_remote_copy(
            src_ref=xbuf.at[t, me], dst_ref=xbuf.at[t, me],
            send_sem=in_send.at[t], recv_sem=in_recv.at[t],
            device_id=at_peer(off), device_id_type=MESH).start())

    def in_wait(sem, t):
        blocks = xbuf.at[t, pl.ds(0, n - 1)]
        pltpu.make_async_copy(blocks, blocks, sem.at[t]).wait()

    @pl.when(first)
    def _():
        in_start(0)
        in_start(1)

    @pl.when(second)
    def _():
        x_copy(0).wait_recv()
        in_start(0)

    load.wait()
    for at in range(0, 2 * width, 128):
        wt[:, at:at + 128] = w[at:at + 128, :].T

    def ag_wait(buf, slot):
        def both(off):
            ag_copy(buf, slot, off).wait_send()
            ag_copy(buf, slot, off).wait_recv()
        over(n, both)

    def rs_wait():
        def both(off):
            rs_copy(off).wait_send()
            rs_copy(off).wait_recv()
        over(n, both)

    def forward(t, _):
        in_wait(in_recv, t)
        gscr[...] = jnp.dot(
            xbuf[t].reshape(total, width), w[:width, :], preferred_element_type=F32) + bias[...]

        @pl.when(t > 0)
        def _():
            ag_wait(hbuf, t)

        gscr[...] += jnp.dot(
            hbuf[t].reshape(total, width), w[width:, :], preferred_element_type=F32)

        def rows_step(k, _):
            at = pl.ds(pl.multiple_of(k * chunk, chunk), chunk)
            g = gscr[at, :]
            i = jax.nn.sigmoid(g[:, :cell])
            f = jax.nn.sigmoid(g[:, cell:2 * cell])
            m = jnp.tanh(g[:, 2 * cell:3 * cell])
            o = jax.nn.sigmoid(g[:, 3 * cell:])
            c = 3.0 * jnp.tanh((i * m + f * cells[t, at, :]) * (1.0 / 3.0))
            cells[t + 1, at, :] = c
            ebuf[t, at, :] = (o * jnp.tanh(c)).astype(BF)
            kind = gates.dtype
            gates[t, at, :cell] = i.astype(kind)
            gates[t, at, cell:2 * cell] = f.astype(kind)
            gates[t, at, 2 * cell:3 * cell] = m.astype(kind)
            gates[t, at, 3 * cell:] = o.astype(kind)
            return 0

        lax.fori_loop(0, total // chunk, rows_step, 0)
        q = jnp.dot(ebuf[t], p[...], preferred_element_type=F32)
        stage[...] = q.astype(BF).reshape(n, rows, width)
        over(n, lambda off: rs_copy(off).start())
        inbox[me] = stage[me]

        @pl.when(first & (t + 2 < steps))
        def _():
            in_start(t + 2)

        @pl.when(second & (t + 1 < steps))
        def _():
            x_copy(t + 1).wait_recv()
            in_start(t + 1)

        rs_wait()
        h = 3.0 * jnp.tanh(jnp.sum(inbox[...].astype(F32), axis=0) * (1.0 / 3.0))
        hown[t] = h
        hbuf[t + 1, me] = h.astype(BF)
        over(n, lambda off: ag_copy(hbuf, t + 1, off).start())

        @pl.when(first)
        def _():
            x_copy(t).start()

        add = jnp.where(second, 1.0, 0.0)
        out_ref[t] = (h + add * xbuf[t, me].astype(F32)).astype(BF)
        return 0

    lax.fori_loop(0, steps, forward, 0)
    ag_wait(hbuf, steps)

    lax.fori_loop(0, steps, lambda t, _: (in_wait(in_send, t), 0)[1], 0)

    @pl.when(first)
    def _():
        lax.fori_loop(0, steps, lambda t, _: (x_copy(t).wait_send(), 0)[1], 0)

    rown[...] = jnp.zeros((rows, width), F32)
    ucell[...] = jnp.zeros((total, cell), F32)
    dwacc[...] = jnp.zeros(dwacc.shape, F32)
    db_ref[...] = jnp.zeros(db_ref.shape, F32)
    dp_ref[...] = jnp.zeros(dp_ref.shape, F32)

    def dx_finish(t):
        slot = lax.rem(t, 2)

        def both(off):
            dx_copy(slot, off).wait_send()
            dx_copy(slot, off).wait_recv()
        over(n, both)
        dx = jnp.sum(inbox2[slot].astype(F32), axis=0)
        dx_ref[t] = dx

        @pl.when(second)
        def _():
            relay[t] = (dx + cot[t].astype(F32)).astype(BF)
            g_copy(t).start()

    def backward(k, _):
        t = steps - 1 - k
        slot = lax.rem(t, 2)
        up = rown[...] + cot[t].astype(F32)
        rown[...] = up

        @pl.when(first)
        def _():
            g_copy(t).wait_recv()
            rown[...] = rown[...] + gbuf[t].astype(F32)

        ratio = hown[t] * (1.0 / 3.0)
        dqbuf[t, me] = (rown[...] * (1.0 - ratio * ratio)).astype(BF)
        over(n, lambda off: ag_copy(dqbuf, t, off).start())

        @pl.when(k > 0)
        def _():
            dx_finish(t + 1)

        ag_wait(dqbuf, t)
        escr[...] = jnp.dot(
            dqbuf[t].reshape(total, width), pt[...], preferred_element_type=F32)

        def rows_step(j, _):
            at = pl.ds(pl.multiple_of(j * chunk, chunk), chunk)
            de = escr[at, :]
            i = gates[t, at, :cell].astype(F32)
            f = gates[t, at, cell:2 * cell].astype(F32)
            m = gates[t, at, 2 * cell:3 * cell].astype(F32)
            o = gates[t, at, 3 * cell:].astype(F32)
            c = cells[t + 1, at, :]
            tc = jnp.tanh(c)
            cr = c * (1.0 / 3.0)
            dc = (de * o * (1.0 - tc * tc) + ucell[at, :]) * (1.0 - cr * cr)
            ucell[at, :] = dc * f
            for block, value in enumerate((
                dc * m * i * (1.0 - i),
                dc * cells[t, at, :] * f * (1.0 - f),
                dc * i * (1.0 - m * m),
                de * tc * o * (1.0 - o),
            )):
                value = value.astype(BF)
                where = pl.ds(block * cell, cell)
                dabuf[0, at, where] = value
                db_ref[:, where] += jnp.sum(value.astype(F32), axis=0, keepdims=True)
            return 0

        lax.fori_loop(0, total // chunk, rows_step, 0)
        r = jnp.dot(dabuf[0], wt[:, width:], preferred_element_type=F32)
        stage[...] = r.astype(BF).reshape(n, rows, width)
        over(n, lambda off: rs_copy(off).start())
        inbox[me] = stage[me]
        dx = jnp.dot(dabuf[0], wt[:, :width], preferred_element_type=F32)
        stage2[slot] = dx.astype(BF).reshape(n, rows, width)
        over(n, lambda off: dx_copy(slot, off).start())
        inbox2[slot, me] = stage2[slot, me]
        for half, buf in enumerate((xbuf, hbuf)):
            dwacc[pl.ds(half * width, width), :] += lax.dot_general(
                buf[t].reshape(total, width), dabuf[0], (((0,), (0,)), ((), ())),
                preferred_element_type=F32)
        dp_ref[...] += lax.dot_general(
            ebuf[t], dqbuf[t].reshape(total, width), (((0,), (0,)), ((), ())),
            preferred_element_type=F32)
        rs_wait()
        rown[...] = jnp.sum(inbox[...].astype(F32), axis=0)
        return 0

    lax.fori_loop(0, steps, backward, 0)
    dx_finish(0)

    @pl.when(second)
    def _():
        lax.fori_loop(0, steps, lambda t, _: (g_copy(t).wait_send(), 0)[1], 0)

    def dw_copy(off):
        return pltpu.make_async_copy(
            dabuf.at[off % 2, pl.ds(0, each)], dw_out[off], st_sem.at[off % 2])

    for off in range(n):
        if off > 1:
            dw_copy(off - 2).wait()
        at = pl.multiple_of(lax.rem(place + off, n) * each, each)
        dabuf[off % 2, :each, :] = dwacc[pl.ds(at, each), :].astype(BF)
        dw_copy(off).start()
    for off in range(n - 2, n):
        dw_copy(off).wait()


def lstm_call(n, x, weights, bias, p, pt, cot, chunk=16):
    steps, rows, width = x.shape
    cell = p.shape[0]
    total = n * rows
    sds = jax.ShapeDtypeStruct
    vm = pl.BlockSpec(memory_space=pltpu.VMEM)
    hb = pl.BlockSpec(memory_space=pl.ANY)
    keep = F32 if n <= 8 else BF
    V = pltpu.VMEM
    dma = pltpu.SemaphoreType.DMA
    return pl.pallas_call(
        functools.partial(lstm_kernel, n, chunk),
        out_shape=(
            sds((steps, rows, width), BF), sds((steps, rows, width), F32),
            sds((1, 4 * cell), F32), sds((cell, width), F32),
            *[sds((2 * width // n, 4 * cell), BF)] * n),
        in_specs=[vm] * 5 + [hb],
        out_specs=[vm] * 4 + [hb] * n,
        scratch_shapes=[
            V((steps, n, rows, width), BF), V((steps + 1, n, rows, width), BF),
            V((steps, n, rows, width), BF), V((steps, total, 4 * cell), keep),
            V((steps + 1, total, cell), F32), V((steps, total, cell), BF),
            V((steps, rows, width), F32), V((total, 4 * cell), F32),
            V((total, cell), F32), V((2, total, 4 * cell), BF), V((total, cell), F32),
            V((2 * width, 4 * cell), F32), V((2 * width, 4 * cell), BF),
            V((4 * cell, 2 * width), BF),
            V((n, rows, width), BF), V((n, rows, width), BF),
            V((2, n, rows, width), BF), V((2, n, rows, width), BF),
            V((steps, rows, width), BF), V((steps, rows, width), BF), V((rows, width), F32),
            dma((steps,)), dma((steps,)), dma((n,)), dma((n,)), dma((n,)), dma((n,)), dma((n,)), dma((n,)), dma((2, n)), dma((2, n)),
            dma((steps,)), dma((steps,)), dma((steps,)), dma((steps,)), dma((2,)), dma,
        ],
        compiler_params=pltpu.CompilerParams(
            collective_id=0, has_side_effects=True, vmem_limit_bytes=60 * 1024 * 1024),
        cost_estimate=pl.CostEstimate(
            flops=300_000_000_000, bytes_accessed=64 * 1024 * 1024, transcendentals=0),
        name="relay_lstm",
    )(x, bias, p, pt, cot, weights)


def split_cells(weight, n):
    rows, gates = weight.shape
    cell = gates // (4 * n)
    wing = n // 2

    def body(src, keep, give):
        pipe = lax.axis_index("pipe")
        for k in range(wing):
            for dst, side in ((keep, pipe), (give, 1 - pipe)):
                at = pl.multiple_of((side * wing + k) * cell, cell)
                dst[k] = src[:, pl.ds(at, cell)].astype(BF)

    return pl.pallas_call(
        body,
        grid=(4,),
        out_shape=[jax.ShapeDtypeStruct((wing, rows, 4 * cell), BF)] * 2,
        in_specs=[pl.BlockSpec((rows, n * cell), lambda b: (0, b))],
        out_specs=[pl.BlockSpec((wing, rows, cell), lambda b: (0, 0, b))] * 2,
        cost_estimate=pl.CostEstimate(
            flops=0, bytes_accessed=6 * rows * gates, transcendentals=0
        ),
        name="split_cells",
    )(weight)


def sort_blocks(blocks):
    n = len(blocks)
    wing = n // 2

    rows, gates = blocks[0].shape
    cell = gates // 4

    def body(*refs):
        src, (keep, give) = refs[:n], refs[n:]
        pipe = lax.axis_index("pipe")
        for off in range(n):
            place = lax.rem(lax.axis_index("dp") + (n - off), n)
            stays = lax.div(place, wing) == pipe

            @pl.when(stays)
            def _():
                keep[lax.rem(place, wing)] = src[off][...]

            @pl.when(jnp.logical_not(stays))
            def _():
                give[lax.rem(place, wing)] = src[off][...]

    return pl.pallas_call(
        body,
        grid=(4,),
        out_shape=[jax.ShapeDtypeStruct((wing, rows, gates), BF)] * 2,
        in_specs=[pl.BlockSpec((rows, cell), lambda b: (0, b))] * n,
        out_specs=[pl.BlockSpec((wing, rows, cell), lambda b: (0, 0, b))] * 2,
        cost_estimate=pl.CostEstimate(
            flops=0, bytes_accessed=4 * n * blocks[0].size, transcendentals=0
        ),
        name="sort_blocks",
    )(*blocks)


def join_cells(keep, came):
    wing, rows, gates = keep.shape
    cell = gates // 4
    n = 2 * wing

    def body(keep, came, dst):
        pipe = lax.axis_index("pipe")
        for k in range(wing):
            for src, side in ((keep, pipe), (came, 1 - pipe)):
                at = pl.multiple_of((side * wing + k) * cell, cell)
                dst[:, pl.ds(at, cell)] = src[k].astype(F32)

    return pl.pallas_call(
        body,
        grid=(4,),
        out_shape=jax.ShapeDtypeStruct((rows, n * gates), F32),
        in_specs=[pl.BlockSpec((wing, rows, cell), lambda b: (0, 0, b))] * 2,
        out_specs=pl.BlockSpec((rows, n * cell), lambda b: (0, b)),
        cost_estimate=pl.CostEstimate(
            flops=0, bytes_accessed=6 * n * rows * gates, transcendentals=0
        ),
        name="join_cells",
    )(keep, came)


def swap_pipes(value):
    return lax.ppermute(value, "pipe", [(0, 1), (1, 0)])


def exchange(blocks):
    n = len(blocks)
    return [blocks[0]] + [
        lax.ppermute(blocks[off], "dp", [(i, (i + off) % n) for i in range(n)])
        for off in range(1, n)
    ]


def rank_pairs(n, off, layers=(0, 1)):
    wing = n // 2
    pairs = []
    for layer in layers:
        for j in range(n):
            rank = (j + off) % n
            pairs.append((layer * n + j, rank // wing * n + layer * wing + rank % wing))
    return pairs


def to_ranks(value, off):
    return lax.ppermute(value, ("pipe", "dp"), rank_pairs(lax.axis_size("dp"), off))


def from_ranks(value, off, layers=(0, 1)):
    pairs = rank_pairs(lax.axis_size("dp"), -off, layers)
    return lax.ppermute(value, ("pipe", "dp"), [(there, here) for here, there in pairs])


def conv_forward(ids, table_low, conv_low, valid_place):
    return jax.nn.logsumexp(conv_response(ids, table_low, conv_low, valid_place)[1], axis=1)


def own_half(value, blocks):
    sub = value.shape[-1] // (2 * blocks)
    split = value.reshape(*value.shape[:-1], blocks, 2, sub)
    mine = lax.dynamic_index_in_dim(split, lax.axis_index("pipe"), split.ndim - 2, keepdims=False)
    return mine.reshape(*value.shape[:-1], blocks * sub)


def both_halves(value, blocks):
    tokens, half = value.shape
    pair = lax.all_gather(value, "pipe").reshape(2, tokens, blocks, half // blocks)
    return jnp.transpose(pair, (1, 2, 0, 3)).reshape(tokens, 2 * half)


def conv_backward(ids, table_low, conv_low, masks, grad_before):
    weight_mask, valid_place = masks
    windows, response = conv_response(ids, table_low, conv_low, valid_place)
    share = jax.nn.softmax(response, axis=1)
    grad_response = (grad_before[:, None, :] * share).astype(BF)
    grad_conv = jnp.einsum("bpk,bpf->kf", windows, grad_response, preferred_element_type=F32)
    grad_windows = jnp.einsum("bpf,kf->bpk", grad_response, conv_low, preferred_element_type=F32)
    grad_embedded = jnp.zeros((ids.shape[0], CHARS + KMAX - 1, CDIM), F32)
    for offset in range(KMAX):
        grad_embedded = grad_embedded + jnp.pad(
            grad_windows[:, :, offset * CDIM : (offset + 1) * CDIM],
            ((0, 0), (offset, KMAX - 1 - offset), (0, 0)),
        )
    grad_embedded = grad_embedded[:, :CHARS].astype(BF)
    one_hot = (ids[:, :, None] == jnp.arange(CVOCAB, dtype=jnp.int32)).astype(BF)
    grad_table = jnp.einsum("bpv,bpc->vc", one_hot, grad_embedded, preferred_element_type=F32)
    return grad_conv * weight_mask, grad_table


def local(
    chars,
    lengths,
    char_emb,
    conv_weight,
    conv_bias,
    highway_weight,
    highway_bias,
    proj_weight,
    proj_bias,
    gate_weight,
    gate_bias,
    cell_proj,
    cotangent,
):
    n = lax.axis_size("dp")
    pipe = lax.axis_index("pipe")
    direction = lax.axis_index("dir")
    me = lax.axis_index("dp")
    everyone = lax.axis_size(ALL)
    holders = lax.axis_size(("dir", "dp"))
    seqs, steps, char_count = chars.shape
    group = seqs // lax.axis_size("dir")
    quarter = group // 2
    group_tokens = group * steps
    tokens = quarter * steps
    width = cell_proj.shape[3]
    cell = cell_proj.shape[2]
    blocks = holders // 2
    sub = FILTERS // holders
    half = FILTERS // 2
    filter_index = (
        (2 * jnp.arange(blocks, dtype=jnp.int32) + pipe)[:, None] * sub
        + jnp.arange(sub, dtype=jnp.int32)[None, :]
    ).reshape(half)
    masks = conv_masks(filter_index)

    proj_rows = proj_weight.shape[0]
    pieces = width // sub
    proj_blocks = jnp.transpose(proj_weight.reshape(proj_rows, pieces, sub), (1, 0, 2))
    proj_blocks = proj_blocks.reshape(2, pieces * proj_rows // 2, sub)
    mine = lax.dynamic_slice_in_dim(highway_weight, pipe * sub, sub, 2)
    gathered = lax.all_gather(
        jnp.concatenate([mine, proj_blocks], axis=1).astype(BF), ("dir", "dp"), axis=2, tiled=True
    )
    conv_full = lax.all_to_all(
        jnp.broadcast_to(conv_weight.astype(BF), (holders, KMAX * CDIM, sub)), ("dir", "dp"), 0, 0
    ).reshape(blocks, 2, KMAX * CDIM, sub)
    conv_low = lax.dynamic_index_in_dim(conv_full, pipe, 1, keepdims=False)
    conv_low = jnp.transpose(conv_low, (1, 0, 2)).reshape(KMAX * CDIM, half)
    conv_low = conv_low * masks[0].astype(BF)
    conv_bias_own = own_half(conv_bias, blocks)
    highway_bias_own = own_half(highway_bias.reshape(2, 2, FILTERS), blocks).reshape(2, FILTERS)

    def order_matrix(sizes):
        place = jnp.arange(steps, dtype=jnp.int32)[None, :]
        live = place < sizes[:, None]
        order = jnp.where(live & (direction == 1), sizes[:, None] - 1 - place, place)
        return ((order[:, :, None] == place[:, None, :]) & live[:, :, None]).astype(BF)

    own_order = order_matrix(lengths)
    cot = jnp.einsum("rts,rsd->trd", own_order, cotangent[0, 0], preferred_element_type=BF)

    ids = lax.dynamic_slice_in_dim(chars, direction * group, group, 0).reshape(
        group_tokens, char_count
    )
    table_low = char_emb.astype(BF)
    pooled = conv_forward(ids, table_low, conv_low, masks[1])
    features = jax.nn.silu(pooled + conv_bias_own)
    features_low = both_halves(features.astype(BF), blocks)
    bias_own = lax.dynamic_index_in_dim(
        gate_bias[0, 0].reshape(4, n, cell), me, 1, keepdims=False
    ).reshape(1, 4 * cell)
    moved = jnp.concatenate([cell_proj[0, 0].astype(BF), cot.reshape(steps * seqs, width)])
    gate_kept, gate_given = split_cells(gate_weight[0, 0], n)
    gate_came = swap_pipes(gate_given)
    gate_low = jnp.concatenate(
        [
            jnp.where(pipe == 0, gate_kept, gate_came),
            jnp.where(pipe == 0, gate_came, gate_kept),
        ]
    )
    direct, local_part = moved[: moved.shape[0] // 2], moved[moved.shape[0] // 2 :]
    swapped = swap_pipes(local_part)
    gate_low, gathered, features_low, bias_own, direct, swapped = lax.optimization_barrier(
        (gate_low, gathered, features_low, bias_own, direct, swapped)
    )
    bias_own = to_ranks(bias_own, 0)
    wing = n // 2
    swapped = lax.ppermute(
        swapped,
        ("pipe", "dp"),
        [(k, wing + k) for k in range(wing)] + [(n + wing + k, n + k) for k in range(wing)],
    )
    moved = jnp.concatenate(
        [to_ranks(direct, 0), jnp.where(lax.div(me, wing) == pipe, local_part, swapped)]
    )
    gate_own = lax.all_to_all(gate_low, "dp", 0, 0).reshape(2 * width, 4 * cell)
    highway_half = gathered[:, :FILTERS]
    proj_full = gathered[:, FILTERS:].reshape(pieces, proj_rows, holders, sub)
    proj_full = jnp.transpose(proj_full, (2, 1, 0, 3)).reshape(FILTERS, width)

    kept = [features]
    kept_low = [features_low]
    mixed = []
    for layer in range(2):
        pre = (
            jnp.dot(kept_low[layer], highway_half[layer], preferred_element_type=F32)
            + highway_bias_own[layer]
        )
        mixed.append(pre)
        gate = jax.nn.sigmoid(pre[:, half:])
        features = gate * features + (1.0 - gate) * jax.nn.silu(pre[:, :half])
        kept.append(features)
        kept_low.append(both_halves(features.astype(BF), blocks))
    own_last = lax.dynamic_slice_in_dim(kept_low[2], pipe * tokens, tokens, 0)
    encoded = jnp.dot(own_last, proj_full, preferred_element_type=F32) + proj_bias
    encoded_own = lax.all_gather(
        encoded.astype(BF).reshape(quarter, steps, width), ("dir", "pipe"), axis=0, tiled=True
    )
    inputs = jnp.einsum("rts,rsd->trd", own_order, encoded_own, preferred_element_type=BF)
    inputs = lax.ppermute(
        inputs,
        ("pipe", "dp"),
        [(k, wing + k) for k in range(wing)] + [(n + k, n + k) for k in range(wing, n)],
    )
    kept_low, gate_own, inputs, moved, bias_own = lax.optimization_barrier(
        (kept_low, gate_own, inputs, moved, bias_own)
    )
    cell_low = moved[:cell]
    cot = moved[cell:].reshape(steps, seqs, width)
    kept_all = [
        lax.all_gather(
            lax.dynamic_slice_in_dim(value, pipe * tokens, tokens, 0),
            ("dir", "dp"),
            axis=0,
            tiled=True,
        )
        for value in kept_low[:2]
    ]

    out_own, dx_own, grad_bias, grad_cell, *grad_gate = lstm_call(
        n, inputs, gate_own, bias_own, cell_low, cell_low.T, cot
    )
    dx_own = from_ranks(dx_own.astype(BF), 0, (1,))
    grad_gate = exchange(grad_gate)
    dx_own, kept_all = lax.optimization_barrier((dx_own, kept_all))

    grad_stored = jnp.einsum(
        "rts,srd->rtd", own_order, dx_own, preferred_element_type=F32
    )
    grad_stored = jnp.where(pipe == 1, grad_stored, 0.0).astype(BF)
    grad_stored = grad_stored.reshape(1, -1, group_tokens, width)
    grad_encoded = lax.all_to_all(
        jnp.concatenate([grad_stored, grad_stored]).reshape(-1, group_tokens, width),
        ("pipe", "dir"),
        0,
        0,
    )
    grad_encoded = jnp.sum(grad_encoded.astype(F32), axis=0).astype(BF)
    own_grads = lax.dynamic_slice_in_dim(grad_encoded, pipe * tokens, tokens, 0)
    encoded_grads = lax.all_gather(own_grads, ("dir", "dp"), axis=0, tiled=True)

    grad_proj_bias = jnp.sum(own_grads.astype(F32), axis=0)
    proj_half = lax.dynamic_index_in_dim(
        proj_full.reshape(blocks, 2, sub, width), pipe, 1, keepdims=False
    ).reshape(half, width)
    grad_features = jnp.einsum("td,fd->tf", grad_encoded, proj_half, preferred_element_type=F32)
    columns = [None, None]
    grad_highway_bias = [None, None]
    for layer in (1, 0):
        nonlinear = mixed[layer][:, :half]
        gate = jax.nn.sigmoid(mixed[layer][:, half:])
        grad_mixed = jnp.concatenate(
            [
                grad_features * (1.0 - gate) * silu_slope(nonlinear),
                grad_features * (kept[layer] - jax.nn.silu(nonlinear)) * gate * (1.0 - gate),
            ],
            axis=1,
        ).astype(BF)
        columns[layer] = grad_mixed
        grad_highway_bias[layer] = jnp.sum(grad_mixed.astype(F32), axis=0)
        partial = jnp.einsum(
            "tg,fg->tf", grad_mixed, highway_half[layer], preferred_element_type=F32
        )
        partial = lax.optimization_barrier(partial).reshape(group_tokens, blocks, 2, sub)
        sent = lax.dynamic_index_in_dim(partial, 1 - pipe, 2, keepdims=False).astype(BF)
        came = lax.ppermute(sent, "pipe", [(0, 1), (1, 0)])
        mine = lax.dynamic_index_in_dim(partial, pipe, 2, keepdims=False)
        grad_features = grad_features * gate + (mine + came.astype(F32)).reshape(
            group_tokens, half
        )
    grad_before = grad_features * silu_slope(pooled + conv_bias_own)
    grad_before, grad_gate[1:5] = lax.optimization_barrier((grad_before, grad_gate[1:5]))
    grad_conv, grad_table = conv_backward(ids, table_low, conv_low, masks, grad_before)

    def spread(value):
        split = value.reshape(*value.shape[:-1], -1, 1, sub)
        shown = jnp.arange(2, dtype=jnp.int32)[:, None] == pipe
        return jnp.where(shown, split, jnp.zeros_like(split)).reshape(*value.shape[:-1], -1)

    cols = FILTERS // everyone
    pair = jnp.stack(columns, axis=1).reshape(2, tokens, 2, 2, blocks, 1, sub)
    sent = lax.dynamic_index_in_dim(pair, 1 - pipe, 0, keepdims=False)
    came = lax.ppermute(sent, "pipe", [(0, 1), (1, 0)])
    mine = lax.dynamic_index_in_dim(pair, pipe, 0, keepdims=False)
    shown = (jnp.arange(2, dtype=jnp.int32) == pipe)[:, None]
    pair = jnp.where(shown, mine, came)
    pair = jnp.transpose(pair, (3, 4, 0, 1, 2, 5)).reshape(holders, tokens, 4 * sub)
    last = jnp.transpose(own_last.reshape(tokens, 2, holders, cols), (2, 0, 1, 3))
    pair = jnp.concatenate([pair, last.reshape(holders, tokens, 2 * cols)], axis=2)
    pair = lax.all_to_all(pair, ("dir", "dp"), 0, 0).reshape(holders * tokens, -1)
    grad_conv, pair, grad_gate, out_own, grad_cell = lax.optimization_barrier(
        (grad_conv, pair, grad_gate, out_own, grad_cell)
    )
    gate_kept, gate_given = sort_blocks(grad_gate)
    gate_given, pair = lax.optimization_barrier((gate_given, pair))
    gate_came = swap_pipes(gate_given)
    small = (
        grad_table,
        spread(jnp.sum(grad_before, axis=0)),
        spread(jnp.stack(grad_highway_bias)),
        grad_proj_bias,
    )
    flat = jnp.concatenate([value.reshape(-1) for value in small])
    share = -(-flat.shape[0] // (everyone * 128)) * 128
    flat = jnp.pad(flat, (0, share * everyone - flat.shape[0])).reshape(everyone, share)
    rank = pipe * wing + lax.rem(me, wing)
    mine = jnp.arange(n, dtype=jnp.int32)[None, :, None] == rank
    bias_parts = jnp.where(mine, grad_bias.reshape(4, 1, cell), 0.0).reshape(1, n, 4 * cell)
    layer = lax.div(me, wing) * lax.axis_size("dir") + direction
    mine = jnp.arange(everyone // n, dtype=jnp.int32) == layer
    bias_parts = jnp.where(mine[:, None, None], bias_parts, 0.0).reshape(everyone, 4 * cell)
    packed = jnp.concatenate(
        [
            jnp.transpose(
                spread(grad_conv).reshape(KMAX * CDIM, everyone, cols), (1, 0, 2)
            ).reshape(everyone, KMAX * CDIM * cols),
            flat,
            bias_parts,
        ],
        axis=1,
    ).astype(BF)
    summed = jnp.sum(lax.all_to_all(packed, ALL, 0, 0).astype(F32), axis=0)
    out_own = from_ranks(out_own, 0)
    grad_cell = from_ranks(grad_cell.astype(BF), 0)
    summed, out_own, grad_cell, gate_came = lax.optimization_barrier(
        (summed, out_own, grad_cell, gate_came)
    )
    grad_gate = join_cells(gate_kept, gate_came)
    activations = jnp.einsum("rts,srd->rtd", own_order, out_own, preferred_element_type=BF)
    grad_cell = grad_cell.astype(F32)
    grad_conv = summed[: KMAX * CDIM * cols].reshape(KMAX * CDIM, cols)
    grad_bias = summed[KMAX * CDIM * cols + share :]
    last = pair[:, 4 * sub :].reshape(holders * tokens, 2, cols)
    pair = pair[:, : 4 * sub].reshape(holders * tokens, 2, 2, sub)

    def partial_sums(owner):
        return [
            jnp.einsum(
                "tf,tg->fg",
                kept_all[layer],
                lax.dynamic_index_in_dim(pair[:, layer], owner, 1, keepdims=False),
                preferred_element_type=F32,
            )
            for layer in range(2)
        ] + [
            jnp.einsum(
                "tf,td->fd",
                lax.dynamic_index_in_dim(last, owner, 1, keepdims=False),
                encoded_grads,
                preferred_element_type=F32,
            )
        ]

    sent = jnp.concatenate(
        [value.astype(BF).reshape(-1, sub) for value in partial_sums(1 - pipe)]
    )
    came = lax.ppermute(sent, "pipe", [(0, 1), (1, 0)]).astype(F32)
    mine = partial_sums(pipe)
    grad_highway = jnp.stack(mine[:2]) + came[: 2 * FILTERS].reshape(2, FILTERS, sub)
    grad_proj = mine[2] + came[2 * FILTERS :].reshape(cols, width)
    shared = lax.all_to_all(
        jnp.broadcast_to(summed[KMAX * CDIM * cols :][:share], (everyone, share)), ALL, 0, 0
    ).reshape(-1)
    small_sums = []
    start = 0
    for value in small:
        small_sums.append(shared[start : start + value.size].reshape(value.shape))
        start += value.size
    return (
        activations[None, None],
        small_sums[0],
        grad_conv,
        small_sums[1],
        grad_highway,
        small_sums[2],
        grad_proj,
        small_sums[3],
        grad_gate[None, None],
        grad_bias[None, None],
        grad_cell[None, None],
    )


def solution(mesh):
    return jax.shard_map(
        local,
        mesh=mesh,
        in_specs=(
            P("dp", None, None),
            P("dp"),
            P(),
            P(None, ("dir", "dp")),
            P(),
            P(None, None, ("dir", "dp")),
            P(),
            P(("dir", "dp"), None),
            P(),
            P("pipe", "dir", "dp", None),
            P("pipe", "dir", None),
            P("pipe", "dir", "dp", None),
            P("pipe", "dir", "dp", None, None),
        ),
        out_specs=(
            P("pipe", "dir", "dp", None, None),
            P(),
            P(None, ("pipe", "dir", "dp")),
            P(),
            P(None, None, ("pipe", "dir", "dp")),
            P(),
            P(("pipe", "dir", "dp"), None),
            P(),
            P("pipe", "dir", "dp", None),
            P("pipe", "dir", "dp"),
            P("pipe", "dir", "dp", None),
        ),
        check_vma=False,
    )
```

```python
import functools
import math

import jax
import jax.numpy as jnp
from jax import lax
from jax.experimental import pallas as pl
from jax.experimental.pallas import tpu as pltpu
from jax.sharding import PartitionSpec as P

FILTERS = 2048
CDIM = 16
CVOCAB = 262
CHARS = 50
KMAX = 7
CLIP_LIMIT = 3.0
MASKED_FILL = -1000000000.0
MESH = pl.DeviceIdType.MESH
BF = jnp.bfloat16
F32 = jnp.float32
ALL = ("pipe", "dir", "dp")


def silu_slope(value):
    sig = jax.nn.sigmoid(value)
    return sig * (1.0 + value * (1.0 - sig))


def conv_masks(filter_index):
    filter_width = jnp.ones(filter_index.shape, jnp.int32)
    for doubling in range(6):
        filter_width = filter_width + (filter_index >= FILTERS // 64 * (1 << doubling)).astype(
            jnp.int32
        )
    offset_rows = jnp.arange(KMAX * CDIM, dtype=jnp.int32) // CDIM
    weight_mask = (offset_rows[:, None] < filter_width[None, :]).astype(jnp.float32)
    valid_place = jnp.arange(CHARS, dtype=jnp.int32)[:, None] <= CHARS - filter_width[None, :]
    return (weight_mask, valid_place)


def make_windows(embedded):
    padded = jnp.pad(embedded, ((0, 0), (0, KMAX - 1), (0, 0)))
    return jnp.concatenate(
        [padded[:, offset : offset + CHARS, :] for offset in range(KMAX)], axis=2
    )


def conv_response(ids_block, table_low, conv_low, valid_place):
    embedded = jnp.take(table_low, ids_block, axis=0)
    windows = make_windows(embedded)
    response = jnp.einsum("bpk,kf->bpf", windows, conv_low, preferred_element_type=jnp.float32)
    return (windows, jnp.where(valid_place[None], response, MASKED_FILL))


def over(count, step):
    if count <= 9:
        for off in range(count - 1, 0, -1):
            step(off)
    else:
        lax.fori_loop(1, count, lambda off, _: (step(off), 0)[1], 0)


def lstm_kernel(n, chunk, x_own, bias, p, pt, cot, w_in, *refs):
    out_ref, dx_ref, db_ref, dp_ref = refs[:4]
    dw_out = refs[4:n + 4]
    (xbuf, hbuf, dqbuf, gates, cells, ebuf, hown, gscr, escr, dabuf, ucell, dwacc, w, wt,
     stage, inbox, stage2, inbox2, relay, gbuf, rown,
     in_send, in_recv, ag_send, ag_recv, dq_send, dq_recv, rs_send, rs_recv,
     dx_send, dx_recv, x_send, x_recv, g_send, g_recv, st_sem, w_sem) = refs[n + 4:]
    steps, _, rows, width = xbuf.shape
    total = n * rows
    cell = cells.shape[2]
    pipe = lax.axis_index("pipe")
    direction = lax.axis_index("dir")
    place = lax.axis_index("dp")
    wing = n // 2
    first = place >= wing
    second = place < wing
    me = pipe * wing + lax.rem(place, wing)
    base = place - lax.rem(place, wing)
    partner = (pipe, direction, lax.rem(place + wing, n))

    def peer(off):
        if n & (n - 1):
            return lax.rem(me + off, n)
        return me ^ off

    def at_peer(off):
        rank = peer(off)
        return (lax.div(rank, wing), direction, base + lax.rem(rank, wing))

    barrier = pltpu.get_barrier_semaphore()
    over(n, lambda off: pl.semaphore_signal(
        barrier, inc=1, device_id=at_peer(off), device_id_type=MESH))
    pl.semaphore_signal(barrier, inc=1, device_id=partner, device_id_type=MESH)

    each = 2 * width // n
    load = pltpu.make_async_copy(w_in, w, w_sem)
    load.start()

    @pl.when(first)
    def _():
        for t in range(steps):
            xbuf[t, me] = x_own[t]

    hbuf[0] = jnp.zeros((n, rows, width), BF)
    cells[0] = jnp.zeros((total, cell), F32)
    pl.semaphore_wait(barrier, n)

    def ag_copy(buf, slot, off):
        out, into = (ag_send, ag_recv) if buf is hbuf else (dq_send, dq_recv)
        return pltpu.make_async_remote_copy(
            src_ref=buf.at[slot, me], dst_ref=buf.at[slot, me],
            send_sem=out.at[off], recv_sem=into.at[off],
            device_id=at_peer(off), device_id_type=MESH)

    def rs_copy(off):
        return pltpu.make_async_remote_copy(
            src_ref=stage.at[peer(off)], dst_ref=inbox.at[me],
            send_sem=rs_send.at[off], recv_sem=rs_recv.at[off],
            device_id=at_peer(off), device_id_type=MESH)

    def dx_copy(slot, off):
        return pltpu.make_async_remote_copy(
            src_ref=stage2.at[slot, peer(off)], dst_ref=inbox2.at[slot, me],
            send_sem=dx_send.at[slot, off], recv_sem=dx_recv.at[slot, off],
            device_id=at_peer(off), device_id_type=MESH)

    def x_copy(t):
        return pltpu.make_async_remote_copy(
            src_ref=hbuf.at[t + 1, me], dst_ref=xbuf.at[t, me],
            send_sem=x_send.at[t], recv_sem=x_recv.at[t],
            device_id=partner, device_id_type=MESH)

    def g_copy(t):
        return pltpu.make_async_remote_copy(
            src_ref=relay.at[t], dst_ref=gbuf.at[t],
            send_sem=g_send.at[t], recv_sem=g_recv.at[t],
            device_id=partner, device_id_type=MESH)

    def in_start(t):
        over(n, lambda off: pltpu.make_async_remote_copy(
            src_ref=xbuf.at[t, me], dst_ref=xbuf.at[t, me],
            send_sem=in_send.at[t], recv_sem=in_recv.at[t],
            device_id=at_peer(off), device_id_type=MESH).start())

    def in_wait(sem, t):
        blocks = xbuf.at[t, pl.ds(0, n - 1)]
        pltpu.make_async_copy(blocks, blocks, sem.at[t]).wait()

    @pl.when(first)
    def _():
        in_start(0)
        in_start(1)

    @pl.when(second)
    def _():
        x_copy(0).wait_recv()
        in_start(0)

    load.wait()
    for at in range(0, 2 * width, 128):
        wt[:, at:at + 128] = w[at:at + 128, :].T

    def ag_wait(buf, slot):
        def both(off):
            ag_copy(buf, slot, off).wait_send()
            ag_copy(buf, slot, off).wait_recv()
        over(n, both)

    def rs_wait():
        def both(off):
            rs_copy(off).wait_send()
            rs_copy(off).wait_recv()
        over(n, both)

    def forward(t, _):
        in_wait(in_recv, t)
        gscr[...] = jnp.dot(
            xbuf[t].reshape(total, width), w[:width, :], preferred_element_type=F32) + bias[...]

        @pl.when(t > 0)
        def _():
            ag_wait(hbuf, t)

        gscr[...] += jnp.dot(
            hbuf[t].reshape(total, width), w[width:, :], preferred_element_type=F32)

        def rows_step(k, _):
            at = pl.ds(pl.multiple_of(k * chunk, chunk), chunk)
            g = gscr[at, :]
            i = jax.nn.sigmoid(g[:, :cell])
            f = jax.nn.sigmoid(g[:, cell:2 * cell])
            m = jnp.tanh(g[:, 2 * cell:3 * cell])
            o = jax.nn.sigmoid(g[:, 3 * cell:])
            c = 3.0 * jnp.tanh((i * m + f * cells[t, at, :]) * (1.0 / 3.0))
            cells[t + 1, at, :] = c
            ebuf[t, at, :] = (o * jnp.tanh(c)).astype(BF)
            kind = gates.dtype
            gates[t, at, :cell] = i.astype(kind)
            gates[t, at, cell:2 * cell] = f.astype(kind)
            gates[t, at, 2 * cell:3 * cell] = m.astype(kind)
            gates[t, at, 3 * cell:] = o.astype(kind)
            return 0

        lax.fori_loop(0, total // chunk, rows_step, 0)
        q = jnp.dot(ebuf[t], p[...], preferred_element_type=F32)
        stage[...] = q.astype(BF).reshape(n, rows, width)
        over(n, lambda off: rs_copy(off).start())
        inbox[me] = stage[me]

        @pl.when(first & (t + 2 < steps))
        def _():
            in_start(t + 2)

        @pl.when(second & (t + 1 < steps))
        def _():
            x_copy(t + 1).wait_recv()
            in_start(t + 1)

        rs_wait()
        h = 3.0 * jnp.tanh(jnp.sum(inbox[...].astype(F32), axis=0) * (1.0 / 3.0))
        hown[t] = h
        hbuf[t + 1, me] = h.astype(BF)
        over(n, lambda off: ag_copy(hbuf, t + 1, off).start())

        @pl.when(first)
        def _():
            x_copy(t).start()

        add = jnp.where(second, 1.0, 0.0)
        out_ref[t] = (h + add * xbuf[t, me].astype(F32)).astype(BF)
        return 0

    lax.fori_loop(0, steps, forward, 0)
    ag_wait(hbuf, steps)

    lax.fori_loop(0, steps, lambda t, _: (in_wait(in_send, t), 0)[1], 0)

    @pl.when(first)
    def _():
        lax.fori_loop(0, steps, lambda t, _: (x_copy(t).wait_send(), 0)[1], 0)

    rown[...] = jnp.zeros((rows, width), F32)
    ucell[...] = jnp.zeros((total, cell), F32)
    dwacc[...] = jnp.zeros(dwacc.shape, F32)
    db_ref[...] = jnp.zeros(db_ref.shape, F32)
    dp_ref[...] = jnp.zeros(dp_ref.shape, F32)

    def dx_finish(t):
        slot = lax.rem(t, 2)

        def both(off):
            dx_copy(slot, off).wait_send()
            dx_copy(slot, off).wait_recv()
        over(n, both)
        dx = jnp.sum(inbox2[slot].astype(F32), axis=0)
        dx_ref[t] = dx

        @pl.when(second)
        def _():
            relay[t] = (dx + cot[t].astype(F32)).astype(BF)
            g_copy(t).start()

    def backward(k, _):
        t = steps - 1 - k
        slot = lax.rem(t, 2)
        up = rown[...] + cot[t].astype(F32)
        rown[...] = up

        @pl.when(first)
        def _():
            g_copy(t).wait_recv()
            rown[...] = rown[...] + gbuf[t].astype(F32)

        ratio = hown[t] * (1.0 / 3.0)
        dqbuf[t, me] = (rown[...] * (1.0 - ratio * ratio)).astype(BF)
        over(n, lambda off: ag_copy(dqbuf, t, off).start())

        @pl.when(k > 0)
        def _():
            dx_finish(t + 1)

        ag_wait(dqbuf, t)
        escr[...] = jnp.dot(
            dqbuf[t].reshape(total, width), pt[...], preferred_element_type=F32)

        def rows_step(j, _):
            at = pl.ds(pl.multiple_of(j * chunk, chunk), chunk)
            de = escr[at, :]
            i = gates[t, at, :cell].astype(F32)
            f = gates[t, at, cell:2 * cell].astype(F32)
            m = gates[t, at, 2 * cell:3 * cell].astype(F32)
            o = gates[t, at, 3 * cell:].astype(F32)
            c = cells[t + 1, at, :]
            tc = jnp.tanh(c)
            cr = c * (1.0 / 3.0)
            dc = (de * o * (1.0 - tc * tc) + ucell[at, :]) * (1.0 - cr * cr)
            ucell[at, :] = dc * f
            for block, value in enumerate((
                dc * m * i * (1.0 - i),
                dc * cells[t, at, :] * f * (1.0 - f),
                dc * i * (1.0 - m * m),
                de * tc * o * (1.0 - o),
            )):
                value = value.astype(BF)
                where = pl.ds(block * cell, cell)
                dabuf[0, at, where] = value
                db_ref[:, where] += jnp.sum(value.astype(F32), axis=0, keepdims=True)
            return 0

        lax.fori_loop(0, total // chunk, rows_step, 0)
        r = jnp.dot(dabuf[0], wt[:, width:], preferred_element_type=F32)
        stage[...] = r.astype(BF).reshape(n, rows, width)
        over(n, lambda off: rs_copy(off).start())
        inbox[me] = stage[me]
        dx = jnp.dot(dabuf[0], wt[:, :width], preferred_element_type=F32)
        stage2[slot] = dx.astype(BF).reshape(n, rows, width)
        over(n, lambda off: dx_copy(slot, off).start())
        inbox2[slot, me] = stage2[slot, me]
        for half, buf in enumerate((xbuf, hbuf)):
            dwacc[pl.ds(half * width, width), :] += lax.dot_general(
                buf[t].reshape(total, width), dabuf[0], (((0,), (0,)), ((), ())),
                preferred_element_type=F32)
        dp_ref[...] += lax.dot_general(
            ebuf[t], dqbuf[t].reshape(total, width), (((0,), (0,)), ((), ())),
            preferred_element_type=F32)
        rs_wait()
        rown[...] = jnp.sum(inbox[...].astype(F32), axis=0)
        return 0

    lax.fori_loop(0, steps, backward, 0)
    dx_finish(0)

    @pl.when(second)
    def _():
        lax.fori_loop(0, steps, lambda t, _: (g_copy(t).wait_send(), 0)[1], 0)

    def dw_copy(off):
        return pltpu.make_async_copy(
            dabuf.at[off % 2, pl.ds(0, each)], dw_out[off], st_sem.at[off % 2])

    for off in range(n):
        if off > 1:
            dw_copy(off - 2).wait()
        at = pl.multiple_of(lax.rem(me + off, n) * each, each)
        dabuf[off % 2, :each, :] = dwacc[pl.ds(at, each), :].astype(BF)
        dw_copy(off).start()
    for off in range(n - 2, n):
        dw_copy(off).wait()


def lstm_call(n, x, weights, bias, p, pt, cot, chunk=16):
    steps, rows, width = x.shape
    cell = p.shape[0]
    total = n * rows
    sds = jax.ShapeDtypeStruct
    vm = pl.BlockSpec(memory_space=pltpu.VMEM)
    hb = pl.BlockSpec(memory_space=pl.ANY)
    keep = F32 if n <= 8 else BF
    V = pltpu.VMEM
    dma = pltpu.SemaphoreType.DMA
    return pl.pallas_call(
        functools.partial(lstm_kernel, n, chunk),
        out_shape=(
            sds((steps, rows, width), BF), sds((steps, rows, width), F32),
            sds((1, 4 * cell), F32), sds((cell, width), F32),
            *[sds((2 * width // n, 4 * cell), BF)] * n),
        in_specs=[vm] * 5 + [hb],
        out_specs=[vm] * 4 + [hb] * n,
        scratch_shapes=[
            V((steps, n, rows, width), BF), V((steps + 1, n, rows, width), BF),
            V((steps, n, rows, width), BF), V((steps, total, 4 * cell), keep),
            V((steps + 1, total, cell), F32), V((steps, total, cell), BF),
            V((steps, rows, width), F32), V((total, 4 * cell), F32),
            V((total, cell), F32), V((2, total, 4 * cell), BF), V((total, cell), F32),
            V((2 * width, 4 * cell), F32), V((2 * width, 4 * cell), BF),
            V((4 * cell, 2 * width), BF),
            V((n, rows, width), BF), V((n, rows, width), BF),
            V((2, n, rows, width), BF), V((2, n, rows, width), BF),
            V((steps, rows, width), BF), V((steps, rows, width), BF), V((rows, width), F32),
            dma((steps,)), dma((steps,)), dma((n,)), dma((n,)), dma((n,)), dma((n,)), dma((n,)), dma((n,)), dma((2, n)), dma((2, n)),
            dma((steps,)), dma((steps,)), dma((steps,)), dma((steps,)), dma((2,)), dma,
        ],
        compiler_params=pltpu.CompilerParams(
            collective_id=0, has_side_effects=True, vmem_limit_bytes=60 * 1024 * 1024),
        cost_estimate=pl.CostEstimate(
            flops=300_000_000_000, bytes_accessed=64 * 1024 * 1024, transcendentals=0),
        name="relay_lstm",
    )(x, bias, p, pt, cot, weights)


def split_cells(weight, n):
    rows, gates = weight.shape
    cell = gates // (4 * n)
    wing = n // 2

    def body(src, keep, give):
        pipe = lax.axis_index("pipe")
        for k in range(wing):
            for dst, side in ((keep, pipe), (give, 1 - pipe)):
                at = pl.multiple_of((side * wing + k) * cell, cell)
                dst[k] = src[:, pl.ds(at, cell)].astype(BF)

    return pl.pallas_call(
        body,
        grid=(4,),
        out_shape=[jax.ShapeDtypeStruct((wing, rows, 4 * cell), BF)] * 2,
        in_specs=[pl.BlockSpec((rows, n * cell), lambda b: (0, b))],
        out_specs=[pl.BlockSpec((wing, rows, cell), lambda b: (0, 0, b))] * 2,
        cost_estimate=pl.CostEstimate(
            flops=0, bytes_accessed=6 * rows * gates, transcendentals=0
        ),
        name="split_cells",
    )(weight)


def join_cells(blocks):
    n = len(blocks)
    rows, gates = blocks[0].shape
    cell = gates // 4

    def body(*refs):
        dst = refs[n]
        for off in range(n):
            rank = lax.rem(lax.axis_index("dp") + (n - off), n)
            dst[:, pl.ds(pl.multiple_of(rank * cell, cell), cell)] = refs[off][...].astype(F32)

    return pl.pallas_call(
        body,
        grid=(4,),
        out_shape=jax.ShapeDtypeStruct((rows, n * gates), F32),
        in_specs=[pl.BlockSpec((rows, cell), lambda b: (0, b))] * n,
        out_specs=pl.BlockSpec((rows, n * cell), lambda b: (0, b)),
        cost_estimate=pl.CostEstimate(
            flops=0, bytes_accessed=6 * n * rows * gates, transcendentals=0
        ),
        name="join_cells",
    )(*blocks)


def swap_pipes(value):
    return lax.ppermute(value, "pipe", [(0, 1), (1, 0)])


def rank_pairs(n, off, layers=(0, 1)):
    wing = n // 2
    pairs = []
    for layer in layers:
        for j in range(n):
            rank = (j + off) % n
            pairs.append((layer * n + j, rank // wing * n + layer * wing + rank % wing))
    return pairs


def to_ranks(value, off):
    return lax.ppermute(value, ("pipe", "dp"), rank_pairs(lax.axis_size("dp"), off))


def from_ranks(value, off, layers=(0, 1)):
    pairs = rank_pairs(lax.axis_size("dp"), -off, layers)
    return lax.ppermute(value, ("pipe", "dp"), [(there, here) for here, there in pairs])


def conv_forward(ids, table_low, conv_low, valid_place):
    return jax.nn.logsumexp(conv_response(ids, table_low, conv_low, valid_place)[1], axis=1)


def own_half(value, blocks):
    sub = value.shape[-1] // (2 * blocks)
    split = value.reshape(*value.shape[:-1], blocks, 2, sub)
    mine = lax.dynamic_index_in_dim(split, lax.axis_index("pipe"), split.ndim - 2, keepdims=False)
    return mine.reshape(*value.shape[:-1], blocks * sub)


def both_halves(value, blocks):
    tokens, half = value.shape
    pair = lax.all_gather(value, "pipe").reshape(2, tokens, blocks, half // blocks)
    return jnp.transpose(pair, (1, 2, 0, 3)).reshape(tokens, 2 * half)


def conv_backward(ids, table_low, conv_low, masks, grad_before):
    weight_mask, valid_place = masks
    windows, response = conv_response(ids, table_low, conv_low, valid_place)
    share = jax.nn.softmax(response, axis=1)
    grad_response = (grad_before[:, None, :] * share).astype(BF)
    grad_conv = jnp.einsum("bpk,bpf->kf", windows, grad_response, preferred_element_type=F32)
    grad_windows = jnp.einsum("bpf,kf->bpk", grad_response, conv_low, preferred_element_type=F32)
    grad_embedded = jnp.zeros((ids.shape[0], CHARS + KMAX - 1, CDIM), F32)
    for offset in range(KMAX):
        grad_embedded = grad_embedded + jnp.pad(
            grad_windows[:, :, offset * CDIM : (offset + 1) * CDIM],
            ((0, 0), (offset, KMAX - 1 - offset), (0, 0)),
        )
    grad_embedded = grad_embedded[:, :CHARS].astype(BF)
    one_hot = (ids[:, :, None] == jnp.arange(CVOCAB, dtype=jnp.int32)).astype(BF)
    grad_table = jnp.einsum("bpv,bpc->vc", one_hot, grad_embedded, preferred_element_type=F32)
    return grad_conv * weight_mask, grad_table


def local(
    chars,
    lengths,
    char_emb,
    conv_weight,
    conv_bias,
    highway_weight,
    highway_bias,
    proj_weight,
    proj_bias,
    gate_weight,
    gate_bias,
    cell_proj,
    cotangent,
):
    n = lax.axis_size("dp")
    pipe = lax.axis_index("pipe")
    direction = lax.axis_index("dir")
    me = lax.axis_index("dp")
    everyone = lax.axis_size(ALL)
    holders = lax.axis_size(("dir", "dp"))
    seqs, steps, char_count = chars.shape
    group = seqs // lax.axis_size("dir")
    quarter = group // 2
    group_tokens = group * steps
    tokens = quarter * steps
    width = cell_proj.shape[3]
    cell = cell_proj.shape[2]
    blocks = holders // 2
    sub = FILTERS // holders
    half = FILTERS // 2
    filter_index = (
        (2 * jnp.arange(blocks, dtype=jnp.int32) + pipe)[:, None] * sub
        + jnp.arange(sub, dtype=jnp.int32)[None, :]
    ).reshape(half)
    masks = conv_masks(filter_index)

    proj_rows = proj_weight.shape[0]
    pieces = width // sub
    proj_blocks = jnp.transpose(proj_weight.reshape(proj_rows, pieces, sub), (1, 0, 2))
    proj_blocks = proj_blocks.reshape(2, pieces * proj_rows // 2, sub)
    mine = lax.dynamic_slice_in_dim(highway_weight, pipe * sub, sub, 2)
    gathered = lax.all_gather(
        jnp.concatenate([mine, proj_blocks], axis=1).astype(BF), ("dir", "dp"), axis=2, tiled=True
    )
    conv_full = lax.all_to_all(
        jnp.broadcast_to(conv_weight.astype(BF), (holders, KMAX * CDIM, sub)), ("dir", "dp"), 0, 0
    ).reshape(blocks, 2, KMAX * CDIM, sub)
    conv_low = lax.dynamic_index_in_dim(conv_full, pipe, 1, keepdims=False)
    conv_low = jnp.transpose(conv_low, (1, 0, 2)).reshape(KMAX * CDIM, half)
    conv_low = conv_low * masks[0].astype(BF)
    conv_bias_own = own_half(conv_bias, blocks)
    highway_bias_own = own_half(highway_bias.reshape(2, 2, FILTERS), blocks).reshape(2, FILTERS)

    def order_matrix(sizes):
        place = jnp.arange(steps, dtype=jnp.int32)[None, :]
        live = place < sizes[:, None]
        order = jnp.where(live & (direction == 1), sizes[:, None] - 1 - place, place)
        return ((order[:, :, None] == place[:, None, :]) & live[:, :, None]).astype(BF)

    own_order = order_matrix(lengths)
    cot = jnp.einsum("rts,rsd->trd", own_order, cotangent[0, 0], preferred_element_type=BF)

    ids = lax.dynamic_slice_in_dim(chars, direction * group, group, 0).reshape(
        group_tokens, char_count
    )
    table_low = char_emb.astype(BF)
    pooled = conv_forward(ids, table_low, conv_low, masks[1])
    features = jax.nn.silu(pooled + conv_bias_own)
    features_low = both_halves(features.astype(BF), blocks)
    bias_own = lax.dynamic_index_in_dim(
        gate_bias[0, 0].reshape(4, n, cell), me, 1, keepdims=False
    ).reshape(1, 4 * cell)
    moved = jnp.concatenate([cell_proj[0, 0].astype(BF), cot.reshape(steps * seqs, width)])
    gate_kept, gate_given = split_cells(gate_weight[0, 0], n)
    gate_came = swap_pipes(gate_given)
    gate_low = jnp.concatenate(
        [
            jnp.where(pipe == 0, gate_kept, gate_came),
            jnp.where(pipe == 0, gate_came, gate_kept),
        ]
    )
    direct, local_part = moved[: moved.shape[0] // 2], moved[moved.shape[0] // 2 :]
    swapped = swap_pipes(local_part)
    gate_low, gathered, features_low, bias_own, direct, swapped = lax.optimization_barrier(
        (gate_low, gathered, features_low, bias_own, direct, swapped)
    )
    bias_own = to_ranks(bias_own, 0)
    wing = n // 2
    swapped = lax.ppermute(
        swapped,
        ("pipe", "dp"),
        [(k, wing + k) for k in range(wing)] + [(n + wing + k, n + k) for k in range(wing)],
    )
    moved = jnp.concatenate(
        [to_ranks(direct, 0), jnp.where(lax.div(me, wing) == pipe, local_part, swapped)]
    )
    gate_own = lax.all_to_all(gate_low, "dp", 0, 0).reshape(2 * width, 4 * cell)
    highway_half = gathered[:, :FILTERS]
    proj_full = gathered[:, FILTERS:].reshape(pieces, proj_rows, holders, sub)
    proj_full = jnp.transpose(proj_full, (2, 1, 0, 3)).reshape(FILTERS, width)

    kept = [features]
    kept_low = [features_low]
    mixed = []
    for layer in range(2):
        pre = (
            jnp.dot(kept_low[layer], highway_half[layer], preferred_element_type=F32)
            + highway_bias_own[layer]
        )
        mixed.append(pre)
        gate = jax.nn.sigmoid(pre[:, half:])
        features = gate * features + (1.0 - gate) * jax.nn.silu(pre[:, :half])
        kept.append(features)
        kept_low.append(both_halves(features.astype(BF), blocks))
    own_last = lax.dynamic_slice_in_dim(kept_low[2], pipe * tokens, tokens, 0)
    encoded = jnp.dot(own_last, proj_full, preferred_element_type=F32) + proj_bias
    encoded_own = lax.all_gather(
        encoded.astype(BF).reshape(quarter, steps, width), ("dir", "pipe"), axis=0, tiled=True
    )
    inputs = jnp.einsum("rts,rsd->trd", own_order, encoded_own, preferred_element_type=BF)
    inputs = lax.ppermute(
        inputs,
        ("pipe", "dp"),
        [(k, wing + k) for k in range(wing)] + [(n + k, n + k) for k in range(wing, n)],
    )
    kept_low, gate_own, inputs, moved, bias_own = lax.optimization_barrier(
        (kept_low, gate_own, inputs, moved, bias_own)
    )
    cell_low = moved[:cell]
    cot = moved[cell:].reshape(steps, seqs, width)
    kept_all = [
        lax.all_gather(
            lax.dynamic_slice_in_dim(value, pipe * tokens, tokens, 0),
            ("dir", "dp"),
            axis=0,
            tiled=True,
        )
        for value in kept_low[:2]
    ]

    out_own, dx_own, grad_bias, grad_cell, *grad_gate = lstm_call(
        n, inputs, gate_own, bias_own, cell_low, cell_low.T, cot
    )
    dx_own = from_ranks(dx_own.astype(BF), 0, (1,))
    grad_gate = [from_ranks(block, off) for off, block in enumerate(grad_gate)]
    dx_own, kept_all = lax.optimization_barrier((dx_own, kept_all))

    grad_stored = jnp.einsum(
        "rts,srd->rtd", own_order, dx_own, preferred_element_type=F32
    )
    grad_stored = jnp.where(pipe == 1, grad_stored, 0.0).astype(BF)
    grad_stored = grad_stored.reshape(1, -1, group_tokens, width)
    grad_encoded = lax.all_to_all(
        jnp.concatenate([grad_stored, grad_stored]).reshape(-1, group_tokens, width),
        ("pipe", "dir"),
        0,
        0,
    )
    grad_encoded = jnp.sum(grad_encoded.astype(F32), axis=0).astype(BF)
    own_grads = lax.dynamic_slice_in_dim(grad_encoded, pipe * tokens, tokens, 0)
    encoded_grads = lax.all_gather(own_grads, ("dir", "dp"), axis=0, tiled=True)

    grad_proj_bias = jnp.sum(own_grads.astype(F32), axis=0)
    proj_half = lax.dynamic_index_in_dim(
        proj_full.reshape(blocks, 2, sub, width), pipe, 1, keepdims=False
    ).reshape(half, width)
    grad_features = jnp.einsum("td,fd->tf", grad_encoded, proj_half, preferred_element_type=F32)
    columns = [None, None]
    grad_highway_bias = [None, None]
    for layer in (1, 0):
        nonlinear = mixed[layer][:, :half]
        gate = jax.nn.sigmoid(mixed[layer][:, half:])
        grad_mixed = jnp.concatenate(
            [
                grad_features * (1.0 - gate) * silu_slope(nonlinear),
                grad_features * (kept[layer] - jax.nn.silu(nonlinear)) * gate * (1.0 - gate),
            ],
            axis=1,
        ).astype(BF)
        columns[layer] = grad_mixed
        grad_highway_bias[layer] = jnp.sum(grad_mixed.astype(F32), axis=0)
        partial = jnp.einsum(
            "tg,fg->tf", grad_mixed, highway_half[layer], preferred_element_type=F32
        )
        partial = lax.optimization_barrier(partial).reshape(group_tokens, blocks, 2, sub)
        sent = lax.dynamic_index_in_dim(partial, 1 - pipe, 2, keepdims=False).astype(BF)
        came = lax.ppermute(sent, "pipe", [(0, 1), (1, 0)])
        mine = lax.dynamic_index_in_dim(partial, pipe, 2, keepdims=False)
        grad_features = grad_features * gate + (mine + came.astype(F32)).reshape(
            group_tokens, half
        )
    grad_before = grad_features * silu_slope(pooled + conv_bias_own)
    grad_before, grad_gate[1:5] = lax.optimization_barrier((grad_before, grad_gate[1:5]))
    grad_conv, grad_table = conv_backward(ids, table_low, conv_low, masks, grad_before)

    def spread(value):
        split = value.reshape(*value.shape[:-1], -1, 1, sub)
        shown = jnp.arange(2, dtype=jnp.int32)[:, None] == pipe
        return jnp.where(shown, split, jnp.zeros_like(split)).reshape(*value.shape[:-1], -1)

    cols = FILTERS // everyone
    pair = jnp.stack(columns, axis=1).reshape(2, tokens, 2, 2, blocks, 1, sub)
    sent = lax.dynamic_index_in_dim(pair, 1 - pipe, 0, keepdims=False)
    came = lax.ppermute(sent, "pipe", [(0, 1), (1, 0)])
    mine = lax.dynamic_index_in_dim(pair, pipe, 0, keepdims=False)
    shown = (jnp.arange(2, dtype=jnp.int32) == pipe)[:, None]
    pair = jnp.where(shown, mine, came)
    pair = jnp.transpose(pair, (3, 4, 0, 1, 2, 5)).reshape(holders, tokens, 4 * sub)
    last = jnp.transpose(own_last.reshape(tokens, 2, holders, cols), (2, 0, 1, 3))
    pair = jnp.concatenate([pair, last.reshape(holders, tokens, 2 * cols)], axis=2)
    pair = lax.all_to_all(pair, ("dir", "dp"), 0, 0).reshape(holders * tokens, -1)
    grad_conv, pair, out_own, grad_cell = lax.optimization_barrier(
        (grad_conv, pair, out_own, grad_cell)
    )
    small = (
        grad_table,
        spread(jnp.sum(grad_before, axis=0)),
        spread(jnp.stack(grad_highway_bias)),
        grad_proj_bias,
    )
    flat = jnp.concatenate([value.reshape(-1) for value in small])
    share = -(-flat.shape[0] // (everyone * 128)) * 128
    flat = jnp.pad(flat, (0, share * everyone - flat.shape[0])).reshape(everyone, share)
    rank = pipe * wing + lax.rem(me, wing)
    mine = jnp.arange(n, dtype=jnp.int32)[None, :, None] == rank
    bias_parts = jnp.where(mine, grad_bias.reshape(4, 1, cell), 0.0).reshape(1, n, 4 * cell)
    layer = lax.div(me, wing) * lax.axis_size("dir") + direction
    mine = jnp.arange(everyone // n, dtype=jnp.int32) == layer
    bias_parts = jnp.where(mine[:, None, None], bias_parts, 0.0).reshape(everyone, 4 * cell)
    packed = jnp.concatenate(
        [
            jnp.transpose(
                spread(grad_conv).reshape(KMAX * CDIM, everyone, cols), (1, 0, 2)
            ).reshape(everyone, KMAX * CDIM * cols),
            flat,
            bias_parts,
        ],
        axis=1,
    ).astype(BF)
    summed = jnp.sum(lax.all_to_all(packed, ALL, 0, 0).astype(F32), axis=0)
    out_own = from_ranks(out_own, 0)
    grad_cell = from_ranks(grad_cell.astype(BF), 0)
    summed, grad_gate = lax.optimization_barrier((summed, grad_gate))
    grad_gate = join_cells(grad_gate)
    activations = jnp.einsum("rts,srd->rtd", own_order, out_own, preferred_element_type=BF)
    grad_cell = grad_cell.astype(F32)
    grad_conv = summed[: KMAX * CDIM * cols].reshape(KMAX * CDIM, cols)
    grad_bias = summed[KMAX * CDIM * cols + share :]
    last = pair[:, 4 * sub :].reshape(holders * tokens, 2, cols)
    pair = pair[:, : 4 * sub].reshape(holders * tokens, 2, 2, sub)

    def partial_sums(owner):
        return [
            jnp.einsum(
                "tf,tg->fg",
                kept_all[layer],
                lax.dynamic_index_in_dim(pair[:, layer], owner, 1, keepdims=False),
                preferred_element_type=F32,
            )
            for layer in range(2)
        ] + [
            jnp.einsum(
                "tf,td->fd",
                lax.dynamic_index_in_dim(last, owner, 1, keepdims=False),
                encoded_grads,
                preferred_element_type=F32,
            )
        ]

    sent = jnp.concatenate(
        [value.astype(BF).reshape(-1, sub) for value in partial_sums(1 - pipe)]
    )
    came = lax.ppermute(sent, "pipe", [(0, 1), (1, 0)]).astype(F32)
    mine = partial_sums(pipe)
    grad_highway = jnp.stack(mine[:2]) + came[: 2 * FILTERS].reshape(2, FILTERS, sub)
    grad_proj = mine[2] + came[2 * FILTERS :].reshape(cols, width)
    shared = lax.all_to_all(
        jnp.broadcast_to(summed[KMAX * CDIM * cols :][:share], (everyone, share)), ALL, 0, 0
    ).reshape(-1)
    small_sums = []
    start = 0
    for value in small:
        small_sums.append(shared[start : start + value.size].reshape(value.shape))
        start += value.size
    return (
        activations[None, None],
        small_sums[0],
        grad_conv,
        small_sums[1],
        grad_highway,
        small_sums[2],
        grad_proj,
        small_sums[3],
        grad_gate[None, None],
        grad_bias[None, None],
        grad_cell[None, None],
    )


def solution(mesh):
    return jax.shard_map(
        local,
        mesh=mesh,
        in_specs=(
            P("dp", None, None),
            P("dp"),
            P(),
            P(None, ("dir", "dp")),
            P(),
            P(None, None, ("dir", "dp")),
            P(),
            P(("dir", "dp"), None),
            P(),
            P("pipe", "dir", "dp", None),
            P("pipe", "dir", None),
            P("pipe", "dir", "dp", None),
            P("pipe", "dir", "dp", None, None),
        ),
        out_specs=(
            P("pipe", "dir", "dp", None, None),
            P(),
            P(None, ("pipe", "dir", "dp")),
            P(),
            P(None, None, ("pipe", "dir", "dp")),
            P(),
            P(("pipe", "dir", "dp"), None),
            P(),
            P("pipe", "dir", "dp", None),
            P("pipe", "dir", "dp"),
            P("pipe", "dir", "dp", None),
        ),
        check_vma=False,
    )
```

```python
import functools
import math

import jax
import jax.numpy as jnp
from jax import lax
from jax.experimental import pallas as pl
from jax.experimental.pallas import tpu as pltpu
from jax.sharding import PartitionSpec as P

FILTERS = 2048
CDIM = 16
CVOCAB = 262
CHARS = 50
KMAX = 7
CLIP_LIMIT = 3.0
MASKED_FILL = -1000000000.0
MESH = pl.DeviceIdType.MESH
BF = jnp.bfloat16
F32 = jnp.float32
ALL = ("pipe", "dir", "dp")


def silu_slope(value):
    sig = jax.nn.sigmoid(value)
    return sig * (1.0 + value * (1.0 - sig))


def conv_masks(filter_index):
    filter_width = jnp.ones(filter_index.shape, jnp.int32)
    for doubling in range(6):
        filter_width = filter_width + (filter_index >= FILTERS // 64 * (1 << doubling)).astype(
            jnp.int32
        )
    offset_rows = jnp.arange(KMAX * CDIM, dtype=jnp.int32) // CDIM
    weight_mask = (offset_rows[:, None] < filter_width[None, :]).astype(jnp.float32)
    valid_place = jnp.arange(CHARS, dtype=jnp.int32)[:, None] <= CHARS - filter_width[None, :]
    return (weight_mask, valid_place)


def make_windows(embedded):
    padded = jnp.pad(embedded, ((0, 0), (0, KMAX - 1), (0, 0)))
    return jnp.concatenate(
        [padded[:, offset : offset + CHARS, :] for offset in range(KMAX)], axis=2
    )


def conv_response(ids_block, table_low, conv_low, valid_place):
    embedded = jnp.take(table_low, ids_block, axis=0)
    windows = make_windows(embedded)
    response = jnp.einsum("bpk,kf->bpf", windows, conv_low, preferred_element_type=jnp.float32)
    return (windows, jnp.where(valid_place[None], response, MASKED_FILL))


def over(count, step):
    if count <= 9:
        for off in range(count - 1, 0, -1):
            step(off)
    else:
        lax.fori_loop(1, count, lambda off, _: (step(off), 0)[1], 0)


def lstm_kernel(n, chunk, x_own, bias, p, pt, cot, w_in, *refs):
    out_ref, dx_ref, db_ref, dp_ref = refs[:4]
    dw_out = refs[4:n + 4]
    (xbuf, hbuf, dqbuf, gates, cells, ebuf, hown, gscr, escr, dabuf, ucell, dwacc, w, wt,
     stage, inbox, stage2, inbox2, relay, gbuf, rown,
     in_send, in_recv, ag_send, ag_recv, dq_send, dq_recv, rs_send, rs_recv,
     dx_send, dx_recv, x_send, x_recv, g_send, g_recv, st_sem, w_sem) = refs[n + 4:]
    steps, _, rows, width = xbuf.shape
    total = n * rows
    cell = cells.shape[2]
    pipe = lax.axis_index("pipe")
    direction = lax.axis_index("dir")
    place = lax.axis_index("dp")
    wing = n // 2
    first = place >= wing
    second = place < wing
    me = pipe * wing + lax.rem(place, wing)
    base = place - lax.rem(place, wing)
    partner = (pipe, direction, lax.rem(place + wing, n))

    def peer(off):
        if n & (n - 1):
            return lax.rem(me + off, n)
        return me ^ off

    def at_peer(off):
        rank = peer(off)
        return (lax.div(rank, wing), direction, base + lax.rem(rank, wing))

    barrier = pltpu.get_barrier_semaphore()
    over(n, lambda off: pl.semaphore_signal(
        barrier, inc=1, device_id=at_peer(off), device_id_type=MESH))
    pl.semaphore_signal(barrier, inc=1, device_id=partner, device_id_type=MESH)

    each = 2 * width // n
    load = pltpu.make_async_copy(w_in, w, w_sem)
    load.start()

    @pl.when(first)
    def _():
        for t in range(steps):
            xbuf[t, me] = x_own[t]

    hbuf[0] = jnp.zeros((n, rows, width), BF)
    cells[0] = jnp.zeros((total, cell), F32)
    pl.semaphore_wait(barrier, n)

    def ag_copy(buf, slot, off):
        out, into = (ag_send, ag_recv) if buf is hbuf else (dq_send, dq_recv)
        return pltpu.make_async_remote_copy(
            src_ref=buf.at[slot, me], dst_ref=buf.at[slot, me],
            send_sem=out.at[off], recv_sem=into.at[off],
            device_id=at_peer(off), device_id_type=MESH)

    def rs_copy(off):
        return pltpu.make_async_remote_copy(
            src_ref=stage.at[peer(off)], dst_ref=inbox.at[me],
            send_sem=rs_send.at[off], recv_sem=rs_recv.at[off],
            device_id=at_peer(off), device_id_type=MESH)

    def dx_copy(slot, off):
        return pltpu.make_async_remote_copy(
            src_ref=stage2.at[slot, peer(off)], dst_ref=inbox2.at[slot, me],
            send_sem=dx_send.at[slot, off], recv_sem=dx_recv.at[slot, off],
            device_id=at_peer(off), device_id_type=MESH)

    def x_copy(t):
        return pltpu.make_async_remote_copy(
            src_ref=hbuf.at[t + 1, me], dst_ref=xbuf.at[t, me],
            send_sem=x_send.at[t], recv_sem=x_recv.at[t],
            device_id=partner, device_id_type=MESH)

    def g_copy(t):
        return pltpu.make_async_remote_copy(
            src_ref=relay.at[t], dst_ref=gbuf.at[t],
            send_sem=g_send.at[t], recv_sem=g_recv.at[t],
            device_id=partner, device_id_type=MESH)

    def in_start(t):
        over(n, lambda off: pltpu.make_async_remote_copy(
            src_ref=xbuf.at[t, me], dst_ref=xbuf.at[t, me],
            send_sem=in_send.at[t], recv_sem=in_recv.at[t],
            device_id=at_peer(off), device_id_type=MESH).start())

    def in_wait(sem, t):
        blocks = xbuf.at[t, pl.ds(0, n - 1)]
        pltpu.make_async_copy(blocks, blocks, sem.at[t]).wait()

    @pl.when(first)
    def _():
        in_start(0)
        in_start(1)

    @pl.when(second)
    def _():
        x_copy(0).wait_recv()
        in_start(0)

    load.wait()
    for at in range(0, 2 * width, 128):
        wt[:, at:at + 128] = w[at:at + 128, :].T

    def ag_wait(buf, slot):
        def both(off):
            ag_copy(buf, slot, off).wait_send()
            ag_copy(buf, slot, off).wait_recv()
        over(n, both)

    def rs_wait():
        def both(off):
            rs_copy(off).wait_send()
            rs_copy(off).wait_recv()
        over(n, both)

    def forward(t, _):
        in_wait(in_recv, t)
        gscr[...] = jnp.dot(
            xbuf[t].reshape(total, width), w[:width, :], preferred_element_type=F32) + bias[...]

        @pl.when(t > 0)
        def _():
            ag_wait(hbuf, t)

        gscr[...] += jnp.dot(
            hbuf[t].reshape(total, width), w[width:, :], preferred_element_type=F32)

        def rows_step(k, _):
            at = pl.ds(pl.multiple_of(k * chunk, chunk), chunk)
            g = gscr[at, :]
            i = jax.nn.sigmoid(g[:, :cell])
            f = jax.nn.sigmoid(g[:, cell:2 * cell])
            m = jnp.tanh(g[:, 2 * cell:3 * cell])
            o = jax.nn.sigmoid(g[:, 3 * cell:])
            c = 3.0 * jnp.tanh((i * m + f * cells[t, at, :]) * (1.0 / 3.0))
            cells[t + 1, at, :] = c
            ebuf[t, at, :] = (o * jnp.tanh(c)).astype(BF)
            kind = gates.dtype
            gates[t, at, :cell] = i.astype(kind)
            gates[t, at, cell:2 * cell] = f.astype(kind)
            gates[t, at, 2 * cell:3 * cell] = m.astype(kind)
            gates[t, at, 3 * cell:] = o.astype(kind)
            return 0

        lax.fori_loop(0, total // chunk, rows_step, 0)
        q = jnp.dot(ebuf[t], p[...], preferred_element_type=F32)
        stage[...] = q.astype(BF).reshape(n, rows, width)
        over(n, lambda off: rs_copy(off).start())
        inbox[me] = stage[me]

        @pl.when(first & (t + 2 < steps))
        def _():
            in_start(t + 2)

        @pl.when(second & (t + 1 < steps))
        def _():
            x_copy(t + 1).wait_recv()
            in_start(t + 1)

        rs_wait()
        h = 3.0 * jnp.tanh(jnp.sum(inbox[...].astype(F32), axis=0) * (1.0 / 3.0))
        hown[t] = h
        hbuf[t + 1, me] = h.astype(BF)
        over(n, lambda off: ag_copy(hbuf, t + 1, off).start())

        @pl.when(first)
        def _():
            x_copy(t).start()

        add = jnp.where(second, 1.0, 0.0)
        out_ref[t] = (h + add * xbuf[t, me].astype(F32)).astype(BF)
        return 0

    lax.fori_loop(0, steps, forward, 0)
    ag_wait(hbuf, steps)

    lax.fori_loop(0, steps, lambda t, _: (in_wait(in_send, t), 0)[1], 0)

    @pl.when(first)
    def _():
        lax.fori_loop(0, steps, lambda t, _: (x_copy(t).wait_send(), 0)[1], 0)

    rown[...] = jnp.zeros((rows, width), F32)
    ucell[...] = jnp.zeros((total, cell), F32)
    dwacc[...] = jnp.zeros(dwacc.shape, F32)
    db_ref[...] = jnp.zeros(db_ref.shape, F32)
    dp_ref[...] = jnp.zeros(dp_ref.shape, F32)

    def dx_finish(t):
        slot = lax.rem(t, 2)

        def both(off):
            dx_copy(slot, off).wait_send()
            dx_copy(slot, off).wait_recv()
        over(n, both)
        dx = jnp.sum(inbox2[slot].astype(F32), axis=0)
        dx_ref[t] = dx

        @pl.when(second)
        def _():
            relay[t] = (dx + cot[t].astype(F32)).astype(BF)
            g_copy(t).start()

    def backward(k, _):
        t = steps - 1 - k
        slot = lax.rem(t, 2)
        up = rown[...] + cot[t].astype(F32)
        rown[...] = up

        @pl.when(first)
        def _():
            g_copy(t).wait_recv()
            rown[...] = rown[...] + gbuf[t].astype(F32)

        ratio = hown[t] * (1.0 / 3.0)
        dqbuf[t, me] = (rown[...] * (1.0 - ratio * ratio)).astype(BF)
        over(n, lambda off: ag_copy(dqbuf, t, off).start())

        @pl.when(k > 0)
        def _():
            dx_finish(t + 1)

        ag_wait(dqbuf, t)
        escr[...] = jnp.dot(
            dqbuf[t].reshape(total, width), pt[...], preferred_element_type=F32)

        def rows_step(j, _):
            at = pl.ds(pl.multiple_of(j * chunk, chunk), chunk)
            de = escr[at, :]
            i = gates[t, at, :cell].astype(F32)
            f = gates[t, at, cell:2 * cell].astype(F32)
            m = gates[t, at, 2 * cell:3 * cell].astype(F32)
            o = gates[t, at, 3 * cell:].astype(F32)
            c = cells[t + 1, at, :]
            tc = jnp.tanh(c)
            cr = c * (1.0 / 3.0)
            dc = (de * o * (1.0 - tc * tc) + ucell[at, :]) * (1.0 - cr * cr)
            ucell[at, :] = dc * f
            for block, value in enumerate((
                dc * m * i * (1.0 - i),
                dc * cells[t, at, :] * f * (1.0 - f),
                dc * i * (1.0 - m * m),
                de * tc * o * (1.0 - o),
            )):
                value = value.astype(BF)
                where = pl.ds(block * cell, cell)
                dabuf[0, at, where] = value
                db_ref[:, where] += jnp.sum(value.astype(F32), axis=0, keepdims=True)
            return 0

        lax.fori_loop(0, total // chunk, rows_step, 0)
        r = jnp.dot(dabuf[0], wt[:, width:], preferred_element_type=F32)
        stage[...] = r.astype(BF).reshape(n, rows, width)
        over(n, lambda off: rs_copy(off).start())
        inbox[me] = stage[me]
        dx = jnp.dot(dabuf[0], wt[:, :width], preferred_element_type=F32)
        stage2[slot] = dx.astype(BF).reshape(n, rows, width)
        over(n, lambda off: dx_copy(slot, off).start())
        inbox2[slot, me] = stage2[slot, me]
        for half, buf in enumerate((xbuf, hbuf)):
            dwacc[pl.ds(half * width, width), :] += lax.dot_general(
                buf[t].reshape(total, width), dabuf[0], (((0,), (0,)), ((), ())),
                preferred_element_type=F32)
        dp_ref[...] += lax.dot_general(
            ebuf[t], dqbuf[t].reshape(total, width), (((0,), (0,)), ((), ())),
            preferred_element_type=F32)
        rs_wait()
        rown[...] = jnp.sum(inbox[...].astype(F32), axis=0)
        return 0

    lax.fori_loop(0, steps, backward, 0)
    dx_finish(0)

    @pl.when(second)
    def _():
        lax.fori_loop(0, steps, lambda t, _: (g_copy(t).wait_send(), 0)[1], 0)

    def dw_copy(off):
        return pltpu.make_async_copy(
            dabuf.at[off % 2, pl.ds(0, each)], dw_out[off], st_sem.at[off % 2])

    for off in range(n):
        if off > 1:
            dw_copy(off - 2).wait()
        at = pl.multiple_of(lax.rem(me + off, n) * each, each)
        dabuf[off % 2, :each, :] = dwacc[pl.ds(at, each), :].astype(BF)
        dw_copy(off).start()
    for off in range(n - 2, n):
        dw_copy(off).wait()


def lstm_call(n, x, weights, bias, p, pt, cot, chunk=16):
    steps, rows, width = x.shape
    cell = p.shape[0]
    total = n * rows
    sds = jax.ShapeDtypeStruct
    vm = pl.BlockSpec(memory_space=pltpu.VMEM)
    hb = pl.BlockSpec(memory_space=pl.ANY)
    keep = F32 if n <= 8 else BF
    V = pltpu.VMEM
    dma = pltpu.SemaphoreType.DMA
    return pl.pallas_call(
        functools.partial(lstm_kernel, n, chunk),
        out_shape=(
            sds((steps, rows, width), BF), sds((steps, rows, width), F32),
            sds((1, 4 * cell), F32), sds((cell, width), F32),
            *[sds((2 * width // n, 4 * cell), BF)] * n),
        in_specs=[vm] * 5 + [hb],
        out_specs=[vm] * 4 + [hb] * n,
        scratch_shapes=[
            V((steps, n, rows, width), BF), V((steps + 1, n, rows, width), BF),
            V((steps, n, rows, width), BF), V((steps, total, 4 * cell), keep),
            V((steps + 1, total, cell), F32), V((steps, total, cell), BF),
            V((steps, rows, width), F32), V((total, 4 * cell), F32),
            V((total, cell), F32), V((2, total, 4 * cell), BF), V((total, cell), F32),
            V((2 * width, 4 * cell), F32), V((2 * width, 4 * cell), BF),
            V((4 * cell, 2 * width), BF),
            V((n, rows, width), BF), V((n, rows, width), BF),
            V((2, n, rows, width), BF), V((2, n, rows, width), BF),
            V((steps, rows, width), BF), V((steps, rows, width), BF), V((rows, width), F32),
            dma((steps,)), dma((steps,)), dma((n,)), dma((n,)), dma((n,)), dma((n,)), dma((n,)), dma((n,)), dma((2, n)), dma((2, n)),
            dma((steps,)), dma((steps,)), dma((steps,)), dma((steps,)), dma((2,)), dma,
        ],
        compiler_params=pltpu.CompilerParams(
            collective_id=0, has_side_effects=True, vmem_limit_bytes=60 * 1024 * 1024),
        cost_estimate=pl.CostEstimate(
            flops=300_000_000_000, bytes_accessed=64 * 1024 * 1024, transcendentals=0),
        name="relay_lstm",
    )(x, bias, p, pt, cot, weights)


def split_cells(weight, n):
    rows, gates = weight.shape
    cell = gates // (4 * n)
    wing = n // 2

    def body(src, keep, give):
        pipe = lax.axis_index("pipe")
        for k in range(wing):
            for dst, side in ((keep, pipe), (give, 1 - pipe)):
                at = pl.multiple_of((side * wing + k) * cell, cell)
                dst[k] = src[:, pl.ds(at, cell)].astype(BF)

    return pl.pallas_call(
        body,
        grid=(4,),
        out_shape=[jax.ShapeDtypeStruct((wing, rows, 4 * cell), BF)] * 2,
        in_specs=[pl.BlockSpec((rows, n * cell), lambda b: (0, b))],
        out_specs=[pl.BlockSpec((wing, rows, cell), lambda b: (0, 0, b))] * 2,
        cost_estimate=pl.CostEstimate(
            flops=0, bytes_accessed=6 * rows * gates, transcendentals=0
        ),
        name="split_cells",
    )(weight)


def join_cells(blocks):
    n = len(blocks)
    rows, gates = blocks[0].shape
    cell = gates // 4

    def body(*refs):
        dst = refs[n]
        for off in range(n):
            rank = lax.rem(lax.axis_index("dp") + (n - off), n)
            dst[:, pl.ds(pl.multiple_of(rank * cell, cell), cell)] = refs[off][...].astype(F32)

    return pl.pallas_call(
        body,
        grid=(4,),
        out_shape=jax.ShapeDtypeStruct((rows, n * gates), F32),
        in_specs=[pl.BlockSpec((rows, cell), lambda b: (0, b))] * n,
        out_specs=pl.BlockSpec((rows, n * cell), lambda b: (0, b)),
        cost_estimate=pl.CostEstimate(
            flops=0, bytes_accessed=6 * n * rows * gates, transcendentals=0
        ),
        name="join_cells",
    )(*blocks)


def swap_pipes(value):
    return lax.ppermute(value, "pipe", [(0, 1), (1, 0)])


def rank_pairs(n, off, layers=(0, 1)):
    wing = n // 2
    pairs = []
    for layer in layers:
        for j in range(n):
            rank = (j + off) % n
            pairs.append((layer * n + j, rank // wing * n + layer * wing + rank % wing))
    return pairs


def to_ranks(value, off):
    return lax.ppermute(value, ("pipe", "dp"), rank_pairs(lax.axis_size("dp"), off))


def from_ranks(value, off, layers=(0, 1)):
    pairs = rank_pairs(lax.axis_size("dp"), -off, layers)
    return lax.ppermute(value, ("pipe", "dp"), [(there, here) for here, there in pairs])


def conv_forward(ids, table_low, conv_low, valid_place):
    return jax.nn.logsumexp(conv_response(ids, table_low, conv_low, valid_place)[1], axis=1)


def own_half(value, blocks):
    sub = value.shape[-1] // (2 * blocks)
    split = value.reshape(*value.shape[:-1], blocks, 2, sub)
    mine = lax.dynamic_index_in_dim(split, lax.axis_index("pipe"), split.ndim - 2, keepdims=False)
    return mine.reshape(*value.shape[:-1], blocks * sub)


def both_halves(value, blocks):
    tokens, half = value.shape
    pair = lax.all_gather(value, "pipe").reshape(2, tokens, blocks, half // blocks)
    return jnp.transpose(pair, (1, 2, 0, 3)).reshape(tokens, 2 * half)


def conv_backward(ids, table_low, conv_low, masks, grad_before):
    weight_mask, valid_place = masks
    windows, response = conv_response(ids, table_low, conv_low, valid_place)
    share = jax.nn.softmax(response, axis=1)
    grad_response = (grad_before[:, None, :] * share).astype(BF)
    grad_conv = jnp.einsum("bpk,bpf->kf", windows, grad_response, preferred_element_type=F32)
    grad_windows = jnp.einsum("bpf,kf->bpk", grad_response, conv_low, preferred_element_type=F32)
    grad_embedded = jnp.zeros((ids.shape[0], CHARS + KMAX - 1, CDIM), F32)
    for offset in range(KMAX):
        grad_embedded = grad_embedded + jnp.pad(
            grad_windows[:, :, offset * CDIM : (offset + 1) * CDIM],
            ((0, 0), (offset, KMAX - 1 - offset), (0, 0)),
        )
    grad_embedded = grad_embedded[:, :CHARS].astype(BF)
    one_hot = (ids[:, :, None] == jnp.arange(CVOCAB, dtype=jnp.int32)).astype(BF)
    grad_table = jnp.einsum("bpv,bpc->vc", one_hot, grad_embedded, preferred_element_type=F32)
    return grad_conv * weight_mask, grad_table


def local(
    chars,
    lengths,
    char_emb,
    conv_weight,
    conv_bias,
    highway_weight,
    highway_bias,
    proj_weight,
    proj_bias,
    gate_weight,
    gate_bias,
    cell_proj,
    cotangent,
):
    n = lax.axis_size("dp")
    pipe = lax.axis_index("pipe")
    direction = lax.axis_index("dir")
    me = lax.axis_index("dp")
    everyone = lax.axis_size(ALL)
    holders = lax.axis_size(("dir", "dp"))
    seqs, steps, char_count = chars.shape
    group = seqs // lax.axis_size("dir")
    quarter = group // 2
    group_tokens = group * steps
    tokens = quarter * steps
    width = cell_proj.shape[3]
    cell = cell_proj.shape[2]
    blocks = holders // 2
    sub = FILTERS // holders
    half = FILTERS // 2
    filter_index = (
        (2 * jnp.arange(blocks, dtype=jnp.int32) + pipe)[:, None] * sub
        + jnp.arange(sub, dtype=jnp.int32)[None, :]
    ).reshape(half)
    masks = conv_masks(filter_index)

    proj_rows = proj_weight.shape[0]
    pieces = width // sub
    proj_blocks = jnp.transpose(proj_weight.reshape(proj_rows, pieces, sub), (1, 0, 2))
    proj_blocks = proj_blocks.reshape(2, pieces * proj_rows // 2, sub)
    mine = lax.dynamic_slice_in_dim(highway_weight, pipe * sub, sub, 2)
    gathered = lax.all_gather(
        jnp.concatenate([mine, proj_blocks], axis=1).astype(BF), ("dir", "dp"), axis=2, tiled=True
    )
    conv_full = lax.all_to_all(
        jnp.broadcast_to(conv_weight.astype(BF), (holders, KMAX * CDIM, sub)), ("dir", "dp"), 0, 0
    ).reshape(blocks, 2, KMAX * CDIM, sub)
    conv_low = lax.dynamic_index_in_dim(conv_full, pipe, 1, keepdims=False)
    conv_low = jnp.transpose(conv_low, (1, 0, 2)).reshape(KMAX * CDIM, half)
    conv_low = conv_low * masks[0].astype(BF)
    conv_bias_own = own_half(conv_bias, blocks)
    highway_bias_own = own_half(highway_bias.reshape(2, 2, FILTERS), blocks).reshape(2, FILTERS)

    def order_matrix(sizes):
        place = jnp.arange(steps, dtype=jnp.int32)[None, :]
        live = place < sizes[:, None]
        order = jnp.where(live & (direction == 1), sizes[:, None] - 1 - place, place)
        return ((order[:, :, None] == place[:, None, :]) & live[:, :, None]).astype(BF)

    own_order = order_matrix(lengths)
    cot = jnp.einsum("rts,rsd->trd", own_order, cotangent[0, 0], preferred_element_type=BF)

    ids = lax.dynamic_slice_in_dim(chars, direction * group, group, 0).reshape(
        group_tokens, char_count
    )
    table_low = char_emb.astype(BF)
    pooled = conv_forward(ids, table_low, conv_low, masks[1])
    features = jax.nn.silu(pooled + conv_bias_own)
    features_low = both_halves(features.astype(BF), blocks)
    bias_own = lax.dynamic_index_in_dim(
        gate_bias[0, 0].reshape(4, n, cell), me, 1, keepdims=False
    ).reshape(1, 4 * cell)
    moved = jnp.concatenate([cell_proj[0, 0].astype(BF), cot.reshape(steps * seqs, width)])
    gate_kept, gate_given = split_cells(gate_weight[0, 0], n)
    gate_came = swap_pipes(gate_given)
    gate_low = jnp.concatenate(
        [
            jnp.where(pipe == 0, gate_kept, gate_came),
            jnp.where(pipe == 0, gate_came, gate_kept),
        ]
    )
    direct, local_part = moved[: moved.shape[0] // 2], moved[moved.shape[0] // 2 :]
    swapped = swap_pipes(local_part)
    gate_low, gathered, features_low, bias_own, direct, swapped = lax.optimization_barrier(
        (gate_low, gathered, features_low, bias_own, direct, swapped)
    )
    bias_own = to_ranks(bias_own, 0)
    wing = n // 2
    swapped = lax.ppermute(
        swapped,
        ("pipe", "dp"),
        [(k, wing + k) for k in range(wing)] + [(n + wing + k, n + k) for k in range(wing)],
    )
    moved = jnp.concatenate(
        [to_ranks(direct, 0), jnp.where(lax.div(me, wing) == pipe, local_part, swapped)]
    )
    gate_own = lax.all_to_all(gate_low, "dp", 0, 0).reshape(2 * width, 4 * cell)
    highway_half = gathered[:, :FILTERS]
    proj_full = gathered[:, FILTERS:].reshape(pieces, proj_rows, holders, sub)
    proj_full = jnp.transpose(proj_full, (2, 1, 0, 3)).reshape(FILTERS, width)

    kept = [features]
    kept_low = [features_low]
    mixed = []
    for layer in range(2):
        pre = (
            jnp.dot(kept_low[layer], highway_half[layer], preferred_element_type=F32)
            + highway_bias_own[layer]
        )
        mixed.append(pre)
        gate = jax.nn.sigmoid(pre[:, half:])
        features = gate * features + (1.0 - gate) * jax.nn.silu(pre[:, :half])
        kept.append(features)
        kept_low.append(both_halves(features.astype(BF), blocks))
    own_last = lax.dynamic_slice_in_dim(kept_low[2], pipe * tokens, tokens, 0)
    encoded = jnp.dot(own_last, proj_full, preferred_element_type=F32) + proj_bias
    encoded_own = lax.all_gather(
        encoded.astype(BF).reshape(quarter, steps, width), ("dir", "pipe"), axis=0, tiled=True
    )
    inputs = jnp.einsum("rts,rsd->trd", own_order, encoded_own, preferred_element_type=BF)
    inputs = lax.ppermute(
        inputs,
        ("pipe", "dp"),
        [(k, wing + k) for k in range(wing)] + [(n + k, n + k) for k in range(wing, n)],
    )
    kept_low, gate_own, inputs, moved, bias_own = lax.optimization_barrier(
        (kept_low, gate_own, inputs, moved, bias_own)
    )
    cell_low = moved[:cell]
    cot = moved[cell:].reshape(steps, seqs, width)
    kept_all = [
        lax.all_gather(
            lax.dynamic_slice_in_dim(value, pipe * tokens, tokens, 0),
            ("dir", "dp"),
            axis=0,
            tiled=True,
        )
        for value in kept_low[:2]
    ]

    out_own, dx_own, grad_bias, grad_cell, *grad_gate = lstm_call(
        n, inputs, gate_own, bias_own, cell_low, cell_low.T, cot
    )
    dx_own = from_ranks(dx_own.astype(BF), 0, (1,))
    grad_gate = [from_ranks(block, off) for off, block in enumerate(grad_gate)]
    dx_own, kept_all = lax.optimization_barrier((dx_own, kept_all))

    grad_stored = jnp.einsum(
        "rts,srd->rtd", own_order, dx_own, preferred_element_type=F32
    )
    grad_stored = jnp.where(pipe == 1, grad_stored, 0.0).astype(BF)
    grad_stored = grad_stored.reshape(1, -1, group_tokens, width)
    grad_encoded = lax.all_to_all(
        jnp.concatenate([grad_stored, grad_stored]).reshape(-1, group_tokens, width),
        ("pipe", "dir"),
        0,
        0,
    )
    grad_encoded = jnp.sum(grad_encoded.astype(F32), axis=0).astype(BF)
    own_grads = lax.dynamic_slice_in_dim(grad_encoded, pipe * tokens, tokens, 0)
    encoded_grads = lax.all_gather(own_grads, ("dir", "dp"), axis=0, tiled=True)

    grad_proj_bias = jnp.sum(own_grads.astype(F32), axis=0)
    proj_half = lax.dynamic_index_in_dim(
        proj_full.reshape(blocks, 2, sub, width), pipe, 1, keepdims=False
    ).reshape(half, width)
    grad_features = jnp.einsum("td,fd->tf", grad_encoded, proj_half, preferred_element_type=F32)
    columns = [None, None]
    grad_highway_bias = [None, None]
    for layer in (1, 0):
        nonlinear = mixed[layer][:, :half]
        gate = jax.nn.sigmoid(mixed[layer][:, half:])
        grad_mixed = jnp.concatenate(
            [
                grad_features * (1.0 - gate) * silu_slope(nonlinear),
                grad_features * (kept[layer] - jax.nn.silu(nonlinear)) * gate * (1.0 - gate),
            ],
            axis=1,
        ).astype(BF)
        columns[layer] = grad_mixed
        grad_highway_bias[layer] = jnp.sum(grad_mixed.astype(F32), axis=0)
        partial = jnp.einsum(
            "tg,fg->tf", grad_mixed, highway_half[layer], preferred_element_type=F32
        )
        partial = lax.optimization_barrier(partial).reshape(group_tokens, blocks, 2, sub)
        sent = lax.dynamic_index_in_dim(partial, 1 - pipe, 2, keepdims=False).astype(BF)
        came = lax.ppermute(sent, "pipe", [(0, 1), (1, 0)])
        mine = lax.dynamic_index_in_dim(partial, pipe, 2, keepdims=False)
        grad_features = grad_features * gate + (mine + came.astype(F32)).reshape(
            group_tokens, half
        )
    grad_before = grad_features * silu_slope(pooled + conv_bias_own)
    grad_before, grad_gate[1:5] = lax.optimization_barrier((grad_before, grad_gate[1:5]))
    grad_conv, grad_table = conv_backward(ids, table_low, conv_low, masks, grad_before)

    def spread(value):
        split = value.reshape(*value.shape[:-1], -1, 1, sub)
        shown = jnp.arange(2, dtype=jnp.int32)[:, None] == pipe
        return jnp.where(shown, split, jnp.zeros_like(split)).reshape(*value.shape[:-1], -1)

    cols = FILTERS // everyone
    pair = jnp.stack(columns, axis=1).reshape(2, tokens, 2, 2, blocks, 1, sub)
    sent = lax.dynamic_index_in_dim(pair, 1 - pipe, 0, keepdims=False)
    came = lax.ppermute(sent, "pipe", [(0, 1), (1, 0)])
    mine = lax.dynamic_index_in_dim(pair, pipe, 0, keepdims=False)
    shown = (jnp.arange(2, dtype=jnp.int32) == pipe)[:, None]
    pair = jnp.where(shown, mine, came)
    pair = jnp.transpose(pair, (3, 4, 0, 1, 2, 5)).reshape(holders, tokens, 4 * sub)
    last = jnp.transpose(own_last.reshape(tokens, 2, holders, cols), (2, 0, 1, 3))
    pair = jnp.concatenate([pair, last.reshape(holders, tokens, 2 * cols)], axis=2)
    pair = lax.all_to_all(pair, ("dir", "dp"), 0, 0).reshape(holders * tokens, -1)
    grad_conv, pair, out_own, grad_cell, grad_gate[5:] = lax.optimization_barrier(
        (grad_conv, pair, out_own, grad_cell, grad_gate[5:])
    )
    small = (
        grad_table,
        spread(jnp.sum(grad_before, axis=0)),
        spread(jnp.stack(grad_highway_bias)),
        grad_proj_bias,
    )
    flat = jnp.concatenate([value.reshape(-1) for value in small])
    share = -(-flat.shape[0] // (everyone * 128)) * 128
    flat = jnp.pad(flat, (0, share * everyone - flat.shape[0])).reshape(everyone, share)
    rank = pipe * wing + lax.rem(me, wing)
    mine = jnp.arange(n, dtype=jnp.int32)[None, :, None] == rank
    bias_parts = jnp.where(mine, grad_bias.reshape(4, 1, cell), 0.0).reshape(1, n, 4 * cell)
    layer = lax.div(me, wing) * lax.axis_size("dir") + direction
    mine = jnp.arange(everyone // n, dtype=jnp.int32) == layer
    bias_parts = jnp.where(mine[:, None, None], bias_parts, 0.0).reshape(everyone, 4 * cell)
    packed = jnp.concatenate(
        [
            jnp.transpose(
                spread(grad_conv).reshape(KMAX * CDIM, everyone, cols), (1, 0, 2)
            ).reshape(everyone, KMAX * CDIM * cols),
            flat,
            bias_parts,
        ],
        axis=1,
    ).astype(BF)
    summed = jnp.sum(lax.all_to_all(packed, ALL, 0, 0).astype(F32), axis=0)
    out_own = from_ranks(out_own, 0)
    grad_cell = from_ranks(grad_cell.astype(BF), 0)
    summed, grad_gate = lax.optimization_barrier((summed, grad_gate))
    grad_gate = join_cells(grad_gate)
    activations = jnp.einsum("rts,srd->rtd", own_order, out_own, preferred_element_type=BF)
    grad_cell = grad_cell.astype(F32)
    grad_conv = summed[: KMAX * CDIM * cols].reshape(KMAX * CDIM, cols)
    grad_bias = summed[KMAX * CDIM * cols + share :]
    last = pair[:, 4 * sub :].reshape(holders * tokens, 2, cols)
    pair = pair[:, : 4 * sub].reshape(holders * tokens, 2, 2, sub)

    def partial_sums(owner):
        return [
            jnp.einsum(
                "tf,tg->fg",
                kept_all[layer],
                lax.dynamic_index_in_dim(pair[:, layer], owner, 1, keepdims=False),
                preferred_element_type=F32,
            )
            for layer in range(2)
        ] + [
            jnp.einsum(
                "tf,td->fd",
                lax.dynamic_index_in_dim(last, owner, 1, keepdims=False),
                encoded_grads,
                preferred_element_type=F32,
            )
        ]

    sent = jnp.concatenate(
        [value.astype(BF).reshape(-1, sub) for value in partial_sums(1 - pipe)]
    )
    came = lax.ppermute(sent, "pipe", [(0, 1), (1, 0)]).astype(F32)
    mine = partial_sums(pipe)
    grad_highway = jnp.stack(mine[:2]) + came[: 2 * FILTERS].reshape(2, FILTERS, sub)
    grad_proj = mine[2] + came[2 * FILTERS :].reshape(cols, width)
    shared = lax.all_to_all(
        jnp.broadcast_to(summed[KMAX * CDIM * cols :][:share], (everyone, share)), ALL, 0, 0
    ).reshape(-1)
    small_sums = []
    start = 0
    for value in small:
        small_sums.append(shared[start : start + value.size].reshape(value.shape))
        start += value.size
    return (
        activations[None, None],
        small_sums[0],
        grad_conv,
        small_sums[1],
        grad_highway,
        small_sums[2],
        grad_proj,
        small_sums[3],
        grad_gate[None, None],
        grad_bias[None, None],
        grad_cell[None, None],
    )


def solution(mesh):
    return jax.shard_map(
        local,
        mesh=mesh,
        in_specs=(
            P("dp", None, None),
            P("dp"),
            P(),
            P(None, ("dir", "dp")),
            P(),
            P(None, None, ("dir", "dp")),
            P(),
            P(("dir", "dp"), None),
            P(),
            P("pipe", "dir", "dp", None),
            P("pipe", "dir", None),
            P("pipe", "dir", "dp", None),
            P("pipe", "dir", "dp", None, None),
        ),
        out_specs=(
            P("pipe", "dir", "dp", None, None),
            P(),
            P(None, ("pipe", "dir", "dp")),
            P(),
            P(None, None, ("pipe", "dir", "dp")),
            P(),
            P(("pipe", "dir", "dp"), None),
            P(),
            P("pipe", "dir", "dp", None),
            P("pipe", "dir", "dp"),
            P("pipe", "dir", "dp", None),
        ),
        check_vma=False,
    )
```

```python
import functools
import math

import jax
import jax.numpy as jnp
from jax import lax
from jax.experimental import pallas as pl
from jax.experimental.pallas import tpu as pltpu
from jax.sharding import PartitionSpec as P

FILTERS = 2048
CDIM = 16
CVOCAB = 262
CHARS = 50
KMAX = 7
CLIP_LIMIT = 3.0
MASKED_FILL = -1000000000.0
MESH = pl.DeviceIdType.MESH
BF = jnp.bfloat16
F32 = jnp.float32
ALL = ("pipe", "dir", "dp")


def silu_slope(value):
    sig = jax.nn.sigmoid(value)
    return sig * (1.0 + value * (1.0 - sig))


def conv_masks(filter_index):
    filter_width = jnp.ones(filter_index.shape, jnp.int32)
    for doubling in range(6):
        filter_width = filter_width + (filter_index >= FILTERS // 64 * (1 << doubling)).astype(
            jnp.int32
        )
    offset_rows = jnp.arange(KMAX * CDIM, dtype=jnp.int32) // CDIM
    weight_mask = (offset_rows[:, None] < filter_width[None, :]).astype(jnp.float32)
    valid_place = jnp.arange(CHARS, dtype=jnp.int32)[:, None] <= CHARS - filter_width[None, :]
    return (weight_mask, valid_place)


def make_windows(embedded):
    padded = jnp.pad(embedded, ((0, 0), (0, KMAX - 1), (0, 0)))
    return jnp.concatenate(
        [padded[:, offset : offset + CHARS, :] for offset in range(KMAX)], axis=2
    )


def conv_response(ids_block, table_low, conv_low, valid_place):
    embedded = jnp.take(table_low, ids_block, axis=0)
    windows = make_windows(embedded)
    response = jnp.einsum("bpk,kf->bpf", windows, conv_low, preferred_element_type=jnp.float32)
    return (windows, jnp.where(valid_place[None], response, MASKED_FILL))


def over(count, step):
    if count <= 9:
        for off in range(count - 1, 0, -1):
            step(off)
    else:
        lax.fori_loop(1, count, lambda off, _: (step(off), 0)[1], 0)


def lstm_kernel(n, chunk, x_own, bias, p, pt, cot, w_in, *refs):
    out_ref, dx_ref, db_ref, dp_ref = refs[:4]
    gate_out = refs[4]
    (xbuf, hbuf, dqbuf, gates, cells, ebuf, hown, gscr, escr, dabuf, ucell, dwacc, w, wt,
     stage, inbox, stage2, inbox2, relay, gbuf, rown,
     in_send, in_recv, ag_send, ag_recv, dq_send, dq_recv, rs_send, rs_recv,
     dx_send, dx_recv, x_send, x_recv, g_send, g_recv, row_send, row_recv, w_sem) = refs[5:]
    steps, _, rows, width = xbuf.shape
    total = n * rows
    cell = cells.shape[2]
    pipe = lax.axis_index("pipe")
    direction = lax.axis_index("dir")
    place = lax.axis_index("dp")
    wing = n // 2
    first = place >= wing
    second = place < wing
    me = pipe * wing + lax.rem(place, wing)
    base = place - lax.rem(place, wing)
    partner = (pipe, direction, lax.rem(place + wing, n))

    def peer(off):
        if n & (n - 1):
            return lax.rem(me + off, n)
        return me ^ off

    def at_peer(off):
        rank = peer(off)
        return (lax.div(rank, wing), direction, base + lax.rem(rank, wing))

    barrier = pltpu.get_barrier_semaphore()

    def greet(side, off):
        pl.semaphore_signal(
            barrier, inc=1, device_id=(side, direction, lax.rem(place + off, n)),
            device_id_type=MESH)

    over(n, lambda off: greet(pipe, off))
    over(n, lambda off: greet(1 - pipe, off))
    greet(1 - pipe, 0)

    each = 2 * width // n
    load = pltpu.make_async_copy(w_in, w, w_sem)
    load.start()

    @pl.when(first)
    def _():
        for t in range(steps):
            xbuf[t, me] = x_own[t]

    hbuf[0] = jnp.zeros((n, rows, width), BF)
    cells[0] = jnp.zeros((total, cell), F32)
    pl.semaphore_wait(barrier, 2 * n - 1)

    def ag_copy(buf, slot, off):
        out, into = (ag_send, ag_recv) if buf is hbuf else (dq_send, dq_recv)
        return pltpu.make_async_remote_copy(
            src_ref=buf.at[slot, me], dst_ref=buf.at[slot, me],
            send_sem=out.at[off], recv_sem=into.at[off],
            device_id=at_peer(off), device_id_type=MESH)

    def rs_copy(off):
        return pltpu.make_async_remote_copy(
            src_ref=stage.at[peer(off)], dst_ref=inbox.at[me],
            send_sem=rs_send.at[off], recv_sem=rs_recv.at[off],
            device_id=at_peer(off), device_id_type=MESH)

    def dx_copy(slot, off):
        return pltpu.make_async_remote_copy(
            src_ref=stage2.at[slot, peer(off)], dst_ref=inbox2.at[slot, me],
            send_sem=dx_send.at[slot, off], recv_sem=dx_recv.at[slot, off],
            device_id=at_peer(off), device_id_type=MESH)

    def x_copy(t):
        return pltpu.make_async_remote_copy(
            src_ref=hbuf.at[t + 1, me], dst_ref=xbuf.at[t, me],
            send_sem=x_send.at[t], recv_sem=x_recv.at[t],
            device_id=partner, device_id_type=MESH)

    def g_copy(t):
        return pltpu.make_async_remote_copy(
            src_ref=relay.at[t], dst_ref=gbuf.at[t],
            send_sem=g_send.at[t], recv_sem=g_recv.at[t],
            device_id=partner, device_id_type=MESH)

    def in_start(t):
        over(n, lambda off: pltpu.make_async_remote_copy(
            src_ref=xbuf.at[t, me], dst_ref=xbuf.at[t, me],
            send_sem=in_send.at[t], recv_sem=in_recv.at[t],
            device_id=at_peer(off), device_id_type=MESH).start())

    def in_wait(sem, t):
        blocks = xbuf.at[t, pl.ds(0, n - 1)]
        pltpu.make_async_copy(blocks, blocks, sem.at[t]).wait()

    @pl.when(first)
    def _():
        in_start(0)
        in_start(1)

    @pl.when(second)
    def _():
        x_copy(0).wait_recv()
        in_start(0)

    load.wait()
    for at in range(0, 2 * width, 128):
        wt[:, at:at + 128] = w[at:at + 128, :].T

    def ag_wait(buf, slot):
        def both(off):
            ag_copy(buf, slot, off).wait_send()
            ag_copy(buf, slot, off).wait_recv()
        over(n, both)

    def rs_wait():
        def both(off):
            rs_copy(off).wait_send()
            rs_copy(off).wait_recv()
        over(n, both)

    def forward(t, _):
        in_wait(in_recv, t)
        gscr[...] = jnp.dot(
            xbuf[t].reshape(total, width), w[:width, :], preferred_element_type=F32) + bias[...]

        @pl.when(t > 0)
        def _():
            ag_wait(hbuf, t)

        gscr[...] += jnp.dot(
            hbuf[t].reshape(total, width), w[width:, :], preferred_element_type=F32)

        def rows_step(k, _):
            at = pl.ds(pl.multiple_of(k * chunk, chunk), chunk)
            g = gscr[at, :]
            i = jax.nn.sigmoid(g[:, :cell])
            f = jax.nn.sigmoid(g[:, cell:2 * cell])
            m = jnp.tanh(g[:, 2 * cell:3 * cell])
            o = jax.nn.sigmoid(g[:, 3 * cell:])
            c = 3.0 * jnp.tanh((i * m + f * cells[t, at, :]) * (1.0 / 3.0))
            cells[t + 1, at, :] = c
            ebuf[t, at, :] = (o * jnp.tanh(c)).astype(BF)
            kind = gates.dtype
            gates[t, at, :cell] = i.astype(kind)
            gates[t, at, cell:2 * cell] = f.astype(kind)
            gates[t, at, 2 * cell:3 * cell] = m.astype(kind)
            gates[t, at, 3 * cell:] = o.astype(kind)
            return 0

        lax.fori_loop(0, total // chunk, rows_step, 0)
        q = jnp.dot(ebuf[t], p[...], preferred_element_type=F32)
        stage[...] = q.astype(BF).reshape(n, rows, width)
        over(n, lambda off: rs_copy(off).start())
        inbox[me] = stage[me]

        @pl.when(first & (t + 2 < steps))
        def _():
            in_start(t + 2)

        @pl.when(second & (t + 1 < steps))
        def _():
            x_copy(t + 1).wait_recv()
            in_start(t + 1)

        rs_wait()
        h = 3.0 * jnp.tanh(jnp.sum(inbox[...].astype(F32), axis=0) * (1.0 / 3.0))
        hown[t] = h
        hbuf[t + 1, me] = h.astype(BF)
        over(n, lambda off: ag_copy(hbuf, t + 1, off).start())

        @pl.when(first)
        def _():
            x_copy(t).start()

        add = jnp.where(second, 1.0, 0.0)
        out_ref[t] = (h + add * xbuf[t, me].astype(F32)).astype(BF)
        return 0

    lax.fori_loop(0, steps, forward, 0)
    ag_wait(hbuf, steps)

    lax.fori_loop(0, steps, lambda t, _: (in_wait(in_send, t), 0)[1], 0)

    @pl.when(first)
    def _():
        lax.fori_loop(0, steps, lambda t, _: (x_copy(t).wait_send(), 0)[1], 0)

    rown[...] = jnp.zeros((rows, width), F32)
    ucell[...] = jnp.zeros((total, cell), F32)
    dwacc[...] = jnp.zeros(dwacc.shape, F32)
    db_ref[...] = jnp.zeros(db_ref.shape, F32)
    dp_ref[...] = jnp.zeros(dp_ref.shape, F32)

    def dx_finish(t):
        slot = lax.rem(t, 2)

        def both(off):
            dx_copy(slot, off).wait_send()
            dx_copy(slot, off).wait_recv()
        over(n, both)
        dx = jnp.sum(inbox2[slot].astype(F32), axis=0)
        dx_ref[t] = dx

        @pl.when(second)
        def _():
            relay[t] = (dx + cot[t].astype(F32)).astype(BF)
            g_copy(t).start()

    def backward(k, _):
        t = steps - 1 - k
        slot = lax.rem(t, 2)
        up = rown[...] + cot[t].astype(F32)
        rown[...] = up

        @pl.when(first)
        def _():
            g_copy(t).wait_recv()
            rown[...] = rown[...] + gbuf[t].astype(F32)

        ratio = hown[t] * (1.0 / 3.0)
        dqbuf[t, me] = (rown[...] * (1.0 - ratio * ratio)).astype(BF)
        over(n, lambda off: ag_copy(dqbuf, t, off).start())

        @pl.when(k > 0)
        def _():
            dx_finish(t + 1)

        ag_wait(dqbuf, t)
        escr[...] = jnp.dot(
            dqbuf[t].reshape(total, width), pt[...], preferred_element_type=F32)

        def rows_step(j, _):
            at = pl.ds(pl.multiple_of(j * chunk, chunk), chunk)
            de = escr[at, :]
            i = gates[t, at, :cell].astype(F32)
            f = gates[t, at, cell:2 * cell].astype(F32)
            m = gates[t, at, 2 * cell:3 * cell].astype(F32)
            o = gates[t, at, 3 * cell:].astype(F32)
            c = cells[t + 1, at, :]
            tc = jnp.tanh(c)
            cr = c * (1.0 / 3.0)
            dc = (de * o * (1.0 - tc * tc) + ucell[at, :]) * (1.0 - cr * cr)
            ucell[at, :] = dc * f
            for block, value in enumerate((
                dc * m * i * (1.0 - i),
                dc * cells[t, at, :] * f * (1.0 - f),
                dc * i * (1.0 - m * m),
                de * tc * o * (1.0 - o),
            )):
                value = value.astype(BF)
                where = pl.ds(block * cell, cell)
                dabuf[0, at, where] = value
                db_ref[:, where] += jnp.sum(value.astype(F32), axis=0, keepdims=True)
            return 0

        lax.fori_loop(0, total // chunk, rows_step, 0)
        r = jnp.dot(dabuf[0], wt[:, width:], preferred_element_type=F32)
        stage[...] = r.astype(BF).reshape(n, rows, width)
        over(n, lambda off: rs_copy(off).start())
        inbox[me] = stage[me]
        dx = jnp.dot(dabuf[0], wt[:, :width], preferred_element_type=F32)
        stage2[slot] = dx.astype(BF).reshape(n, rows, width)
        over(n, lambda off: dx_copy(slot, off).start())
        inbox2[slot, me] = stage2[slot, me]
        for half, buf in enumerate((xbuf, hbuf)):
            dwacc[pl.ds(half * width, width), :] += lax.dot_general(
                buf[t].reshape(total, width), dabuf[0], (((0,), (0,)), ((), ())),
                preferred_element_type=F32)
        dp_ref[...] += lax.dot_general(
            ebuf[t], dqbuf[t].reshape(total, width), (((0,), (0,)), ((), ())),
            preferred_element_type=F32)
        rs_wait()
        rown[...] = jnp.sum(inbox[...].astype(F32), axis=0)
        return 0

    lax.fori_loop(0, steps, backward, 0)
    dx_finish(0)

    @pl.when(second)
    def _():
        lax.fori_loop(0, steps, lambda t, _: (g_copy(t).wait_send(), 0)[1], 0)

    layer = lax.div(place, wing)
    at_home = layer == pipe

    def row_copy(row, rank):
        return pltpu.make_async_remote_copy(
            src_ref=w.at[pl.ds(pl.multiple_of(row * each, each), each)],
            dst_ref=gate_out.at[rank], send_sem=row_send.at[row], recv_sem=row_recv.at[rank],
            device_id=(layer, direction, row), device_id_type=MESH)

    def own_copy():
        return pltpu.make_async_copy(
            w.at[pl.ds(pl.multiple_of(place * each, each), each)], gate_out.at[me], w_sem)

    def send_row(off, _):
        row = lax.rem(me + off, n)
        at = pl.ds(pl.multiple_of(row * each, each), each)
        w[at, :] = dwacc[at, :].astype(BF)
        mine = at_home & (row == place)

        @pl.when(mine)
        def _():
            own_copy().start()

        @pl.when(jnp.logical_not(mine))
        def _():
            row_copy(row, me).start()
        return 0

    def end_row(row, _):
        mine = at_home & (row == place)

        @pl.when(mine)
        def _():
            own_copy().wait()

        @pl.when(jnp.logical_not(mine))
        def _():
            row_copy(row, me).wait_send()
        return 0

    def end_rank(rank, _):
        @pl.when(jnp.logical_not(at_home & (rank == me)))
        def _():
            row_copy(0, rank).wait_recv()
        return 0

    lax.fori_loop(0, n, send_row, 0)
    lax.fori_loop(0, n, end_row, 0)
    lax.fori_loop(0, n, end_rank, 0)


def lstm_call(n, x, weights, bias, p, pt, cot, chunk=16):
    steps, rows, width = x.shape
    cell = p.shape[0]
    total = n * rows
    sds = jax.ShapeDtypeStruct
    vm = pl.BlockSpec(memory_space=pltpu.VMEM)
    hb = pl.BlockSpec(memory_space=pl.ANY)
    keep = F32 if n <= 8 else BF
    V = pltpu.VMEM
    dma = pltpu.SemaphoreType.DMA
    return pl.pallas_call(
        functools.partial(lstm_kernel, n, chunk),
        out_shape=(
            sds((steps, rows, width), BF), sds((steps, rows, width), F32),
            sds((1, 4 * cell), F32), sds((cell, width), F32),
            sds((n, 2 * width // n, 4 * cell), BF)),
        in_specs=[vm] * 5 + [hb],
        out_specs=[vm] * 4 + [hb],
        scratch_shapes=[
            V((steps, n, rows, width), BF), V((steps + 1, n, rows, width), BF),
            V((steps, n, rows, width), BF), V((steps, total, 4 * cell), keep),
            V((steps + 1, total, cell), F32), V((steps, total, cell), BF),
            V((steps, rows, width), F32), V((total, 4 * cell), F32),
            V((total, cell), F32), V((2, total, 4 * cell), BF), V((total, cell), F32),
            V((2 * width, 4 * cell), F32), V((2 * width, 4 * cell), BF),
            V((4 * cell, 2 * width), BF),
            V((n, rows, width), BF), V((n, rows, width), BF),
            V((2, n, rows, width), BF), V((2, n, rows, width), BF),
            V((steps, rows, width), BF), V((steps, rows, width), BF), V((rows, width), F32),
            dma((steps,)), dma((steps,)), dma((n,)), dma((n,)), dma((n,)), dma((n,)), dma((n,)), dma((n,)), dma((2, n)), dma((2, n)),
            dma((steps,)), dma((steps,)), dma((steps,)), dma((steps,)), dma((n,)), dma((n,)), dma,
        ],
        compiler_params=pltpu.CompilerParams(
            collective_id=0, has_side_effects=True, vmem_limit_bytes=60 * 1024 * 1024),
        cost_estimate=pl.CostEstimate(
            flops=300_000_000_000, bytes_accessed=64 * 1024 * 1024, transcendentals=0),
        name="relay_lstm",
    )(x, bias, p, pt, cot, weights)


def split_cells(weight, n):
    rows, gates = weight.shape
    cell = gates // (4 * n)
    wing = n // 2

    def body(src, keep, give):
        pipe = lax.axis_index("pipe")
        for k in range(wing):
            for dst, side in ((keep, pipe), (give, 1 - pipe)):
                at = pl.multiple_of((side * wing + k) * cell, cell)
                dst[k] = src[:, pl.ds(at, cell)].astype(BF)

    return pl.pallas_call(
        body,
        grid=(4,),
        out_shape=[jax.ShapeDtypeStruct((wing, rows, 4 * cell), BF)] * 2,
        in_specs=[pl.BlockSpec((rows, n * cell), lambda b: (0, b))],
        out_specs=[pl.BlockSpec((wing, rows, cell), lambda b: (0, 0, b))] * 2,
        cost_estimate=pl.CostEstimate(
            flops=0, bytes_accessed=6 * rows * gates, transcendentals=0
        ),
        name="split_cells",
    )(weight)


def join_cells(blocks):
    n, rows, gates = blocks.shape
    cell = gates // 4

    def body(src, dst):
        for k in range(n):
            dst[:, k * cell : (k + 1) * cell] = src[k].astype(F32)

    return pl.pallas_call(
        body,
        grid=(4,),
        out_shape=jax.ShapeDtypeStruct((rows, n * gates), F32),
        in_specs=[pl.BlockSpec((n, rows, cell), lambda b: (0, 0, b))],
        out_specs=pl.BlockSpec((rows, n * cell), lambda b: (0, b)),
        cost_estimate=pl.CostEstimate(
            flops=0, bytes_accessed=6 * n * rows * gates, transcendentals=0
        ),
        name="join_cells",
    )(blocks)


def swap_pipes(value):
    return lax.ppermute(value, "pipe", [(0, 1), (1, 0)])


def rank_pairs(n, off, layers=(0, 1)):
    wing = n // 2
    pairs = []
    for layer in layers:
        for j in range(n):
            rank = (j + off) % n
            pairs.append((layer * n + j, rank // wing * n + layer * wing + rank % wing))
    return pairs


def to_ranks(value, off):
    return lax.ppermute(value, ("pipe", "dp"), rank_pairs(lax.axis_size("dp"), off))


def from_ranks(value, off, layers=(0, 1)):
    pairs = rank_pairs(lax.axis_size("dp"), -off, layers)
    return lax.ppermute(value, ("pipe", "dp"), [(there, here) for here, there in pairs])


def conv_forward(ids, table_low, conv_low, valid_place):
    return jax.nn.logsumexp(conv_response(ids, table_low, conv_low, valid_place)[1], axis=1)


def own_half(value, blocks):
    sub = value.shape[-1] // (2 * blocks)
    split = value.reshape(*value.shape[:-1], blocks, 2, sub)
    mine = lax.dynamic_index_in_dim(split, lax.axis_index("pipe"), split.ndim - 2, keepdims=False)
    return mine.reshape(*value.shape[:-1], blocks * sub)


def both_halves(value, blocks):
    tokens, half = value.shape
    pair = lax.all_gather(value, "pipe").reshape(2, tokens, blocks, half // blocks)
    return jnp.transpose(pair, (1, 2, 0, 3)).reshape(tokens, 2 * half)


def conv_backward(ids, table_low, conv_low, masks, grad_before):
    weight_mask, valid_place = masks
    windows, response = conv_response(ids, table_low, conv_low, valid_place)
    share = jax.nn.softmax(response, axis=1)
    grad_response = (grad_before[:, None, :] * share).astype(BF)
    grad_conv = jnp.einsum("bpk,bpf->kf", windows, grad_response, preferred_element_type=F32)
    grad_windows = jnp.einsum("bpf,kf->bpk", grad_response, conv_low, preferred_element_type=F32)
    grad_embedded = jnp.zeros((ids.shape[0], CHARS + KMAX - 1, CDIM), F32)
    for offset in range(KMAX):
        grad_embedded = grad_embedded + jnp.pad(
            grad_windows[:, :, offset * CDIM : (offset + 1) * CDIM],
            ((0, 0), (offset, KMAX - 1 - offset), (0, 0)),
        )
    grad_embedded = grad_embedded[:, :CHARS].astype(BF)
    one_hot = (ids[:, :, None] == jnp.arange(CVOCAB, dtype=jnp.int32)).astype(BF)
    grad_table = jnp.einsum("bpv,bpc->vc", one_hot, grad_embedded, preferred_element_type=F32)
    return grad_conv * weight_mask, grad_table


def local(
    chars,
    lengths,
    char_emb,
    conv_weight,
    conv_bias,
    highway_weight,
    highway_bias,
    proj_weight,
    proj_bias,
    gate_weight,
    gate_bias,
    cell_proj,
    cotangent,
):
    n = lax.axis_size("dp")
    pipe = lax.axis_index("pipe")
    direction = lax.axis_index("dir")
    me = lax.axis_index("dp")
    everyone = lax.axis_size(ALL)
    holders = lax.axis_size(("dir", "dp"))
    seqs, steps, char_count = chars.shape
    group = seqs // lax.axis_size("dir")
    quarter = group // 2
    group_tokens = group * steps
    tokens = quarter * steps
    width = cell_proj.shape[3]
    cell = cell_proj.shape[2]
    blocks = holders // 2
    sub = FILTERS // holders
    half = FILTERS // 2
    filter_index = (
        (2 * jnp.arange(blocks, dtype=jnp.int32) + pipe)[:, None] * sub
        + jnp.arange(sub, dtype=jnp.int32)[None, :]
    ).reshape(half)
    masks = conv_masks(filter_index)

    proj_rows = proj_weight.shape[0]
    pieces = width // sub
    proj_blocks = jnp.transpose(proj_weight.reshape(proj_rows, pieces, sub), (1, 0, 2))
    proj_blocks = proj_blocks.reshape(2, pieces * proj_rows // 2, sub)
    mine = lax.dynamic_slice_in_dim(highway_weight, pipe * sub, sub, 2)
    gathered = lax.all_gather(
        jnp.concatenate([mine, proj_blocks], axis=1).astype(BF), ("dir", "dp"), axis=2, tiled=True
    )
    conv_full = lax.all_to_all(
        jnp.broadcast_to(conv_weight.astype(BF), (holders, KMAX * CDIM, sub)), ("dir", "dp"), 0, 0
    ).reshape(blocks, 2, KMAX * CDIM, sub)
    conv_low = lax.dynamic_index_in_dim(conv_full, pipe, 1, keepdims=False)
    conv_low = jnp.transpose(conv_low, (1, 0, 2)).reshape(KMAX * CDIM, half)
    conv_low = conv_low * masks[0].astype(BF)
    conv_bias_own = own_half(conv_bias, blocks)
    highway_bias_own = own_half(highway_bias.reshape(2, 2, FILTERS), blocks).reshape(2, FILTERS)

    def order_matrix(sizes):
        place = jnp.arange(steps, dtype=jnp.int32)[None, :]
        live = place < sizes[:, None]
        order = jnp.where(live & (direction == 1), sizes[:, None] - 1 - place, place)
        return ((order[:, :, None] == place[:, None, :]) & live[:, :, None]).astype(BF)

    own_order = order_matrix(lengths)
    cot = jnp.einsum("rts,rsd->trd", own_order, cotangent[0, 0], preferred_element_type=BF)

    ids = lax.dynamic_slice_in_dim(chars, direction * group, group, 0).reshape(
        group_tokens, char_count
    )
    table_low = char_emb.astype(BF)
    pooled = conv_forward(ids, table_low, conv_low, masks[1])
    features = jax.nn.silu(pooled + conv_bias_own)
    features_low = both_halves(features.astype(BF), blocks)
    bias_own = lax.dynamic_index_in_dim(
        gate_bias[0, 0].reshape(4, n, cell), me, 1, keepdims=False
    ).reshape(1, 4 * cell)
    moved = jnp.concatenate([cell_proj[0, 0].astype(BF), cot.reshape(steps * seqs, width)])
    gate_kept, gate_given = split_cells(gate_weight[0, 0], n)
    gate_came = swap_pipes(gate_given)
    gate_low = jnp.concatenate(
        [
            jnp.where(pipe == 0, gate_kept, gate_came),
            jnp.where(pipe == 0, gate_came, gate_kept),
        ]
    )
    direct, local_part = moved[: moved.shape[0] // 2], moved[moved.shape[0] // 2 :]
    swapped = swap_pipes(local_part)
    gate_low, gathered, features_low, bias_own, direct, swapped = lax.optimization_barrier(
        (gate_low, gathered, features_low, bias_own, direct, swapped)
    )
    bias_own = to_ranks(bias_own, 0)
    wing = n // 2
    swapped = lax.ppermute(
        swapped,
        ("pipe", "dp"),
        [(k, wing + k) for k in range(wing)] + [(n + wing + k, n + k) for k in range(wing)],
    )
    moved = jnp.concatenate(
        [to_ranks(direct, 0), jnp.where(lax.div(me, wing) == pipe, local_part, swapped)]
    )
    gate_own = lax.all_to_all(gate_low, "dp", 0, 0).reshape(2 * width, 4 * cell)
    highway_half = gathered[:, :FILTERS]
    proj_full = gathered[:, FILTERS:].reshape(pieces, proj_rows, holders, sub)
    proj_full = jnp.transpose(proj_full, (2, 1, 0, 3)).reshape(FILTERS, width)

    kept = [features]
    kept_low = [features_low]
    mixed = []
    for layer in range(2):
        pre = (
            jnp.dot(kept_low[layer], highway_half[layer], preferred_element_type=F32)
            + highway_bias_own[layer]
        )
        mixed.append(pre)
        gate = jax.nn.sigmoid(pre[:, half:])
        features = gate * features + (1.0 - gate) * jax.nn.silu(pre[:, :half])
        kept.append(features)
        kept_low.append(both_halves(features.astype(BF), blocks))
    own_last = lax.dynamic_slice_in_dim(kept_low[2], pipe * tokens, tokens, 0)
    encoded = jnp.dot(own_last, proj_full, preferred_element_type=F32) + proj_bias
    encoded_own = lax.all_gather(
        encoded.astype(BF).reshape(quarter, steps, width), ("dir", "pipe"), axis=0, tiled=True
    )
    inputs = jnp.einsum("rts,rsd->trd", own_order, encoded_own, preferred_element_type=BF)
    inputs = lax.ppermute(
        inputs,
        ("pipe", "dp"),
        [(k, wing + k) for k in range(wing)] + [(n + k, n + k) for k in range(wing, n)],
    )
    kept_low, gate_own, inputs, moved, bias_own = lax.optimization_barrier(
        (kept_low, gate_own, inputs, moved, bias_own)
    )
    cell_low = moved[:cell]
    cot = moved[cell:].reshape(steps, seqs, width)
    kept_all = [
        lax.all_gather(
            lax.dynamic_slice_in_dim(value, pipe * tokens, tokens, 0),
            ("dir", "dp"),
            axis=0,
            tiled=True,
        )
        for value in kept_low[:2]
    ]

    out_own, dx_own, grad_bias, grad_cell, grad_gate = lstm_call(
        n, inputs, gate_own, bias_own, cell_low, cell_low.T, cot
    )
    dx_own = from_ranks(dx_own.astype(BF), 0, (1,))
    dx_own, kept_all = lax.optimization_barrier((dx_own, kept_all))

    grad_stored = jnp.einsum(
        "rts,srd->rtd", own_order, dx_own, preferred_element_type=F32
    )
    grad_stored = jnp.where(pipe == 1, grad_stored, 0.0).astype(BF)
    grad_stored = grad_stored.reshape(1, -1, group_tokens, width)
    grad_encoded = lax.all_to_all(
        jnp.concatenate([grad_stored, grad_stored]).reshape(-1, group_tokens, width),
        ("pipe", "dir"),
        0,
        0,
    )
    grad_encoded = jnp.sum(grad_encoded.astype(F32), axis=0).astype(BF)
    own_grads = lax.dynamic_slice_in_dim(grad_encoded, pipe * tokens, tokens, 0)
    encoded_grads = lax.all_gather(own_grads, ("dir", "dp"), axis=0, tiled=True)

    grad_proj_bias = jnp.sum(own_grads.astype(F32), axis=0)
    proj_half = lax.dynamic_index_in_dim(
        proj_full.reshape(blocks, 2, sub, width), pipe, 1, keepdims=False
    ).reshape(half, width)
    grad_features = jnp.einsum("td,fd->tf", grad_encoded, proj_half, preferred_element_type=F32)
    columns = [None, None]
    grad_highway_bias = [None, None]
    for layer in (1, 0):
        nonlinear = mixed[layer][:, :half]
        gate = jax.nn.sigmoid(mixed[layer][:, half:])
        grad_mixed = jnp.concatenate(
            [
                grad_features * (1.0 - gate) * silu_slope(nonlinear),
                grad_features * (kept[layer] - jax.nn.silu(nonlinear)) * gate * (1.0 - gate),
            ],
            axis=1,
        ).astype(BF)
        columns[layer] = grad_mixed
        grad_highway_bias[layer] = jnp.sum(grad_mixed.astype(F32), axis=0)
        partial = jnp.einsum(
            "tg,fg->tf", grad_mixed, highway_half[layer], preferred_element_type=F32
        )
        partial = lax.optimization_barrier(partial).reshape(group_tokens, blocks, 2, sub)
        sent = lax.dynamic_index_in_dim(partial, 1 - pipe, 2, keepdims=False).astype(BF)
        came = lax.ppermute(sent, "pipe", [(0, 1), (1, 0)])
        mine = lax.dynamic_index_in_dim(partial, pipe, 2, keepdims=False)
        grad_features = grad_features * gate + (mine + came.astype(F32)).reshape(
            group_tokens, half
        )
    grad_before = grad_features * silu_slope(pooled + conv_bias_own)
    grad_conv, grad_table = conv_backward(ids, table_low, conv_low, masks, grad_before)

    def spread(value):
        split = value.reshape(*value.shape[:-1], -1, 1, sub)
        shown = jnp.arange(2, dtype=jnp.int32)[:, None] == pipe
        return jnp.where(shown, split, jnp.zeros_like(split)).reshape(*value.shape[:-1], -1)

    cols = FILTERS // everyone
    pair = jnp.stack(columns, axis=1).reshape(2, tokens, 2, 2, blocks, 1, sub)
    sent = lax.dynamic_index_in_dim(pair, 1 - pipe, 0, keepdims=False)
    came = lax.ppermute(sent, "pipe", [(0, 1), (1, 0)])
    mine = lax.dynamic_index_in_dim(pair, pipe, 0, keepdims=False)
    shown = (jnp.arange(2, dtype=jnp.int32) == pipe)[:, None]
    pair = jnp.where(shown, mine, came)
    pair = jnp.transpose(pair, (3, 4, 0, 1, 2, 5)).reshape(holders, tokens, 4 * sub)
    last = jnp.transpose(own_last.reshape(tokens, 2, holders, cols), (2, 0, 1, 3))
    pair = jnp.concatenate([pair, last.reshape(holders, tokens, 2 * cols)], axis=2)
    pair = lax.all_to_all(pair, ("dir", "dp"), 0, 0).reshape(holders * tokens, -1)
    grad_conv, pair, out_own, grad_cell = lax.optimization_barrier(
        (grad_conv, pair, out_own, grad_cell)
    )
    small = (
        grad_table,
        spread(jnp.sum(grad_before, axis=0)),
        spread(jnp.stack(grad_highway_bias)),
        grad_proj_bias,
    )
    flat = jnp.concatenate([value.reshape(-1) for value in small])
    share = -(-flat.shape[0] // (everyone * 128)) * 128
    flat = jnp.pad(flat, (0, share * everyone - flat.shape[0])).reshape(everyone, share)
    rank = pipe * wing + lax.rem(me, wing)
    mine = jnp.arange(n, dtype=jnp.int32)[None, :, None] == rank
    bias_parts = jnp.where(mine, grad_bias.reshape(4, 1, cell), 0.0).reshape(1, n, 4 * cell)
    layer = lax.div(me, wing) * lax.axis_size("dir") + direction
    mine = jnp.arange(everyone // n, dtype=jnp.int32) == layer
    bias_parts = jnp.where(mine[:, None, None], bias_parts, 0.0).reshape(everyone, 4 * cell)
    packed = jnp.concatenate(
        [
            jnp.transpose(
                spread(grad_conv).reshape(KMAX * CDIM, everyone, cols), (1, 0, 2)
            ).reshape(everyone, KMAX * CDIM * cols),
            flat,
            bias_parts,
        ],
        axis=1,
    ).astype(BF)
    summed = jnp.sum(lax.all_to_all(packed, ALL, 0, 0).astype(F32), axis=0)
    out_own = from_ranks(out_own, 0)
    grad_cell = from_ranks(grad_cell.astype(BF), 0)
    grad_gate = join_cells(grad_gate)
    activations = jnp.einsum("rts,srd->rtd", own_order, out_own, preferred_element_type=BF)
    grad_cell = grad_cell.astype(F32)
    grad_conv = summed[: KMAX * CDIM * cols].reshape(KMAX * CDIM, cols)
    grad_bias = summed[KMAX * CDIM * cols + share :]
    last = pair[:, 4 * sub :].reshape(holders * tokens, 2, cols)
    pair = pair[:, : 4 * sub].reshape(holders * tokens, 2, 2, sub)

    def partial_sums(owner):
        return [
            jnp.einsum(
                "tf,tg->fg",
                kept_all[layer],
                lax.dynamic_index_in_dim(pair[:, layer], owner, 1, keepdims=False),
                preferred_element_type=F32,
            )
            for layer in range(2)
        ] + [
            jnp.einsum(
                "tf,td->fd",
                lax.dynamic_index_in_dim(last, owner, 1, keepdims=False),
                encoded_grads,
                preferred_element_type=F32,
            )
        ]

    sent = jnp.concatenate(
        [value.astype(BF).reshape(-1, sub) for value in partial_sums(1 - pipe)]
    )
    came = lax.ppermute(sent, "pipe", [(0, 1), (1, 0)]).astype(F32)
    mine = partial_sums(pipe)
    grad_highway = jnp.stack(mine[:2]) + came[: 2 * FILTERS].reshape(2, FILTERS, sub)
    grad_proj = mine[2] + came[2 * FILTERS :].reshape(cols, width)
    shared = lax.all_to_all(
        jnp.broadcast_to(summed[KMAX * CDIM * cols :][:share], (everyone, share)), ALL, 0, 0
    ).reshape(-1)
    small_sums = []
    start = 0
    for value in small:
        small_sums.append(shared[start : start + value.size].reshape(value.shape))
        start += value.size
    return (
        activations[None, None],
        small_sums[0],
        grad_conv,
        small_sums[1],
        grad_highway,
        small_sums[2],
        grad_proj,
        small_sums[3],
        grad_gate[None, None],
        grad_bias[None, None],
        grad_cell[None, None],
    )


def solution(mesh):
    return jax.shard_map(
        local,
        mesh=mesh,
        in_specs=(
            P("dp", None, None),
            P("dp"),
            P(),
            P(None, ("dir", "dp")),
            P(),
            P(None, None, ("dir", "dp")),
            P(),
            P(("dir", "dp"), None),
            P(),
            P("pipe", "dir", "dp", None),
            P("pipe", "dir", None),
            P("pipe", "dir", "dp", None),
            P("pipe", "dir", "dp", None, None),
        ),
        out_specs=(
            P("pipe", "dir", "dp", None, None),
            P(),
            P(None, ("pipe", "dir", "dp")),
            P(),
            P(None, None, ("pipe", "dir", "dp")),
            P(),
            P(("pipe", "dir", "dp"), None),
            P(),
            P("pipe", "dir", "dp", None),
            P("pipe", "dir", "dp"),
            P("pipe", "dir", "dp", None),
        ),
        check_vma=False,
    )
```

```python
import functools
import math

import jax
import jax.numpy as jnp
from jax import lax
from jax.experimental import pallas as pl
from jax.experimental.pallas import tpu as pltpu
from jax.sharding import PartitionSpec as P

FILTERS = 2048
CDIM = 16
CVOCAB = 262
CHARS = 50
KMAX = 7
CLIP_LIMIT = 3.0
MASKED_FILL = -1000000000.0
MESH = pl.DeviceIdType.MESH
BF = jnp.bfloat16
F32 = jnp.float32
ALL = ("pipe", "dir", "dp")


def silu_slope(value):
    sig = jax.nn.sigmoid(value)
    return sig * (1.0 + value * (1.0 - sig))


def conv_masks(filter_index):
    filter_width = jnp.ones(filter_index.shape, jnp.int32)
    for doubling in range(6):
        filter_width = filter_width + (filter_index >= FILTERS // 64 * (1 << doubling)).astype(
            jnp.int32
        )
    offset_rows = jnp.arange(KMAX * CDIM, dtype=jnp.int32) // CDIM
    weight_mask = (offset_rows[:, None] < filter_width[None, :]).astype(jnp.float32)
    valid_place = jnp.arange(CHARS, dtype=jnp.int32)[:, None] <= CHARS - filter_width[None, :]
    return (weight_mask, valid_place)


def make_windows(embedded):
    padded = jnp.pad(embedded, ((0, 0), (0, KMAX - 1), (0, 0)))
    return jnp.concatenate(
        [padded[:, offset : offset + CHARS, :] for offset in range(KMAX)], axis=2
    )


def conv_response(ids_block, table_low, conv_low, valid_place):
    embedded = jnp.take(table_low, ids_block, axis=0)
    windows = make_windows(embedded)
    response = jnp.einsum("bpk,kf->bpf", windows, conv_low, preferred_element_type=jnp.float32)
    return (windows, jnp.where(valid_place[None], response, MASKED_FILL))


def over(count, step):
    if count <= 9:
        for off in range(count - 1, 0, -1):
            step(off)
    else:
        lax.fori_loop(1, count, lambda off, _: (step(off), 0)[1], 0)


def lstm_kernel(n, chunk, x_own, bias, p, pt, cot, w_in, *refs):
    out_ref, dx_ref, db_ref, dp_ref = refs[:4]
    dw_out = refs[4:n + 4]
    (xbuf, hbuf, dqbuf, gates, cells, ebuf, hown, gscr, escr, dabuf, ucell, dwacc, w, wt,
     stage, inbox, stage2, inbox2, relay, gbuf, rown,
     in_send, in_recv, ag_send, ag_recv, dq_send, dq_recv, rs_send, rs_recv,
     dx_send, dx_recv, x_send, x_recv, g_send, g_recv, st_sem, w_sem) = refs[n + 4:]
    steps, _, rows, width = xbuf.shape
    total = n * rows
    cell = cells.shape[2]
    pipe = lax.axis_index("pipe")
    direction = lax.axis_index("dir")
    place = lax.axis_index("dp")
    wing = n // 2
    first = place >= wing
    second = place < wing
    me = pipe * wing + lax.rem(place, wing)
    base = place - lax.rem(place, wing)
    partner = (pipe, direction, lax.rem(place + wing, n))

    def peer(off):
        if n & (n - 1):
            return lax.rem(me + off, n)
        return me ^ off

    def at_peer(off):
        rank = peer(off)
        return (lax.div(rank, wing), direction, base + lax.rem(rank, wing))

    barrier = pltpu.get_barrier_semaphore()
    over(n, lambda off: pl.semaphore_signal(
        barrier, inc=1, device_id=at_peer(off), device_id_type=MESH))
    pl.semaphore_signal(barrier, inc=1, device_id=partner, device_id_type=MESH)

    each = 2 * width // n
    load = pltpu.make_async_copy(w_in, w, w_sem)
    load.start()

    @pl.when(first)
    def _():
        for t in range(steps):
            xbuf[t, me] = x_own[t]

    hbuf[0] = jnp.zeros((n, rows, width), BF)
    cells[0] = jnp.zeros((total, cell), F32)
    pl.semaphore_wait(barrier, n)

    def ag_copy(buf, slot, off):
        out, into = (ag_send, ag_recv) if buf is hbuf else (dq_send, dq_recv)
        return pltpu.make_async_remote_copy(
            src_ref=buf.at[slot, me], dst_ref=buf.at[slot, me],
            send_sem=out.at[off], recv_sem=into.at[off],
            device_id=at_peer(off), device_id_type=MESH)

    def rs_copy(off):
        return pltpu.make_async_remote_copy(
            src_ref=stage.at[peer(off)], dst_ref=inbox.at[me],
            send_sem=rs_send.at[off], recv_sem=rs_recv.at[off],
            device_id=at_peer(off), device_id_type=MESH)

    def dx_copy(slot, off):
        return pltpu.make_async_remote_copy(
            src_ref=stage2.at[slot, peer(off)], dst_ref=inbox2.at[slot, me],
            send_sem=dx_send.at[slot, off], recv_sem=dx_recv.at[slot, off],
            device_id=at_peer(off), device_id_type=MESH)

    def x_copy(t):
        return pltpu.make_async_remote_copy(
            src_ref=hbuf.at[t + 1, me], dst_ref=xbuf.at[t, me],
            send_sem=x_send.at[t], recv_sem=x_recv.at[t],
            device_id=partner, device_id_type=MESH)

    def g_copy(t):
        return pltpu.make_async_remote_copy(
            src_ref=relay.at[t], dst_ref=gbuf.at[t],
            send_sem=g_send.at[t], recv_sem=g_recv.at[t],
            device_id=partner, device_id_type=MESH)

    def in_start(t):
        over(n, lambda off: pltpu.make_async_remote_copy(
            src_ref=xbuf.at[t, me], dst_ref=xbuf.at[t, me],
            send_sem=in_send.at[t], recv_sem=in_recv.at[t],
            device_id=at_peer(off), device_id_type=MESH).start())

    def in_wait(sem, t):
        blocks = xbuf.at[t, pl.ds(0, n - 1)]
        pltpu.make_async_copy(blocks, blocks, sem.at[t]).wait()

    @pl.when(first)
    def _():
        in_start(0)
        in_start(1)

    @pl.when(second)
    def _():
        x_copy(0).wait_recv()
        in_start(0)

    load.wait()
    for at in range(0, 2 * width, 128):
        wt[:, at:at + 128] = w[at:at + 128, :].T

    def ag_wait(buf, slot):
        def both(off):
            ag_copy(buf, slot, off).wait_send()
            ag_copy(buf, slot, off).wait_recv()
        over(n, both)

    def rs_wait():
        def both(off):
            rs_copy(off).wait_send()
            rs_copy(off).wait_recv()
        over(n, both)

    def forward(t, _):
        in_wait(in_recv, t)
        gscr[...] = jnp.dot(
            xbuf[t].reshape(total, width), w[:width, :], preferred_element_type=F32) + bias[...]

        @pl.when(t > 0)
        def _():
            ag_wait(hbuf, t)

        gscr[...] += jnp.dot(
            hbuf[t].reshape(total, width), w[width:, :], preferred_element_type=F32)

        def rows_step(k, _):
            at = pl.ds(pl.multiple_of(k * chunk, chunk), chunk)
            g = gscr[at, :]
            i = jax.nn.sigmoid(g[:, :cell])
            f = jax.nn.sigmoid(g[:, cell:2 * cell])
            m = jnp.tanh(g[:, 2 * cell:3 * cell])
            o = jax.nn.sigmoid(g[:, 3 * cell:])
            c = 3.0 * jnp.tanh((i * m + f * cells[t, at, :]) * (1.0 / 3.0))
            cells[t + 1, at, :] = c
            ebuf[t, at, :] = (o * jnp.tanh(c)).astype(BF)
            kind = gates.dtype
            gates[t, at, :cell] = i.astype(kind)
            gates[t, at, cell:2 * cell] = f.astype(kind)
            gates[t, at, 2 * cell:3 * cell] = m.astype(kind)
            gates[t, at, 3 * cell:] = o.astype(kind)
            return 0

        lax.fori_loop(0, total // chunk, rows_step, 0)
        q = jnp.dot(ebuf[t], p[...], preferred_element_type=F32)
        stage[...] = q.astype(BF).reshape(n, rows, width)
        over(n, lambda off: rs_copy(off).start())
        inbox[me] = stage[me]

        @pl.when(first & (t + 2 < steps))
        def _():
            in_start(t + 2)

        @pl.when(second & (t + 1 < steps))
        def _():
            x_copy(t + 1).wait_recv()
            in_start(t + 1)

        rs_wait()
        h = 3.0 * jnp.tanh(jnp.sum(inbox[...].astype(F32), axis=0) * (1.0 / 3.0))
        hown[t] = h
        hbuf[t + 1, me] = h.astype(BF)
        over(n, lambda off: ag_copy(hbuf, t + 1, off).start())

        @pl.when(first)
        def _():
            x_copy(t).start()

        add = jnp.where(second, 1.0, 0.0)
        out_ref[t] = (h + add * xbuf[t, me].astype(F32)).astype(BF)
        return 0

    lax.fori_loop(0, steps, forward, 0)
    ag_wait(hbuf, steps)

    lax.fori_loop(0, steps, lambda t, _: (in_wait(in_send, t), 0)[1], 0)

    @pl.when(first)
    def _():
        lax.fori_loop(0, steps, lambda t, _: (x_copy(t).wait_send(), 0)[1], 0)

    rown[...] = jnp.zeros((rows, width), F32)
    ucell[...] = jnp.zeros((total, cell), F32)
    dwacc[...] = jnp.zeros(dwacc.shape, F32)
    db_ref[...] = jnp.zeros(db_ref.shape, F32)
    dp_ref[...] = jnp.zeros(dp_ref.shape, F32)

    def dx_finish(t):
        slot = lax.rem(t, 2)

        def both(off):
            dx_copy(slot, off).wait_send()
            dx_copy(slot, off).wait_recv()
        over(n, both)
        dx = jnp.sum(inbox2[slot].astype(F32), axis=0)
        dx_ref[t] = dx

        @pl.when(second)
        def _():
            relay[t] = (dx + cot[t].astype(F32)).astype(BF)
            g_copy(t).start()

    def backward(k, _):
        t = steps - 1 - k
        slot = lax.rem(t, 2)
        up = rown[...] + cot[t].astype(F32)
        rown[...] = up

        @pl.when(first)
        def _():
            g_copy(t).wait_recv()
            rown[...] = rown[...] + gbuf[t].astype(F32)

        ratio = hown[t] * (1.0 / 3.0)
        dqbuf[t, me] = (rown[...] * (1.0 - ratio * ratio)).astype(BF)
        over(n, lambda off: ag_copy(dqbuf, t, off).start())

        @pl.when(k > 0)
        def _():
            dx_finish(t + 1)

        ag_wait(dqbuf, t)
        escr[...] = jnp.dot(
            dqbuf[t].reshape(total, width), pt[...], preferred_element_type=F32)

        def rows_step(j, _):
            at = pl.ds(pl.multiple_of(j * chunk, chunk), chunk)
            de = escr[at, :]
            i = gates[t, at, :cell].astype(F32)
            f = gates[t, at, cell:2 * cell].astype(F32)
            m = gates[t, at, 2 * cell:3 * cell].astype(F32)
            o = gates[t, at, 3 * cell:].astype(F32)
            c = cells[t + 1, at, :]
            tc = jnp.tanh(c)
            cr = c * (1.0 / 3.0)
            dc = (de * o * (1.0 - tc * tc) + ucell[at, :]) * (1.0 - cr * cr)
            ucell[at, :] = dc * f
            for block, value in enumerate((
                dc * m * i * (1.0 - i),
                dc * cells[t, at, :] * f * (1.0 - f),
                dc * i * (1.0 - m * m),
                de * tc * o * (1.0 - o),
            )):
                value = value.astype(BF)
                where = pl.ds(block * cell, cell)
                dabuf[0, at, where] = value
                db_ref[:, where] += jnp.sum(value.astype(F32), axis=0, keepdims=True)
            return 0

        lax.fori_loop(0, total // chunk, rows_step, 0)
        r = jnp.dot(dabuf[0], wt[:, width:], preferred_element_type=F32)
        stage[...] = r.astype(BF).reshape(n, rows, width)
        over(n, lambda off: rs_copy(off).start())
        inbox[me] = stage[me]
        dx = jnp.dot(dabuf[0], wt[:, :width], preferred_element_type=F32)
        stage2[slot] = dx.astype(BF).reshape(n, rows, width)
        over(n, lambda off: dx_copy(slot, off).start())
        inbox2[slot, me] = stage2[slot, me]
        for half, buf in enumerate((xbuf, hbuf)):
            dwacc[pl.ds(half * width, width), :] += lax.dot_general(
                buf[t].reshape(total, width), dabuf[0], (((0,), (0,)), ((), ())),
                preferred_element_type=F32)
        dp_ref[...] += lax.dot_general(
            ebuf[t], dqbuf[t].reshape(total, width), (((0,), (0,)), ((), ())),
            preferred_element_type=F32)
        rs_wait()
        rown[...] = jnp.sum(inbox[...].astype(F32), axis=0)
        return 0

    lax.fori_loop(0, steps, backward, 0)
    dx_finish(0)

    @pl.when(second)
    def _():
        lax.fori_loop(0, steps, lambda t, _: (g_copy(t).wait_send(), 0)[1], 0)

    def dw_copy(off):
        return pltpu.make_async_copy(
            dabuf.at[off % 2, pl.ds(0, each)], dw_out[off], st_sem.at[off % 2])

    for off in range(n):
        if off > 1:
            dw_copy(off - 2).wait()
        at = pl.multiple_of(lax.rem(me + off, n) * each, each)
        dabuf[off % 2, :each, :] = dwacc[pl.ds(at, each), :].astype(BF)
        dw_copy(off).start()
    for off in range(n - 2, n):
        dw_copy(off).wait()


def lstm_call(n, x, weights, bias, p, pt, cot, chunk=16):
    steps, rows, width = x.shape
    cell = p.shape[0]
    total = n * rows
    sds = jax.ShapeDtypeStruct
    vm = pl.BlockSpec(memory_space=pltpu.VMEM)
    hb = pl.BlockSpec(memory_space=pl.ANY)
    keep = F32 if n <= 8 else BF
    V = pltpu.VMEM
    dma = pltpu.SemaphoreType.DMA
    return pl.pallas_call(
        functools.partial(lstm_kernel, n, chunk),
        out_shape=(
            sds((steps, rows, width), BF), sds((steps, rows, width), F32),
            sds((1, 4 * cell), F32), sds((cell, width), F32),
            *[sds((2 * width // n, 4 * cell), BF)] * n),
        in_specs=[vm] * 5 + [hb],
        out_specs=[vm] * 4 + [hb] * n,
        scratch_shapes=[
            V((steps, n, rows, width), BF), V((steps + 1, n, rows, width), BF),
            V((steps, n, rows, width), BF), V((steps, total, 4 * cell), keep),
            V((steps + 1, total, cell), F32), V((steps, total, cell), BF),
            V((steps, rows, width), F32), V((total, 4 * cell), F32),
            V((total, cell), F32), V((2, total, 4 * cell), BF), V((total, cell), F32),
            V((2 * width, 4 * cell), F32), V((2 * width, 4 * cell), BF),
            V((4 * cell, 2 * width), BF),
            V((n, rows, width), BF), V((n, rows, width), BF),
            V((2, n, rows, width), BF), V((2, n, rows, width), BF),
            V((steps, rows, width), BF), V((steps, rows, width), BF), V((rows, width), F32),
            dma((steps,)), dma((steps,)), dma((n,)), dma((n,)), dma((n,)), dma((n,)), dma((n,)), dma((n,)), dma((2, n)), dma((2, n)),
            dma((steps,)), dma((steps,)), dma((steps,)), dma((steps,)), dma((2,)), dma,
        ],
        compiler_params=pltpu.CompilerParams(
            collective_id=0, has_side_effects=True, vmem_limit_bytes=60 * 1024 * 1024),
        cost_estimate=pl.CostEstimate(
            flops=300_000_000_000, bytes_accessed=64 * 1024 * 1024, transcendentals=0),
        name="relay_lstm",
    )(x, bias, p, pt, cot, weights)


def split_cells(weight, n):
    rows, gates = weight.shape
    cell = gates // (4 * n)
    wing = n // 2

    def body(src, keep, give):
        pipe = lax.axis_index("pipe")
        for k in range(wing):
            for dst, side in ((keep, pipe), (give, 1 - pipe)):
                at = pl.multiple_of((side * wing + k) * cell, cell)
                dst[k] = src[:, pl.ds(at, cell)].astype(BF)

    return pl.pallas_call(
        body,
        grid=(4,),
        out_shape=[jax.ShapeDtypeStruct((wing, rows, 4 * cell), BF)] * 2,
        in_specs=[pl.BlockSpec((rows, n * cell), lambda b: (0, b))],
        out_specs=[pl.BlockSpec((wing, rows, cell), lambda b: (0, 0, b))] * 2,
        cost_estimate=pl.CostEstimate(
            flops=0, bytes_accessed=6 * rows * gates, transcendentals=0
        ),
        name="split_cells",
    )(weight)


def join_cells(blocks):
    n = len(blocks)
    rows, gates = blocks[0].shape
    cell = gates // 4

    def body(*refs):
        dst = refs[n]
        for off in range(n):
            rank = lax.rem(lax.axis_index("dp") + (n - off), n)
            dst[:, pl.ds(pl.multiple_of(rank * cell, cell), cell)] = refs[off][...].astype(F32)

    return pl.pallas_call(
        body,
        grid=(4,),
        out_shape=jax.ShapeDtypeStruct((rows, n * gates), F32),
        in_specs=[pl.BlockSpec((rows, cell), lambda b: (0, b))] * n,
        out_specs=pl.BlockSpec((rows, n * cell), lambda b: (0, b)),
        cost_estimate=pl.CostEstimate(
            flops=0, bytes_accessed=6 * n * rows * gates, transcendentals=0
        ),
        name="join_cells",
    )(*blocks)


def swap_pipes(value):
    return lax.ppermute(value, "pipe", [(0, 1), (1, 0)])


def rank_pairs(n, off, layers=(0, 1)):
    wing = n // 2
    pairs = []
    for layer in layers:
        for j in range(n):
            rank = (j + off) % n
            pairs.append((layer * n + j, rank // wing * n + layer * wing + rank % wing))
    return pairs


def to_ranks(value, off):
    return lax.ppermute(value, ("pipe", "dp"), rank_pairs(lax.axis_size("dp"), off))


def from_ranks(value, off, layers=(0, 1)):
    pairs = rank_pairs(lax.axis_size("dp"), -off, layers)
    return lax.ppermute(value, ("pipe", "dp"), [(there, here) for here, there in pairs])


def conv_forward(ids, table_low, conv_low, valid_place):
    return jax.nn.logsumexp(conv_response(ids, table_low, conv_low, valid_place)[1], axis=1)


def own_half(value, blocks):
    sub = value.shape[-1] // (2 * blocks)
    split = value.reshape(*value.shape[:-1], blocks, 2, sub)
    mine = lax.dynamic_index_in_dim(split, lax.axis_index("pipe"), split.ndim - 2, keepdims=False)
    return mine.reshape(*value.shape[:-1], blocks * sub)


def both_halves(value, blocks):
    tokens, half = value.shape
    pair = lax.all_gather(value, "pipe").reshape(2, tokens, blocks, half // blocks)
    return jnp.transpose(pair, (1, 2, 0, 3)).reshape(tokens, 2 * half)


def conv_backward(ids, table_low, conv_low, masks, grad_before):
    weight_mask, valid_place = masks
    windows, response = conv_response(ids, table_low, conv_low, valid_place)
    share = jax.nn.softmax(response, axis=1)
    grad_response = (grad_before[:, None, :] * share).astype(BF)
    grad_conv = jnp.einsum("bpk,bpf->kf", windows, grad_response, preferred_element_type=F32)
    grad_windows = jnp.einsum("bpf,kf->bpk", grad_response, conv_low, preferred_element_type=F32)
    grad_embedded = jnp.zeros((ids.shape[0], CHARS + KMAX - 1, CDIM), F32)
    for offset in range(KMAX):
        grad_embedded = grad_embedded + jnp.pad(
            grad_windows[:, :, offset * CDIM : (offset + 1) * CDIM],
            ((0, 0), (offset, KMAX - 1 - offset), (0, 0)),
        )
    grad_embedded = grad_embedded[:, :CHARS].astype(BF)
    one_hot = (ids[:, :, None] == jnp.arange(CVOCAB, dtype=jnp.int32)).astype(BF)
    grad_table = jnp.einsum("bpv,bpc->vc", one_hot, grad_embedded, preferred_element_type=F32)
    return grad_conv * weight_mask, grad_table


def local(
    chars,
    lengths,
    char_emb,
    conv_weight,
    conv_bias,
    highway_weight,
    highway_bias,
    proj_weight,
    proj_bias,
    gate_weight,
    gate_bias,
    cell_proj,
    cotangent,
):
    n = lax.axis_size("dp")
    pipe = lax.axis_index("pipe")
    direction = lax.axis_index("dir")
    me = lax.axis_index("dp")
    everyone = lax.axis_size(ALL)
    holders = lax.axis_size(("dir", "dp"))
    seqs, steps, char_count = chars.shape
    group = seqs // lax.axis_size("dir")
    quarter = group // 2
    group_tokens = group * steps
    tokens = quarter * steps
    width = cell_proj.shape[3]
    cell = cell_proj.shape[2]
    blocks = holders // 2
    sub = FILTERS // holders
    half = FILTERS // 2
    filter_index = (
        (2 * jnp.arange(blocks, dtype=jnp.int32) + pipe)[:, None] * sub
        + jnp.arange(sub, dtype=jnp.int32)[None, :]
    ).reshape(half)
    masks = conv_masks(filter_index)

    proj_rows = proj_weight.shape[0]
    pieces = width // sub
    proj_blocks = jnp.transpose(proj_weight.reshape(proj_rows, pieces, sub), (1, 0, 2))
    proj_blocks = proj_blocks.reshape(2, pieces * proj_rows // 2, sub)
    mine = lax.dynamic_slice_in_dim(highway_weight, pipe * sub, sub, 2)
    gathered = lax.all_gather(
        jnp.concatenate([mine, proj_blocks], axis=1).astype(BF), ("dir", "dp"), axis=2, tiled=True
    )
    conv_full = lax.all_to_all(
        jnp.broadcast_to(conv_weight.astype(BF), (holders, KMAX * CDIM, sub)), ("dir", "dp"), 0, 0
    ).reshape(blocks, 2, KMAX * CDIM, sub)
    conv_low = lax.dynamic_index_in_dim(conv_full, pipe, 1, keepdims=False)
    conv_low = jnp.transpose(conv_low, (1, 0, 2)).reshape(KMAX * CDIM, half)
    conv_low = conv_low * masks[0].astype(BF)
    conv_bias_own = own_half(conv_bias, blocks)
    highway_bias_own = own_half(highway_bias.reshape(2, 2, FILTERS), blocks).reshape(2, FILTERS)

    def order_matrix(sizes):
        place = jnp.arange(steps, dtype=jnp.int32)[None, :]
        live = place < sizes[:, None]
        order = jnp.where(live & (direction == 1), sizes[:, None] - 1 - place, place)
        return ((order[:, :, None] == place[:, None, :]) & live[:, :, None]).astype(BF)

    own_order = order_matrix(lengths)
    cot = jnp.einsum("rts,rsd->trd", own_order, cotangent[0, 0], preferred_element_type=BF)

    ids = lax.dynamic_slice_in_dim(chars, direction * group, group, 0).reshape(
        group_tokens, char_count
    )
    table_low = char_emb.astype(BF)
    pooled = conv_forward(ids, table_low, conv_low, masks[1])
    features = jax.nn.silu(pooled + conv_bias_own)
    features_low = both_halves(features.astype(BF), blocks)
    bias_own = lax.dynamic_index_in_dim(
        gate_bias[0, 0].reshape(4, n, cell), me, 1, keepdims=False
    ).reshape(1, 4 * cell)
    moved = jnp.concatenate([cell_proj[0, 0].astype(BF), cot.reshape(steps * seqs, width)])
    gate_kept, gate_given = split_cells(gate_weight[0, 0], n)
    gate_came = swap_pipes(gate_given)
    gate_low = jnp.concatenate(
        [
            jnp.where(pipe == 0, gate_kept, gate_came),
            jnp.where(pipe == 0, gate_came, gate_kept),
        ]
    )
    direct, local_part = moved[: moved.shape[0] // 2], moved[moved.shape[0] // 2 :]
    swapped = swap_pipes(local_part)
    gathered, features_low, bias_own, direct, swapped = lax.optimization_barrier(
        (gathered, features_low, bias_own, direct, swapped)
    )
    bias_own = to_ranks(bias_own, 0)
    wing = n // 2
    swapped = lax.ppermute(
        swapped,
        ("pipe", "dp"),
        [(k, wing + k) for k in range(wing)] + [(n + wing + k, n + k) for k in range(wing)],
    )
    moved = jnp.concatenate(
        [to_ranks(direct, 0), jnp.where(lax.div(me, wing) == pipe, local_part, swapped)]
    )
    gate_own = lax.all_to_all(gate_low, "dp", 0, 0).reshape(2 * width, 4 * cell)
    highway_half = gathered[:, :FILTERS]
    proj_full = gathered[:, FILTERS:].reshape(pieces, proj_rows, holders, sub)
    proj_full = jnp.transpose(proj_full, (2, 1, 0, 3)).reshape(FILTERS, width)

    kept = [features]
    kept_low = [features_low]
    mixed = []
    for layer in range(2):
        pre = (
            jnp.dot(kept_low[layer], highway_half[layer], preferred_element_type=F32)
            + highway_bias_own[layer]
        )
        mixed.append(pre)
        gate = jax.nn.sigmoid(pre[:, half:])
        features = gate * features + (1.0 - gate) * jax.nn.silu(pre[:, :half])
        kept.append(features)
        kept_low.append(both_halves(features.astype(BF), blocks))
    own_last = lax.dynamic_slice_in_dim(kept_low[2], pipe * tokens, tokens, 0)
    encoded = jnp.dot(own_last, proj_full, preferred_element_type=F32) + proj_bias
    encoded_own = lax.all_gather(
        encoded.astype(BF).reshape(quarter, steps, width), ("dir", "pipe"), axis=0, tiled=True
    )
    inputs = jnp.einsum("rts,rsd->trd", own_order, encoded_own, preferred_element_type=BF)
    inputs = lax.ppermute(
        inputs,
        ("pipe", "dp"),
        [(k, wing + k) for k in range(wing)] + [(n + k, n + k) for k in range(wing, n)],
    )
    kept_low, gate_own, inputs, moved, bias_own = lax.optimization_barrier(
        (kept_low, gate_own, inputs, moved, bias_own)
    )
    cell_low = moved[:cell]
    cot = moved[cell:].reshape(steps, seqs, width)
    kept_all = [
        lax.all_gather(
            lax.dynamic_slice_in_dim(value, pipe * tokens, tokens, 0),
            ("dir", "dp"),
            axis=0,
            tiled=True,
        )
        for value in kept_low[:2]
    ]

    out_own, dx_own, grad_bias, grad_cell, *grad_gate = lstm_call(
        n, inputs, gate_own, bias_own, cell_low, cell_low.T, cot
    )
    dx_own = from_ranks(dx_own.astype(BF), 0, (1,))
    grad_gate = [from_ranks(block, off) for off, block in enumerate(grad_gate)]
    dx_own, kept_all = lax.optimization_barrier((dx_own, kept_all))

    grad_stored = jnp.einsum(
        "rts,srd->rtd", own_order, dx_own, preferred_element_type=F32
    )
    grad_stored = jnp.where(pipe == 1, grad_stored, 0.0).astype(BF)
    grad_stored = grad_stored.reshape(1, -1, group_tokens, width)
    grad_encoded = lax.all_to_all(
        jnp.concatenate([grad_stored, grad_stored]).reshape(-1, group_tokens, width),
        ("pipe", "dir"),
        0,
        0,
    )
    grad_encoded = jnp.sum(grad_encoded.astype(F32), axis=0).astype(BF)
    own_grads = lax.dynamic_slice_in_dim(grad_encoded, pipe * tokens, tokens, 0)
    encoded_grads = lax.all_gather(own_grads, ("dir", "dp"), axis=0, tiled=True)

    grad_proj_bias = jnp.sum(own_grads.astype(F32), axis=0)
    proj_half = lax.dynamic_index_in_dim(
        proj_full.reshape(blocks, 2, sub, width), pipe, 1, keepdims=False
    ).reshape(half, width)
    grad_features = jnp.einsum("td,fd->tf", grad_encoded, proj_half, preferred_element_type=F32)
    columns = [None, None]
    grad_highway_bias = [None, None]
    for layer in (1, 0):
        nonlinear = mixed[layer][:, :half]
        gate = jax.nn.sigmoid(mixed[layer][:, half:])
        grad_mixed = jnp.concatenate(
            [
                grad_features * (1.0 - gate) * silu_slope(nonlinear),
                grad_features * (kept[layer] - jax.nn.silu(nonlinear)) * gate * (1.0 - gate),
            ],
            axis=1,
        ).astype(BF)
        columns[layer] = grad_mixed
        grad_highway_bias[layer] = jnp.sum(grad_mixed.astype(F32), axis=0)
        partial = jnp.einsum(
            "tg,fg->tf", grad_mixed, highway_half[layer], preferred_element_type=F32
        )
        partial = lax.optimization_barrier(partial).reshape(group_tokens, blocks, 2, sub)
        sent = lax.dynamic_index_in_dim(partial, 1 - pipe, 2, keepdims=False).astype(BF)
        came = lax.ppermute(sent, "pipe", [(0, 1), (1, 0)])
        mine = lax.dynamic_index_in_dim(partial, pipe, 2, keepdims=False)
        grad_features = grad_features * gate + (mine + came.astype(F32)).reshape(
            group_tokens, half
        )
    grad_before = grad_features * silu_slope(pooled + conv_bias_own)
    grad_before, grad_gate[1:5] = lax.optimization_barrier((grad_before, grad_gate[1:5]))
    grad_conv, grad_table = conv_backward(ids, table_low, conv_low, masks, grad_before)

    def spread(value):
        split = value.reshape(*value.shape[:-1], -1, 1, sub)
        shown = jnp.arange(2, dtype=jnp.int32)[:, None] == pipe
        return jnp.where(shown, split, jnp.zeros_like(split)).reshape(*value.shape[:-1], -1)

    cols = FILTERS // everyone
    pair = jnp.stack(columns, axis=1).reshape(2, tokens, 2, 2, blocks, 1, sub)
    sent = lax.dynamic_index_in_dim(pair, 1 - pipe, 0, keepdims=False)
    came = lax.ppermute(sent, "pipe", [(0, 1), (1, 0)])
    mine = lax.dynamic_index_in_dim(pair, pipe, 0, keepdims=False)
    shown = (jnp.arange(2, dtype=jnp.int32) == pipe)[:, None]
    pair = jnp.where(shown, mine, came)
    pair = jnp.transpose(pair, (3, 4, 0, 1, 2, 5)).reshape(holders, tokens, 4 * sub)
    last = jnp.transpose(own_last.reshape(tokens, 2, holders, cols), (2, 0, 1, 3))
    pair = jnp.concatenate([pair, last.reshape(holders, tokens, 2 * cols)], axis=2)
    pair = lax.all_to_all(pair, ("dir", "dp"), 0, 0).reshape(holders * tokens, -1)
    grad_conv, pair, out_own, grad_cell = lax.optimization_barrier(
        (grad_conv, pair, out_own, grad_cell)
    )
    small = (
        grad_table,
        spread(jnp.sum(grad_before, axis=0)),
        spread(jnp.stack(grad_highway_bias)),
        grad_proj_bias,
    )
    flat = jnp.concatenate([value.reshape(-1) for value in small])
    share = -(-flat.shape[0] // (everyone * 128)) * 128
    flat = jnp.pad(flat, (0, share * everyone - flat.shape[0])).reshape(everyone, share)
    rank = pipe * wing + lax.rem(me, wing)
    mine = jnp.arange(n, dtype=jnp.int32)[None, :, None] == rank
    bias_parts = jnp.where(mine, grad_bias.reshape(4, 1, cell), 0.0).reshape(1, n, 4 * cell)
    layer = lax.div(me, wing) * lax.axis_size("dir") + direction
    mine = jnp.arange(everyone // n, dtype=jnp.int32) == layer
    bias_parts = jnp.where(mine[:, None, None], bias_parts, 0.0).reshape(everyone, 4 * cell)
    packed = jnp.concatenate(
        [
            jnp.transpose(
                spread(grad_conv).reshape(KMAX * CDIM, everyone, cols), (1, 0, 2)
            ).reshape(everyone, KMAX * CDIM * cols),
            flat,
            bias_parts,
        ],
        axis=1,
    ).astype(BF)
    summed = jnp.sum(lax.all_to_all(packed, ALL, 0, 0).astype(F32), axis=0)
    out_own = from_ranks(out_own, 0)
    grad_cell = from_ranks(grad_cell.astype(BF), 0)
    summed, grad_gate = lax.optimization_barrier((summed, grad_gate))
    grad_gate = join_cells(grad_gate)
    activations = jnp.einsum("rts,srd->rtd", own_order, out_own, preferred_element_type=BF)
    grad_cell = grad_cell.astype(F32)
    grad_conv = summed[: KMAX * CDIM * cols].reshape(KMAX * CDIM, cols)
    grad_bias = summed[KMAX * CDIM * cols + share :]
    last = pair[:, 4 * sub :].reshape(holders * tokens, 2, cols)
    pair = pair[:, : 4 * sub].reshape(holders * tokens, 2, 2, sub)

    def partial_sums(owner):
        return [
            jnp.einsum(
                "tf,tg->fg",
                kept_all[layer],
                lax.dynamic_index_in_dim(pair[:, layer], owner, 1, keepdims=False),
                preferred_element_type=F32,
            )
            for layer in range(2)
        ] + [
            jnp.einsum(
                "tf,td->fd",
                lax.dynamic_index_in_dim(last, owner, 1, keepdims=False),
                encoded_grads,
                preferred_element_type=F32,
            )
        ]

    sent = jnp.concatenate(
        [value.astype(BF).reshape(-1, sub) for value in partial_sums(1 - pipe)]
    )
    came = lax.ppermute(sent, "pipe", [(0, 1), (1, 0)]).astype(F32)
    mine = partial_sums(pipe)
    grad_highway = jnp.stack(mine[:2]) + came[: 2 * FILTERS].reshape(2, FILTERS, sub)
    grad_proj = mine[2] + came[2 * FILTERS :].reshape(cols, width)
    shared = lax.all_to_all(
        jnp.broadcast_to(summed[KMAX * CDIM * cols :][:share], (everyone, share)), ALL, 0, 0
    ).reshape(-1)
    small_sums = []
    start = 0
    for value in small:
        small_sums.append(shared[start : start + value.size].reshape(value.shape))
        start += value.size
    return (
        activations[None, None],
        small_sums[0],
        grad_conv,
        small_sums[1],
        grad_highway,
        small_sums[2],
        grad_proj,
        small_sums[3],
        grad_gate[None, None],
        grad_bias[None, None],
        grad_cell[None, None],
    )


def solution(mesh):
    return jax.shard_map(
        local,
        mesh=mesh,
        in_specs=(
            P("dp", None, None),
            P("dp"),
            P(),
            P(None, ("dir", "dp")),
            P(),
            P(None, None, ("dir", "dp")),
            P(),
            P(("dir", "dp"), None),
            P(),
            P("pipe", "dir", "dp", None),
            P("pipe", "dir", None),
            P("pipe", "dir", "dp", None),
            P("pipe", "dir", "dp", None, None),
        ),
        out_specs=(
            P("pipe", "dir", "dp", None, None),
            P(),
            P(None, ("pipe", "dir", "dp")),
            P(),
            P(None, None, ("pipe", "dir", "dp")),
            P(),
            P(("pipe", "dir", "dp"), None),
            P(),
            P("pipe", "dir", "dp", None),
            P("pipe", "dir", "dp"),
            P("pipe", "dir", "dp", None),
        ),
        check_vma=False,
    )
```

```python
import functools
import math

import jax
import jax.numpy as jnp
from jax import lax
from jax.experimental import pallas as pl
from jax.experimental.pallas import tpu as pltpu
from jax.sharding import PartitionSpec as P

FILTERS = 2048
CDIM = 16
CVOCAB = 262
CHARS = 50
KMAX = 7
CLIP_LIMIT = 3.0
MASKED_FILL = -1000000000.0
MESH = pl.DeviceIdType.MESH
BF = jnp.bfloat16
F32 = jnp.float32
ALL = ("pipe", "dir", "dp")


def silu_slope(value):
    sig = jax.nn.sigmoid(value)
    return sig * (1.0 + value * (1.0 - sig))


def conv_masks(filter_index):
    filter_width = jnp.ones(filter_index.shape, jnp.int32)
    for doubling in range(6):
        filter_width = filter_width + (filter_index >= FILTERS // 64 * (1 << doubling)).astype(
            jnp.int32
        )
    offset_rows = jnp.arange(KMAX * CDIM, dtype=jnp.int32) // CDIM
    weight_mask = (offset_rows[:, None] < filter_width[None, :]).astype(jnp.float32)
    valid_place = jnp.arange(CHARS, dtype=jnp.int32)[:, None] <= CHARS - filter_width[None, :]
    return (weight_mask, valid_place)


def make_windows(embedded):
    padded = jnp.pad(embedded, ((0, 0), (0, KMAX - 1), (0, 0)))
    return jnp.concatenate(
        [padded[:, offset : offset + CHARS, :] for offset in range(KMAX)], axis=2
    )


def conv_response(ids_block, table_low, conv_low, valid_place):
    embedded = jnp.take(table_low, ids_block, axis=0)
    windows = make_windows(embedded)
    response = jnp.einsum("bpk,kf->bpf", windows, conv_low, preferred_element_type=jnp.float32)
    return (windows, jnp.where(valid_place[None], response, MASKED_FILL))


def over(count, step):
    if count <= 9:
        for off in range(count - 1, 0, -1):
            step(off)
    else:
        lax.fori_loop(1, count, lambda off, _: (step(off), 0)[1], 0)


def lstm_kernel(n, chunk, x_own, bias, p, pt, cot, w_in, *refs):
    out_ref, dx_ref, db_ref, dp_ref = refs[:4]
    dw_out = refs[4:n + 4]
    (xbuf, hbuf, dqbuf, gates, cells, ebuf, hown, gscr, escr, dabuf, ucell, dwacc, w, wt,
     stage, inbox, stage2, inbox2, relay, gbuf, rown,
     in_send, in_recv, ag_send, ag_recv, dq_send, dq_recv, rs_send, rs_recv,
     dx_send, dx_recv, x_send, x_recv, g_send, g_recv, st_sem, w_sem) = refs[n + 4:]
    steps, _, rows, width = xbuf.shape
    total = n * rows
    cell = cells.shape[2]
    pipe = lax.axis_index("pipe")
    direction = lax.axis_index("dir")
    place = lax.axis_index("dp")
    wing = n // 2
    first = place >= wing
    second = place < wing
    me = pipe * wing + lax.rem(place, wing)
    base = place - lax.rem(place, wing)
    partner = (pipe, direction, lax.rem(place + wing, n))

    def peer(off):
        if n & (n - 1):
            return lax.rem(me + off, n)
        return me ^ off

    def at_peer(off):
        rank = peer(off)
        return (lax.div(rank, wing), direction, base + lax.rem(rank, wing))

    barrier = pltpu.get_barrier_semaphore()
    over(n, lambda off: pl.semaphore_signal(
        barrier, inc=1, device_id=at_peer(off), device_id_type=MESH))
    pl.semaphore_signal(barrier, inc=1, device_id=partner, device_id_type=MESH)

    each = 2 * width // n
    load = pltpu.make_async_copy(w_in, w, w_sem)
    load.start()

    @pl.when(first)
    def _():
        for t in range(steps):
            xbuf[t, me] = x_own[t]

    hbuf[0] = jnp.zeros((n, rows, width), BF)
    cells[0] = jnp.zeros((total, cell), F32)
    pl.semaphore_wait(barrier, n)

    def ag_copy(buf, slot, off):
        out, into = (ag_send, ag_recv) if buf is hbuf else (dq_send, dq_recv)
        return pltpu.make_async_remote_copy(
            src_ref=buf.at[slot, me], dst_ref=buf.at[slot, me],
            send_sem=out.at[off], recv_sem=into.at[off],
            device_id=at_peer(off), device_id_type=MESH)

    def rs_copy(off):
        return pltpu.make_async_remote_copy(
            src_ref=stage.at[peer(off)], dst_ref=inbox.at[me],
            send_sem=rs_send.at[off], recv_sem=rs_recv.at[off],
            device_id=at_peer(off), device_id_type=MESH)

    def dx_copy(slot, off):
        return pltpu.make_async_remote_copy(
            src_ref=stage2.at[slot, peer(off)], dst_ref=inbox2.at[slot, me],
            send_sem=dx_send.at[slot, off], recv_sem=dx_recv.at[slot, off],
            device_id=at_peer(off), device_id_type=MESH)

    def x_copy(t):
        return pltpu.make_async_remote_copy(
            src_ref=hbuf.at[t + 1, me], dst_ref=xbuf.at[t, me],
            send_sem=x_send.at[t], recv_sem=x_recv.at[t],
            device_id=partner, device_id_type=MESH)

    def g_copy(t):
        return pltpu.make_async_remote_copy(
            src_ref=relay.at[t], dst_ref=gbuf.at[t],
            send_sem=g_send.at[t], recv_sem=g_recv.at[t],
            device_id=partner, device_id_type=MESH)

    def in_start(t):
        over(n, lambda off: pltpu.make_async_remote_copy(
            src_ref=xbuf.at[t, me], dst_ref=xbuf.at[t, me],
            send_sem=in_send.at[t], recv_sem=in_recv.at[t],
            device_id=at_peer(off), device_id_type=MESH).start())

    def in_wait(sem, t):
        blocks = xbuf.at[t, pl.ds(0, n - 1)]
        pltpu.make_async_copy(blocks, blocks, sem.at[t]).wait()

    @pl.when(first)
    def _():
        in_start(0)
        in_start(1)

    @pl.when(second)
    def _():
        x_copy(0).wait_recv()
        in_start(0)

    load.wait()
    for at in range(0, 2 * width, 128):
        wt[:, at:at + 128] = w[at:at + 128, :].T

    def ag_wait(buf, slot):
        def both(off):
            ag_copy(buf, slot, off).wait_send()
            ag_copy(buf, slot, off).wait_recv()
        over(n, both)

    def rs_wait():
        def both(off):
            rs_copy(off).wait_send()
            rs_copy(off).wait_recv()
        over(n, both)

    def forward(t, _):
        in_wait(in_recv, t)
        gscr[...] = jnp.dot(
            xbuf[t].reshape(total, width), w[:width, :], preferred_element_type=F32) + bias[...]

        @pl.when(t > 0)
        def _():
            ag_wait(hbuf, t)

        gscr[...] += jnp.dot(
            hbuf[t].reshape(total, width), w[width:, :], preferred_element_type=F32)

        def rows_step(k, _):
            at = pl.ds(pl.multiple_of(k * chunk, chunk), chunk)
            g = gscr[at, :]
            i = jax.nn.sigmoid(g[:, :cell])
            f = jax.nn.sigmoid(g[:, cell:2 * cell])
            m = jnp.tanh(g[:, 2 * cell:3 * cell])
            o = jax.nn.sigmoid(g[:, 3 * cell:])
            c = 3.0 * jnp.tanh((i * m + f * cells[t, at, :]) * (1.0 / 3.0))
            cells[t + 1, at, :] = c
            ebuf[t, at, :] = (o * jnp.tanh(c)).astype(BF)
            kind = gates.dtype
            gates[t, at, :cell] = i.astype(kind)
            gates[t, at, cell:2 * cell] = f.astype(kind)
            gates[t, at, 2 * cell:3 * cell] = m.astype(kind)
            gates[t, at, 3 * cell:] = o.astype(kind)
            return 0

        lax.fori_loop(0, total // chunk, rows_step, 0)
        q = jnp.dot(ebuf[t], p[...], preferred_element_type=F32)
        stage[...] = q.astype(BF).reshape(n, rows, width)
        over(n, lambda off: rs_copy(off).start())
        inbox[me] = stage[me]

        @pl.when(first & (t + 2 < steps))
        def _():
            in_start(t + 2)

        @pl.when(second & (t + 1 < steps))
        def _():
            x_copy(t + 1).wait_recv()
            in_start(t + 1)

        rs_wait()
        h = 3.0 * jnp.tanh(jnp.sum(inbox[...].astype(F32), axis=0) * (1.0 / 3.0))
        hown[t] = h
        hbuf[t + 1, me] = h.astype(BF)
        over(n, lambda off: ag_copy(hbuf, t + 1, off).start())

        @pl.when(first)
        def _():
            x_copy(t).start()

        add = jnp.where(second, 1.0, 0.0)
        out_ref[t] = (h + add * xbuf[t, me].astype(F32)).astype(BF)
        return 0

    lax.fori_loop(0, steps, forward, 0)
    ag_wait(hbuf, steps)

    lax.fori_loop(0, steps, lambda t, _: (in_wait(in_send, t), 0)[1], 0)

    @pl.when(first)
    def _():
        lax.fori_loop(0, steps, lambda t, _: (x_copy(t).wait_send(), 0)[1], 0)

    rown[...] = jnp.zeros((rows, width), F32)
    ucell[...] = jnp.zeros((total, cell), F32)
    dwacc[...] = jnp.zeros(dwacc.shape, F32)
    db_ref[...] = jnp.zeros(db_ref.shape, F32)
    dp_ref[...] = jnp.zeros(dp_ref.shape, F32)

    def dx_finish(t):
        slot = lax.rem(t, 2)

        def both(off):
            dx_copy(slot, off).wait_send()
            dx_copy(slot, off).wait_recv()
        over(n, both)
        dx = jnp.sum(inbox2[slot].astype(F32), axis=0)
        dx_ref[t] = dx

        @pl.when(second)
        def _():
            relay[t] = (dx + cot[t].astype(F32)).astype(BF)
            g_copy(t).start()

    def backward(k, _):
        t = steps - 1 - k
        slot = lax.rem(t, 2)
        up = rown[...] + cot[t].astype(F32)
        rown[...] = up

        @pl.when(first)
        def _():
            g_copy(t).wait_recv()
            rown[...] = rown[...] + gbuf[t].astype(F32)

        ratio = hown[t] * (1.0 / 3.0)
        dqbuf[t, me] = (rown[...] * (1.0 - ratio * ratio)).astype(BF)
        over(n, lambda off: ag_copy(dqbuf, t, off).start())

        @pl.when(k > 0)
        def _():
            dx_finish(t + 1)

        ag_wait(dqbuf, t)
        escr[...] = jnp.dot(
            dqbuf[t].reshape(total, width), pt[...], preferred_element_type=F32)

        def rows_step(j, _):
            at = pl.ds(pl.multiple_of(j * chunk, chunk), chunk)
            de = escr[at, :]
            i = gates[t, at, :cell].astype(F32)
            f = gates[t, at, cell:2 * cell].astype(F32)
            m = gates[t, at, 2 * cell:3 * cell].astype(F32)
            o = gates[t, at, 3 * cell:].astype(F32)
            c = cells[t + 1, at, :]
            tc = jnp.tanh(c)
            cr = c * (1.0 / 3.0)
            dc = (de * o * (1.0 - tc * tc) + ucell[at, :]) * (1.0 - cr * cr)
            ucell[at, :] = dc * f
            for block, value in enumerate((
                dc * m * i * (1.0 - i),
                dc * cells[t, at, :] * f * (1.0 - f),
                dc * i * (1.0 - m * m),
                de * tc * o * (1.0 - o),
            )):
                value = value.astype(BF)
                where = pl.ds(block * cell, cell)
                dabuf[0, at, where] = value
                db_ref[:, where] += jnp.sum(value.astype(F32), axis=0, keepdims=True)
            return 0

        lax.fori_loop(0, total // chunk, rows_step, 0)
        r = jnp.dot(dabuf[0], wt[:, width:], preferred_element_type=F32)
        stage[...] = r.astype(BF).reshape(n, rows, width)
        over(n, lambda off: rs_copy(off).start())
        inbox[me] = stage[me]
        dx = jnp.dot(dabuf[0], wt[:, :width], preferred_element_type=F32)
        stage2[slot] = dx.astype(BF).reshape(n, rows, width)
        over(n, lambda off: dx_copy(slot, off).start())
        inbox2[slot, me] = stage2[slot, me]
        for half, buf in enumerate((xbuf, hbuf)):
            dwacc[pl.ds(half * width, width), :] += lax.dot_general(
                buf[t].reshape(total, width), dabuf[0], (((0,), (0,)), ((), ())),
                preferred_element_type=F32)
        dp_ref[...] += lax.dot_general(
            ebuf[t], dqbuf[t].reshape(total, width), (((0,), (0,)), ((), ())),
            preferred_element_type=F32)
        rs_wait()
        rown[...] = jnp.sum(inbox[...].astype(F32), axis=0)
        return 0

    lax.fori_loop(0, steps, backward, 0)
    dx_finish(0)

    @pl.when(second)
    def _():
        lax.fori_loop(0, steps, lambda t, _: (g_copy(t).wait_send(), 0)[1], 0)

    def dw_copy(off):
        return pltpu.make_async_copy(
            dabuf.at[off % 2, pl.ds(0, each)], dw_out[off], st_sem.at[off % 2])

    for off in range(n):
        if off > 1:
            dw_copy(off - 2).wait()
        at = pl.multiple_of(lax.rem(me + off, n) * each, each)
        dabuf[off % 2, :each, :] = dwacc[pl.ds(at, each), :].astype(BF)
        dw_copy(off).start()
    for off in range(n - 2, n):
        dw_copy(off).wait()


def lstm_call(n, x, weights, bias, p, pt, cot, chunk=16):
    steps, rows, width = x.shape
    cell = p.shape[0]
    total = n * rows
    sds = jax.ShapeDtypeStruct
    vm = pl.BlockSpec(memory_space=pltpu.VMEM)
    hb = pl.BlockSpec(memory_space=pl.ANY)
    keep = F32 if n <= 8 else BF
    V = pltpu.VMEM
    dma = pltpu.SemaphoreType.DMA
    return pl.pallas_call(
        functools.partial(lstm_kernel, n, chunk),
        out_shape=(
            sds((steps, rows, width), BF), sds((steps, rows, width), F32),
            sds((1, 4 * cell), F32), sds((cell, width), F32),
            *[sds((2 * width // n, 4 * cell), BF)] * n),
        in_specs=[vm] * 5 + [hb],
        out_specs=[vm] * 4 + [hb] * n,
        scratch_shapes=[
            V((steps, n, rows, width), BF), V((steps + 1, n, rows, width), BF),
            V((steps, n, rows, width), BF), V((steps, total, 4 * cell), keep),
            V((steps + 1, total, cell), F32), V((steps, total, cell), BF),
            V((steps, rows, width), F32), V((total, 4 * cell), F32),
            V((total, cell), F32), V((2, total, 4 * cell), BF), V((total, cell), F32),
            V((2 * width, 4 * cell), F32), V((2 * width, 4 * cell), BF),
            V((4 * cell, 2 * width), BF),
            V((n, rows, width), BF), V((n, rows, width), BF),
            V((2, n, rows, width), BF), V((2, n, rows, width), BF),
            V((steps, rows, width), BF), V((steps, rows, width), BF), V((rows, width), F32),
            dma((steps,)), dma((steps,)), dma((n,)), dma((n,)), dma((n,)), dma((n,)), dma((n,)), dma((n,)), dma((2, n)), dma((2, n)),
            dma((steps,)), dma((steps,)), dma((steps,)), dma((steps,)), dma((2,)), dma,
        ],
        compiler_params=pltpu.CompilerParams(
            collective_id=0, has_side_effects=True, vmem_limit_bytes=60 * 1024 * 1024),
        cost_estimate=pl.CostEstimate(
            flops=300_000_000_000, bytes_accessed=64 * 1024 * 1024, transcendentals=0),
        name="relay_lstm",
    )(x, bias, p, pt, cot, weights)


def split_cells(weight, n):
    rows, gates = weight.shape
    cell = gates // (4 * n)
    wing = n // 2

    def body(src, keep, give):
        pipe = lax.axis_index("pipe")
        for k in range(wing):
            for dst, side in ((keep, pipe), (give, 1 - pipe)):
                at = pl.multiple_of((side * wing + k) * cell, cell)
                dst[k] = src[:, pl.ds(at, cell)].astype(BF)

    return pl.pallas_call(
        body,
        grid=(4,),
        out_shape=[jax.ShapeDtypeStruct((wing, rows, 4 * cell), BF)] * 2,
        in_specs=[pl.BlockSpec((rows, n * cell), lambda b: (0, b))],
        out_specs=[pl.BlockSpec((wing, rows, cell), lambda b: (0, 0, b))] * 2,
        cost_estimate=pl.CostEstimate(
            flops=0, bytes_accessed=6 * rows * gates, transcendentals=0
        ),
        name="split_cells",
    )(weight)


def join_cells(blocks):
    n = len(blocks)
    rows, gates = blocks[0].shape
    cell = gates // 4

    def body(*refs):
        dst = refs[n]
        for off in range(n):
            rank = lax.rem(lax.axis_index("dp") + (n - off), n)
            dst[:, pl.ds(pl.multiple_of(rank * cell, cell), cell)] = refs[off][...].astype(F32)

    return pl.pallas_call(
        body,
        grid=(4,),
        out_shape=jax.ShapeDtypeStruct((rows, n * gates), F32),
        in_specs=[pl.BlockSpec((rows, cell), lambda b: (0, b))] * n,
        out_specs=pl.BlockSpec((rows, n * cell), lambda b: (0, b)),
        cost_estimate=pl.CostEstimate(
            flops=0, bytes_accessed=6 * n * rows * gates, transcendentals=0
        ),
        name="join_cells",
    )(*blocks)


def swap_pipes(value):
    return lax.ppermute(value, "pipe", [(0, 1), (1, 0)])


def rank_pairs(n, off, layers=(0, 1)):
    wing = n // 2
    pairs = []
    for layer in layers:
        for j in range(n):
            rank = (j + off) % n
            pairs.append((layer * n + j, rank // wing * n + layer * wing + rank % wing))
    return pairs


def to_ranks(value, off):
    return lax.ppermute(value, ("pipe", "dp"), rank_pairs(lax.axis_size("dp"), off))


def from_ranks(value, off, layers=(0, 1)):
    pairs = rank_pairs(lax.axis_size("dp"), -off, layers)
    return lax.ppermute(value, ("pipe", "dp"), [(there, here) for here, there in pairs])


def conv_forward(ids, table_low, conv_low, valid_place):
    return jax.nn.logsumexp(conv_response(ids, table_low, conv_low, valid_place)[1], axis=1)


def own_half(value, blocks):
    sub = value.shape[-1] // (2 * blocks)
    split = value.reshape(*value.shape[:-1], blocks, 2, sub)
    mine = lax.dynamic_index_in_dim(split, lax.axis_index("pipe"), split.ndim - 2, keepdims=False)
    return mine.reshape(*value.shape[:-1], blocks * sub)


def both_halves(value, blocks):
    tokens, half = value.shape
    pair = lax.all_gather(value, "pipe").reshape(2, tokens, blocks, half // blocks)
    return jnp.transpose(pair, (1, 2, 0, 3)).reshape(tokens, 2 * half)


def conv_backward(ids, table_low, conv_low, masks, grad_before):
    weight_mask, valid_place = masks
    windows, response = conv_response(ids, table_low, conv_low, valid_place)
    share = jax.nn.softmax(response, axis=1)
    grad_response = (grad_before[:, None, :] * share).astype(BF)
    grad_conv = jnp.einsum("bpk,bpf->kf", windows, grad_response, preferred_element_type=F32)
    grad_windows = jnp.einsum("bpf,kf->bpk", grad_response, conv_low, preferred_element_type=F32)
    grad_embedded = jnp.zeros((ids.shape[0], CHARS + KMAX - 1, CDIM), F32)
    for offset in range(KMAX):
        grad_embedded = grad_embedded + jnp.pad(
            grad_windows[:, :, offset * CDIM : (offset + 1) * CDIM],
            ((0, 0), (offset, KMAX - 1 - offset), (0, 0)),
        )
    grad_embedded = grad_embedded[:, :CHARS].astype(BF)
    one_hot = (ids[:, :, None] == jnp.arange(CVOCAB, dtype=jnp.int32)).astype(BF)
    grad_table = jnp.einsum("bpv,bpc->vc", one_hot, grad_embedded, preferred_element_type=F32)
    return grad_conv * weight_mask, grad_table


def local(
    chars,
    lengths,
    char_emb,
    conv_weight,
    conv_bias,
    highway_weight,
    highway_bias,
    proj_weight,
    proj_bias,
    gate_weight,
    gate_bias,
    cell_proj,
    cotangent,
):
    n = lax.axis_size("dp")
    pipe = lax.axis_index("pipe")
    direction = lax.axis_index("dir")
    me = lax.axis_index("dp")
    everyone = lax.axis_size(ALL)
    holders = lax.axis_size(("dir", "dp"))
    seqs, steps, char_count = chars.shape
    group = seqs // lax.axis_size("dir")
    quarter = group // 2
    group_tokens = group * steps
    tokens = quarter * steps
    width = cell_proj.shape[3]
    cell = cell_proj.shape[2]
    blocks = holders // 2
    sub = FILTERS // holders
    half = FILTERS // 2
    filter_index = (
        (2 * jnp.arange(blocks, dtype=jnp.int32) + pipe)[:, None] * sub
        + jnp.arange(sub, dtype=jnp.int32)[None, :]
    ).reshape(half)
    masks = conv_masks(filter_index)

    proj_rows = proj_weight.shape[0]
    pieces = width // sub
    proj_blocks = jnp.transpose(proj_weight.reshape(proj_rows, pieces, sub), (1, 0, 2))
    proj_blocks = proj_blocks.reshape(2, pieces * proj_rows // 2, sub)
    mine = lax.dynamic_slice_in_dim(highway_weight, pipe * sub, sub, 2)
    gathered = lax.all_gather(
        jnp.concatenate([mine, proj_blocks], axis=1).astype(BF), ("dir", "dp"), axis=2, tiled=True
    )
    conv_full = lax.all_to_all(
        jnp.broadcast_to(conv_weight.astype(BF), (holders, KMAX * CDIM, sub)), ("dir", "dp"), 0, 0
    ).reshape(blocks, 2, KMAX * CDIM, sub)
    conv_low = lax.dynamic_index_in_dim(conv_full, pipe, 1, keepdims=False)
    conv_low = jnp.transpose(conv_low, (1, 0, 2)).reshape(KMAX * CDIM, half)
    conv_low = conv_low * masks[0].astype(BF)
    conv_bias_own = own_half(conv_bias, blocks)
    highway_bias_own = own_half(highway_bias.reshape(2, 2, FILTERS), blocks).reshape(2, FILTERS)

    def order_matrix(sizes):
        place = jnp.arange(steps, dtype=jnp.int32)[None, :]
        live = place < sizes[:, None]
        order = jnp.where(live & (direction == 1), sizes[:, None] - 1 - place, place)
        return ((order[:, :, None] == place[:, None, :]) & live[:, :, None]).astype(BF)

    own_order = order_matrix(lengths)
    cot = jnp.einsum("rts,rsd->trd", own_order, cotangent[0, 0], preferred_element_type=BF)

    ids = lax.dynamic_slice_in_dim(chars, direction * group, group, 0).reshape(
        group_tokens, char_count
    )
    table_low = char_emb.astype(BF)
    pooled = conv_forward(ids, table_low, conv_low, masks[1])
    features = jax.nn.silu(pooled + conv_bias_own)
    features_low = both_halves(features.astype(BF), blocks)
    bias_own = lax.dynamic_index_in_dim(
        gate_bias[0, 0].reshape(4, n, cell), me, 1, keepdims=False
    ).reshape(1, 4 * cell)
    moved = jnp.concatenate([cell_proj[0, 0].astype(BF), cot.reshape(steps * seqs, width)])
    gate_kept, gate_given = split_cells(gate_weight[0, 0], n)
    gate_came = swap_pipes(gate_given)
    gate_low = jnp.concatenate(
        [
            jnp.where(pipe == 0, gate_kept, gate_came),
            jnp.where(pipe == 0, gate_came, gate_kept),
        ]
    )
    direct, local_part = moved[: moved.shape[0] // 2], moved[moved.shape[0] // 2 :]
    swapped = swap_pipes(local_part)
    gate_low, gathered, features_low, bias_own, direct, swapped = lax.optimization_barrier(
        (gate_low, gathered, features_low, bias_own, direct, swapped)
    )
    bias_own = to_ranks(bias_own, 0)
    wing = n // 2
    swapped = lax.ppermute(
        swapped,
        ("pipe", "dp"),
        [(k, wing + k) for k in range(wing)] + [(n + wing + k, n + k) for k in range(wing)],
    )
    moved = jnp.concatenate(
        [to_ranks(direct, 0), jnp.where(lax.div(me, wing) == pipe, local_part, swapped)]
    )
    gate_own = lax.all_to_all(gate_low, "dp", 0, 0).reshape(2 * width, 4 * cell)
    highway_half = gathered[:, :FILTERS]
    proj_full = gathered[:, FILTERS:].reshape(pieces, proj_rows, holders, sub)
    proj_full = jnp.transpose(proj_full, (2, 1, 0, 3)).reshape(FILTERS, width)

    kept = [features]
    kept_low = [features_low]
    mixed = []
    for layer in range(2):
        pre = (
            jnp.dot(kept_low[layer], highway_half[layer], preferred_element_type=F32)
            + highway_bias_own[layer]
        )
        mixed.append(pre)
        gate = jax.nn.sigmoid(pre[:, half:])
        features = gate * features + (1.0 - gate) * jax.nn.silu(pre[:, :half])
        kept.append(features)
        kept_low.append(both_halves(features.astype(BF), blocks))
    own_last = lax.dynamic_slice_in_dim(kept_low[2], pipe * tokens, tokens, 0)
    encoded = jnp.dot(own_last, proj_full, preferred_element_type=F32) + proj_bias
    encoded_own = lax.all_gather(
        encoded.astype(BF).reshape(quarter, steps, width), ("dir", "pipe"), axis=0, tiled=True
    )
    inputs = jnp.einsum("rts,rsd->trd", own_order, encoded_own, preferred_element_type=BF)
    inputs = lax.ppermute(
        inputs,
        ("pipe", "dp"),
        [(k, wing + k) for k in range(wing)] + [(n + k, n + k) for k in range(wing, n)],
    )
    kept_low, gate_own, inputs, moved, bias_own = lax.optimization_barrier(
        (kept_low, gate_own, inputs, moved, bias_own)
    )
    cell_low = moved[:cell]
    cot = moved[cell:].reshape(steps, seqs, width)
    kept_all = [
        lax.all_gather(
            lax.dynamic_slice_in_dim(value, pipe * tokens, tokens, 0),
            ("dir", "dp"),
            axis=0,
            tiled=True,
        )
        for value in kept_low[:2]
    ]

    out_own, dx_own, grad_bias, grad_cell, *grad_gate = lstm_call(
        n, inputs, gate_own, bias_own, cell_low, cell_low.T, cot
    )
    dx_own = from_ranks(dx_own.astype(BF), 0, (1,))
    grad_gate = [from_ranks(block, off) for off, block in enumerate(grad_gate)]
    dx_own, kept_all = lax.optimization_barrier((dx_own, kept_all))

    grad_stored = jnp.einsum(
        "rts,srd->rtd", own_order, dx_own, preferred_element_type=F32
    )
    grad_stored = jnp.where(pipe == 1, grad_stored, 0.0).astype(BF)
    grad_stored = grad_stored.reshape(1, -1, group_tokens, width)
    grad_encoded = lax.all_to_all(
        jnp.concatenate([grad_stored, grad_stored]).reshape(-1, group_tokens, width),
        ("pipe", "dir"),
        0,
        0,
    )
    grad_encoded = jnp.sum(grad_encoded.astype(F32), axis=0).astype(BF)
    own_grads = lax.dynamic_slice_in_dim(grad_encoded, pipe * tokens, tokens, 0)
    encoded_grads = lax.all_gather(own_grads, ("dir", "dp"), axis=0, tiled=True)

    grad_proj_bias = jnp.sum(own_grads.astype(F32), axis=0)
    proj_half = lax.dynamic_index_in_dim(
        proj_full.reshape(blocks, 2, sub, width), pipe, 1, keepdims=False
    ).reshape(half, width)
    grad_features = jnp.einsum("td,fd->tf", grad_encoded, proj_half, preferred_element_type=F32)
    columns = [None, None]
    grad_highway_bias = [None, None]
    for layer in (1, 0):
        nonlinear = mixed[layer][:, :half]
        gate = jax.nn.sigmoid(mixed[layer][:, half:])
        grad_mixed = jnp.concatenate(
            [
                grad_features * (1.0 - gate) * silu_slope(nonlinear),
                grad_features * (kept[layer] - jax.nn.silu(nonlinear)) * gate * (1.0 - gate),
            ],
            axis=1,
        ).astype(BF)
        columns[layer] = grad_mixed
        grad_highway_bias[layer] = jnp.sum(grad_mixed.astype(F32), axis=0)
        partial = jnp.einsum(
            "tg,fg->tf", grad_mixed, highway_half[layer], preferred_element_type=F32
        )
        partial = lax.optimization_barrier(partial).reshape(group_tokens, blocks, 2, sub)
        sent = lax.dynamic_index_in_dim(partial, 1 - pipe, 2, keepdims=False).astype(BF)
        came = lax.ppermute(sent, "pipe", [(0, 1), (1, 0)])
        mine = lax.dynamic_index_in_dim(partial, pipe, 2, keepdims=False)
        grad_features = grad_features * gate + (mine + came.astype(F32)).reshape(
            group_tokens, half
        )
    grad_before = grad_features * silu_slope(pooled + conv_bias_own)
    grad_before, grad_gate[1:5] = lax.optimization_barrier((grad_before, grad_gate[1:5]))
    grad_conv, grad_table = conv_backward(ids, table_low, conv_low, masks, grad_before)

    def spread(value):
        split = value.reshape(*value.shape[:-1], -1, 1, sub)
        shown = jnp.arange(2, dtype=jnp.int32)[:, None] == pipe
        return jnp.where(shown, split, jnp.zeros_like(split)).reshape(*value.shape[:-1], -1)

    cols = FILTERS // everyone
    pair = jnp.stack(columns, axis=1).reshape(2, tokens, 2, 2, blocks, 1, sub)
    sent = lax.dynamic_index_in_dim(pair, 1 - pipe, 0, keepdims=False)
    came = lax.ppermute(sent, "pipe", [(0, 1), (1, 0)])
    mine = lax.dynamic_index_in_dim(pair, pipe, 0, keepdims=False)
    shown = (jnp.arange(2, dtype=jnp.int32) == pipe)[:, None]
    pair = jnp.where(shown, mine, came)
    pair = jnp.transpose(pair, (3, 4, 0, 1, 2, 5)).reshape(holders, tokens, 4 * sub)
    last = jnp.transpose(own_last.reshape(tokens, 2, holders, cols), (2, 0, 1, 3))
    pair = jnp.concatenate([pair, last.reshape(holders, tokens, 2 * cols)], axis=2)
    pair = lax.all_to_all(pair, ("dir", "dp"), 0, 0).reshape(holders * tokens, -1)
    grad_conv, pair = lax.optimization_barrier((grad_conv, pair))
    small = (
        grad_table,
        spread(jnp.sum(grad_before, axis=0)),
        spread(jnp.stack(grad_highway_bias)),
        grad_proj_bias,
    )
    flat = jnp.concatenate([value.reshape(-1) for value in small])
    share = -(-flat.shape[0] // (everyone * 128)) * 128
    flat = jnp.pad(flat, (0, share * everyone - flat.shape[0])).reshape(everyone, share)
    rank = pipe * wing + lax.rem(me, wing)
    mine = jnp.arange(n, dtype=jnp.int32)[None, :, None] == rank
    bias_parts = jnp.where(mine, grad_bias.reshape(4, 1, cell), 0.0).reshape(1, n, 4 * cell)
    layer = lax.div(me, wing) * lax.axis_size("dir") + direction
    mine = jnp.arange(everyone // n, dtype=jnp.int32) == layer
    bias_parts = jnp.where(mine[:, None, None], bias_parts, 0.0).reshape(everyone, 4 * cell)
    packed = jnp.concatenate(
        [
            jnp.transpose(
                spread(grad_conv).reshape(KMAX * CDIM, everyone, cols), (1, 0, 2)
            ).reshape(everyone, KMAX * CDIM * cols),
            flat,
            bias_parts,
        ],
        axis=1,
    ).astype(BF)
    summed = jnp.sum(lax.all_to_all(packed, ALL, 0, 0).astype(F32), axis=0)
    summed, grad_gate, out_own, grad_cell = lax.optimization_barrier(
        (summed, grad_gate, out_own, grad_cell)
    )
    out_own = from_ranks(out_own, 0)
    grad_cell = from_ranks(grad_cell.astype(BF), 0)
    activations = jnp.einsum("rts,srd->rtd", own_order, out_own, preferred_element_type=BF)
    grad_cell = grad_cell.astype(F32)
    grad_gate = join_cells(grad_gate)
    grad_conv = summed[: KMAX * CDIM * cols].reshape(KMAX * CDIM, cols)
    grad_bias = summed[KMAX * CDIM * cols + share :]
    last = pair[:, 4 * sub :].reshape(holders * tokens, 2, cols)
    pair = pair[:, : 4 * sub].reshape(holders * tokens, 2, 2, sub)

    def partial_sums(owner):
        return [
            jnp.einsum(
                "tf,tg->fg",
                kept_all[layer],
                lax.dynamic_index_in_dim(pair[:, layer], owner, 1, keepdims=False),
                preferred_element_type=F32,
            )
            for layer in range(2)
        ] + [
            jnp.einsum(
                "tf,td->fd",
                lax.dynamic_index_in_dim(last, owner, 1, keepdims=False),
                encoded_grads,
                preferred_element_type=F32,
            )
        ]

    sent = jnp.concatenate(
        [value.astype(BF).reshape(-1, sub) for value in partial_sums(1 - pipe)]
    )
    came = lax.ppermute(sent, "pipe", [(0, 1), (1, 0)]).astype(F32)
    mine = partial_sums(pipe)
    grad_highway = jnp.stack(mine[:2]) + came[: 2 * FILTERS].reshape(2, FILTERS, sub)
    grad_proj = mine[2] + came[2 * FILTERS :].reshape(cols, width)
    shared = lax.all_to_all(
        jnp.broadcast_to(summed[KMAX * CDIM * cols :][:share], (everyone, share)), ALL, 0, 0
    ).reshape(-1)
    small_sums = []
    start = 0
    for value in small:
        small_sums.append(shared[start : start + value.size].reshape(value.shape))
        start += value.size
    return (
        activations[None, None],
        small_sums[0],
        grad_conv,
        small_sums[1],
        grad_highway,
        small_sums[2],
        grad_proj,
        small_sums[3],
        grad_gate[None, None],
        grad_bias[None, None],
        grad_cell[None, None],
    )


def solution(mesh):
    return jax.shard_map(
        local,
        mesh=mesh,
        in_specs=(
            P("dp", None, None),
            P("dp"),
            P(),
            P(None, ("dir", "dp")),
            P(),
            P(None, None, ("dir", "dp")),
            P(),
            P(("dir", "dp"), None),
            P(),
            P("pipe", "dir", "dp", None),
            P("pipe", "dir", None),
            P("pipe", "dir", "dp", None),
            P("pipe", "dir", "dp", None, None),
        ),
        out_specs=(
            P("pipe", "dir", "dp", None, None),
            P(),
            P(None, ("pipe", "dir", "dp")),
            P(),
            P(None, None, ("pipe", "dir", "dp")),
            P(),
            P(("pipe", "dir", "dp"), None),
            P(),
            P("pipe", "dir", "dp", None),
            P("pipe", "dir", "dp"),
            P("pipe", "dir", "dp", None),
        ),
        check_vma=False,
    )
```
